32 devices in a mesh: dp: 16 (over z, y, x), rep: 2 (over core).
Axes of the slice: x: 2, y: 2, z: 4, core: 2. Of those that a mesh axis runs over, the one named last changes fastest.
Arguments:
- patches: bfloat16 [192, 196, 768], P(('dp', 'rep')), may hold values from -6 to 6
- targets: bfloat16 [192, 196, 768], P(('dp', 'rep')), may hold values from -5.5 to 5.5
- keep: int32 [192, 49], P(('dp', 'rep')), may hold values from 0 to 195, as said below
- counts: int32 [16, 2], P('dp', 'rep'), may hold values from 1 to 6, as said below
- step: int32 [1], replicated, may hold values from 2 to 20
- master: float32 [1629760], P(('dp', 'rep')), may hold values from -2.5 to 2.5
- first: float32 [1629760], P(('dp', 'rep')), may hold values from -0.00046999087 to 0.00046999087
- second: float32 [1629760], P(('dp', 'rep')), may hold values from 1.5339682e-09 to 9.817396e-08
Outputs:
- new_master: float32 [1629760], P(('dp', 'rep'))
- new_first: float32 [1629760], P(('dp', 'rep'))
- new_second: float32 [1629760], P(('dp', 'rep'))
- copy: bfloat16 [1629760], P(('dp', 'rep'))
- loss: float32 [], replicated
- norm: float32 [], replicated
The draws below stay inside these ranges and needn't reach their ends.
Inputs may be any that keep to these rules, and one draw needn't show every extreme that they name: `keep`: each row lists 49 distinct patch numbers of one image. A device's live image slots are its first counts[d, r]. In each aligned group of four devices along dp (for each r) exactly one device, never the first or last of the group, holds 3 to 6 live images; the others hold 1 or 2. Some device holds 6 in every draw.
All inputs are finite; a program needn't handle non-finite values.
Results may differ from the reference program's by a relative error of at most 0.0081.
Values may be sent and summed in bfloat16 or wider, within the bound.
A program may use at most 128 MiB of HBM per device.

```python
import math
import jax
import jax.numpy as jnp
from jax import lax

D = 192
HEADS = 3
FF = 768
E = 256
DHEADS = 8
DFF = 1024
PIX = 768
GRID = 14
VIS = 49
IMG_CAP = 6
NP = 196
IMAGES = 192
PRAW = 1629760
P_SIZE = 1629760
N_DP = 16
N_REP = 2


def block_table_drawn(prefix, width, hidden, proj_fan, rate):
    return [(prefix + 'ln1g', (width,), 'gain', 1, rate), (prefix + 'ln1b', (width,), 'bias', 1, rate), (prefix + 'qkv', (width, 3 * width), 'matrix', width, rate), (prefix + 'qvb', (2 * width,), 'bias', 1, rate), (prefix + 'proj', (width, width), 'matrix', proj_fan, rate), (prefix + 'projb', (width,), 'bias', 1, rate), (prefix + 'ln2g', (width,), 'gain', 1, rate), (prefix + 'ln2b', (width,), 'bias', 1, rate), (prefix + 'fc1', (width, hidden), 'matrix', width, rate), (prefix + 'fc1b', (hidden,), 'bias', 1, rate), (prefix + 'fc2', (hidden, width), 'matrix', hidden, rate), (prefix + 'fc2b', (width,), 'bias', 1, rate)]


def param_table_drawn():
    table = [('patch', (PIX, D), 'matrix', PIX, 0.75), ('patchb', (D,), 'bias', 1, 0.75)]
    table = table + block_table_drawn('enc_', D, FF, D // 4, 0.9)
    table = table + [('encg', (D,), 'gain', 1, 1.0), ('encb', (D,), 'bias', 1, 1.0), ('embed', (D, E), 'matrix', D, 1.0), ('embedb', (E,), 'bias', 1, 1.0), ('mask', (E,), 'token', 1, 1.0)]
    table = table + block_table_drawn('dec_', E, DFF, E // 8, 1.0)
    table = table + [('decg', (E,), 'gain', 1, 1.0), ('decb', (E,), 'bias', 1, 1.0), ('head', (E, PIX), 'matrix', E, 1.0), ('headb', (PIX,), 'bias', 1, 1.0)]
    return table


def clipped_normal(key, shape):
    return jnp.clip(jax.random.normal(key, shape, jnp.float32), -4.0, 4.0)


def draw_master(key, part):
    pieces = []
    base = jax.random.fold_in(key, 11)
    for number, (name, shape, kind, fan, rate) in enumerate(param_table_drawn()):
        noise = clipped_normal(jax.random.fold_in(base, number), (math.prod(shape),))
        if kind == 'matrix':
            pieces.append(noise * fan ** (-0.5))
        elif kind == 'gain':
            pieces.append(1.0 + 0.1 * noise)
        elif kind == 'bias':
            pieces.append(0.3 * noise)
        else:
            pieces.append(0.5 * noise)
    pieces.append(0.5 * clipped_normal(jax.random.fold_in(base, 999), (P_SIZE - PRAW,)))
    return jnp.concatenate(pieces)


def moment_scale():
    pieces = []
    base = 0.05 * P_SIZE ** (-0.5)
    for name, shape, kind, fan, rate in param_table_drawn():
        pieces.append(jnp.full((math.prod(shape),), base if kind == 'matrix' else 4.0 * base, jnp.float32))
    pieces.append(jnp.full((P_SIZE - PRAW,), 4.0 * base, jnp.float32))
    return jnp.concatenate(pieces)


def draw_first(key, part):
    noise = jnp.clip(jax.random.normal(jax.random.fold_in(key, 12), (P_SIZE,), jnp.float32), -3.0, 3.0)
    return moment_scale() * noise


def draw_second(key, part):
    factor = jax.random.uniform(jax.random.fold_in(key, 13), (P_SIZE,), jnp.float32, 1.0, 4.0)
    scale = moment_scale()
    return scale * scale * factor


def draw_targets(key, part):
    noise_key, shift_key = jax.random.split(jax.random.fold_in(key, 21))
    noise = clipped_normal(noise_key, (IMAGES, NP, PIX))
    offset = jax.random.uniform(shift_key, (PIX,), jnp.float32, -1.0, 1.0)
    return (noise + offset).astype(jnp.bfloat16)


def draw_keep(key, part):

    def one_image(sub):
        return jax.random.permutation(sub, NP)[:VIS].astype(jnp.int32)
    return jax.vmap(one_image)(jax.random.split(jax.random.fold_in(key, 31), IMAGES))


def draw_counts(key, part):
    light_key, heavy_key, top_key, hub_key = jax.random.split(jax.random.fold_in(key, 41), 4)
    groups = N_DP // 4
    light = jax.random.randint(light_key, (N_DP, N_REP), 1, 3)
    heavy = jax.random.randint(heavy_key, (groups, N_REP), 3, IMG_CAP + 1)
    top = jax.random.randint(top_key, (N_REP,), 0, groups)
    heavy = jnp.where(jnp.arange(groups)[:, None] == top[None, :], IMG_CAP, heavy)
    hub = jax.random.randint(hub_key, (groups, N_REP), 1, 3)
    place = jnp.arange(N_DP) % 4
    group = jnp.arange(N_DP) // 4
    is_hub = place[:, None] == hub[group]
    return jnp.where(is_hub, heavy[group], light).astype(jnp.int32)


def block_levels(rng, shape, cuts, least, top_value):
    def one(dim, blocks):
        heights = jax.random.uniform(jax.random.fold_in(jax.random.fold_in(rng, 6), dim), (blocks,), jnp.float32, least / len(cuts), top_value / len(cuts))
        return jnp.repeat(jnp.exp(heights), shape[dim] // blocks).reshape((-1,) + (1,) * (len(shape) - dim - 1))

    factor_of = one(*cuts[0])
    for cut in cuts[1:]:
        factor_of = factor_of * one(*cut)
    return factor_of


def gaussian(rng, shape, scale, reach, cuts=(), held_as=jnp.bfloat16):
    array = jax.random.normal(rng, shape, jnp.float32) * scale
    if len(cuts) > 0:
        array = block_levels(rng, shape, cuts, -0.22, 0.18) * array
    return jnp.clip(array, min=-reach, max=reach).astype(held_as)


def setup_inputs(seed: int = 0) -> dict:
    streams_of = jax.random.split(jax.random.key(seed), 9)
    return {
        "patches": gaussian(streams_of[0], (IMAGES, NP, PIX), 1.0, 6.0, ((0, 32),)),
        "targets": draw_targets(jax.random.fold_in(streams_of[8], 71), 0),
        "keep": draw_keep(jax.random.fold_in(streams_of[8], 71), 0),
        "counts": draw_counts(jax.random.fold_in(streams_of[8], 71), 0),
        "step": jax.random.randint(streams_of[4], (1,), 2, 21).astype(jnp.int32),
        "master": draw_master(jax.random.fold_in(streams_of[8], 71), 0),
        "first": draw_first(jax.random.fold_in(streams_of[8], 71), 0),
        "second": draw_second(jax.random.fold_in(streams_of[8], 71), 0),
    }


@jax.custom_vjp
def low(v):
    return lax.optimization_barrier(v.astype(jnp.bfloat16)).astype(jnp.float32)

@jax.custom_vjp
def low_back(v):
    return v

def low_keep(v):
    return (low(v), None)

def low_pass(kept, grad):
    return (grad,)

def back_keep(v):
    return (v, None)

def back_low(kept, grad):
    return (low(grad),)
low.defvjp(low_keep, low_pass)
low_back.defvjp(back_keep, back_low)
HIGH = lax.Precision.HIGHEST
CLIP = 0.05
BETA_ONE = 0.5
BETA_TWO = 0.5
LEARN = 0.01
DECAY = 0.05
EPSILON = 1e-08
LN_EPS = 1e-06

def block_table(prefix, width, hidden, proj_fan, rate):
    return [(prefix + 'ln1g', (width,), 'gain', 1, rate), (prefix + 'ln1b', (width,), 'bias', 1, rate), (prefix + 'qkv', (width, 3 * width), 'matrix', width, rate), (prefix + 'qvb', (2 * width,), 'bias', 1, rate), (prefix + 'proj', (width, width), 'matrix', proj_fan, rate), (prefix + 'projb', (width,), 'bias', 1, rate), (prefix + 'ln2g', (width,), 'gain', 1, rate), (prefix + 'ln2b', (width,), 'bias', 1, rate), (prefix + 'fc1', (width, hidden), 'matrix', width, rate), (prefix + 'fc1b', (hidden,), 'bias', 1, rate), (prefix + 'fc2', (hidden, width), 'matrix', hidden, rate), (prefix + 'fc2b', (width,), 'bias', 1, rate)]

def param_table():
    table = [('patch', (PIX, D), 'matrix', PIX, 0.75), ('patchb', (D,), 'bias', 1, 0.75)]
    table = table + block_table('enc_', D, FF, D // 4, 0.9)
    table = table + [('encg', (D,), 'gain', 1, 1.0), ('encb', (D,), 'bias', 1, 1.0), ('embed', (D, E), 'matrix', D, 1.0), ('embedb', (E,), 'bias', 1, 1.0), ('mask', (E,), 'token', 1, 1.0)]
    table = table + block_table('dec_', E, DFF, E // 8, 1.0)
    table = table + [('decg', (E,), 'gain', 1, 1.0), ('decb', (E,), 'bias', 1, 1.0), ('head', (E, PIX), 'matrix', E, 1.0), ('headb', (PIX,), 'bias', 1, 1.0)]
    return table

def unpack(flat):
    parts = {}
    offset = 0
    for name, shape, kind, fan, rate in param_table():
        size = math.prod(shape)
        parts[name] = flat[offset:offset + size].reshape(shape)
        offset += size
    return parts

def factor_vectors():
    rate_list = []
    decay_list = []
    for name, shape, kind, fan, rate in param_table():
        size = math.prod(shape)
        rate_list.append(jnp.full((size,), rate, jnp.float32))
        decay_list.append(jnp.full((size,), DECAY if kind == 'matrix' else 0.0, jnp.float32))
    rate_list.append(jnp.full((P_SIZE - PRAW,), 1.0, jnp.float32))
    decay_list.append(jnp.zeros((P_SIZE - PRAW,), jnp.float32))
    return (jnp.concatenate(rate_list), jnp.concatenate(decay_list))

def layer_norm(value, gain, shift):
    center = value - lax.optimization_barrier(jnp.mean(value, axis=-1, keepdims=True))
    spread = lax.optimization_barrier(jnp.mean(center * center, axis=-1, keepdims=True))
    return center * lax.rsqrt(spread + LN_EPS) * gain + shift

def sincos(index, width):
    quarter = width // 4
    omega = 1.0 / 10000.0 ** (jnp.arange(quarter).astype(jnp.float32) / quarter)
    across = (index // GRID).astype(jnp.float32)[..., None] * omega
    along = (index % GRID).astype(jnp.float32)[..., None] * omega
    return jnp.concatenate([jnp.sin(across), jnp.cos(across), jnp.sin(along), jnp.cos(along)], axis=-1)

def attention_block(hidden, params, prefix, heads):
    count, length, width = hidden.shape
    size = width // heads
    normed = low(layer_norm(hidden, params[prefix + 'ln1g'], params[prefix + 'ln1b']))
    bias = params[prefix + 'qvb']
    full_bias = jnp.concatenate([bias[:width], jnp.zeros((width,), jnp.float32), bias[width:]])
    projected = low(low_back(jnp.dot(normed, params[prefix + 'qkv'], precision=HIGH) + full_bias))
    shaped = projected.reshape(count, length, 3, heads, size)
    query, keys, values = (shaped[:, :, 0], shaped[:, :, 1], shaped[:, :, 2])
    scores = low_back(jnp.einsum('nqhc,nkhc->nhqk', query, keys, precision=HIGH) * size ** (-0.5))
    attend = low(jax.nn.softmax(scores, axis=-1))
    mixed = jnp.einsum('nhqk,nkhc->nqhc', attend, values, precision=HIGH).reshape(count, length, width)
    mixed = low(low_back(mixed))
    middle = hidden + low_back(jnp.dot(mixed, params[prefix + 'proj'], precision=HIGH) + params[prefix + 'projb'])
    second = low(layer_norm(middle, params[prefix + 'ln2g'], params[prefix + 'ln2b']))
    inner = low_back(jnp.dot(second, params[prefix + 'fc1'], precision=HIGH) + params[prefix + 'fc1b'])
    active = low(jax.nn.gelu(inner, approximate=False))
    return middle + low_back(jnp.dot(active, params[prefix + 'fc2'], precision=HIGH) + params[prefix + 'fc2b'])

def group_loss(params, patch_rows, target_rows, keep_rows, live_rows):
    patch_rows = patch_rows.astype(jnp.float32)
    target_rows = target_rows.astype(jnp.float32)
    visible = jnp.take_along_axis(patch_rows, keep_rows[:, :, None], axis=1)
    start = jnp.dot(visible, params['patch'], precision=HIGH) + params['patchb'] + sincos(keep_rows, D)
    start = low_back(start)
    encoded = attention_block(start, params, 'enc_', HEADS)
    encoded = low(low_back(layer_norm(encoded, params['encg'], params['encb'])))
    embedded = low_back(jnp.dot(encoded, params['embed'], precision=HIGH) + params['embedb'])
    placement = (keep_rows[:, :, None] == jnp.arange(NP)[None, None, :]).astype(jnp.float32)
    seen = lax.optimization_barrier(jnp.sum(placement, axis=1))
    grid_in = jnp.einsum('gvp,gve->gpe', placement, embedded, precision=HIGH)
    grid_in = grid_in + (1.0 - seen)[:, :, None] * params['mask'] + sincos(jnp.arange(NP), E)
    decoded = attention_block(grid_in, params, 'dec_', DHEADS)
    final = low(layer_norm(decoded, params['decg'], params['decb']))
    predicted = low_back(jnp.dot(final, params['head'], precision=HIGH) + params['headb'])
    error = predicted - target_rows
    weight = (0.1 * seen + (1.0 - seen)) * live_rows[:, None]
    return jnp.sum(weight * lax.optimization_barrier(jnp.mean(error * error, axis=-1)))

def reference(patches, targets, keep, counts, step, master, first, second):
    images = patches.shape[0]
    group_size = 4 * IMG_CAP
    groups = images // group_size
    live = (jnp.arange(images) % IMG_CAP < jnp.repeat(counts.reshape(-1), IMG_CAP)).astype(jnp.float32)
    stacked = (patches.reshape(groups, group_size, NP, PIX), targets.reshape(groups, group_size, NP, PIX), keep.reshape(groups, group_size, VIS), live.reshape(groups, group_size))

    def total_loss(flat):
        params = unpack(low(flat))

        def one_group(carry, inputs):
            return (carry + jax.checkpoint(group_loss)(params, *inputs), None)
        total, unused = lax.scan(one_group, jnp.zeros((), jnp.float32), stacked)
        return total
    loss_sum, pull = jax.vjp(total_loss, master)
    raw, = pull(jnp.ones((), jnp.float32))
    weight_total = jnp.sum(live) * (0.1 * VIS + (NP - VIS))
    gradient = raw / weight_total
    norm = jnp.sqrt(jnp.sum(gradient * gradient))
    clipped = gradient * jnp.minimum(1.0, CLIP / norm)
    new_first = BETA_ONE * first + (1.0 - BETA_ONE) * clipped
    new_second = BETA_TWO * second + (1.0 - BETA_TWO) * clipped * clipped
    count = step[0].astype(jnp.float32)
    first_hat = new_first / (1.0 - jnp.power(BETA_ONE, count))
    second_hat = new_second / (1.0 - jnp.power(BETA_TWO, count))
    rate_part, decay_part = factor_vectors()
    new_master = master - LEARN * rate_part * (first_hat / (jnp.sqrt(second_hat) + EPSILON) + decay_part * master)
    return (new_master, new_first, new_second, new_master.astype(jnp.bfloat16), loss_sum / weight_total, norm)
```

```python
import functools
import itertools
import math

import jax
import jax.numpy as jnp
from jax import lax
from jax.experimental import pallas as pl
from jax.experimental.pallas import tpu as pltpu
from jax.sharding import PartitionSpec as P

D = 192
HEADS = 3
FF = 768
E = 256
DHEADS = 8
DFF = 1024
PIX = 768
GRID = 14
VIS = 49
SLOT = 64
NP = 196


HIGH = lax.Precision.HIGHEST
FLOAT = jnp.float32
BRAIN = jnp.bfloat16
CLIP = 0.05
BETA_ONE = 0.5
BETA_TWO = 0.5
LEARN = 0.01
DECAY = 0.05
EPSILON = 1e-08
LN_EPS = 1e-06


def as_sent(array):

    def short(part):
        return part.astype(jnp.bfloat16) if part.dtype == jnp.float32 else part

    return jax.tree.map(short, array)


def block_table(prefix, width, hidden, proj_fan, rate):
    return [
        (prefix + "ln1g", (width,), "gain", 1, rate),
        (prefix + "ln1b", (width,), "bias", 1, rate),
        (prefix + "qkv", (width, 3 * width), "matrix", width, rate),
        (prefix + "qvb", (2 * width,), "bias", 1, rate),
        (prefix + "proj", (width, width), "matrix", proj_fan, rate),
        (prefix + "projb", (width,), "bias", 1, rate),
        (prefix + "ln2g", (width,), "gain", 1, rate),
        (prefix + "ln2b", (width,), "bias", 1, rate),
        (prefix + "fc1", (width, hidden), "matrix", width, rate),
        (prefix + "fc1b", (hidden,), "bias", 1, rate),
        (prefix + "fc2", (hidden, width), "matrix", hidden, rate),
        (prefix + "fc2b", (width,), "bias", 1, rate),
    ]


def param_table():
    table = [("patch", (PIX, D), "matrix", PIX, 0.75), ("patchb", (D,), "bias", 1, 0.75)]
    table = table + block_table("enc_", D, FF, D // 4, 0.9)
    table = table + [
        ("encg", (D,), "gain", 1, 1.0),
        ("encb", (D,), "bias", 1, 1.0),
        ("embed", (D, E), "matrix", D, 1.0),
        ("embedb", (E,), "bias", 1, 1.0),
        ("mask", (E,), "token", 1, 1.0),
    ]
    table = table + block_table("dec_", E, DFF, E // 8, 1.0)
    table = table + [
        ("decg", (E,), "gain", 1, 1.0),
        ("decb", (E,), "bias", 1, 1.0),
        ("head", (E, PIX), "matrix", E, 1.0),
        ("headb", (PIX,), "bias", 1, 1.0),
    ]
    return table


def unpack(flat):
    parts = {}
    offset = 0
    for name, shape, kind, fan, rate in param_table():
        size = math.prod(shape)
        parts[name] = flat[offset : offset + size].reshape(shape)
        offset += size
    return parts


def shard_factors(start, length):
    index = start + jnp.arange(length, dtype=jnp.int32)
    rate_part = jnp.ones((length,), FLOAT)
    decay_part = jnp.zeros((length,), FLOAT)
    offset = 0
    for name, shape, kind, fan, rate in param_table():
        size = math.prod(shape)
        inside = (index >= offset) & (index < offset + size)
        rate_part = jnp.where(inside, rate, rate_part)
        decay_part = jnp.where(inside, DECAY if kind == "matrix" else 0.0, decay_part)
        offset += size
    return (rate_part, decay_part)


def layer_norm(value, gain, shift):
    center = value - jnp.mean(value, axis=-1, keepdims=True)
    spread = jnp.mean(center * center, axis=-1, keepdims=True)
    return center * lax.rsqrt(spread + LN_EPS) * gain + shift


def sincos(index, width):
    quarter = width // 4
    omega = 1.0 / 10000.0 ** (jnp.arange(quarter).astype(FLOAT) / quarter)
    across = (index // GRID).astype(FLOAT)[..., None] * omega
    along = (index % GRID).astype(FLOAT)[..., None] * omega
    return jnp.concatenate(
        [jnp.sin(across), jnp.cos(across), jnp.sin(along), jnp.cos(along)], axis=-1
    )


def gelu_exact(value):
    return jax.nn.gelu(value, approximate=False)


def matmul(left, right):
    return jnp.dot(left, right, preferred_element_type=FLOAT)


def matmul_back(grad, weight):
    return jnp.einsum("nlj,ij->nli", grad, weight, preferred_element_type=FLOAT)


def outer_sum(left, right):
    return jnp.einsum("nli,nlj->ij", left, right, preferred_element_type=FLOAT)


def column_sum(grad):
    return jnp.sum(grad.astype(FLOAT), axis=(0, 1))


def split_heads(projected, heads):
    count, length, triple = projected.shape
    shaped = projected.reshape(count, length, 3, heads, triple // (3 * heads))
    return (shaped[:, :, 0], shaped[:, :, 1], shaped[:, :, 2])


def scaled_scores(query, keys, usable):
    size = query.shape[-1]
    raw = jnp.einsum("nqhc,nkhc->nhqk", query, keys, preferred_element_type=FLOAT) * size ** (-0.5)
    return jnp.where(usable, raw, -1e30)


def block_forward(hidden, params, floats, prefix, heads, usable):
    count, length, width = hidden.shape
    normed = layer_norm(hidden, floats[prefix + "ln1g"], floats[prefix + "ln1b"]).astype(BRAIN)
    bias = floats[prefix + "qvb"]
    full_bias = jnp.concatenate([bias[:width], jnp.zeros((width,), FLOAT), bias[width:]])
    projected = (matmul(normed, params[prefix + "qkv"]) + full_bias).astype(BRAIN)
    query, keys, values = split_heads(projected, heads)
    scores = scaled_scores(query, keys, usable)
    log_total = jax.nn.logsumexp(scores, axis=-1, keepdims=True)
    attend = jnp.exp(scores - log_total).astype(BRAIN)
    mixed = jnp.einsum("nhqk,nkhc->nqhc", attend, values, preferred_element_type=FLOAT)
    mixed = mixed.reshape(count, length, width).astype(BRAIN)
    middle = hidden + matmul(mixed, params[prefix + "proj"]) + floats[prefix + "projb"]
    second = layer_norm(middle, floats[prefix + "ln2g"], floats[prefix + "ln2b"]).astype(BRAIN)
    inner = matmul(second, params[prefix + "fc1"]) + floats[prefix + "fc1b"]
    active = gelu_exact(inner).astype(BRAIN)
    output = middle + matmul(active, params[prefix + "fc2"]) + floats[prefix + "fc2b"]
    return (output, (hidden, normed, projected, log_total, mixed, middle, second, inner, active))


def block_backward(grad, kept, params, floats, prefix, heads, usable, grads):
    hidden, normed, projected, log_total, mixed, middle, second, inner, active = kept
    count, length, width = hidden.shape
    size = width // heads
    d_branch = grad.astype(BRAIN)
    grads[prefix + "fc2"] = outer_sum(active, d_branch)
    grads[prefix + "fc2b"] = column_sum(d_branch)
    d_active = matmul_back(d_branch, params[prefix + "fc2"])
    unused, gelu_pull = jax.vjp(gelu_exact, inner)
    d_inner = gelu_pull(d_active)[0].astype(BRAIN)
    grads[prefix + "fc1"] = outer_sum(second, d_inner)
    grads[prefix + "fc1b"] = column_sum(d_inner)
    d_second = matmul_back(d_inner, params[prefix + "fc1"])
    unused, norm_pull = jax.vjp(
        layer_norm, middle, floats[prefix + "ln2g"], floats[prefix + "ln2b"]
    )
    d_middle, grads[prefix + "ln2g"], grads[prefix + "ln2b"] = norm_pull(d_second)
    d_middle = d_middle + grad
    d_output = d_middle.astype(BRAIN)
    grads[prefix + "proj"] = outer_sum(mixed, d_output)
    grads[prefix + "projb"] = column_sum(d_output)
    d_mixed = matmul_back(d_output, params[prefix + "proj"]).astype(BRAIN)
    d_heads = d_mixed.reshape(count, length, heads, size)
    query, keys, values = split_heads(projected, heads)
    attend = jnp.exp(scaled_scores(query, keys, usable) - log_total)
    d_attend = jnp.einsum("nqhc,nkhc->nhqk", d_heads, values, preferred_element_type=FLOAT)
    d_values = jnp.einsum(
        "nhqk,nqhc->nkhc", attend.astype(BRAIN), d_heads, preferred_element_type=FLOAT
    )
    d_scores = attend * (d_attend - jnp.sum(attend * d_attend, axis=-1, keepdims=True))
    d_scores = d_scores.astype(BRAIN)
    d_query = jnp.einsum(
        "nhqk,nkhc->nqhc", d_scores, keys, preferred_element_type=FLOAT
    ) * size ** (-0.5)
    d_keys = jnp.einsum(
        "nhqk,nqhc->nkhc", d_scores, query, preferred_element_type=FLOAT
    ) * size ** (-0.5)
    d_projected = (
        jnp.stack([d_query, d_keys, d_values], axis=2)
        .reshape(count, length, 3 * width)
        .astype(BRAIN)
    )
    grads[prefix + "qkv"] = outer_sum(normed, d_projected)
    summed = column_sum(d_projected)
    grads[prefix + "qvb"] = jnp.concatenate([summed[:width], summed[2 * width :]])
    d_normed = matmul_back(d_projected, params[prefix + "qkv"])
    unused, first_pull = jax.vjp(
        layer_norm, hidden, floats[prefix + "ln1g"], floats[prefix + "ln1b"]
    )
    d_hidden, grads[prefix + "ln1g"], grads[prefix + "ln1b"] = first_pull(d_normed)
    return d_middle + d_hidden


MESH = pl.DeviceIdType.MESH
LANES = 128


def layout():
    table = {}
    offset = 0
    for name, shape, kind, fan, rate in param_table():
        table[name] = (offset, shape)
        offset += math.prod(shape)
    return table


class Plan:
    def __init__(self, length, count):
        self.length = length
        self.count = count
        self.outer = count // 8
        self.rows = -(-((LANES - 1 + length + LANES - 1) // LANES) // 16) * 16
        units = self.rows // 16
        first = max(1, min(round(0.389 * units), (units - 1) // 2))
        sizes = (first * 16, first * 16, self.rows - 2 * first * 16)
        starts = (0, sizes[0], sizes[0] + sizes[1])
        self.parts = tuple(zip(starts, sizes))
        self.orders = ("ACB", "ABC", "CBA")
        self.frame_rows = -(-(length * count) // LANES // 8 * 8) + 64

    def base(self, index):
        return index * self.length // LANES

    def lead(self, index):
        return index * self.length % LANES

    def used(self, index):
        return (self.lead(index) + self.length + LANES - 1) // LANES


def position():
    chip = lax.axis_index("dp")
    core = lax.axis_index("rep")
    return {"A": chip // 4, "B": chip // 2 % 2, "C": chip % 2, "r": core}


def device_of(place):
    return (place["A"] * 4 + place["B"] * 2 + place["C"], place["r"])


def moved(place, dim, value):
    changed = dict(place)
    changed[dim] = value
    return changed


def peer_values(place, dim, outer):
    if dim == "A":
        return [lax.rem(place["A"] + step, outer) for step in range(1, outer)]
    return [1 - place[dim]]


def source_values(place, dim, outer):
    if dim == "A":
        return [lax.rem(place["A"] + outer - step, outer) for step in range(1, outer)]
    return [1 - place[dim]]


def meet(places):
    barrier = pltpu.get_barrier_semaphore()
    for place in places:
        pl.semaphore_signal(barrier, inc=1, device_id=device_of(place), device_id_type=MESH)
    pl.semaphore_wait(barrier, len(places))


def neighbours(place, outer):
    found = []
    for dim in "ABCr":
        for value in peer_values(place, dim, outer):
            found.append(moved(place, dim, value))
    return found


class Sender:
    def __init__(self, send, recv):
        self.send, self.recv, self.used = send, recv, 0

    def start(self, source, target, place):
        copy = pltpu.make_async_remote_copy(
            src_ref=source,
            dst_ref=target,
            send_sem=self.send.at[self.used],
            recv_sem=self.recv.at[self.used],
            device_id=device_of(place),
            device_id_type=MESH,
        )
        self.used += 1
        copy.start()
        return copy


def lane_iota(rows):
    return lax.broadcasted_iota(jnp.int32, (rows, LANES), 1)


def gather_body(plan, x_ref, out_ref, line, rolled, send, recv):
    outer, rows = plan.outer, plan.rows
    place = position()
    a, b, c, r = (place[dim] for dim in "ABCr")
    index = ((a * 2 + b) * 2 + c) * 2 + r
    lead = lax.rem(index * plan.length, LANES)
    line[...] = jnp.zeros_like(line)
    line[pl.ds(0, plan.length)] = x_ref[...]
    turned = pltpu.roll(line[...].reshape(rows, LANES), lead, 1)
    rolled[pl.ds(0, 8), :] = jnp.zeros((8, LANES), FLOAT)
    rolled[pl.ds(8, rows), :] = turned
    block = jnp.where(lane_iota(rows) >= lead, turned, rolled[pl.ds(7, rows), :])
    out_ref[a, b, c, r] = block.astype(BRAIN)
    meet(neighbours(place, outer))
    sender = Sender(send, recv)
    everything = []

    def region(part, whole, fixed):
        start, size = plan.parts[part]
        index = []
        for dim, extent in (("A", outer), ("B", 2), ("C", 2)):
            if dim in fixed:
                index.append(fixed[dim])
            else:
                index.append(pl.ds(0, extent) if dim in whole else place[dim])
        return out_ref.at[(*index, r, pl.ds(start, size))]

    fresh = [(part, "", [{}]) for part in range(3)]
    sibling = moved(place, "r", 1 - r)
    for phase in range(4):
        flights = []
        if phase < 3:
            for part in range(3):
                order = plan.orders[part]
                dim = order[phase]
                source = region(part, order[:phase], {})
                for value in peer_values(place, dim, outer):
                    flights.append(sender.start(source, source, moved(place, dim, value)))
        for part, whole, news in fresh:
            for fixed in news:
                source = region(part, whole, fixed)
                everything.append(sender.start(source, source, sibling))
        fresh = []
        if phase < 3:
            for part in range(3):
                order = plan.orders[part]
                dim = order[phase]
                news = [{dim: value} for value in source_values(place, dim, outer)]
                fresh.append((part, order[:phase], news))
        for copy in flights:
            copy.wait()
    for copy in everything:
        copy.wait()


def gather_params(master, plan):
    outer, rows = plan.outer, plan.rows
    copies = 3 * (outer + 1 + outer + 2)
    return pl.pallas_call(
        functools.partial(gather_body, plan),
        out_shape=jax.ShapeDtypeStruct((outer, 2, 2, 2, rows, LANES), BRAIN),
        in_specs=[pl.BlockSpec(memory_space=pltpu.VMEM)],
        out_specs=pl.BlockSpec(memory_space=pltpu.VMEM),
        scratch_shapes=[
            pltpu.VMEM((rows * LANES,), FLOAT),
            pltpu.VMEM((rows + 8, LANES), FLOAT),
            pltpu.SemaphoreType.DMA((copies,)),
            pltpu.SemaphoreType.DMA((copies,)),
        ],
        compiler_params=pltpu.CompilerParams(
            collective_id=0, has_side_effects=True, vmem_limit_bytes=40 << 20
        ),
    )(master)


def reduce_scratch(plan):
    shapes = []
    for part in range(3):
        size = plan.parts[part][1]
        left = list("ABC")
        for dim in reversed(plan.orders[part]):
            left.remove(dim)
            others = tuple(plan.outer if other == "A" else 2 for other in left)
            peers = plan.outer - 1 if dim == "A" else 1
            shapes.append(pltpu.VMEM((peers, *others, size, LANES), BRAIN))
            shapes.append(pltpu.VMEM((peers, *others, size, LANES), BRAIN))
            shapes.append(pltpu.VMEM((*others, size, LANES), FLOAT))
    return shapes


def in_segments(index, segments):
    inside = None
    for start, stop in segments:
        here = (index >= start) & (index < stop)
        inside = here if inside is None else inside | here
    return inside


def matrix_segments():
    found = []
    for name, shape, kind, fan, rate in param_table():
        if kind == "matrix":
            start = layout()[name][0]
            found.append((start, start + math.prod(shape)))
    return found


def reduce_body(
    plan, step_ref, held_ref, loss_ref, grad_ref, master_ref, first_ref, second_ref,
    master_out, first_out, second_out, copy_out, scalars_out, *scratch
):
    outer, rows = plan.outer, plan.rows
    core_in, line, rolled, near, far, mine, send, recv = scratch[:8]
    held_refs = scratch[8:]
    place = position()
    a, b, c, r = (place[dim] for dim in "ABCr")
    digits = {"A": a, "B": b, "C": c}
    device = ((a * 2 + b) * 2 + c) * 2 + r
    lead = lax.rem(device * plan.length, LANES)
    group = [
        {"A": a, "B": (b + k // 4) % 2, "C": (c + k // 2 % 2) % 2, "r": (r + k % 2) % 2}
        for k in range(1, 8)
    ]
    column = [moved(place, "A", value) for value in peer_values(place, "A", outer)]
    meet(group + column)
    sender = Sender(send, recv)
    sibling = moved(place, "r", 1 - r)
    pending = []
    core = []
    for part in range(3):
        start, size = plan.parts[part]
        span = pl.ds(start, size)
        full = (pl.ds(0, outer), pl.ds(0, 2), pl.ds(0, 2))
        core.append(
            sender.start(
                grad_ref.at[(*full, 1 - r, span)], core_in.at[(*full, span)], sibling
            )
        )
    state = []
    for part in range(3):
        core[part].wait_recv()
        pending.append(core[part])
        start, size = plan.parts[part]
        span = pl.ds(start, size)

        def current(at, span=span):
            index = tuple(at[dim] for dim in "ABC")
            own = grad_ref[(*index, r, span)].astype(FLOAT)
            return own + core_in[(*index, span)].astype(FLOAT)

        state.append((list("ABC"), current))
    flights = [None] * 3

    def launch(part, phase):
        left, current = state[part]
        dim = plan.orders[part][2 - phase]
        staged, received, kept = held_refs[(part * 3 + phase) * 3 : (part * 3 + phase) * 3 + 3]
        others = [other for other in left if other != dim]
        extents = [outer if other == "A" else 2 for other in others]
        started = []
        for number, value in enumerate(peer_values(place, dim, outer)):
            for picks in itertools.product(*[range(extent) for extent in extents]):
                at = dict(zip(others, picks))
                at[dim] = value
                staged[(number, *picks)] = current(at).astype(BRAIN)
            copy = sender.start(
                staged.at[number], received.at[number], moved(place, dim, value)
            )
            started.append(copy)
            pending.append(copy)
        for picks in itertools.product(*[range(extent) for extent in extents]):
            at = dict(zip(others, picks))
            at[dim] = digits[dim]
            kept[picks] = current(at)
        flights[part] = started

        def after(at, kept=kept, received=received, others=tuple(others), count=len(started)):
            index = tuple(at[other] for other in others)
            total = kept[index]
            for number in range(count):
                total = total + received[(number, *index)].astype(FLOAT)
            return total

        state[part] = (others, after)

    for phase in range(3):
        for part in range(3):
            if phase > 0:
                for copy in flights[part]:
                    copy.wait_recv()
            launch(part, phase)
    position_in = lax.broadcasted_iota(jnp.int32, (rows, LANES), 0) * LANES + lane_iota(rows)
    flat = position_in + device * plan.length
    table = layout()
    early, late = table["enc_ln1g"][0], table["encg"][0]
    rate_part = jnp.where(flat < early, 0.75, jnp.where(flat < late, 0.9, 1.0))
    decay_part = jnp.where(in_segments(flat, matrix_segments()), DECAY, 0.0)
    line[...] = jnp.zeros_like(line)
    line[pl.ds(0, plan.length)] = master_ref[...]
    master = line[...].reshape(rows, LANES)
    line[pl.ds(0, plan.length)] = first_ref[...]
    first = line[...].reshape(rows, LANES)
    line[pl.ds(0, plan.length)] = second_ref[...]
    second = line[...].reshape(rows, LANES)
    for part in range(3):
        for copy in flights[part]:
            copy.wait_recv()
        start, size = plan.parts[part]
        left, current = state[part]
        rolled[pl.ds(start, size), :] = current({})
    rolled[pl.ds(rows, 8), :] = jnp.zeros((8, LANES), FLOAT)
    shift = lax.rem(LANES - lead, LANES)
    here = pltpu.roll(rolled[pl.ds(0, rows), :], shift, 1)
    below = pltpu.roll(rolled[pl.ds(1, rows), :], shift, 1)
    total = jnp.where(lane_iota(rows) < LANES - lead, here, below)
    total = jnp.where(position_in < plan.length, total, 0.0)
    squares = jnp.sum(total * total)
    lane = lane_iota(8)
    mine[...] = jnp.where(lane == 0, squares, 0.0)
    mine[...] = jnp.where(lane == 1, held_ref[0].astype(FLOAT), mine[...])
    mine[...] = jnp.where(lane == 2, loss_ref[0], mine[...])
    spot = (b * 2 + c) * 2 + r
    near[spot] = mine[...]
    nears = [sender.start(mine, near.at[spot], other) for other in group]
    for copy in nears:
        copy.wait_recv()
    together = near[0]
    for other in range(1, 8):
        together = together + near[other]
    far[a] = together
    rolled[pl.ds(0, 8), :] = together
    fars = [sender.start(rolled.at[pl.ds(0, 8)], far.at[a], other) for other in column]
    for copy in fars:
        copy.wait_recv()
    whole = far[0]
    for other in range(1, outer):
        whole = whole + far[other]
    held = jnp.sum(jnp.where(lane == 1, whole, 0.0)[0:1, :])
    weight_total = held * (0.1 * VIS + (NP - VIS))
    scalars = whole[0:1, :]
    weights = jnp.full((1, LANES), weight_total)
    norms = jnp.sqrt(jnp.full((1, LANES), jnp.sum(jnp.where(lane[0:1] == 0, scalars, 0.0)))) / weights
    losses = jnp.full((1, LANES), jnp.sum(jnp.where(lane[0:1] == 2, scalars, 0.0))) / weights
    scalars_out[...] = jnp.where(lane[0:1] == 0, losses, norms)
    gradient = total / weights
    clipped = gradient * jnp.minimum(1.0, CLIP / norms)
    fade = 1.0 / jnp.full((1, LANES), lax.shift_left(1, step_ref[0]).astype(FLOAT))
    new_first = BETA_ONE * first + (1.0 - BETA_ONE) * clipped
    new_second = BETA_TWO * second + (1.0 - BETA_TWO) * clipped * clipped
    first_hat = new_first / (1.0 - fade)
    second_hat = new_second / (1.0 - fade)
    new_master = master - LEARN * rate_part * (
        first_hat / (jnp.sqrt(second_hat) + EPSILON) + decay_part * master
    )
    length = plan.length
    master_out[...] = new_master.reshape(rows * LANES)[:length]
    first_out[...] = new_first.reshape(rows * LANES)[:length]
    second_out[...] = new_second.reshape(rows * LANES)[:length]
    copy_out[...] = new_master.reshape(rows * LANES)[:length].astype(BRAIN)
    for copy in pending + nears + fars:
        copy.wait_send()


def reduce_update(step, held, loss, grads, master, first, second, plan):
    outer, rows, length = plan.outer, plan.rows, plan.length
    copies = 3 + 3 * (outer + 1) + 7 + outer - 1
    vmem = pl.BlockSpec(memory_space=pltpu.VMEM)
    smem = pl.BlockSpec(memory_space=pltpu.SMEM)
    flat = jax.ShapeDtypeStruct((length,), FLOAT)
    return pl.pallas_call(
        functools.partial(reduce_body, plan),
        out_shape=(
            flat,
            flat,
            flat,
            jax.ShapeDtypeStruct((length,), BRAIN),
            jax.ShapeDtypeStruct((1, LANES), FLOAT),
        ),
        in_specs=[smem, smem, smem, vmem, vmem, vmem, vmem],
        out_specs=(vmem,) * 5,
        scratch_shapes=[
            pltpu.VMEM((outer, 2, 2, rows, LANES), BRAIN),
            pltpu.VMEM((rows * LANES,), FLOAT),
            pltpu.VMEM((rows + 8, LANES), FLOAT),
            pltpu.VMEM((8, 8, LANES), FLOAT),
            pltpu.VMEM((outer, 8, LANES), FLOAT),
            pltpu.VMEM((8, LANES), FLOAT),
            pltpu.SemaphoreType.DMA((copies,)),
            pltpu.SemaphoreType.DMA((copies,)),
            *reduce_scratch(plan),
        ],
        compiler_params=pltpu.CompilerParams(
            collective_id=1, has_side_effects=True, vmem_limit_bytes=56 << 20
        ),
    )(step, held, loss, grads, master, first, second)


def half_turn(frame, start, rows):
    here = pltpu.roll(frame[pl.ds(start, rows), :], 64, 1)
    below = pltpu.roll(frame[pl.ds(start + 1, rows), :], 64, 1)
    return jnp.where(lane_iota(rows) < 64, here, below)


def assemble(plan, slots, even, odd):
    for index in range(plan.count):
        base, used = plan.base(index), plan.used(index)
        a, rest = divmod(index, 8)
        block = slots[a, rest // 4, rest // 2 % 2, rest % 2].astype(FLOAT)[:used]
        if plan.lead(index):
            before = even[pl.ds(base, 1), :]
            even[pl.ds(base, used), :] = block
            even[pl.ds(base, 1), :] = before + block[0:1]
        else:
            even[pl.ds(base, used), :] = block
    span = 256
    total = (plan.frame_rows - 16) // span

    @pl.loop(0, total)
    def _(step):
        start = pl.multiple_of(step * span, span)
        odd[pl.ds(start, span), :] = half_turn(even, start, span)

    rest = plan.frame_rows - 16 - total * span
    odd[pl.ds(total * span, rest), :] = half_turn(even, total * span, rest)


def read_param(even, odd, name, target):
    offset, shape = layout()[name]
    rows, width = (1, shape[0]) if len(shape) == 1 else shape
    base, late = divmod(offset, LANES)
    frames = (even, odd) if late == 0 else (odd, even)
    whole, half = divmod(width, LANES)
    kind = target.dtype
    if rows == 1:
        for col in range(whole):
            target[:, pl.ds(col * LANES, LANES)] = frames[0][pl.ds(base + col, 1), :].astype(kind)
        if half:
            tail = frames[0][pl.ds(base + whole, 1), :]
            target[:, pl.ds(whole * LANES, half)] = tail[:, :half].astype(kind)
        return
    if not half:
        for col in range(whole):
            piece = frames[0][pl.ds(base + col, rows, stride=whole), :]
            target[:, pl.ds(col * LANES, LANES)] = piece.astype(kind)
        return
    stride = 2 * width // LANES
    shift = whole + (1 if late else 0)

    def interleave(scratch):
        for col in range(whole + 1):
            size = LANES if col < whole else half
            upper = frames[0][pl.ds(base + col, rows // 2, stride=stride), :]
            lower = frames[1][pl.ds(base + shift + col, rows // 2, stride=stride), :]
            scratch[pl.ds(0, rows // 2, stride=2), :] = upper
            scratch[pl.ds(1, rows // 2, stride=2), :] = lower
            target[:, pl.ds(col * LANES, size)] = scratch[...][:, :size].astype(kind)

    pl.run_scoped(interleave, pltpu.VMEM((rows, LANES), FLOAT))


def write_grad(even, odd, name, value):
    offset, shape = layout()[name]
    rows, width = (1, shape[0]) if len(shape) == 1 else shape
    base, late = divmod(offset, LANES)
    frames = (even, odd) if late == 0 else (odd, even)
    whole, half = divmod(width, LANES)

    def column(col):
        if col < whole:
            return value(col * LANES, LANES)
        tail = value(whole * LANES, half)
        return jnp.concatenate([tail, jnp.zeros((rows, LANES - half), FLOAT)], axis=1)

    count = whole + (1 if half else 0)
    if rows == 1:
        for col in range(count):
            frames[0][pl.ds(base + col, 1), :] += column(col)
        return
    if not half:
        for col in range(whole):
            frames[0][pl.ds(base + col, rows, stride=whole), :] = column(col)
        return
    stride = 2 * width // LANES
    shift = whole + (1 if late else 0)

    def interleave(scratch):
        for col in range(count):
            scratch[...] = column(col)
            upper = scratch[pl.ds(0, rows // 2, stride=2), :]
            lower = scratch[pl.ds(1, rows // 2, stride=2), :]
            frames[0][pl.ds(base + col, rows // 2, stride=stride), :] = upper
            frames[1][pl.ds(base + shift + col, rows // 2, stride=stride), :] = lower

    pl.run_scoped(interleave, pltpu.VMEM((rows, LANES), FLOAT))


def emit_slots(plan, even, odd, slots):
    for index in range(plan.count):
        base, used = plan.base(index), plan.used(index)
        a, rest = divmod(index, 8)
        spot = (a, rest // 4, rest // 2 % 2, rest % 2)
        here = pltpu.roll(odd[pl.ds(base + 8, plan.rows), :], 64, 1)
        above = pltpu.roll(odd[pl.ds(base + 7, plan.rows), :], 64, 1)
        late = jnp.where(lane_iota(plan.rows) < 64, above, here)
        slots[spot] = (even[pl.ds(base, plan.rows), :] + late).astype(BRAIN)


def unpack_body(plan, slots, *refs):
    outs, (even, odd) = refs[:-2], refs[-2:]
    assemble(plan, slots, even, odd)
    for name, target in zip(layout(), outs):
        read_param(even, odd, name, target)


def two_dim(shape):
    return (1, *shape) if len(shape) == 1 else shape


def unpack_params(slots, plan):
    vmem = pl.BlockSpec(memory_space=pltpu.VMEM)
    shapes = [jax.ShapeDtypeStruct(two_dim(s), BRAIN) for o, s in layout().values()]
    outs = pl.pallas_call(
        functools.partial(unpack_body, plan),
        out_shape=shapes,
        in_specs=[vmem],
        out_specs=[vmem] * len(shapes),
        scratch_shapes=[pltpu.VMEM((plan.frame_rows, LANES), FLOAT)] * 2,
        compiler_params=pltpu.CompilerParams(vmem_limit_bytes=50 << 20),
    )(slots)
    return {n: v.reshape(s) for (n, (o, s)), v in zip(layout().items(), outs)}


def pack_body(plan, *refs):
    count = len(layout())
    grads, slots, even, odd = refs[:count], refs[count], refs[count + 1], refs[count + 2]
    even[...] = jnp.zeros_like(even)
    odd[...] = jnp.zeros_like(odd)
    view = odd.at[pl.ds(8, plan.frame_rows)]
    for name, ref in zip(layout(), grads):
        write_grad(even, view, name, lambda start, size, ref=ref: ref[:, pl.ds(start, size)])
    emit_slots(plan, even, odd, slots)


def pack_grads(grads, plan):
    vmem = pl.BlockSpec(memory_space=pltpu.VMEM)
    values = [grads[n].reshape(two_dim(s)) for n, (o, s) in layout().items()]
    return pl.pallas_call(
        functools.partial(pack_body, plan),
        out_shape=jax.ShapeDtypeStruct((plan.outer, 2, 2, 2, plan.rows, LANES), BRAIN),
        in_specs=[vmem] * len(values),
        out_specs=vmem,
        scratch_shapes=[
            pltpu.VMEM((plan.frame_rows, LANES), FLOAT),
            pltpu.VMEM((plan.frame_rows + 8, LANES), FLOAT),
        ],
        compiler_params=pltpu.CompilerParams(vmem_limit_bytes=50 << 20),
    )(*values)


def on_device(patches, targets, keep, counts, step, master, first, second):
    plan = Plan(master.shape[0], lax.axis_size(("dp", "rep")))
    params = unpack_params(gather_params(master, plan), plan)
    floats = {name: value.astype(FLOAT) for name, value in params.items() if value.ndim == 1}
    slots = patches.shape[0]
    held = counts[0, 0]
    live = (jnp.arange(slots) < held).astype(FLOAT)
    padding = SLOT - VIS
    visible = jnp.pad(
        jnp.take_along_axis(patches, keep[:, :, None], axis=1), ((0, 0), (0, padding), (0, 0))
    )
    marks = jnp.pad(keep + 1, ((0, 0), (0, padding)))
    usable = jnp.arange(SLOT) < VIS
    first_in = matmul(visible, params["patch"]) + floats["patchb"] + sincos(marks - 1, D)
    encoded, encoder_kept = block_forward(first_in, params, floats, "enc_", HEADS, usable)
    encoder_out = layer_norm(encoded, floats["encg"], floats["encb"]).astype(BRAIN)
    seen_rows = encoder_out[:, :VIS]
    embedded = matmul(seen_rows, params["embed"]) + floats["embedb"]
    placement = (keep[:, :, None] == jnp.arange(NP)[None, None, :]).astype(FLOAT)
    seen = jnp.sum(placement, axis=1)
    grid_in = jnp.einsum("gvp,gve->gpe", placement, embedded, precision=HIGH)
    grid_in = grid_in + (1.0 - seen)[:, :, None] * floats["mask"] + sincos(jnp.arange(NP), E)
    every_key = jnp.ones((NP,), bool)
    decoded, decoder_kept = block_forward(grid_in, params, floats, "dec_", DHEADS, every_key)
    final = layer_norm(decoded, floats["decg"], floats["decb"]).astype(BRAIN)
    predicted = matmul(final, params["head"]) + floats["headb"]
    weight = (0.1 * seen + (1.0 - seen)) * live[:, None]
    error = predicted - targets.astype(FLOAT)
    local_sum = jnp.sum(weight * jnp.mean(error * error, axis=-1))
    grads = {}
    d_pred = (weight[:, :, None] * (2.0 / PIX) * error).astype(BRAIN)
    grads["head"] = outer_sum(final, d_pred)
    grads["headb"] = column_sum(d_pred)
    d_final = matmul_back(d_pred, params["head"])
    unused, final_pull = jax.vjp(layer_norm, decoded, floats["decg"], floats["decb"])
    d_decoded, grads["decg"], grads["decb"] = final_pull(d_final)
    d_grid = block_backward(
        d_decoded, decoder_kept, params, floats, "dec_", DHEADS, every_key, grads
    )
    grads["mask"] = jnp.sum((1.0 - seen)[:, :, None] * d_grid, axis=(0, 1))
    d_embedded = jnp.einsum("gvp,gpe->gve", placement, d_grid, precision=HIGH).astype(BRAIN)
    grads["embed"] = outer_sum(seen_rows, d_embedded)
    grads["embedb"] = column_sum(d_embedded)
    d_seen = matmul_back(d_embedded, params["embed"]).astype(BRAIN)
    d_home = jnp.pad(d_seen, ((0, 0), (0, padding), (0, 0)))
    unused, encoder_pull = jax.vjp(layer_norm, encoded, floats["encg"], floats["encb"])
    d_encoded, grads["encg"], grads["encb"] = encoder_pull(d_home.astype(FLOAT))
    d_first = block_backward(d_encoded, encoder_kept, params, floats, "enc_", HEADS, usable, grads)
    d_first = d_first.astype(BRAIN)
    grads["patch"] = outer_sum(visible, d_first)
    grads["patchb"] = column_sum(d_first)
    packed = pack_grads(grads, plan)
    new_master, new_first, new_second, copy, scalars = reduce_update(
        step, counts.reshape(1), local_sum.reshape(1), packed, master, first, second, plan
    )
    return (new_master, new_first, new_second, copy, scalars[0, 0], scalars[0, 1])


def solution(mesh):
    return jax.shard_map(
        on_device,
        mesh=mesh,
        in_specs=(
            P(("dp", "rep"), None, None),
            P(("dp", "rep"), None, None),
            P(("dp", "rep"), None),
            P("dp", "rep"),
            P(),
            P(("dp", "rep")),
            P(("dp", "rep")),
            P(("dp", "rep")),
        ),
        out_specs=(
            P(("dp", "rep")),
            P(("dp", "rep")),
            P(("dp", "rep")),
            P(("dp", "rep")),
            P(),
            P(),
        ),
        check_vma=False,
    )
```

```python
import functools
import itertools
import math

import jax
import jax.numpy as jnp
import numpy as np
from jax import lax
from jax.experimental import pallas as pl
from jax.experimental.pallas import tpu as pltpu
from jax.sharding import PartitionSpec as P

D = 192
HEADS = 3
FF = 768
E = 256
DHEADS = 8
DFF = 1024
PIX = 768
GRID = 14
VIS = 49
NP = 196

FLOAT = jnp.float32
BRAIN = jnp.bfloat16
CLIP = 0.05
BETA_ONE = 0.5
BETA_TWO = 0.5
LEARN = 0.01
DECAY = 0.05
EPSILON = 1e-08
LN_EPS = 1e-06

ROWS = 208
HOME = 64
LIVE_CAP = 3
PAIR = ((1,), (1,)), ((), ())
DEEP = ((0,), (0,)), ((), ())
LOG_TWO_E = 1.4426950408889634


def block_table(prefix, width, hidden, proj_fan, rate):
    return [
        (prefix + "ln1g", (width,), "gain", 1, rate),
        (prefix + "ln1b", (width,), "bias", 1, rate),
        (prefix + "qkv", (width, 3 * width), "matrix", width, rate),
        (prefix + "qvb", (2 * width,), "bias", 1, rate),
        (prefix + "proj", (width, width), "matrix", proj_fan, rate),
        (prefix + "projb", (width,), "bias", 1, rate),
        (prefix + "ln2g", (width,), "gain", 1, rate),
        (prefix + "ln2b", (width,), "bias", 1, rate),
        (prefix + "fc1", (width, hidden), "matrix", width, rate),
        (prefix + "fc1b", (hidden,), "bias", 1, rate),
        (prefix + "fc2", (hidden, width), "matrix", hidden, rate),
        (prefix + "fc2b", (width,), "bias", 1, rate),
    ]


def param_table():
    table = [("patch", (PIX, D), "matrix", PIX, 0.75), ("patchb", (D,), "bias", 1, 0.75)]
    table = table + block_table("enc_", D, FF, D // 4, 0.9)
    table = table + [
        ("encg", (D,), "gain", 1, 1.0),
        ("encb", (D,), "bias", 1, 1.0),
        ("embed", (D, E), "matrix", D, 1.0),
        ("embedb", (E,), "bias", 1, 1.0),
        ("mask", (E,), "token", 1, 1.0),
    ]
    table = table + block_table("dec_", E, DFF, E // 8, 1.0)
    table = table + [
        ("decg", (E,), "gain", 1, 1.0),
        ("decb", (E,), "bias", 1, 1.0),
        ("head", (E, PIX), "matrix", E, 1.0),
        ("headb", (PIX,), "bias", 1, 1.0),
    ]
    return table


MESH = pl.DeviceIdType.MESH
LANES = 128


def layout():
    table = {}
    offset = 0
    for name, shape, kind, fan, rate in param_table():
        table[name] = (offset, shape)
        offset += math.prod(shape)
    return table


class Plan:
    def __init__(self, length, count):
        self.length = length
        self.count = count
        self.outer = count // 8
        self.rows = -(-((LANES - 1 + length + LANES - 1) // LANES) // 16) * 16
        units = self.rows // 16
        first = max(1, min(round(0.389 * units), (units - 1) // 2))
        sizes = (first * 16, first * 16, self.rows - 2 * first * 16)
        starts = (0, sizes[0], sizes[0] + sizes[1])
        self.parts = tuple(zip(starts, sizes))
        self.orders = ("ACB", "ABC", "CBA")
        self.frame_rows = -(-(length * count) // LANES // 8 * 8) + 64

    def base(self, index):
        return index * self.length // LANES

    def lead(self, index):
        return index * self.length % LANES

    def used(self, index):
        return (self.lead(index) + self.length + LANES - 1) // LANES


def position():
    chip = lax.axis_index("dp")
    core = lax.axis_index("rep")
    return {"A": chip // 4, "B": chip // 2 % 2, "C": chip % 2, "r": core}


def device_of(place):
    return (place["A"] * 4 + place["B"] * 2 + place["C"], place["r"])


def moved(place, dim, value):
    changed = dict(place)
    changed[dim] = value
    return changed


def peer_values(place, dim, outer):
    if dim == "A":
        return [lax.rem(place["A"] + step, outer) for step in range(1, outer)]
    return [1 - place[dim]]


def source_values(place, dim, outer):
    if dim == "A":
        return [lax.rem(place["A"] + outer - step, outer) for step in range(1, outer)]
    return [1 - place[dim]]


def meet(places):
    barrier = pltpu.get_barrier_semaphore()
    for place in places:
        pl.semaphore_signal(barrier, inc=1, device_id=device_of(place), device_id_type=MESH)
    pl.semaphore_wait(barrier, len(places))


def neighbours(place, outer):
    found = []
    for dim in "ABCr":
        for value in peer_values(place, dim, outer):
            found.append(moved(place, dim, value))
    return found


class Sender:
    def __init__(self, send, recv):
        self.send, self.recv, self.used = send, recv, 0

    def start(self, source, target, place):
        copy = pltpu.make_async_remote_copy(
            src_ref=source,
            dst_ref=target,
            send_sem=self.send.at[self.used],
            recv_sem=self.recv.at[self.used],
            device_id=device_of(place),
            device_id_type=MESH,
        )
        self.used += 1
        copy.start()
        return copy


def lane_iota(rows):
    return lax.broadcasted_iota(jnp.int32, (rows, LANES), 1)


HUBS = (1, 2)


def others_of(hub):
    return [spot for spot in range(4) if spot != hub]


def gather_body(
    plan, counts_ref, keep_ref, x_ref, patches_ref, targets_ref,
    out_ref, seen_ref, tgt_ref, meta_ref,
    line, rolled, pixels, spare, send, recv, local, hand, taken
):
    outer, rows = plan.outer, plan.rows
    place = position()
    a, b, c, r = (place[dim] for dim in "ABCr")
    spot = b * 2 + c
    pixel_copy = pltpu.make_async_copy(patches_ref, pixels, local.at[0])
    pixel_copy.start()
    target_copy = pltpu.make_async_copy(
        targets_ref.at[pl.ds(0, LIVE_CAP)], tgt_ref.at[pl.ds(0, LIVE_CAP)], local.at[1]
    )
    target_copy.start()
    index = ((a * 2 + b) * 2 + c) * 2 + r
    lead = lax.rem(index * plan.length, LANES)
    line[...] = jnp.zeros_like(line)
    line[pl.ds(0, plan.length)] = x_ref[...]
    turned = pltpu.roll(line[...].reshape(rows, LANES), lead, 1)
    rolled[pl.ds(0, 8), :] = jnp.zeros((8, LANES), FLOAT)
    rolled[pl.ds(8, rows), :] = turned
    block = jnp.where(lane_iota(rows) >= lead, turned, rolled[pl.ds(7, rows), :])
    out_ref[a, b, c, r] = block.astype(BRAIN)
    meet(neighbours(place, outer) + [moved(moved(place, "B", 1 - b), "C", 1 - c)])
    sender = Sender(send, recv)
    everything = []

    def region(part, whole, fixed):
        start, size = plan.parts[part]
        index = []
        for dim, extent in (("A", outer), ("B", 2), ("C", 2)):
            if dim in fixed:
                index.append(fixed[dim])
            else:
                index.append(pl.ds(0, extent) if dim in whole else place[dim])
        return out_ref.at[(*index, r, pl.ds(start, size))]

    def hand_over(hub, number):
        other = others_of(hub)[number]
        target = {"A": a, "B": other // 2, "C": other % 2, "r": r}
        pairs = (
            (spare.at[number], seen_ref.at[2 + hub]),
            (meta_ref.at[0], meta_ref.at[hub]),
            (targets_ref.at[3 + number], tgt_ref.at[2 + hub]),
        )
        return [
            pltpu.make_async_remote_copy(
                src_ref=source,
                dst_ref=to,
                send_sem=hand.at[hub - 1, number, kind],
                recv_sem=taken.at[hub - 1, kind],
                device_id=device_of(target),
                device_id_type=MESH,
            )
            for kind, (source, to) in enumerate(pairs)
        ]

    fresh = [(part, "", [{}]) for part in range(3)]
    sibling = moved(place, "r", 1 - r)
    for phase in range(4):
        flights = []
        if phase < 3:
            for part in range(3):
                order = plan.orders[part]
                dim = order[phase]
                source = region(part, order[:phase], {})
                for value in peer_values(place, dim, outer):
                    flights.append(sender.start(source, source, moved(place, dim, value)))
        for part, whole, news in fresh:
            for fixed in news:
                source = region(part, whole, fixed)
                everything.append(sender.start(source, source, sibling))
        fresh = []
        if phase < 3:
            for part in range(3):
                order = plan.orders[part]
                dim = order[phase]
                news = [{dim: value} for value in source_values(place, dim, outer)]
                fresh.append((part, order[:phase], news))
        if phase == 0:
            lane = lane_iota(8)
            row = lax.broadcasted_iota(jnp.int32, (8, LANES), 0)
            mine = jnp.where((lane == LANES - 1) & (row == 0), counts_ref[0, 0].astype(FLOAT), -1.0)
            meta_ref[0] = mine
            meta_ref[0, pl.ds(0, keep_ref.shape[0]), pl.ds(0, VIS)] = keep_ref[...].astype(FLOAT)
            pixel_copy.wait()

            def visible(image):
                number = lax.broadcasted_iota(jnp.int32, (NP, HOME), 0).astype(FLOAT)
                where = (number == meta_ref[0, pl.ds(image, 1), :][:, :HOME]).astype(BRAIN)
                return dot(where, pixels[image], DEEP).astype(BRAIN)

            for hub in HUBS:

                @pl.when(spot == hub)
                def _(hub=hub):
                    for number in range(3):
                        spare[number] = visible(3 + number)
                    for number in range(3):
                        for copy in hand_over(hub, number):
                            copy.start()

            for image in range(LIVE_CAP):
                seen_ref[image] = visible(image)
        for copy in flights:
            copy.wait()
    for copy in everything:
        copy.wait()
    for hub in HUBS:

        @pl.when(spot == hub)
        def _(hub=hub):
            for number in range(3):
                for copy in hand_over(hub, number):
                    copy.wait_send()

        @pl.when(spot != hub)
        def _(hub=hub):
            for copy in hand_over(hub, 0):
                copy.wait_recv()

    target_copy.wait()


def gather_params(counts, keep, master, patches, targets, plan):
    outer, rows = plan.outer, plan.rows
    copies = 3 * (outer + 1 + outer + 2)
    vmem = pl.BlockSpec(memory_space=pltpu.VMEM)
    smem = pl.BlockSpec(memory_space=pltpu.SMEM)
    far = pl.BlockSpec(memory_space=pl.ANY)
    return pl.pallas_call(
        functools.partial(gather_body, plan),
        out_shape=(
            jax.ShapeDtypeStruct((outer, 2, 2, 2, rows, LANES), BRAIN),
            jax.ShapeDtypeStruct((5, HOME, PIX), BRAIN),
            jax.ShapeDtypeStruct((5, NP, PIX), BRAIN),
            jax.ShapeDtypeStruct((3, 8, LANES), FLOAT),
        ),
        in_specs=[smem, vmem, vmem, far, far],
        out_specs=(vmem,) * 4,
        scratch_shapes=[
            pltpu.VMEM((rows * LANES,), FLOAT),
            pltpu.VMEM((rows + 8, LANES), FLOAT),
            pltpu.VMEM(patches.shape, BRAIN),
            pltpu.VMEM((3, HOME, PIX), BRAIN),
            pltpu.SemaphoreType.DMA((copies,)),
            pltpu.SemaphoreType.DMA((copies,)),
            pltpu.SemaphoreType.DMA((2,)),
            pltpu.SemaphoreType.DMA((2, 3, 3)),
            pltpu.SemaphoreType.DMA((2, 3)),
        ],
        compiler_params=pltpu.CompilerParams(
            collective_id=0, has_side_effects=True, vmem_limit_bytes=40 << 20
        ),
    )(counts, keep, master, patches, targets)


def reduce_scratch(plan):
    shapes = []
    for part in range(3):
        size = plan.parts[part][1]
        left = list("ABC")
        for dim in reversed(plan.orders[part]):
            left.remove(dim)
            others = tuple(plan.outer if other == "A" else 2 for other in left)
            peers = plan.outer - 1 if dim == "A" else 1
            shapes.append(pltpu.VMEM((peers, *others, size, LANES), BRAIN))
            shapes.append(pltpu.VMEM((peers, *others, size, LANES), BRAIN))
            shapes.append(pltpu.VMEM((*others, size, LANES), FLOAT))
    return shapes


def in_segments(index, segments):
    inside = None
    for start, stop in segments:
        here = (index >= start) & (index < stop)
        inside = here if inside is None else inside | here
    return inside


def matrix_segments():
    found = []
    for name, shape, kind, fan, rate in param_table():
        if kind == "matrix":
            start = layout()[name][0]
            found.append((start, start + math.prod(shape)))
    return found


def reduce_body(
    plan, held_ref, loss_ref, grad_ref, total_out, scalars_out, *scratch
):
    outer, rows = plan.outer, plan.rows
    core_in, rolled, near, far, mine, send, recv = scratch[:7]
    held_refs = scratch[7:]
    place = position()
    a, b, c, r = (place[dim] for dim in "ABCr")
    digits = {"A": a, "B": b, "C": c}
    device = ((a * 2 + b) * 2 + c) * 2 + r
    lead = lax.rem(device * plan.length, LANES)
    group = [
        {"A": a, "B": (b + k // 4) % 2, "C": (c + k // 2 % 2) % 2, "r": (r + k % 2) % 2}
        for k in range(1, 8)
    ]
    column = [moved(place, "A", value) for value in peer_values(place, "A", outer)]
    meet(group + column)
    sender = Sender(send, recv)
    sibling = moved(place, "r", 1 - r)
    pending = []
    core = []
    for part in range(3):
        start, size = plan.parts[part]
        span = pl.ds(start, size)
        full = (pl.ds(0, outer), pl.ds(0, 2), pl.ds(0, 2))
        core.append(
            sender.start(
                grad_ref.at[(*full, 1 - r, span)], core_in.at[(*full, span)], sibling
            )
        )
    state = []
    for part in range(3):
        core[part].wait_recv()
        pending.append(core[part])
        start, size = plan.parts[part]
        span = pl.ds(start, size)

        def current(at, span=span):
            index = tuple(at[dim] for dim in "ABC")
            own = grad_ref[(*index, r, span)].astype(FLOAT)
            return own + core_in[(*index, span)].astype(FLOAT)

        state.append((list("ABC"), current))
    flights = [None] * 3

    def launch(part, phase):
        left, current = state[part]
        dim = plan.orders[part][2 - phase]
        staged, received, kept = held_refs[(part * 3 + phase) * 3 : (part * 3 + phase) * 3 + 3]
        others = [other for other in left if other != dim]
        extents = [outer if other == "A" else 2 for other in others]
        started = []
        for number, value in enumerate(peer_values(place, dim, outer)):
            for picks in itertools.product(*[range(extent) for extent in extents]):
                at = dict(zip(others, picks))
                at[dim] = value
                staged[(number, *picks)] = current(at).astype(BRAIN)
            copy = sender.start(
                staged.at[number], received.at[number], moved(place, dim, value)
            )
            started.append(copy)
            pending.append(copy)
        for picks in itertools.product(*[range(extent) for extent in extents]):
            at = dict(zip(others, picks))
            at[dim] = digits[dim]
            kept[picks] = current(at)
        flights[part] = started

        def after(at, kept=kept, received=received, others=tuple(others), count=len(started)):
            index = tuple(at[other] for other in others)
            total = kept[index]
            for number in range(count):
                total = total + received[(number, *index)].astype(FLOAT)
            return total

        state[part] = (others, after)

    for phase in range(3):
        for part in range(3):
            if phase > 0:
                for copy in flights[part]:
                    copy.wait_recv()
            launch(part, phase)
    position_in = lax.broadcasted_iota(jnp.int32, (rows, LANES), 0) * LANES + lane_iota(rows)
    for part in range(3):
        for copy in flights[part]:
            copy.wait_recv()
        start, size = plan.parts[part]
        left, current = state[part]
        rolled[pl.ds(start, size), :] = current({})
    rolled[pl.ds(rows, 8), :] = jnp.zeros((8, LANES), FLOAT)
    shift = lax.rem(LANES - lead, LANES)
    here = pltpu.roll(rolled[pl.ds(0, rows), :], shift, 1)
    below = pltpu.roll(rolled[pl.ds(1, rows), :], shift, 1)
    total = jnp.where(lane_iota(rows) < LANES - lead, here, below)
    total = jnp.where(position_in < plan.length, total, 0.0)
    squares = jnp.sum(total * total)
    lane = lane_iota(8)
    mine[...] = jnp.where(lane == 0, squares, 0.0)
    mine[...] = jnp.where(lane == 1, held_ref[0, 0].astype(FLOAT), mine[...])
    mine[...] = jnp.where(lane == 2, loss_ref[0], mine[...])
    spot = (b * 2 + c) * 2 + r
    near[spot] = mine[...]
    nears = [sender.start(mine, near.at[spot], other) for other in group]
    for copy in nears:
        copy.wait_recv()
    together = near[0]
    for other in range(1, 8):
        together = together + near[other]
    far[a] = together
    rolled[pl.ds(0, 8), :] = together
    fars = [sender.start(rolled.at[pl.ds(0, 8)], far.at[a], other) for other in column]
    for copy in fars:
        copy.wait_recv()
    whole = far[0]
    for other in range(1, outer):
        whole = whole + far[other]
    held = jnp.sum(jnp.where(lane == 1, whole, 0.0)[0:1, :])
    weight_total = held * (0.1 * VIS + (NP - VIS))
    scalars = whole[0:1, :]
    weights = jnp.full((1, LANES), weight_total)
    norms = jnp.sqrt(jnp.full((1, LANES), jnp.sum(jnp.where(lane[0:1] == 0, scalars, 0.0)))) / weights
    losses = jnp.full((1, LANES), jnp.sum(jnp.where(lane[0:1] == 2, scalars, 0.0))) / weights
    scalars_out[...] = jnp.where(lane[0:1] == 0, losses, jnp.where(lane[0:1] == 1, norms, weights))
    total_out[...] = total
    for copy in pending + nears + fars:
        copy.wait_send()


def reduce_grads(held, loss, grads, plan):
    outer, rows = plan.outer, plan.rows
    copies = 3 + 3 * (outer + 1) + 7 + outer - 1
    vmem = pl.BlockSpec(memory_space=pltpu.VMEM)
    smem = pl.BlockSpec(memory_space=pltpu.SMEM)
    return pl.pallas_call(
        functools.partial(reduce_body, plan),
        out_shape=(
            jax.ShapeDtypeStruct((rows, LANES), FLOAT),
            jax.ShapeDtypeStruct((1, LANES), FLOAT),
        ),
        in_specs=[smem, smem, vmem],
        out_specs=(vmem,) * 2,
        scratch_shapes=[
            pltpu.VMEM((outer, 2, 2, rows, LANES), BRAIN),
            pltpu.VMEM((rows + 8, LANES), FLOAT),
            pltpu.VMEM((8, 8, LANES), FLOAT),
            pltpu.VMEM((outer, 8, LANES), FLOAT),
            pltpu.VMEM((8, LANES), FLOAT),
            pltpu.SemaphoreType.DMA((copies,)),
            pltpu.SemaphoreType.DMA((copies,)),
            *reduce_scratch(plan),
        ],
        compiler_params=pltpu.CompilerParams(
            collective_id=1, has_side_effects=True, vmem_limit_bytes=56 << 20
        ),
    )(held, loss, grads)


def update_body(
    plan, step_ref, total_ref, scalars_ref, master_ref, first_ref, second_ref,
    master_out, first_out, second_out, copy_out, loss_out, norm_out, line
):
    rows, length = plan.rows, plan.length
    device = lax.axis_index("dp") * 2 + lax.axis_index("rep")
    position_in = lax.broadcasted_iota(jnp.int32, (rows, LANES), 0) * LANES + lane_iota(rows)
    flat = position_in + device * length
    table = layout()
    early, late = table["enc_ln1g"][0], table["encg"][0]
    rate_part = jnp.where(flat < early, 0.75, jnp.where(flat < late, 0.9, 1.0))
    decay_part = jnp.where(in_segments(flat, matrix_segments()), DECAY, 0.0)
    line[...] = jnp.zeros_like(line)
    line[pl.ds(0, length)] = master_ref[...]
    master = line[...].reshape(rows, LANES)
    line[pl.ds(0, length)] = first_ref[...]
    first = line[...].reshape(rows, LANES)
    line[pl.ds(0, length)] = second_ref[...]
    second = line[...].reshape(rows, LANES)
    loss_out[0, 0] = scalars_ref[0, 0]
    norm_out[0, 0] = scalars_ref[0, 1]
    norms = jnp.full((1, LANES), scalars_ref[0, 1])
    weights = jnp.full((1, LANES), scalars_ref[0, 2])
    gradient = total_ref[...] / weights
    clipped = gradient * jnp.minimum(1.0, CLIP / norms)
    fade = 1.0 / jnp.full((1, LANES), lax.shift_left(1, step_ref[0]).astype(FLOAT))
    new_first = BETA_ONE * first + (1.0 - BETA_ONE) * clipped
    new_second = BETA_TWO * second + (1.0 - BETA_TWO) * clipped * clipped
    first_hat = new_first / (1.0 - fade)
    second_hat = new_second / (1.0 - fade)
    new_master = master - LEARN * rate_part * (
        first_hat / (jnp.sqrt(second_hat) + EPSILON) + decay_part * master
    )
    master_out[...] = new_master.reshape(rows * LANES)[:length]
    first_out[...] = new_first.reshape(rows * LANES)[:length]
    second_out[...] = new_second.reshape(rows * LANES)[:length]
    copy_out[...] = new_master.reshape(rows * LANES)[:length].astype(BRAIN)


def update(step, total, scalars, master, first, second, plan):
    vmem = pl.BlockSpec(memory_space=pltpu.VMEM)
    smem = pl.BlockSpec(memory_space=pltpu.SMEM)
    flat = jax.ShapeDtypeStruct((plan.length,), FLOAT)
    single = jax.ShapeDtypeStruct((1, 1), FLOAT)
    return pl.pallas_call(
        functools.partial(update_body, plan),
        out_shape=(flat, flat, flat, jax.ShapeDtypeStruct((plan.length,), BRAIN), single, single),
        in_specs=[smem, vmem, smem, vmem, vmem, vmem],
        out_specs=(vmem, vmem, vmem, vmem, smem, smem),
        scratch_shapes=[pltpu.VMEM((plan.rows * LANES,), FLOAT)],
        compiler_params=pltpu.CompilerParams(vmem_limit_bytes=16 << 20),
    )(step, total, scalars, master, first, second)


def half_turn(frame, start, rows):
    here = pltpu.roll(frame[pl.ds(start, rows), :], 64, 1)
    below = pltpu.roll(frame[pl.ds(start + 1, rows), :], 64, 1)
    return jnp.where(lane_iota(rows) < 64, here, below)


def assemble(plan, slots, even, odd):
    for index in range(plan.count):
        base, used = plan.base(index), plan.used(index)
        a, rest = divmod(index, 8)
        block = slots[a, rest // 4, rest // 2 % 2, rest % 2].astype(FLOAT)[:used]
        if plan.lead(index):
            before = even[pl.ds(base, 1), :]
            even[pl.ds(base, used), :] = block
            even[pl.ds(base, 1), :] = before + block[0:1]
        else:
            even[pl.ds(base, used), :] = block
    span = 256
    total = (plan.frame_rows - 16) // span

    @pl.loop(0, total)
    def _(step):
        start = pl.multiple_of(step * span, span)
        odd[pl.ds(start, span), :] = half_turn(even, start, span)

    rest = plan.frame_rows - 16 - total * span
    odd[pl.ds(total * span, rest), :] = half_turn(even, total * span, rest)


def read_param(even, odd, name, target):
    offset, shape = layout()[name]
    rows, width = (1, shape[0]) if len(shape) == 1 else shape
    base, late = divmod(offset, LANES)
    frames = (even, odd) if late == 0 else (odd, even)
    whole, half = divmod(width, LANES)
    kind = target.dtype
    if rows == 1:
        for col in range(whole):
            target[:, pl.ds(col * LANES, LANES)] = frames[0][pl.ds(base + col, 1), :].astype(kind)
        if half:
            tail = frames[0][pl.ds(base + whole, 1), :]
            target[:, pl.ds(whole * LANES, half)] = tail[:, :half].astype(kind)
        return
    if not half:
        for col in range(whole):
            piece = frames[0][pl.ds(base + col, rows, stride=whole), :]
            target[:, pl.ds(col * LANES, LANES)] = piece.astype(kind)
        return
    stride = 2 * width // LANES
    shift = whole + (1 if late else 0)

    def interleave(scratch):
        for col in range(whole + 1):
            size = LANES if col < whole else half
            upper = frames[0][pl.ds(base + col, rows // 2, stride=stride), :]
            lower = frames[1][pl.ds(base + shift + col, rows // 2, stride=stride), :]
            scratch[pl.ds(0, rows // 2, stride=2), :] = upper
            scratch[pl.ds(1, rows // 2, stride=2), :] = lower
            target[:, pl.ds(col * LANES, size)] = scratch[...][:, :size].astype(kind)

    pl.run_scoped(interleave, pltpu.VMEM((rows, LANES), FLOAT))


def write_grad(even, odd, name, value):
    offset, shape = layout()[name]
    rows, width = (1, shape[0]) if len(shape) == 1 else shape
    base, late = divmod(offset, LANES)
    frames = (even, odd) if late == 0 else (odd, even)
    whole, half = divmod(width, LANES)

    def columns():
        for col in range(0, whole, 2):
            size = min(2, whole - col) * LANES
            both = value(col * LANES, size)
            for part in range(size // LANES):
                yield col + part, both[:, part * LANES : (part + 1) * LANES]
        if half:
            tail = value(whole * LANES, half)
            yield whole, jnp.concatenate([tail, jnp.zeros((rows, LANES - half), FLOAT)], axis=1)

    if rows == 1:
        for col, piece in columns():
            frames[0][pl.ds(base + col, 1), :] = piece
        return
    if not half:
        for col, piece in columns():
            frames[0][pl.ds(base + col, rows, stride=whole), :] = piece
        return
    stride = 2 * width // LANES
    shift = whole + (1 if late else 0)

    def interleave(scratch):
        for col, piece in columns():
            scratch[...] = piece
            upper = scratch[pl.ds(0, rows // 2, stride=2), :]
            lower = scratch[pl.ds(1, rows // 2, stride=2), :]
            frames[0][pl.ds(base + col, rows // 2, stride=stride), :] = upper
            frames[1][pl.ds(base + shift + col, rows // 2, stride=stride), :] = lower

    pl.run_scoped(interleave, pltpu.VMEM((rows, LANES), FLOAT))


def emit_slots(plan, even, odd, slots):
    for index in range(plan.count):
        base, used = plan.base(index), plan.used(index)
        a, rest = divmod(index, 8)
        spot = (a, rest // 4, rest // 2 % 2, rest % 2)
        here = pltpu.roll(odd[pl.ds(base + 8, plan.rows), :], 64, 1)
        above = pltpu.roll(odd[pl.ds(base + 7, plan.rows), :], 64, 1)
        late = jnp.where(lane_iota(plan.rows) < 64, above, here)
        slots[spot] = (even[pl.ds(base, plan.rows), :] + late).astype(BRAIN)


def dot(left, right, dims=(((1,), (0,)), ((), ()))):
    return lax.dot_general(left, right, dims, preferred_element_type=FLOAT)


def place_table(count, rows, width):
    quarter = width // 4
    omega = 1.0 / 10000.0 ** (np.arange(quarter) / quarter)
    index = np.arange(count)
    across = (index // GRID)[:, None] * omega
    along = (index % GRID)[:, None] * omega
    table = np.zeros((rows, width), np.float32)
    table[:count] = np.concatenate(
        [np.sin(across), np.cos(across), np.sin(along), np.cos(along)], axis=-1
    )
    return table


def split_two(value):
    upper = value.astype(BRAIN)
    return upper, (value - upper.astype(FLOAT)).astype(BRAIN)


def norm_parts(value):
    center = value - jnp.mean(value, axis=-1, keepdims=True)
    spread = lax.rsqrt(jnp.mean(center * center, axis=-1, keepdims=True) + LN_EPS)
    return center * spread, spread


def norm_back(grad, value, gain):
    unit, spread = norm_parts(value)
    d_gain = jnp.sum(grad * unit, axis=0, keepdims=True)
    d_shift = jnp.sum(grad, axis=0, keepdims=True)
    scaled = grad * gain
    middle = jnp.mean(scaled, axis=-1, keepdims=True)
    along = jnp.mean(scaled * unit, axis=-1, keepdims=True)
    return spread * (scaled - middle - unit * along), d_gain, d_shift


def gelu_parts(value):
    half = 0.5 + 0.5 * lax.erf(value * 0.7071067811865476)
    bell = jnp.exp2(value * value * (-0.5 * LOG_TWO_E)) * 0.3989422804014327
    return value * half, half + value * bell


def head_only(value, head, size):
    lane = lax.broadcasted_iota(jnp.int32, value.shape, 1)
    inside = (lane >= head * size) & (lane < (head + 1) * size)
    return jnp.where(inside, value, jnp.zeros_like(value))


def attend(t_ref, chance_ref, usable, width, heads):
    size = width // heads
    query, keys = t_ref[:, pl.ds(0, width)], t_ref[:, pl.ds(width, width)]
    values = t_ref[:, pl.ds(2 * width, width)].T
    factor = size ** (-0.5) * LOG_TWO_E
    mixed = []
    for head in range(heads):
        raw = dot(head_only(keys, head, size), query, PAIR)
        raw = jnp.where(usable, raw, -1e30)
        top = jnp.max(raw, axis=0, keepdims=True)
        power = jnp.exp2((raw - top) * factor)
        chance = power * (1.0 / jnp.sum(power, axis=0, keepdims=True))
        chance_ref[head] = chance
        mixed.append(dot(values[head * size : (head + 1) * size], chance.astype(BRAIN)))
    return jnp.concatenate(mixed, axis=0).astype(BRAIN).T


def attend_back(d_mixed, t_ref, dt_ref, chance_ref, width, heads):
    size = width // heads
    scale = size ** (-0.5)
    query, keys = t_ref[:, pl.ds(0, width)], t_ref[:, pl.ds(width, width)]
    values = t_ref[:, pl.ds(2 * width, width)]
    across = keys.T
    d_query = []
    d_keys = d_values = None
    for head in range(heads):
        chance = chance_ref[head]
        d_here = head_only(d_mixed, head, size)
        d_chance = dot(head_only(values, head, size), d_mixed, PAIR)
        along = jnp.sum(chance * d_chance, axis=0, keepdims=True)
        d_scores = (chance * (d_chance - along)).astype(BRAIN)
        part = dot(chance.astype(BRAIN), d_here)
        d_values = part if d_values is None else d_values + part
        part = dot(d_scores, head_only(query, head, size))
        d_keys = part if d_keys is None else d_keys + part
        d_query.append(dot(across[head * size : (head + 1) * size], d_scores))
    d_query = (jnp.concatenate(d_query, axis=0) * scale).astype(BRAIN).T
    dt_ref[:, pl.ds(0, width)] = d_query
    dt_ref[:, pl.ds(width, width)] = (d_keys * scale).astype(BRAIN)
    dt_ref[:, pl.ds(2 * width, width)] = d_values.astype(BRAIN)


class Weights:
    def __init__(self, refs):
        self.refs = dict(zip(layout(), refs))

    def __call__(self, name):
        return self.refs[name][...]


def block_ahead(hidden, keep, weights, prefix, heads, usable):
    width = hidden.shape[1]
    keep["x"][...] = hidden
    unit, unused = norm_parts(hidden)
    normed = (unit * weights(prefix + "ln1g") + weights(prefix + "ln1b")).astype(BRAIN)
    keep["a"][...] = normed
    bias = weights(prefix + "qvb")
    t_ref = keep["t"]
    for part in range(3):
        cols = pl.ds(part * width, width)
        value = dot(normed, weights.refs[prefix + "qkv"][:, cols])
        if part != 1:
            value = value + bias[:, (part // 2) * width : (part // 2 + 1) * width]
        t_ref[:, cols] = value.astype(BRAIN)
    mixed = attend(t_ref, keep["p"], usable, width, heads)
    keep["o"][...] = mixed
    middle = hidden + (dot(mixed, weights(prefix + "proj")) + weights(prefix + "projb"))
    keep["m"][...] = middle
    unit, unused = norm_parts(middle)
    second = (unit * weights(prefix + "ln2g") + weights(prefix + "ln2b")).astype(BRAIN)
    keep["b"][...] = second
    inner = dot(second, weights(prefix + "fc1")) + weights(prefix + "fc1b")
    active, slope = gelu_parts(inner)
    keep["s"][...] = slope
    keep["g"][...] = active.astype(BRAIN)
    return middle + (dot(keep["g"][...], weights(prefix + "fc2")) + weights(prefix + "fc2b"))


def block_home(grad, keep, weights, prefix, heads, sums):
    width = grad.shape[1]
    d_branch = grad.astype(BRAIN)
    keep["dz"][...] = d_branch
    d_inner = (dot(d_branch, weights(prefix + "fc2"), PAIR) * keep["s"][...]).astype(BRAIN)
    keep["du"][...] = d_inner
    d_second = dot(d_inner, weights(prefix + "fc1"), PAIR)
    d_middle, d_gain, d_shift = norm_back(d_second, keep["m"][...], weights(prefix + "ln2g"))
    sums(prefix + "ln2g", d_gain)
    sums(prefix + "ln2b", d_shift)
    d_middle = d_middle + grad
    d_output = d_middle.astype(BRAIN)
    keep["dy"][...] = d_output
    d_mixed = dot(d_output, weights(prefix + "proj"), PAIR).astype(BRAIN)
    attend_back(d_mixed, keep["t"], keep["dt"], keep["p"], width, heads)
    d_normed = dot(keep["dt"][...], weights(prefix + "qkv"), PAIR)
    d_hidden, d_gain, d_shift = norm_back(d_normed, keep["x"][...], weights(prefix + "ln1g"))
    sums(prefix + "ln1g", d_gain)
    sums(prefix + "ln1b", d_shift)
    return d_middle + d_hidden


def kept_shapes(count, rows, width, hidden, heads):
    return {
        "x": (False, (rows, width), FLOAT),
        "a": (True, (rows, width), BRAIN),
        "t": (False, (rows, 3 * width), BRAIN),
        "p": (False, (heads, rows, rows), FLOAT),
        "o": (True, (rows, width), BRAIN),
        "m": (False, (rows, width), FLOAT),
        "b": (True, (rows, width), BRAIN),
        "s": (False, (rows, hidden), FLOAT),
        "g": (True, (rows, hidden), BRAIN),
        "dz": (True, (rows, width), BRAIN),
        "du": (True, (rows, hidden), BRAIN),
        "dy": (True, (rows, width), BRAIN),
        "dt": (True, (rows, 3 * width), BRAIN),
    }


def kept_scratch(count, rows, width, hidden, heads):
    shapes = []
    for every, shape, kind in kept_shapes(count, rows, width, hidden, heads).values():
        shapes.append(pltpu.VMEM(((count,) + shape) if every and count > 1 else shape, kind))
    return shapes


def kept_view(refs, count, rows, width, hidden, heads, image=None):
    view = {}
    table = kept_shapes(count, rows, width, hidden, heads)
    for ref, (name, (every, shape, kind)) in zip(refs, table.items()):
        view[name] = ref.at[image] if every and count > 1 and image is not None else ref
    return view


def block_grads(keep, prefix, emit):
    def rows_of(name):
        value = keep[name][...]
        return value.reshape(-1, value.shape[-1])

    for left, right, name, bias in (
        ("g", "dz", "fc2", "fc2b"),
        ("b", "du", "fc1", "fc1b"),
        ("o", "dy", "proj", "projb"),
        ("a", "dt", "qkv", "qvb"),
    ):
        emit(prefix + name, prefix + bias, rows_of(left), rows_of(right))


def step_body(plan, counts_ref, slots, seen_ref, tgt_ref, meta_ref, spot_enc, spot_dec, grad_out, loss_out, *scratch):
    names = list(layout())
    even, odd, sums_ref, y_hi, y_lo, dy_home, final_all, dpred_all = scratch[:8]
    weights = Weights(scratch[8 : 8 + len(names)])
    enc_refs = scratch[8 + len(names) : 8 + len(names) + 13]
    dec_refs = scratch[8 + len(names) + 13 :]
    assemble(plan, slots, even, odd)
    for name in names:
        read_param(even, odd, name, weights.refs[name])
    even[...] = jnp.zeros_like(even)
    odd[...] = jnp.zeros_like(odd)
    view = odd.at[pl.ds(8, plan.frame_rows)]
    sums_ref[...] = jnp.zeros_like(sums_ref)
    order = {name: number for number, name in enumerate(names)}

    def add_sum(name, value):
        sums_ref[pl.ds(order[name], 1), pl.ds(0, value.shape[1])] += value

    spot = lax.rem(lax.axis_index("dp"), 4)
    own = counts_ref[0, 0]
    lane = lane_iota(8)
    row = lax.broadcasted_iota(jnp.int32, (8, LANES), 0)

    def count_of(hub):
        return jnp.sum(jnp.where((lane == 127) & (row == 0), meta_ref[hub], 0.0)).astype(jnp.int32)

    one, two = count_of(1), count_of(2)
    from_one = jnp.where(spot == 0, 3, jnp.where(spot == 2, 4, 5))
    from_two = jnp.where(spot == 0, 3, jnp.where(spot == 1, 4, 5))
    use_one = (spot == 2) | ((spot != 1) & (one > 2))
    third = jnp.where(own > 2, 2, jnp.where(use_one, 3, 4))
    third_row = jnp.where(own > 2, 2, jnp.where(use_one, from_one, from_two))
    third_count = jnp.where(own > 2, own, jnp.where(use_one, one, two))
    third_meta = jnp.where(own > 2, 0, jnp.where(use_one, 1, 2))

    def pick(image):
        last = image == 2
        source = jnp.where(last, third, image)
        line = jnp.where(last, third_row, image)
        live = jnp.where(last, third_count, own) > line
        kept = meta_ref[jnp.where(last, third_meta, 0), pl.ds(line, 1), :][:, :HOME]
        return source, kept, live.astype(FLOAT)

    def placement(kept):
        number = lax.broadcasted_iota(jnp.int32, (ROWS, HOME), 0).astype(FLOAT)
        return (number == kept).astype(FLOAT)

    visible, begin = [], []
    for image in range(LIVE_CAP):
        source, kept, live = pick(image)
        where = placement(kept).astype(BRAIN)
        visible.append(seen_ref[source])
        begin.append(dot(where, spot_enc[0], DEEP) + dot(where, spot_enc[1], DEEP))
    visible = jnp.concatenate(visible, axis=0)
    begin = jnp.concatenate(begin, axis=0)
    enc_rows = LIVE_CAP * HOME
    enc_shape = (1, enc_rows, D, FF, HEADS)
    enc = kept_view(enc_refs, *enc_shape)
    down = lax.broadcasted_iota(jnp.int32, (enc_rows, enc_rows), 0)
    over = lax.broadcasted_iota(jnp.int32, (enc_rows, enc_rows), 1)
    usable = (down // HOME == over // HOME) & (down % HOME < VIS)
    first_in = dot(visible, weights("patch")) + weights("patchb") + begin
    encoded = block_ahead(first_in, enc, weights, "enc_", HEADS, usable)
    unit, unused = norm_parts(encoded)
    encoder_out = (unit * weights("encg") + weights("encb")).astype(BRAIN)
    embedded = dot(encoder_out, weights("embed")) + weights("embedb")
    upper, lower = split_two(embedded)
    for image in range(LIVE_CAP):
        y_hi[image] = upper[image * HOME : (image + 1) * HOME]
        y_lo[image] = lower[image * HOME : (image + 1) * HOME]
    dec_shape = (LIVE_CAP, ROWS, E, DFF, DHEADS)
    real = lax.broadcasted_iota(jnp.int32, (ROWS, 1), 0) < NP
    usable_dec = lax.broadcasted_iota(jnp.int32, (ROWS, ROWS), 0) < NP

    def one_image(image, total):
        source, kept, live = pick(image)
        where = placement(kept)
        seen = jnp.sum(where, axis=1, keepdims=True)
        where = where.astype(BRAIN)
        grid_in = dot(where, y_hi[image]) + dot(where, y_lo[image])
        grid_in = grid_in + (1.0 - seen) * weights("mask") + spot_dec[...]
        keep = kept_view(dec_refs, *dec_shape, image)
        decoded = block_ahead(grid_in, keep, weights, "dec_", DHEADS, usable_dec)
        unit, unused = norm_parts(decoded)
        final = (unit * weights("decg") + weights("decb")).astype(BRAIN)
        final_all[image] = final
        predicted = dot(final, weights("head")) + weights("headb")
        weight = jnp.where(real, (1.0 - 0.9 * seen) * live, 0.0)
        error = predicted[:NP] - tgt_ref[source].astype(FLOAT)
        weighted = error * weight[:NP]
        total = total + jnp.sum(weighted * error, axis=0, keepdims=True)
        dpred_all[image, pl.ds(0, NP)] = (weighted * (2.0 / PIX)).astype(BRAIN)
        dpred_all[image, pl.ds(NP, ROWS - NP)] = jnp.zeros((ROWS - NP, PIX), BRAIN)
        d_final = dot(dpred_all[image], weights("head"), PAIR)
        d_decoded, d_gain, d_shift = norm_back(d_final, decoded, weights("decg"))
        add_sum("decg", d_gain)
        add_sum("decb", d_shift)
        d_grid = block_home(d_decoded, keep, weights, "dec_", DHEADS, add_sum)
        add_sum("mask", jnp.sum((1.0 - seen) * d_grid, axis=0, keepdims=True))
        dy_home[image] = dot(where, d_grid.astype(BRAIN), DEEP).astype(BRAIN)
        return total

    total = lax.fori_loop(0, LIVE_CAP, one_image, jnp.zeros((1, PIX), FLOAT))
    loss_out[0] = jnp.sum(total) * (1.0 / PIX)

    def emit(name, bias, left, right):
        ones = jnp.ones((16, right.shape[0]), BRAIN)
        summed = dot(ones, right)[0:1]
        if bias.endswith("qvb"):
            width = summed.shape[1] // 3
            summed = jnp.concatenate([summed[:, :width], summed[:, 2 * width :]], axis=1)
        write_grad(even, view, bias, lambda start, size: summed[:, start : start + size])
        turned = left.T
        write_grad(even, view, name, lambda start, size: dot(turned, right[:, start : start + size]))

    d_embedded = dy_home[...].reshape(enc_rows, E)
    emit("embed", "embedb", encoder_out, d_embedded)
    d_seen = dot(d_embedded, weights("embed"), PAIR).astype(BRAIN).astype(FLOAT)
    d_encoded, d_gain, d_shift = norm_back(d_seen, encoded, weights("encg"))
    add_sum("encg", d_gain)
    add_sum("encb", d_shift)
    d_first = block_home(d_encoded, enc, weights, "enc_", HEADS, add_sum).astype(BRAIN)
    emit("patch", "patchb", visible, d_first)
    block_grads(enc, "enc_", emit)
    block_grads(kept_view(dec_refs, *dec_shape), "dec_", emit)
    emit("head", "headb", final_all[...].reshape(-1, E), dpred_all[...].reshape(-1, PIX))
    for name, (offset, shape) in layout().items():
        if name[-4:] in ("ln1g", "ln1b", "ln2g", "ln2b", "encg", "encb", "decg", "decb", "mask"):
            write_grad(
                even,
                view,
                name,
                lambda start, size, name=name: sums_ref[pl.ds(order[name], 1), pl.ds(start, size)],
            )
    emit_slots(plan, even, odd, grad_out)


def weight_scratch():
    shapes = []
    for name, (offset, shape) in layout().items():
        if len(shape) == 1:
            shapes.append(pltpu.VMEM((1, *shape), FLOAT))
        else:
            shapes.append(pltpu.VMEM(shape, BRAIN))
    return shapes


def local_step(counts, slots, seen, targets, meta, plan):
    vmem = pl.BlockSpec(memory_space=pltpu.VMEM)
    smem = pl.BlockSpec(memory_space=pltpu.SMEM)
    table = place_table(NP, ROWS, D)
    upper = table.astype(BRAIN)
    spot_enc = jnp.asarray(np.stack([upper, (table - upper.astype(np.float32)).astype(BRAIN)]))
    spot_dec = jnp.asarray(place_table(NP, ROWS, E))
    return pl.pallas_call(
        functools.partial(step_body, plan),
        out_shape=(
            jax.ShapeDtypeStruct((plan.outer, 2, 2, 2, plan.rows, LANES), BRAIN),
            jax.ShapeDtypeStruct((1,), FLOAT),
        ),
        in_specs=[smem] + [vmem] * 6,
        out_specs=(vmem, smem),
        scratch_shapes=[
            pltpu.VMEM((plan.frame_rows, LANES), FLOAT),
            pltpu.VMEM((plan.frame_rows + 8, LANES), FLOAT),
            pltpu.VMEM((48, E), FLOAT),
            pltpu.VMEM((LIVE_CAP, HOME, E), BRAIN),
            pltpu.VMEM((LIVE_CAP, HOME, E), BRAIN),
            pltpu.VMEM((LIVE_CAP, HOME, E), BRAIN),
            pltpu.VMEM((LIVE_CAP, ROWS, E), BRAIN),
            pltpu.VMEM((LIVE_CAP, ROWS, PIX), BRAIN),
            *weight_scratch(),
            *kept_scratch(1, LIVE_CAP * HOME, D, FF, HEADS),
            *kept_scratch(LIVE_CAP, ROWS, E, DFF, DHEADS),
        ],
        compiler_params=pltpu.CompilerParams(vmem_limit_bytes=58 << 20),
    )(counts, slots, seen, targets, meta, spot_enc, spot_dec)


def on_device(patches, targets, keep, counts, step, master, first, second):
    plan = Plan(master.shape[0], lax.axis_size(("dp", "rep")))
    slots, seen, wanted, meta = gather_params(counts, keep, master, patches, targets, plan)
    grads, loss = local_step(counts, slots, seen, wanted, meta, plan)
    total, scalars = reduce_grads(counts, loss, grads, plan)
    outs = update(step, total, scalars, master, first, second, plan)
    return (*outs[:4], outs[4].reshape(()), outs[5].reshape(()))


def solution(mesh):
    return jax.shard_map(
        on_device,
        mesh=mesh,
        in_specs=(
            P(("dp", "rep"), None, None),
            P(("dp", "rep"), None, None),
            P(("dp", "rep"), None),
            P("dp", "rep"),
            P(),
            P(("dp", "rep")),
            P(("dp", "rep")),
            P(("dp", "rep")),
        ),
        out_specs=(
            P(("dp", "rep")),
            P(("dp", "rep")),
            P(("dp", "rep")),
            P(("dp", "rep")),
            P(),
            P(),
        ),
        check_vma=False,
    )
```

```python
import functools
import itertools
import math

import jax
import jax.numpy as jnp
import numpy as np
from jax import lax
from jax.experimental import pallas as pl
from jax.experimental.pallas import tpu as pltpu
from jax.sharding import PartitionSpec as P

D = 192
HEADS = 3
FF = 768
E = 256
DHEADS = 8
DFF = 1024
PIX = 768
GRID = 14
VIS = 49
NP = 196

FLOAT = jnp.float32
BRAIN = jnp.bfloat16
CLIP = 0.05
BETA_ONE = 0.5
BETA_TWO = 0.5
LEARN = 0.01
DECAY = 0.05
EPSILON = 1e-08
LN_EPS = 1e-06

ROWS = 208
HOME = 64
LIVE_CAP = 3
PAIR = ((1,), (1,)), ((), ())
DEEP = ((0,), (0,)), ((), ())
LOG_TWO_E = 1.4426950408889634


def block_table(prefix, width, hidden, proj_fan, rate):
    return [
        (prefix + "ln1g", (width,), "gain", 1, rate),
        (prefix + "ln1b", (width,), "bias", 1, rate),
        (prefix + "qkv", (width, 3 * width), "matrix", width, rate),
        (prefix + "qvb", (2 * width,), "bias", 1, rate),
        (prefix + "proj", (width, width), "matrix", proj_fan, rate),
        (prefix + "projb", (width,), "bias", 1, rate),
        (prefix + "ln2g", (width,), "gain", 1, rate),
        (prefix + "ln2b", (width,), "bias", 1, rate),
        (prefix + "fc1", (width, hidden), "matrix", width, rate),
        (prefix + "fc1b", (hidden,), "bias", 1, rate),
        (prefix + "fc2", (hidden, width), "matrix", hidden, rate),
        (prefix + "fc2b", (width,), "bias", 1, rate),
    ]


def param_table():
    table = [("patch", (PIX, D), "matrix", PIX, 0.75), ("patchb", (D,), "bias", 1, 0.75)]
    table = table + block_table("enc_", D, FF, D // 4, 0.9)
    table = table + [
        ("encg", (D,), "gain", 1, 1.0),
        ("encb", (D,), "bias", 1, 1.0),
        ("embed", (D, E), "matrix", D, 1.0),
        ("embedb", (E,), "bias", 1, 1.0),
        ("mask", (E,), "token", 1, 1.0),
    ]
    table = table + block_table("dec_", E, DFF, E // 8, 1.0)
    table = table + [
        ("decg", (E,), "gain", 1, 1.0),
        ("decb", (E,), "bias", 1, 1.0),
        ("head", (E, PIX), "matrix", E, 1.0),
        ("headb", (PIX,), "bias", 1, 1.0),
    ]
    return table


MESH = pl.DeviceIdType.MESH
LANES = 128


def layout():
    table = {}
    offset = 0
    for name, shape, kind, fan, rate in param_table():
        table[name] = (offset, shape)
        offset += math.prod(shape)
    return table


class Plan:
    def __init__(self, length, count):
        self.length = length
        self.count = count
        self.outer = count // 8
        self.rows = -(-((LANES - 1 + length + LANES - 1) // LANES) // 16) * 16
        units = self.rows // 16
        first = max(1, min(round(0.389 * units), (units - 1) // 2))
        sizes = (first * 16, first * 16, self.rows - 2 * first * 16)
        starts = (0, sizes[0], sizes[0] + sizes[1])
        self.parts = tuple(zip(starts, sizes))
        self.orders = ("ACB", "ABC", "CBA")
        self.frame_rows = -(-(length * count) // LANES // 8 * 8) + 64

    def base(self, index):
        return index * self.length // LANES

    def lead(self, index):
        return index * self.length % LANES

    def used(self, index):
        return (self.lead(index) + self.length + LANES - 1) // LANES


def position():
    chip = lax.axis_index("dp")
    core = lax.axis_index("rep")
    return {"A": chip // 4, "B": chip // 2 % 2, "C": chip % 2, "r": core}


def device_of(place):
    return (place["A"] * 4 + place["B"] * 2 + place["C"], place["r"])


def moved(place, dim, value):
    changed = dict(place)
    changed[dim] = value
    return changed


def peer_values(place, dim, outer):
    if dim == "A":
        return [lax.rem(place["A"] + step, outer) for step in range(1, outer)]
    return [1 - place[dim]]


def source_values(place, dim, outer):
    if dim == "A":
        return [lax.rem(place["A"] + outer - step, outer) for step in range(1, outer)]
    return [1 - place[dim]]


def meet(places):
    barrier = pltpu.get_barrier_semaphore()
    for place in places:
        pl.semaphore_signal(barrier, inc=1, device_id=device_of(place), device_id_type=MESH)
    pl.semaphore_wait(barrier, len(places))


def partners(place, outer):
    a, b, c, r = (place[dim] for dim in "ABCr")
    group = [
        {"A": a, "B": (b + k // 4) % 2, "C": (c + k // 2 % 2) % 2, "r": (r + k % 2) % 2}
        for k in range(1, 8)
    ]
    return group, [moved(place, "A", value) for value in peer_values(place, "A", outer)]


class Sender:
    def __init__(self, send, recv):
        self.send, self.recv, self.used = send, recv, 0

    def start(self, source, target, place):
        copy = pltpu.make_async_remote_copy(
            src_ref=source,
            dst_ref=target,
            send_sem=self.send.at[self.used],
            recv_sem=self.recv.at[self.used],
            device_id=device_of(place),
            device_id_type=MESH,
        )
        self.used += 1
        copy.start()
        return copy


def lane_iota(rows):
    return lax.broadcasted_iota(jnp.int32, (rows, LANES), 1)


HUBS = (1, 2)


def others_of(hub):
    return [spot for spot in range(4) if spot != hub]


def gather_body(
    plan, counts_ref, keep_ref, x_ref, patches_ref, targets_ref,
    out_ref, seen_ref, tgt_ref, meta_ref,
    line, rolled, pixels, spare, send, recv, local, hand, taken
):
    outer, rows = plan.outer, plan.rows
    place = position()
    a, b, c, r = (place[dim] for dim in "ABCr")
    spot = b * 2 + c
    pixel_copy = pltpu.make_async_copy(patches_ref, pixels, local.at[0])
    pixel_copy.start()
    target_copy = pltpu.make_async_copy(
        targets_ref.at[pl.ds(0, LIVE_CAP)], tgt_ref.at[pl.ds(0, LIVE_CAP)], local.at[1]
    )
    target_copy.start()
    index = ((a * 2 + b) * 2 + c) * 2 + r
    lead = lax.rem(index * plan.length, LANES)
    line[...] = jnp.zeros_like(line)
    line[pl.ds(0, plan.length)] = x_ref[...]
    turned = pltpu.roll(line[...].reshape(rows, LANES), lead, 1)
    rolled[pl.ds(0, 8), :] = jnp.zeros((8, LANES), FLOAT)
    rolled[pl.ds(8, rows), :] = turned
    block = jnp.where(lane_iota(rows) >= lead, turned, rolled[pl.ds(7, rows), :])
    out_ref[a, b, c, r] = block.astype(BRAIN)
    group, column = partners(place, outer)
    meet(group + column)
    sender = Sender(send, recv)
    everything = []

    def region(part, whole, fixed):
        start, size = plan.parts[part]
        index = []
        for dim, extent in (("A", outer), ("B", 2), ("C", 2)):
            if dim in fixed:
                index.append(fixed[dim])
            else:
                index.append(pl.ds(0, extent) if dim in whole else place[dim])
        return out_ref.at[(*index, r, pl.ds(start, size))]

    def hand_over(hub, number):
        other = others_of(hub)[number]
        target = {"A": a, "B": other // 2, "C": other % 2, "r": r}
        pairs = (
            (spare.at[number], seen_ref.at[2 + hub]),
            (meta_ref.at[0], meta_ref.at[hub]),
            (targets_ref.at[3 + number], tgt_ref.at[2 + hub]),
        )
        return [
            pltpu.make_async_remote_copy(
                src_ref=source,
                dst_ref=to,
                send_sem=hand.at[hub - 1, number, kind],
                recv_sem=taken.at[hub - 1, kind],
                device_id=device_of(target),
                device_id_type=MESH,
            )
            for kind, (source, to) in enumerate(pairs)
        ]

    fresh = [(part, "", [{}]) for part in range(3)]
    sibling = moved(place, "r", 1 - r)
    for phase in range(4):
        flights = []
        if phase < 3:
            for part in range(3):
                order = plan.orders[part]
                dim = order[phase]
                source = region(part, order[:phase], {})
                for value in peer_values(place, dim, outer):
                    flights.append(sender.start(source, source, moved(place, dim, value)))
        for part, whole, news in fresh:
            for fixed in news:
                source = region(part, whole, fixed)
                everything.append(sender.start(source, source, sibling))
        fresh = []
        if phase < 3:
            for part in range(3):
                order = plan.orders[part]
                dim = order[phase]
                news = [{dim: value} for value in source_values(place, dim, outer)]
                fresh.append((part, order[:phase], news))
        if phase == 0:
            lane = lane_iota(8)
            row = lax.broadcasted_iota(jnp.int32, (8, LANES), 0)
            mine = jnp.where((lane == LANES - 1) & (row == 0), counts_ref[0, 0].astype(FLOAT), -1.0)
            meta_ref[0] = mine
            meta_ref[0, pl.ds(0, keep_ref.shape[0]), pl.ds(0, VIS)] = keep_ref[...].astype(FLOAT)
            pixel_copy.wait()

            def visible(image):
                number = lax.broadcasted_iota(jnp.int32, (NP, HOME), 0).astype(FLOAT)
                where = (number == meta_ref[0, pl.ds(image, 1), :][:, :HOME]).astype(BRAIN)
                return dot(where, pixels[image], DEEP).astype(BRAIN)

            for hub in HUBS:

                @pl.when(spot == hub)
                def _(hub=hub):
                    for number in range(3):
                        spare[number] = visible(3 + number)
                    for number in range(3):
                        for copy in hand_over(hub, number):
                            copy.start()

            for image in range(LIVE_CAP):
                seen_ref[image] = visible(image)
        for copy in flights:
            copy.wait()
    for copy in everything:
        copy.wait()
    for hub in HUBS:

        @pl.when(spot == hub)
        def _(hub=hub):
            for number in range(3):
                for copy in hand_over(hub, number):
                    copy.wait_send()

        @pl.when(spot != hub)
        def _(hub=hub):
            for copy in hand_over(hub, 0):
                copy.wait_recv()

    target_copy.wait()


def reduce_scratch(plan):
    shapes = []
    for part in range(3):
        size = plan.parts[part][1]
        left = list("ABC")
        for dim in reversed(plan.orders[part]):
            left.remove(dim)
            others = tuple(plan.outer if other == "A" else 2 for other in left)
            peers = plan.outer - 1 if dim == "A" else 1
            shapes.append(pltpu.VMEM((peers, *others, size, LANES), BRAIN))
            shapes.append(pltpu.VMEM((peers, *others, size, LANES), BRAIN))
            shapes.append(pltpu.VMEM((*others, size, LANES), FLOAT))
    return shapes


def in_segments(index, segments):
    inside = None
    for start, stop in segments:
        here = (index >= start) & (index < stop)
        inside = here if inside is None else inside | here
    return inside


def matrix_segments():
    found = []
    for name, shape, kind, fan, rate in param_table():
        if kind == "matrix":
            start = layout()[name][0]
            found.append((start, start + math.prod(shape)))
    return found


def reduce_body(
    plan, held_ref, loss_ref, grad_ref, total_out, scalars_out, *scratch
):
    outer, rows = plan.outer, plan.rows
    core_in, rolled, near, far, mine, send, recv = scratch[:7]
    held_refs = scratch[7:]
    place = position()
    a, b, c, r = (place[dim] for dim in "ABCr")
    digits = {"A": a, "B": b, "C": c}
    device = ((a * 2 + b) * 2 + c) * 2 + r
    lead = lax.rem(device * plan.length, LANES)
    group, column = partners(place, outer)
    sender = Sender(send, recv)
    sibling = moved(place, "r", 1 - r)
    pending = []
    core = []
    for part in range(3):
        start, size = plan.parts[part]
        span = pl.ds(start, size)
        full = (pl.ds(0, outer), pl.ds(0, 2), pl.ds(0, 2))
        core.append(
            sender.start(
                grad_ref.at[(*full, 1 - r, span)], core_in.at[(*full, span)], sibling
            )
        )
    state = []
    for part in range(3):
        core[part].wait_recv()
        pending.append(core[part])
        start, size = plan.parts[part]
        span = pl.ds(start, size)

        def current(at, span=span):
            index = tuple(at[dim] for dim in "ABC")
            own = grad_ref[(*index, r, span)].astype(FLOAT)
            return own + core_in[(*index, span)].astype(FLOAT)

        state.append((list("ABC"), current))
    flights = [None] * 3

    def launch(part, phase):
        left, current = state[part]
        dim = plan.orders[part][2 - phase]
        staged, received, kept = held_refs[(part * 3 + phase) * 3 : (part * 3 + phase) * 3 + 3]
        others = [other for other in left if other != dim]
        extents = [outer if other == "A" else 2 for other in others]
        started = []
        for number, value in enumerate(peer_values(place, dim, outer)):
            for picks in itertools.product(*[range(extent) for extent in extents]):
                at = dict(zip(others, picks))
                at[dim] = value
                staged[(number, *picks)] = current(at).astype(BRAIN)
            copy = sender.start(
                staged.at[number], received.at[number], moved(place, dim, value)
            )
            started.append(copy)
            pending.append(copy)
        for picks in itertools.product(*[range(extent) for extent in extents]):
            at = dict(zip(others, picks))
            at[dim] = digits[dim]
            kept[picks] = current(at)
        flights[part] = started

        def after(at, kept=kept, received=received, others=tuple(others), count=len(started)):
            index = tuple(at[other] for other in others)
            total = kept[index]
            for number in range(count):
                total = total + received[(number, *index)].astype(FLOAT)
            return total

        state[part] = (others, after)

    for phase in range(3):
        for part in range(3):
            if phase > 0:
                for copy in flights[part]:
                    copy.wait_recv()
            launch(part, phase)
    position_in = lax.broadcasted_iota(jnp.int32, (rows, LANES), 0) * LANES + lane_iota(rows)
    for part in range(3):
        for copy in flights[part]:
            copy.wait_recv()
        start, size = plan.parts[part]
        left, current = state[part]
        rolled[pl.ds(start, size), :] = current({})
    rolled[pl.ds(rows, 8), :] = jnp.zeros((8, LANES), FLOAT)
    shift = lax.rem(LANES - lead, LANES)
    here = pltpu.roll(rolled[pl.ds(0, rows), :], shift, 1)
    below = pltpu.roll(rolled[pl.ds(1, rows), :], shift, 1)
    total = jnp.where(lane_iota(rows) < LANES - lead, here, below)
    total = jnp.where(position_in < plan.length, total, 0.0)
    squares = jnp.sum(total * total)
    lane = lane_iota(8)
    mine[...] = jnp.where(lane == 0, squares, 0.0)
    mine[...] = jnp.where(lane == 1, held_ref[0, 0].astype(FLOAT), mine[...])
    mine[...] = jnp.where(lane == 2, loss_ref[0], mine[...])
    spot = (b * 2 + c) * 2 + r
    near[spot] = mine[...]
    nears = [sender.start(mine, near.at[spot], other) for other in group]
    for copy in nears:
        copy.wait_recv()
    together = near[0]
    for other in range(1, 8):
        together = together + near[other]
    far[a] = together
    rolled[pl.ds(0, 8), :] = together
    fars = [sender.start(rolled.at[pl.ds(0, 8)], far.at[a], other) for other in column]
    for copy in fars:
        copy.wait_recv()
    whole = far[0]
    for other in range(1, outer):
        whole = whole + far[other]
    held = jnp.sum(jnp.where(lane == 1, whole, 0.0)[0:1, :])
    weight_total = held * (0.1 * VIS + (NP - VIS))
    scalars = whole[0:1, :]
    weights = jnp.full((1, LANES), weight_total)
    norms = jnp.sqrt(jnp.full((1, LANES), jnp.sum(jnp.where(lane[0:1] == 0, scalars, 0.0)))) / weights
    losses = jnp.full((1, LANES), jnp.sum(jnp.where(lane[0:1] == 2, scalars, 0.0))) / weights
    scalars_out[...] = jnp.where(lane[0:1] == 0, losses, jnp.where(lane[0:1] == 1, norms, weights))
    total_out[...] = total
    for copy in pending + nears + fars:
        copy.wait_send()


def update_body(
    plan, step_ref, total_ref, scalars_ref, master_ref, first_ref, second_ref,
    master_out, first_out, second_out, copy_out, loss_out, norm_out, line
):
    rows, length = plan.rows, plan.length
    device = lax.axis_index("dp") * 2 + lax.axis_index("rep")
    position_in = lax.broadcasted_iota(jnp.int32, (rows, LANES), 0) * LANES + lane_iota(rows)
    flat = position_in + device * length
    table = layout()
    early, late = table["enc_ln1g"][0], table["encg"][0]
    rate_part = jnp.where(flat < early, 0.75, jnp.where(flat < late, 0.9, 1.0))
    decay_part = jnp.where(in_segments(flat, matrix_segments()), DECAY, 0.0)
    line[...] = jnp.zeros_like(line)
    line[pl.ds(0, length)] = master_ref[...]
    master = line[...].reshape(rows, LANES)
    line[pl.ds(0, length)] = first_ref[...]
    first = line[...].reshape(rows, LANES)
    line[pl.ds(0, length)] = second_ref[...]
    second = line[...].reshape(rows, LANES)
    loss_out[0, 0] = scalars_ref[0, 0]
    norm_out[0, 0] = scalars_ref[0, 1]
    norms = jnp.full((1, LANES), scalars_ref[0, 1])
    weights = jnp.full((1, LANES), scalars_ref[0, 2])
    gradient = total_ref[...] / weights
    clipped = gradient * jnp.minimum(1.0, CLIP / norms)
    fade = 1.0 / jnp.full((1, LANES), lax.shift_left(1, step_ref[0]).astype(FLOAT))
    new_first = BETA_ONE * first + (1.0 - BETA_ONE) * clipped
    new_second = BETA_TWO * second + (1.0 - BETA_TWO) * clipped * clipped
    first_hat = new_first / (1.0 - fade)
    second_hat = new_second / (1.0 - fade)
    new_master = master - LEARN * rate_part * (
        first_hat / (jnp.sqrt(second_hat) + EPSILON) + decay_part * master
    )
    master_out[...] = new_master.reshape(rows * LANES)[:length]
    first_out[...] = new_first.reshape(rows * LANES)[:length]
    second_out[...] = new_second.reshape(rows * LANES)[:length]
    copy_out[...] = new_master.reshape(rows * LANES)[:length].astype(BRAIN)


def update(step, total, scalars, master, first, second, plan):
    vmem = pl.BlockSpec(memory_space=pltpu.VMEM)
    smem = pl.BlockSpec(memory_space=pltpu.SMEM)
    flat = jax.ShapeDtypeStruct((plan.length,), FLOAT)
    single = jax.ShapeDtypeStruct((1, 1), FLOAT)
    return pl.pallas_call(
        functools.partial(update_body, plan),
        out_shape=(flat, flat, flat, jax.ShapeDtypeStruct((plan.length,), BRAIN), single, single),
        in_specs=[smem, vmem, smem, vmem, vmem, vmem],
        out_specs=(vmem, vmem, vmem, vmem, smem, smem),
        scratch_shapes=[pltpu.VMEM((plan.rows * LANES,), FLOAT)],
        compiler_params=pltpu.CompilerParams(vmem_limit_bytes=16 << 20),
    )(step, total, scalars, master, first, second)


def half_turn(frame, start, rows):
    here = pltpu.roll(frame[pl.ds(start, rows), :], 64, 1)
    below = pltpu.roll(frame[pl.ds(start + 1, rows), :], 64, 1)
    return jnp.where(lane_iota(rows) < 64, here, below)


def assemble(plan, slots, even, odd):
    for index in range(plan.count):
        base, used = plan.base(index), plan.used(index)
        a, rest = divmod(index, 8)
        block = slots[a, rest // 4, rest // 2 % 2, rest % 2].astype(FLOAT)[:used]
        if plan.lead(index):
            before = even[pl.ds(base, 1), :]
            even[pl.ds(base, used), :] = block
            even[pl.ds(base, 1), :] = before + block[0:1]
        else:
            even[pl.ds(base, used), :] = block
    span = 256
    total = (plan.frame_rows - 16) // span

    @pl.loop(0, total)
    def _(step):
        start = pl.multiple_of(step * span, span)
        odd[pl.ds(start, span), :] = half_turn(even, start, span)

    rest = plan.frame_rows - 16 - total * span
    odd[pl.ds(total * span, rest), :] = half_turn(even, total * span, rest)


def read_param(even, odd, name, target):
    offset, shape = layout()[name]
    rows, width = (1, shape[0]) if len(shape) == 1 else shape
    base, late = divmod(offset, LANES)
    frames = (even, odd) if late == 0 else (odd, even)
    whole, half = divmod(width, LANES)
    kind = target.dtype
    if rows == 1:
        for col in range(whole):
            target[:, pl.ds(col * LANES, LANES)] = frames[0][pl.ds(base + col, 1), :].astype(kind)
        if half:
            tail = frames[0][pl.ds(base + whole, 1), :]
            target[:, pl.ds(whole * LANES, half)] = tail[:, :half].astype(kind)
        return
    if not half:
        for col in range(whole):
            piece = frames[0][pl.ds(base + col, rows, stride=whole), :]
            target[:, pl.ds(col * LANES, LANES)] = piece.astype(kind)
        return
    stride = 2 * width // LANES
    shift = whole + (1 if late else 0)

    def interleave(scratch):
        for col in range(whole + 1):
            size = LANES if col < whole else half
            upper = frames[0][pl.ds(base + col, rows // 2, stride=stride), :]
            lower = frames[1][pl.ds(base + shift + col, rows // 2, stride=stride), :]
            scratch[pl.ds(0, rows // 2, stride=2), :] = upper
            scratch[pl.ds(1, rows // 2, stride=2), :] = lower
            target[:, pl.ds(col * LANES, size)] = scratch[...][:, :size].astype(kind)

    pl.run_scoped(interleave, pltpu.VMEM((rows, LANES), FLOAT))


def write_grad(even, odd, name, value):
    offset, shape = layout()[name]
    rows, width = (1, shape[0]) if len(shape) == 1 else shape
    base, late = divmod(offset, LANES)
    frames = (even, odd) if late == 0 else (odd, even)
    whole, half = divmod(width, LANES)

    def columns():
        for col in range(0, whole, 2):
            size = min(2, whole - col) * LANES
            both = value(col * LANES, size)
            for part in range(size // LANES):
                yield col + part, both[:, part * LANES : (part + 1) * LANES]
        if half:
            tail = value(whole * LANES, half)
            yield whole, jnp.concatenate([tail, jnp.zeros((rows, LANES - half), FLOAT)], axis=1)

    if rows == 1:
        for col, piece in columns():
            frames[0][pl.ds(base + col, 1), :] = piece
        return
    if not half:
        for col, piece in columns():
            frames[0][pl.ds(base + col, rows, stride=whole), :] = piece
        return
    stride = 2 * width // LANES
    shift = whole + (1 if late else 0)

    def interleave(scratch):
        for col, piece in columns():
            scratch[...] = piece
            upper = scratch[pl.ds(0, rows // 2, stride=2), :]
            lower = scratch[pl.ds(1, rows // 2, stride=2), :]
            frames[0][pl.ds(base + col, rows // 2, stride=stride), :] = upper
            frames[1][pl.ds(base + shift + col, rows // 2, stride=stride), :] = lower

    pl.run_scoped(interleave, pltpu.VMEM((rows, LANES), FLOAT))


def emit_slots(plan, even, odd, slots):
    for index in range(plan.count):
        base, used = plan.base(index), plan.used(index)
        a, rest = divmod(index, 8)
        spot = (a, rest // 4, rest // 2 % 2, rest % 2)
        here = pltpu.roll(odd[pl.ds(base + 8, plan.rows), :], 64, 1)
        above = pltpu.roll(odd[pl.ds(base + 7, plan.rows), :], 64, 1)
        late = jnp.where(lane_iota(plan.rows) < 64, above, here)
        slots[spot] = (even[pl.ds(base, plan.rows), :] + late).astype(BRAIN)


def dot(left, right, dims=(((1,), (0,)), ((), ()))):
    return lax.dot_general(left, right, dims, preferred_element_type=FLOAT)


def place_table(count, rows, width):
    quarter = width // 4
    omega = 1.0 / 10000.0 ** (np.arange(quarter) / quarter)
    index = np.arange(count)
    across = (index // GRID)[:, None] * omega
    along = (index % GRID)[:, None] * omega
    table = np.zeros((rows, width), np.float32)
    table[:count] = np.concatenate(
        [np.sin(across), np.cos(across), np.sin(along), np.cos(along)], axis=-1
    )
    return table


def split_two(value):
    upper = value.astype(BRAIN)
    return upper, (value - upper.astype(FLOAT)).astype(BRAIN)


def norm_parts(value):
    center = value - jnp.mean(value, axis=-1, keepdims=True)
    spread = lax.rsqrt(jnp.mean(center * center, axis=-1, keepdims=True) + LN_EPS)
    return center * spread, spread


def norm_back(grad, value, gain):
    unit, spread = norm_parts(value)
    d_gain = jnp.sum(grad * unit, axis=0, keepdims=True)
    d_shift = jnp.sum(grad, axis=0, keepdims=True)
    scaled = grad * gain
    middle = jnp.mean(scaled, axis=-1, keepdims=True)
    along = jnp.mean(scaled * unit, axis=-1, keepdims=True)
    return spread * (scaled - middle - unit * along), d_gain, d_shift


def gelu_parts(value):
    half = 0.5 + 0.5 * lax.erf(value * 0.7071067811865476)
    bell = jnp.exp2(value * value * (-0.5 * LOG_TWO_E)) * 0.3989422804014327
    return value * half, half + value * bell


def head_only(value, head, size):
    lane = lax.broadcasted_iota(jnp.int32, value.shape, 1)
    inside = (lane >= head * size) & (lane < (head + 1) * size)
    return jnp.where(inside, value, jnp.zeros_like(value))


def attend(t_ref, chance_ref, usable, width, heads):
    size = width // heads
    query, keys = t_ref[:, pl.ds(0, width)], t_ref[:, pl.ds(width, width)]
    values = t_ref[:, pl.ds(2 * width, width)].T
    factor = size ** (-0.5) * LOG_TWO_E
    mixed = []
    for head in range(heads):
        raw = dot(head_only(keys, head, size), query, PAIR)
        raw = jnp.where(usable, raw, -1e30)
        top = jnp.max(raw, axis=0, keepdims=True)
        power = jnp.exp2((raw - top) * factor)
        chance = power * (1.0 / jnp.sum(power, axis=0, keepdims=True))
        chance_ref[head] = chance
        mixed.append(dot(values[head * size : (head + 1) * size], chance.astype(BRAIN)))
    return jnp.concatenate(mixed, axis=0).astype(BRAIN).T


def attend_back(d_mixed, t_ref, dt_ref, chance_ref, width, heads):
    size = width // heads
    scale = size ** (-0.5)
    query, keys = t_ref[:, pl.ds(0, width)], t_ref[:, pl.ds(width, width)]
    values = t_ref[:, pl.ds(2 * width, width)]
    across = keys.T
    d_query = []
    d_keys = d_values = None
    for head in range(heads):
        chance = chance_ref[head]
        d_here = head_only(d_mixed, head, size)
        d_chance = dot(head_only(values, head, size), d_mixed, PAIR)
        along = jnp.sum(chance * d_chance, axis=0, keepdims=True)
        d_scores = (chance * (d_chance - along)).astype(BRAIN)
        part = dot(chance.astype(BRAIN), d_here)
        d_values = part if d_values is None else d_values + part
        part = dot(d_scores, head_only(query, head, size))
        d_keys = part if d_keys is None else d_keys + part
        d_query.append(dot(across[head * size : (head + 1) * size], d_scores))
    d_query = (jnp.concatenate(d_query, axis=0) * scale).astype(BRAIN).T
    dt_ref[:, pl.ds(0, width)] = d_query
    dt_ref[:, pl.ds(width, width)] = (d_keys * scale).astype(BRAIN)
    dt_ref[:, pl.ds(2 * width, width)] = d_values.astype(BRAIN)


class Weights:
    def __init__(self, refs):
        self.refs = dict(zip(layout(), refs))

    def __call__(self, name):
        return self.refs[name][...]


def block_ahead(hidden, keep, weights, prefix, heads, usable):
    width = hidden.shape[1]
    keep["x"][...] = hidden
    unit, unused = norm_parts(hidden)
    normed = (unit * weights(prefix + "ln1g") + weights(prefix + "ln1b")).astype(BRAIN)
    keep["a"][...] = normed
    bias = weights(prefix + "qvb")
    t_ref = keep["t"]
    for part in range(3):
        cols = pl.ds(part * width, width)
        value = dot(normed, weights.refs[prefix + "qkv"][:, cols])
        if part != 1:
            value = value + bias[:, (part // 2) * width : (part // 2 + 1) * width]
        t_ref[:, cols] = value.astype(BRAIN)
    mixed = attend(t_ref, keep["p"], usable, width, heads)
    keep["o"][...] = mixed
    middle = hidden + (dot(mixed, weights(prefix + "proj")) + weights(prefix + "projb"))
    keep["m"][...] = middle
    unit, unused = norm_parts(middle)
    second = (unit * weights(prefix + "ln2g") + weights(prefix + "ln2b")).astype(BRAIN)
    keep["b"][...] = second
    inner = dot(second, weights(prefix + "fc1")) + weights(prefix + "fc1b")
    active, slope = gelu_parts(inner)
    keep["s"][...] = slope
    keep["g"][...] = active.astype(BRAIN)
    return middle + (dot(keep["g"][...], weights(prefix + "fc2")) + weights(prefix + "fc2b"))


def block_home(grad, keep, weights, prefix, heads, sums):
    width = grad.shape[1]
    d_branch = grad.astype(BRAIN)
    keep["dz"][...] = d_branch
    d_inner = (dot(d_branch, weights(prefix + "fc2"), PAIR) * keep["s"][...]).astype(BRAIN)
    keep["du"][...] = d_inner
    d_second = dot(d_inner, weights(prefix + "fc1"), PAIR)
    d_middle, d_gain, d_shift = norm_back(d_second, keep["m"][...], weights(prefix + "ln2g"))
    sums(prefix + "ln2g", d_gain)
    sums(prefix + "ln2b", d_shift)
    d_middle = d_middle + grad
    d_output = d_middle.astype(BRAIN)
    keep["dy"][...] = d_output
    d_mixed = dot(d_output, weights(prefix + "proj"), PAIR).astype(BRAIN)
    attend_back(d_mixed, keep["t"], keep["dt"], keep["p"], width, heads)
    d_normed = dot(keep["dt"][...], weights(prefix + "qkv"), PAIR)
    d_hidden, d_gain, d_shift = norm_back(d_normed, keep["x"][...], weights(prefix + "ln1g"))
    sums(prefix + "ln1g", d_gain)
    sums(prefix + "ln1b", d_shift)
    return d_middle + d_hidden


def kept_shapes(count, rows, width, hidden, heads):
    return {
        "x": (False, (rows, width), FLOAT),
        "a": (True, (rows, width), BRAIN),
        "t": (False, (rows, 3 * width), BRAIN),
        "p": (False, (heads, rows, rows), FLOAT),
        "o": (True, (rows, width), BRAIN),
        "m": (False, (rows, width), FLOAT),
        "b": (True, (rows, width), BRAIN),
        "s": (False, (rows, hidden), FLOAT),
        "g": (True, (rows, hidden), BRAIN),
        "dz": (True, (rows, width), BRAIN),
        "du": (True, (rows, hidden), BRAIN),
        "dy": (True, (rows, width), BRAIN),
        "dt": (True, (rows, 3 * width), BRAIN),
    }


def kept_scratch(count, rows, width, hidden, heads):
    shapes = []
    for every, shape, kind in kept_shapes(count, rows, width, hidden, heads).values():
        shapes.append(pltpu.VMEM(((count,) + shape) if every and count > 1 else shape, kind))
    return shapes


def kept_view(refs, count, rows, width, hidden, heads, image=None):
    view = {}
    table = kept_shapes(count, rows, width, hidden, heads)
    for ref, (name, (every, shape, kind)) in zip(refs, table.items()):
        view[name] = ref.at[image] if every and count > 1 and image is not None else ref
    return view


def block_grads(keep, prefix, emit):
    def rows_of(name):
        value = keep[name][...]
        return value.reshape(-1, value.shape[-1])

    for left, right, name, bias in (
        ("g", "dz", "fc2", "fc2b"),
        ("b", "du", "fc1", "fc1b"),
        ("o", "dy", "proj", "projb"),
        ("a", "dt", "qkv", "qvb"),
    ):
        emit(prefix + name, prefix + bias, rows_of(left), rows_of(right))


def step_body(plan, counts_ref, slots, seen_ref, tgt_ref, meta_ref, spot_enc, spot_dec, grad_out, loss_out, *scratch):
    names = list(layout())
    even, odd, sums_ref, y_hi, y_lo, dy_home, final_all, dpred_all = scratch[:8]
    weights = Weights(scratch[8 : 8 + len(names)])
    enc_refs = scratch[8 + len(names) : 8 + len(names) + 13]
    dec_refs = scratch[8 + len(names) + 13 :]
    assemble(plan, slots, even, odd)
    for name in names:
        read_param(even, odd, name, weights.refs[name])
    even[...] = jnp.zeros_like(even)
    odd[...] = jnp.zeros_like(odd)
    view = odd.at[pl.ds(8, plan.frame_rows)]
    sums_ref[...] = jnp.zeros_like(sums_ref)
    order = {name: number for number, name in enumerate(names)}

    def add_sum(name, value):
        sums_ref[pl.ds(order[name], 1), pl.ds(0, value.shape[1])] += value

    spot = lax.rem(lax.axis_index("dp"), 4)
    own = counts_ref[0, 0]
    lane = lane_iota(8)
    row = lax.broadcasted_iota(jnp.int32, (8, LANES), 0)

    def count_of(hub):
        return jnp.sum(jnp.where((lane == 127) & (row == 0), meta_ref[hub], 0.0)).astype(jnp.int32)

    one, two = count_of(1), count_of(2)
    from_one = jnp.where(spot == 0, 3, jnp.where(spot == 2, 4, 5))
    from_two = jnp.where(spot == 0, 3, jnp.where(spot == 1, 4, 5))
    use_one = (spot == 2) | ((spot != 1) & (one > 2))
    third = jnp.where(own > 2, 2, jnp.where(use_one, 3, 4))
    third_row = jnp.where(own > 2, 2, jnp.where(use_one, from_one, from_two))
    third_count = jnp.where(own > 2, own, jnp.where(use_one, one, two))
    third_meta = jnp.where(own > 2, 0, jnp.where(use_one, 1, 2))

    def pick(image):
        last = image == 2
        source = jnp.where(last, third, image)
        line = jnp.where(last, third_row, image)
        live = jnp.where(last, third_count, own) > line
        kept = meta_ref[jnp.where(last, third_meta, 0), pl.ds(line, 1), :][:, :HOME]
        return source, kept, live.astype(FLOAT)

    def placement(kept):
        number = lax.broadcasted_iota(jnp.int32, (ROWS, HOME), 0).astype(FLOAT)
        return (number == kept).astype(FLOAT)

    visible, begin = [], []
    for image in range(LIVE_CAP):
        source, kept, live = pick(image)
        where = placement(kept).astype(BRAIN)
        visible.append(seen_ref[source])
        begin.append(dot(where, spot_enc[0], DEEP) + dot(where, spot_enc[1], DEEP))
    visible = jnp.concatenate(visible, axis=0)
    begin = jnp.concatenate(begin, axis=0)
    enc_rows = LIVE_CAP * HOME
    enc_shape = (1, enc_rows, D, FF, HEADS)
    enc = kept_view(enc_refs, *enc_shape)
    down = lax.broadcasted_iota(jnp.int32, (enc_rows, enc_rows), 0)
    over = lax.broadcasted_iota(jnp.int32, (enc_rows, enc_rows), 1)
    usable = (down // HOME == over // HOME) & (down % HOME < VIS)
    first_in = dot(visible, weights("patch")) + weights("patchb") + begin
    encoded = block_ahead(first_in, enc, weights, "enc_", HEADS, usable)
    unit, unused = norm_parts(encoded)
    encoder_out = (unit * weights("encg") + weights("encb")).astype(BRAIN)
    embedded = dot(encoder_out, weights("embed")) + weights("embedb")
    upper, lower = split_two(embedded)
    for image in range(LIVE_CAP):
        y_hi[image] = upper[image * HOME : (image + 1) * HOME]
        y_lo[image] = lower[image * HOME : (image + 1) * HOME]
    dec_shape = (LIVE_CAP, ROWS, E, DFF, DHEADS)
    real = lax.broadcasted_iota(jnp.int32, (ROWS, 1), 0) < NP
    usable_dec = lax.broadcasted_iota(jnp.int32, (ROWS, ROWS), 0) < NP

    def one_image(image, total):
        source, kept, live = pick(image)
        where = placement(kept)
        seen = jnp.sum(where, axis=1, keepdims=True)
        where = where.astype(BRAIN)
        grid_in = dot(where, y_hi[image]) + dot(where, y_lo[image])
        grid_in = grid_in + (1.0 - seen) * weights("mask") + spot_dec[...]
        keep = kept_view(dec_refs, *dec_shape, image)
        decoded = block_ahead(grid_in, keep, weights, "dec_", DHEADS, usable_dec)
        unit, unused = norm_parts(decoded)
        final = (unit * weights("decg") + weights("decb")).astype(BRAIN)
        final_all[image] = final
        predicted = dot(final, weights("head")) + weights("headb")
        weight = jnp.where(real, (1.0 - 0.9 * seen) * live, 0.0)
        error = predicted[:NP] - tgt_ref[source].astype(FLOAT)
        weighted = error * weight[:NP]
        total = total + jnp.sum(weighted * error, axis=0, keepdims=True)
        dpred_all[image, pl.ds(0, NP)] = (weighted * (2.0 / PIX)).astype(BRAIN)
        dpred_all[image, pl.ds(NP, ROWS - NP)] = jnp.zeros((ROWS - NP, PIX), BRAIN)
        d_final = dot(dpred_all[image], weights("head"), PAIR)
        d_decoded, d_gain, d_shift = norm_back(d_final, decoded, weights("decg"))
        add_sum("decg", d_gain)
        add_sum("decb", d_shift)
        d_grid = block_home(d_decoded, keep, weights, "dec_", DHEADS, add_sum)
        add_sum("mask", jnp.sum((1.0 - seen) * d_grid, axis=0, keepdims=True))
        dy_home[image] = dot(where, d_grid.astype(BRAIN), DEEP).astype(BRAIN)
        return total

    total = lax.fori_loop(0, LIVE_CAP, one_image, jnp.zeros((1, PIX), FLOAT))
    loss_out[0] = jnp.sum(total) * (1.0 / PIX)

    def emit(name, bias, left, right):
        ones = jnp.ones((16, right.shape[0]), BRAIN)
        summed = dot(ones, right)[0:1]
        if bias.endswith("qvb"):
            width = summed.shape[1] // 3
            summed = jnp.concatenate([summed[:, :width], summed[:, 2 * width :]], axis=1)
        write_grad(even, view, bias, lambda start, size: summed[:, start : start + size])
        turned = left.T
        write_grad(even, view, name, lambda start, size: dot(turned, right[:, start : start + size]))

    d_embedded = dy_home[...].reshape(enc_rows, E)
    emit("embed", "embedb", encoder_out, d_embedded)
    d_seen = dot(d_embedded, weights("embed"), PAIR).astype(BRAIN).astype(FLOAT)
    d_encoded, d_gain, d_shift = norm_back(d_seen, encoded, weights("encg"))
    add_sum("encg", d_gain)
    add_sum("encb", d_shift)
    d_first = block_home(d_encoded, enc, weights, "enc_", HEADS, add_sum).astype(BRAIN)
    emit("patch", "patchb", visible, d_first)
    block_grads(enc, "enc_", emit)
    block_grads(kept_view(dec_refs, *dec_shape), "dec_", emit)
    emit("head", "headb", final_all[...].reshape(-1, E), dpred_all[...].reshape(-1, PIX))
    for name, (offset, shape) in layout().items():
        if name[-4:] in ("ln1g", "ln1b", "ln2g", "ln2b", "encg", "encb", "decg", "decb", "mask"):
            write_grad(
                even,
                view,
                name,
                lambda start, size, name=name: sums_ref[pl.ds(order[name], 1), pl.ds(start, size)],
            )
    emit_slots(plan, even, odd, grad_out)


def weight_scratch():
    shapes = []
    for name, (offset, shape) in layout().items():
        if len(shape) == 1:
            shapes.append(pltpu.VMEM((1, *shape), FLOAT))
        else:
            shapes.append(pltpu.VMEM(shape, BRAIN))
    return shapes


def whole_body(
    plan, counts_ref, keep_ref, x_ref, patches_ref, targets_ref, enc_table, dec_table,
    total_out, scalars_out, *scratch
):
    scratch = list(scratch)

    def take(count):
        taken = scratch[:count]
        del scratch[:count]
        return taken

    (slots, seen, tgt, meta, grad, loss, spot_enc, spot_dec, tables) = take(9)
    copies = [
        pltpu.make_async_copy(enc_table, spot_enc, tables.at[0]),
        pltpu.make_async_copy(dec_table, spot_dec, tables.at[1]),
    ]
    for copy in copies:
        copy.start()
    gather_body(
        plan, counts_ref, keep_ref, x_ref, patches_ref, targets_ref, slots, seen, tgt, meta, *take(9)
    )
    for copy in copies:
        copy.wait()
    names = len(layout())
    step_body(
        plan, counts_ref, slots, seen, tgt, meta, spot_enc, spot_dec, grad, loss, *take(8 + names + 26)
    )
    reduce_body(plan, counts_ref, loss, grad, total_out, scalars_out, *scratch)


def whole_step(counts, keep, master, patches, targets, plan):
    outer, rows = plan.outer, plan.rows
    vmem = pl.BlockSpec(memory_space=pltpu.VMEM)
    smem = pl.BlockSpec(memory_space=pltpu.SMEM)
    far = pl.BlockSpec(memory_space=pl.ANY)
    table = place_table(NP, ROWS, D)
    upper = table.astype(BRAIN)
    spot_enc = jnp.asarray(np.stack([upper, (table - upper.astype(np.float32)).astype(BRAIN)]))
    spot_dec = jnp.asarray(place_table(NP, ROWS, E))
    block = pltpu.VMEM((outer, 2, 2, 2, rows, LANES), BRAIN)
    out_copies = 3 * (outer + 1 + outer + 2)
    home_copies = 3 + 3 * (outer + 1) + 7 + outer - 1
    dma = pltpu.SemaphoreType.DMA
    return pl.pallas_call(
        functools.partial(whole_body, plan),
        out_shape=(
            jax.ShapeDtypeStruct((rows, LANES), FLOAT),
            jax.ShapeDtypeStruct((1, LANES), FLOAT),
        ),
        in_specs=[smem, vmem, vmem, far, far, far, far],
        out_specs=(vmem, vmem),
        scratch_shapes=[
            block,
            pltpu.VMEM((5, HOME, PIX), BRAIN),
            pltpu.VMEM((5, NP, PIX), BRAIN),
            pltpu.VMEM((3, 8, LANES), FLOAT),
            block,
            pltpu.SMEM((1,), FLOAT),
            pltpu.VMEM(spot_enc.shape, BRAIN),
            pltpu.VMEM(spot_dec.shape, FLOAT),
            dma((2,)),
            pltpu.VMEM((rows * LANES,), FLOAT),
            pltpu.VMEM((rows + 8, LANES), FLOAT),
            pltpu.VMEM(patches.shape, BRAIN),
            pltpu.VMEM((3, HOME, PIX), BRAIN),
            dma((out_copies,)),
            dma((out_copies,)),
            dma((2,)),
            dma((2, 3, 3)),
            dma((2, 3)),
            pltpu.VMEM((plan.frame_rows, LANES), FLOAT),
            pltpu.VMEM((plan.frame_rows + 8, LANES), FLOAT),
            pltpu.VMEM((48, E), FLOAT),
            pltpu.VMEM((LIVE_CAP, HOME, E), BRAIN),
            pltpu.VMEM((LIVE_CAP, HOME, E), BRAIN),
            pltpu.VMEM((LIVE_CAP, HOME, E), BRAIN),
            pltpu.VMEM((LIVE_CAP, ROWS, E), BRAIN),
            pltpu.VMEM((LIVE_CAP, ROWS, PIX), BRAIN),
            *weight_scratch(),
            *kept_scratch(1, LIVE_CAP * HOME, D, FF, HEADS),
            *kept_scratch(LIVE_CAP, ROWS, E, DFF, DHEADS),
            pltpu.VMEM((outer, 2, 2, rows, LANES), BRAIN),
            pltpu.VMEM((rows + 8, LANES), FLOAT),
            pltpu.VMEM((8, 8, LANES), FLOAT),
            pltpu.VMEM((outer, 8, LANES), FLOAT),
            pltpu.VMEM((8, LANES), FLOAT),
            dma((home_copies,)),
            dma((home_copies,)),
            *reduce_scratch(plan),
        ],
        compiler_params=pltpu.CompilerParams(
            collective_id=0, has_side_effects=True, vmem_limit_bytes=60 << 20
        ),
    )(counts, keep, master, patches, targets, spot_enc, spot_dec)


def on_device(patches, targets, keep, counts, step, master, first, second):
    plan = Plan(master.shape[0], lax.axis_size(("dp", "rep")))
    total, scalars = whole_step(counts, keep, master, patches, targets, plan)
    outs = update(step, total, scalars, master, first, second, plan)
    return (*outs[:4], outs[4].reshape(()), outs[5].reshape(()))


def solution(mesh):
    return jax.shard_map(
        on_device,
        mesh=mesh,
        in_specs=(
            P(("dp", "rep"), None, None),
            P(("dp", "rep"), None, None),
            P(("dp", "rep"), None),
            P("dp", "rep"),
            P(),
            P(("dp", "rep")),
            P(("dp", "rep")),
            P(("dp", "rep")),
        ),
        out_specs=(
            P(("dp", "rep")),
            P(("dp", "rep")),
            P(("dp", "rep")),
            P(("dp", "rep")),
            P(),
            P(),
        ),
        check_vma=False,
    )
```

```python
import functools
import itertools
import math

import jax
import jax.numpy as jnp
import numpy as np
from jax import lax
from jax.experimental import pallas as pl
from jax.experimental.pallas import tpu as pltpu
from jax.sharding import PartitionSpec as P

D = 192
HEADS = 3
FF = 768
E = 256
DHEADS = 8
DFF = 1024
PIX = 768
GRID = 14
VIS = 49
NP = 196

FLOAT = jnp.float32
BRAIN = jnp.bfloat16
CLIP = 0.05
BETA_ONE = 0.5
BETA_TWO = 0.5
LEARN = 0.01
DECAY = 0.05
EPSILON = 1e-08
LN_EPS = 1e-06

ROWS = 208
HOME = 64
LIVE_CAP = 3
PAIR = ((1,), (1,)), ((), ())
DEEP = ((0,), (0,)), ((), ())
LOG_TWO_E = 1.4426950408889634


def block_table(prefix, width, hidden, proj_fan, rate):
    return [
        (prefix + "ln1g", (width,), "gain", 1, rate),
        (prefix + "ln1b", (width,), "bias", 1, rate),
        (prefix + "qkv", (width, 3 * width), "matrix", width, rate),
        (prefix + "qvb", (2 * width,), "bias", 1, rate),
        (prefix + "proj", (width, width), "matrix", proj_fan, rate),
        (prefix + "projb", (width,), "bias", 1, rate),
        (prefix + "ln2g", (width,), "gain", 1, rate),
        (prefix + "ln2b", (width,), "bias", 1, rate),
        (prefix + "fc1", (width, hidden), "matrix", width, rate),
        (prefix + "fc1b", (hidden,), "bias", 1, rate),
        (prefix + "fc2", (hidden, width), "matrix", hidden, rate),
        (prefix + "fc2b", (width,), "bias", 1, rate),
    ]


def param_table():
    table = [("patch", (PIX, D), "matrix", PIX, 0.75), ("patchb", (D,), "bias", 1, 0.75)]
    table = table + block_table("enc_", D, FF, D // 4, 0.9)
    table = table + [
        ("encg", (D,), "gain", 1, 1.0),
        ("encb", (D,), "bias", 1, 1.0),
        ("embed", (D, E), "matrix", D, 1.0),
        ("embedb", (E,), "bias", 1, 1.0),
        ("mask", (E,), "token", 1, 1.0),
    ]
    table = table + block_table("dec_", E, DFF, E // 8, 1.0)
    table = table + [
        ("decg", (E,), "gain", 1, 1.0),
        ("decb", (E,), "bias", 1, 1.0),
        ("head", (E, PIX), "matrix", E, 1.0),
        ("headb", (PIX,), "bias", 1, 1.0),
    ]
    return table


MESH = pl.DeviceIdType.MESH
LANES = 128


def layout():
    table = {}
    offset = 0
    for name, shape, kind, fan, rate in param_table():
        table[name] = (offset, shape)
        offset += math.prod(shape)
    return table


class Plan:
    def __init__(self, length, count):
        self.length = length
        self.count = count
        self.outer = count // 16
        self.lines = -(-length // LANES // 8 * 8)
        self.rows = -(-(7 + (2 * LANES - 2 + length) // LANES) // 16) * 16
        self.split = layout()["embed"][0]
        if self.outer > 2:
            self.parts, self.orders = ((0, self.rows),), ("LCB",)
        else:
            units = self.rows // 16
            first, second = round(0.385 * units), round(0.346 * units)
            sizes = (first * 16, second * 16, (units - first - second) * 16)
            self.parts = ((0, sizes[0]), (sizes[0], sizes[1]), (sizes[0] + sizes[1], sizes[2]))
            self.orders = ("LCB", "BLC", "CBL")
        self.first_late = -(-self.split // length)
        self.edge = -(-self.split // (16 * length))
        last = self.first_late - 1
        self.border = (self.base(last) + self.used(last) + 1 + 7) // 8 * 8 + 8
        self.frame_rows = (length * count // LANES + 7) // 8 * 8 + self.rows + 16

    def late(self, index):
        return index >= self.first_late

    def start(self, index):
        return index * self.length - (64 if self.late(index) else 0)

    def base(self, index):
        return self.start(index) // LANES

    def lead(self, index):
        return self.start(index) % LANES

    def used(self, index):
        return (self.lead(index) + self.length + LANES - 1) // LANES

    def own(self, index):
        start = index * self.length - jnp.where(index >= self.first_late, 64, 0)
        return lax.rem(lax.div(start, LANES), 8), lax.rem(start, LANES)


def spot_of(index):
    return (index // 16, index // 8 % 2, index // 4 % 2, index // 2 % 2, index % 2)


def position():
    chip = lax.axis_index("dp")
    core = lax.axis_index("rep")
    return {"H": chip // 8, "L": chip // 4 % 2, "B": chip // 2 % 2, "C": chip % 2, "r": core}


def index_of(place):
    return (((place["H"] * 2 + place["L"]) * 2 + place["B"]) * 2 + place["C"]) * 2 + place["r"]


def device_of(place):
    return (((place["H"] * 2 + place["L"]) * 2 + place["B"]) * 2 + place["C"], place["r"])


def moved(place, dim, value):
    changed = dict(place)
    changed[dim] = value
    return changed


def flipped(place, dims):
    changed = dict(place)
    for dim in dims:
        changed[dim] = 1 - place[dim]
    return changed


def meet(places):
    barrier = pltpu.get_barrier_semaphore()
    for place in places:
        pl.semaphore_signal(barrier, inc=1, device_id=device_of(place), device_id_type=MESH)
    pl.semaphore_wait(barrier, len(places))


def partners(place, outer):
    group = []
    for number in range(1, 16):
        dims = [dim for bit, dim in enumerate("rCBL") if number >> bit & 1]
        group.append(flipped(place, dims))
    column = [moved(place, "H", lax.rem(place["H"] + step, outer)) for step in range(1, outer)]
    return group, column


def branches(order):
    nodes = []
    for count in range(len(order) + 1):
        for dims in itertools.combinations(order, count):
            reach = max([order.index(dim) for dim in dims], default=-1)
            nodes.append((reach, count, "".join(dims), order[reach + 1 :]))
    nodes.sort(key=lambda node: node[:2])
    return [(dims, onward) for reach, count, dims, onward in nodes]


class Sender:
    def __init__(self, send, recv):
        self.send, self.recv, self.used = send, recv, 0

    def start(self, source, target, place):
        copy = pltpu.make_async_remote_copy(
            src_ref=source,
            dst_ref=target,
            send_sem=self.send.at[self.used],
            recv_sem=self.recv.at[self.used],
            device_id=device_of(place),
            device_id_type=MESH,
        )
        self.used += 1
        copy.start()
        return copy


def lane_iota(rows):
    return lax.broadcasted_iota(jnp.int32, (rows, LANES), 1)


HUBS = (1, 2)


def others_of(hub):
    return [spot for spot in range(4) if spot != hub]


def hand_over(place, hub, number, pairs, hand, taken):
    other = others_of(hub)[number]
    target = {**place, "B": other // 2, "C": other % 2}
    return [
        pltpu.make_async_remote_copy(
            src_ref=source,
            dst_ref=to,
            send_sem=hand.at[hub - 1, number, kind],
            recv_sem=taken.at[hub - 1, kind],
            device_id=device_of(target),
            device_id_type=MESH,
        )
        for kind, (source, to) in pairs.items()
    ]


class Handing:
    def __init__(self, place, spare, seen_ref, meta_ref, targets_ref, tgt_ref, hand, taken):
        self.place, self.hand, self.taken = place, hand, taken
        self.spot = place["B"] * 2 + place["C"]
        self.refs = (spare, seen_ref, meta_ref, targets_ref, tgt_ref)

    def copies(self, hub, number, kinds):
        spare, seen_ref, meta_ref, targets_ref, tgt_ref = self.refs
        pairs = {
            0: (spare.at[number], seen_ref.at[2 + hub]),
            1: (meta_ref.at[0], meta_ref.at[hub]),
            2: (targets_ref.at[3 + number], tgt_ref.at[hub]),
        }
        pairs = {kind: pairs[kind] for kind in kinds}
        return hand_over(self.place, hub, number, pairs, self.hand, self.taken)

    def on_hub(self, act):
        for hub in HUBS:

            @pl.when(self.spot == hub)
            def _(hub=hub):
                act(hub)

    def start(self, kinds):
        def act(hub):
            for number in range(3):
                for copy in self.copies(hub, number, kinds):
                    copy.start()

        self.on_hub(act)

    def receive(self, kinds):
        for hub in HUBS:

            @pl.when(self.spot != hub)
            def _(hub=hub):
                for copy in self.copies(hub, 0, kinds):
                    copy.wait_recv()

    def finish(self, kinds):
        def act(hub):
            for number in range(3):
                for copy in self.copies(hub, number, kinds):
                    copy.wait_send()

        self.on_hub(act)


def own_block(plan, device, x_ref, line, rolled):
    rows, lines = plan.rows, plan.lines
    skip, lead = plan.own(device)
    line[...] = jnp.zeros_like(line)
    line[pl.ds(0, plan.length)] = x_ref[...]
    turned = pltpu.roll(line[...].reshape(lines, LANES), lead, 1)
    rolled[...] = jnp.zeros_like(rolled)
    rolled[pl.ds(8 + skip, lines), :] = turned
    upper, lower = rolled[pl.ds(8, rows), :], rolled[pl.ds(7, rows), :]
    return jnp.where(lane_iota(rows) >= lead, upper, lower).astype(BRAIN)


def gather_body(plan, place, out_ref, sender, between):
    outer = plan.outer
    high = place["H"]
    sibling = flipped(place, "r")
    count = len(plan.parts)

    def region(value, part, fixed, free=""):
        start, size = plan.parts[part]
        index = [value]
        for dim in "LBC":
            if dim in free:
                index.append(pl.ds(0, 2))
            else:
                index.append(1 - place[dim] if dim in fixed else place[dim])
        return out_ref.at[(*index, place["r"], pl.ds(start, size))]

    column = []
    for part in range(count):
        for step in range(1, outer):
            source = region(high, part, "")
            target = moved(place, "H", lax.rem(high + step, outer))
            column.append((step, part, sender.start(source, source, target)))
    flights, onwards, siblings = {}, [], []

    values = [lax.rem(high + outer - step, outer) for step in range(outer)]

    def spread(number, part, dims, onward):
        for dim in onward:
            source = region(values[number], part, dims)
            copy = sender.start(source, source, flipped(place, dim))
            flights[number, part, frozenset(dims + dim)] = copy
            onwards.append(copy)

    for number in range(outer):
        for part in range(count):
            if number > 0:
                for step, which, copy in column:
                    if step == number and which == part:
                        copy.wait_recv()
            spread(number, part, "", plan.orders[part])
        between(number)
    trees = [branches(order) for order in plan.orders]
    for place_in_tree in range(len(trees[0])):
        for number, value in enumerate(values):
            for part in range(count):
                dims, onward = trees[part][place_in_tree]
                order = plan.orders[part]
                if dims:
                    flights[number, part, frozenset(dims)].wait_recv()
                    spread(number, part, dims, onward)
                reach = order.index(dims[-1]) if dims else -1
                if place_in_tree + 1 == len(trees[0]) or (
                    order.index(trees[part][place_in_tree + 1][0][-1]) > reach
                ):
                    fixed = order[reach] if dims else ""
                    source = region(value, part, fixed, order[: max(reach, 0)])
                    siblings.append(sender.start(source, source, sibling))
        between(outer + place_in_tree)
    for copy in siblings:
        copy.wait_recv()
    return [copy for step, part, copy in column] + onwards + siblings


class Reducer:
    def __init__(self, plan, place, grad_ref, core_in, tree_in, column_in, own_ref, sender, columns):
        self.plan, self.place, self.sender = plan, place, sender
        self.grad_ref, self.core_in, self.tree_in = grad_ref, core_in, tree_in
        self.column_in, self.own_ref, self.columns = column_in, own_ref, columns
        self.cores = {}
        self.pending = []
        self.trees = [branches(order) for order in plan.orders]
        self.flights = {}

    def share(self, value):
        place = self.place
        for part, (start, size) in enumerate(self.plan.parts):
            whole = (value, pl.ds(0, 2), pl.ds(0, 2), pl.ds(0, 2))
            span = pl.ds(start, size)
            copy = self.sender.start(
                self.grad_ref.at[(*whole, 1 - place["r"], span)],
                self.core_in.at[(*whole, span)],
                flipped(place, "r"),
            )
            self.cores[value, part] = copy
            self.pending.append(copy)

    def stage(self, value, reach):
        plan, place = self.plan, self.place
        steps = []
        for part in range(len(plan.parts)):
            order = plan.orders[part]
            nodes = [
                (dims, onward)
                for dims, onward in reversed(self.trees[part])
                if (order.index(dims[-1]) if dims else -1) == reach
            ]
            steps.append([(part, *node) for node in nodes])
        for group in zip(*steps):
            for part, dims, onward in group:
                self.node(value, part, dims, onward)

    def node(self, value, part, dims, onward):
        plan, place = self.plan, self.place
        start, size = plan.parts[part]
        span = pl.ds(start, size)
        if (value, part) in self.cores:
            self.cores.pop((value, part)).wait_recv()
        for dim in onward:
            self.flights.pop((value, part, frozenset(dims + dim))).wait_recv()
        index = [value] + [1 - place[dim] if dim in dims else place[dim] for dim in "LBC"]
        total = self.grad_ref[(*index, place["r"], span)].astype(FLOAT)
        total = total + self.core_in[(*index, span)].astype(FLOAT)
        order = plan.orders[part]

        def number(dims):
            return sum(1 << "LBC".index(dim) for dim in dims)

        for dim in onward:
            total = total + self.tree_in[value, number(dims + dim), span].astype(FLOAT)
        mine = self.grad_ref.at[(*index, place["r"], span)]
        if dims:
            mine[...] = total.astype(BRAIN)
            copy = self.sender.start(
                mine, self.tree_in.at[value, number(dims), span], flipped(place, dims[-1])
            )
            self.flights[value, part, frozenset(dims)] = copy
            self.pending.append(copy)
            return
        high = place["H"]

        @pl.when(high == value)
        def _():
            self.own_ref[span, :] = total

        @pl.when(high != value)
        def _():
            mine[...] = total.astype(BRAIN)
            self.column(value, part).start()

    def column(self, value, part):
        plan, place = self.plan, self.place
        start, size = plan.parts[part]
        send, recv = self.columns
        index = (value, place["L"], place["B"], place["C"], place["r"], pl.ds(start, size))
        return pltpu.make_async_remote_copy(
            src_ref=self.grad_ref.at[index],
            dst_ref=self.column_in.at[place["H"], pl.ds(start, size)],
            send_sem=send.at[value, part],
            recv_sem=recv.at[place["H"], part],
            device_id=device_of(moved(place, "H", value)),
            device_id_type=MESH,
        )

    def arrival(self, source, part):
        plan, place = self.plan, self.place
        start, size = plan.parts[part]
        send, recv = self.columns
        return pltpu.make_async_remote_copy(
            src_ref=self.own_in(part),
            dst_ref=self.column_in.at[source, pl.ds(start, size)],
            send_sem=send.at[source, part],
            recv_sem=recv.at[source, part],
            device_id=device_of(moved(place, "H", source)),
            device_id_type=MESH,
        )

    def own_in(self, part):
        place = self.place
        start, size = self.plan.parts[part]
        index = (0, place["L"], place["B"], place["C"], place["r"], pl.ds(start, size))
        return self.grad_ref.at[index]

    def finish(self):
        plan, place = self.plan, self.place
        for part, (start, size) in enumerate(plan.parts):
            for source in range(plan.outer):

                @pl.when(place["H"] != source)
                def _(part=part, source=source, start=start, size=size):
                    self.arrival(source, part).wait_recv()
                    span = pl.ds(start, size)
                    self.own_ref[span, :] += self.column_in[source, span].astype(FLOAT)

    def close(self):
        plan, place = self.plan, self.place
        for copy in self.pending:
            copy.wait_send()
        for part in range(len(plan.parts)):
            for value in range(plan.outer):

                @pl.when(place["H"] != value)
                def _(part=part, value=value):
                    self.column(value, part).wait_send()


def finish_body(plan, place, held_ref, loss_ref, own_ref, total_out, scalars_out, turned, near, far, mine, sender):
    outer, rows, lines = plan.outer, plan.rows, plan.lines
    group, column = partners(place, outer)
    skip, lead = plan.own(index_of(place))
    position_in = lax.broadcasted_iota(jnp.int32, (lines, LANES), 0) * LANES + lane_iota(lines)
    shift = lax.rem(LANES - lead, LANES)
    turned[pl.ds(0, rows), :] = pltpu.roll(own_ref[...], shift, 1)
    here, below = turned[pl.ds(skip, lines), :], turned[pl.ds(skip + 1, lines), :]
    total = jnp.where(lane_iota(lines) < LANES - lead, here, below)
    total = jnp.where(position_in < plan.length, total, 0.0)
    squares = jnp.sum(total * total)
    lane = lane_iota(8)
    stats = jnp.where(lane == 0, squares, 0.0)
    stats = jnp.where(lane == 1, held_ref[0, 0].astype(FLOAT), stats)
    mine[0] = jnp.where(lane == 2, loss_ref[0], stats)
    spot = ((place["L"] * 2 + place["B"]) * 2 + place["C"]) * 2 + place["r"]
    near[spot] = mine[0]
    nears = [sender.start(mine.at[0], near.at[spot], other) for other in group]
    total_out[...] = total
    for copy in nears:
        copy.wait_recv()
    together = near[0]
    for other in range(1, 16):
        together = together + near[other]
    far[place["H"]] = together
    mine[1] = together
    fars = [sender.start(mine.at[1], far.at[place["H"]], other) for other in column]
    for copy in fars:
        copy.wait_recv()
    whole = far[0]
    for other in range(1, outer):
        whole = whole + far[other]
    row = whole[0:1, :]
    lane = lane[0:1]
    held = jnp.sum(jnp.where(lane == 1, row, 0.0))
    weights = jnp.full((1, LANES), held * (0.1 * VIS + (NP - VIS)))
    norms = jnp.sqrt(jnp.full((1, LANES), jnp.sum(jnp.where(lane == 0, row, 0.0)))) / weights
    losses = jnp.full((1, LANES), jnp.sum(jnp.where(lane == 2, row, 0.0))) / weights
    scalars_out[...] = jnp.where(lane == 0, losses, jnp.where(lane == 1, norms, weights))
    return nears + fars


def in_segments(index, segments):
    inside = None
    for start, stop in segments:
        here = (index >= start) & (index < stop)
        inside = here if inside is None else inside | here
    return inside


def matrix_segments():
    found = []
    for name, shape, kind, fan, rate in param_table():
        if kind == "matrix":
            start = layout()[name][0]
            found.append((start, start + math.prod(shape)))
    return found


def update_body(
    plan, step_ref, total_ref, scalars_ref, master_ref, first_ref, second_ref,
    master_out, first_out, second_out, copy_out, loss_out, norm_out, line
):
    rows, length = plan.lines, plan.length
    device = lax.axis_index("dp") * 2 + lax.axis_index("rep")
    position_in = lax.broadcasted_iota(jnp.int32, (rows, LANES), 0) * LANES + lane_iota(rows)
    flat = position_in + device * length
    table = layout()
    early, late = table["enc_ln1g"][0], table["encg"][0]
    rate_part = jnp.where(flat < early, 0.75, jnp.where(flat < late, 0.9, 1.0))
    decay_part = jnp.where(in_segments(flat, matrix_segments()), DECAY, 0.0)
    line[...] = jnp.zeros_like(line)
    line[pl.ds(0, length)] = master_ref[...]
    master = line[...].reshape(rows, LANES)
    line[pl.ds(0, length)] = first_ref[...]
    first = line[...].reshape(rows, LANES)
    line[pl.ds(0, length)] = second_ref[...]
    second = line[...].reshape(rows, LANES)
    loss_out[0, 0] = scalars_ref[0, 0]
    norm_out[0, 0] = scalars_ref[0, 1]
    norms = jnp.full((1, LANES), scalars_ref[0, 1])
    weights = jnp.full((1, LANES), scalars_ref[0, 2])
    gradient = total_ref[...] / weights
    clipped = gradient * jnp.minimum(1.0, CLIP / norms)
    fade = 1.0 / jnp.full((1, LANES), lax.shift_left(1, step_ref[0]).astype(FLOAT))
    new_first = BETA_ONE * first + (1.0 - BETA_ONE) * clipped
    new_second = BETA_TWO * second + (1.0 - BETA_TWO) * clipped * clipped
    first_hat = new_first / (1.0 - fade)
    second_hat = new_second / (1.0 - fade)
    new_master = master - LEARN * rate_part * (
        first_hat / (jnp.sqrt(second_hat) + EPSILON) + decay_part * master
    )
    master_out[...] = new_master.reshape(rows * LANES)[:length]
    first_out[...] = new_first.reshape(rows * LANES)[:length]
    second_out[...] = new_second.reshape(rows * LANES)[:length]
    copy_out[...] = new_master.reshape(rows * LANES)[:length].astype(BRAIN)


def update(step, total, scalars, master, first, second, plan):
    vmem = pl.BlockSpec(memory_space=pltpu.VMEM)
    smem = pl.BlockSpec(memory_space=pltpu.SMEM)
    flat = jax.ShapeDtypeStruct((plan.length,), FLOAT)
    single = jax.ShapeDtypeStruct((1, 1), FLOAT)
    return pl.pallas_call(
        functools.partial(update_body, plan),
        out_shape=(flat, flat, flat, jax.ShapeDtypeStruct((plan.length,), BRAIN), single, single),
        in_specs=[smem, vmem, smem, vmem, vmem, vmem],
        out_specs=(vmem, vmem, vmem, vmem, smem, smem),
        scratch_shapes=[pltpu.VMEM((plan.lines * LANES,), FLOAT)],
        compiler_params=pltpu.CompilerParams(vmem_limit_bytes=16 << 20),
    )(step, total, scalars, master, first, second)


def assemble(plan, slots, even, odd):
    filled = 0
    for index in range(plan.count):
        if index == plan.first_late:
            even[pl.ds(filled, plan.border - filled), :] = jnp.zeros((plan.border - filled, LANES), FLOAT)
            half_turn(plan, even, odd)
            filled = plan.border
        frame = odd if plan.late(index) else even
        start = plan.base(index) // 8 * 8
        rows = -(-(plan.base(index) - start + plan.used(index)) // 8) * 8
        block = slots[(*spot_of(index), pl.ds(0, plan.rows))].astype(FLOAT)
        if start < filled:
            frame[pl.ds(start, 8), :] += block[:8]
            frame[pl.ds(start + 8, rows - 8), :] = block[8:rows]
        else:
            frame[pl.ds(start, rows), :] = block[:rows]
        filled = start + rows


def half_turn(plan, even, odd):
    total = plan.border - 8
    span = 256

    def turn(start, rows):
        here = pltpu.roll(even[pl.ds(start, rows), :], 64, 1)
        below = pltpu.roll(even[pl.ds(start + 1, rows), :], 64, 1)
        odd[pl.ds(start, rows), :] = jnp.where(lane_iota(rows) < 64, here, below)

    @pl.loop(0, total // span)
    def _(step):
        turn(pl.multiple_of(step * span, span), span)

    if total % span:
        turn(total // span * span, total % span)


def read_param(even, odd, name, target):
    offset, shape = layout()[name]
    rows, width = (1, shape[0]) if len(shape) == 1 else shape
    base, late = divmod(offset, LANES)
    frames = (even, odd) if late == 0 else (odd, even)
    whole, half = divmod(width, LANES)
    kind = target.dtype
    if rows == 1:
        for col in range(whole):
            target[:, pl.ds(col * LANES, LANES)] = frames[0][pl.ds(base + col, 1), :].astype(kind)
        if half:
            tail = frames[0][pl.ds(base + whole, 1), :]
            target[:, pl.ds(whole * LANES, half)] = tail[:, :half].astype(kind)
        return
    if not half:
        for col in range(whole):
            piece = frames[0][pl.ds(base + col, rows, stride=whole), :]
            target[:, pl.ds(col * LANES, LANES)] = piece.astype(kind)
        return
    stride = 2 * width // LANES
    shift = whole + (1 if late else 0)

    def interleave(scratch):
        for col in range(whole + 1):
            size = LANES if col < whole else half
            upper = frames[0][pl.ds(base + col, rows // 2, stride=stride), :]
            lower = frames[1][pl.ds(base + shift + col, rows // 2, stride=stride), :]
            scratch[pl.ds(0, rows // 2, stride=2), :] = upper
            scratch[pl.ds(1, rows // 2, stride=2), :] = lower
            target[:, pl.ds(col * LANES, size)] = scratch[...][:, :size].astype(kind)

    pl.run_scoped(interleave, pltpu.VMEM((rows, LANES), FLOAT))


def write_grad(even, odd, name, value):
    offset, shape = layout()[name]
    rows, width = (1, shape[0]) if len(shape) == 1 else shape
    base, late = divmod(offset, LANES)
    frames = (even, odd) if late == 0 else (odd, even)
    whole, half = divmod(width, LANES)

    def columns():
        for col in range(0, whole, 2):
            size = min(2, whole - col) * LANES
            both = value(col * LANES, size)
            for part in range(size // LANES):
                yield col + part, both[:, part * LANES : (part + 1) * LANES]
        if half:
            tail = value(whole * LANES, half)
            yield whole, jnp.concatenate([tail, jnp.zeros((rows, LANES - half), FLOAT)], axis=1)

    if rows == 1:
        for col, piece in columns():
            frames[0][pl.ds(base + col, 1), :] = piece
        return
    if not half:
        for col, piece in columns():
            frames[0][pl.ds(base + col, rows, stride=whole), :] = piece
        return
    stride = 2 * width // LANES
    shift = whole + (1 if late else 0)

    def interleave(scratch):
        for col, piece in columns():
            scratch[...] = piece
            upper = scratch[pl.ds(0, rows // 2, stride=2), :]
            lower = scratch[pl.ds(1, rows // 2, stride=2), :]
            frames[0][pl.ds(base + col, rows // 2, stride=stride), :] = upper
            frames[1][pl.ds(base + shift + col, rows // 2, stride=stride), :] = lower

    pl.run_scoped(interleave, pltpu.VMEM((rows, LANES), FLOAT))


def clear_frames(plan, even, odd):
    even[...] = jnp.zeros_like(even)
    odd[pl.ds(0, plan.border + 16), :] = jnp.zeros((plan.border + 16, LANES), FLOAT)
    table = layout()
    final = (table["headb"][0] // LANES) // 8 * 8
    odd[pl.ds(final, odd.shape[0] - final), :] = jnp.zeros((odd.shape[0] - final, LANES), FLOAT)


def emit_slots(plan, even, odd, slots, values):
    rows = plan.rows
    for index in range(values[0] * 16, values[-1] * 16 + 16):
        start = plan.base(index) // 8 * 8
        if plan.late(index):
            block = odd[pl.ds(start + 8, rows), :]
        else:
            here = pltpu.roll(odd[pl.ds(start + 8, rows), :], 64, 1)
            above = pltpu.roll(odd[pl.ds(start + 7, rows), :], 64, 1)
            block = even[pl.ds(start, rows), :] + jnp.where(lane_iota(rows) < 64, above, here)
        slots[spot_of(index)] = block.astype(BRAIN)


def dot(left, right, dims=(((1,), (0,)), ((), ()))):
    return lax.dot_general(left, right, dims, preferred_element_type=FLOAT)


def place_table(count, rows, width):
    quarter = width // 4
    omega = 1.0 / 10000.0 ** (np.arange(quarter) / quarter)
    index = np.arange(count)
    across = (index // GRID)[:, None] * omega
    along = (index % GRID)[:, None] * omega
    table = np.zeros((rows, width), np.float32)
    table[:count] = np.concatenate(
        [np.sin(across), np.cos(across), np.sin(along), np.cos(along)], axis=-1
    )
    return table


def split_two(value):
    upper = value.astype(BRAIN)
    return upper, (value - upper.astype(FLOAT)).astype(BRAIN)


def norm_parts(value):
    center = value - jnp.mean(value, axis=-1, keepdims=True)
    spread = lax.rsqrt(jnp.mean(center * center, axis=-1, keepdims=True) + LN_EPS)
    return center * spread, spread


def norm_back(grad, value, gain):
    unit, spread = norm_parts(value)
    d_gain = jnp.sum(grad * unit, axis=0, keepdims=True)
    d_shift = jnp.sum(grad, axis=0, keepdims=True)
    scaled = grad * gain
    middle = jnp.mean(scaled, axis=-1, keepdims=True)
    along = jnp.mean(scaled * unit, axis=-1, keepdims=True)
    return spread * (scaled - middle - unit * along), d_gain, d_shift


def gelu_parts(value):
    half = 0.5 + 0.5 * lax.erf(value * 0.7071067811865476)
    bell = jnp.exp2(value * value * (-0.5 * LOG_TWO_E)) * 0.3989422804014327
    return value * half, half + value * bell


def head_only(value, head, size):
    lane = lax.broadcasted_iota(jnp.int32, value.shape, 1)
    inside = (lane >= head * size) & (lane < (head + 1) * size)
    return jnp.where(inside, value, jnp.zeros_like(value))


def attend(t_ref, chance_ref, usable, width, heads):
    size = width // heads
    query, keys = t_ref[:, pl.ds(0, width)], t_ref[:, pl.ds(width, width)]
    values = t_ref[:, pl.ds(2 * width, width)].T
    factor = size ** (-0.5) * LOG_TWO_E
    mixed = []
    for head in range(heads):
        raw = dot(head_only(keys, head, size), query, PAIR)
        raw = jnp.where(usable, raw, -1e30)
        top = jnp.max(raw, axis=0, keepdims=True)
        power = jnp.exp2((raw - top) * factor)
        chance = power * (1.0 / jnp.sum(power, axis=0, keepdims=True))
        chance_ref[head] = chance
        mixed.append(dot(values[head * size : (head + 1) * size], chance.astype(BRAIN)))
    return jnp.concatenate(mixed, axis=0).astype(BRAIN).T


def attend_back(d_mixed, t_ref, dt_ref, chance_ref, width, heads):
    size = width // heads
    scale = size ** (-0.5)
    query, keys = t_ref[:, pl.ds(0, width)], t_ref[:, pl.ds(width, width)]
    values = t_ref[:, pl.ds(2 * width, width)]
    across = keys.T
    d_query = []
    d_keys = d_values = None
    for head in range(heads):
        chance = chance_ref[head]
        d_here = head_only(d_mixed, head, size)
        d_chance = dot(head_only(values, head, size), d_mixed, PAIR)
        along = jnp.sum(chance * d_chance, axis=0, keepdims=True)
        d_scores = (chance * (d_chance - along)).astype(BRAIN)
        part = dot(chance.astype(BRAIN), d_here)
        d_values = part if d_values is None else d_values + part
        part = dot(d_scores, head_only(query, head, size))
        d_keys = part if d_keys is None else d_keys + part
        d_query.append(dot(across[head * size : (head + 1) * size], d_scores))
    d_query = (jnp.concatenate(d_query, axis=0) * scale).astype(BRAIN).T
    dt_ref[:, pl.ds(0, width)] = d_query
    dt_ref[:, pl.ds(width, width)] = (d_keys * scale).astype(BRAIN)
    dt_ref[:, pl.ds(2 * width, width)] = d_values.astype(BRAIN)


class Weights:
    def __init__(self, refs):
        self.refs = dict(zip(layout(), refs))

    def __call__(self, name):
        return self.refs[name][...]


def block_ahead(hidden, keep, weights, prefix, heads, usable):
    width = hidden.shape[1]
    keep["x"][...] = hidden
    unit, unused = norm_parts(hidden)
    normed = (unit * weights(prefix + "ln1g") + weights(prefix + "ln1b")).astype(BRAIN)
    keep["a"][...] = normed
    bias = weights(prefix + "qvb")
    t_ref = keep["t"]
    for part in range(3):
        cols = pl.ds(part * width, width)
        value = dot(normed, weights.refs[prefix + "qkv"][:, cols])
        if part != 1:
            value = value + bias[:, (part // 2) * width : (part // 2 + 1) * width]
        t_ref[:, cols] = value.astype(BRAIN)
    mixed = attend(t_ref, keep["p"], usable, width, heads)
    keep["o"][...] = mixed
    middle = hidden + (dot(mixed, weights(prefix + "proj")) + weights(prefix + "projb"))
    keep["m"][...] = middle
    unit, unused = norm_parts(middle)
    second = (unit * weights(prefix + "ln2g") + weights(prefix + "ln2b")).astype(BRAIN)
    keep["b"][...] = second
    inner = dot(second, weights(prefix + "fc1")) + weights(prefix + "fc1b")
    active, slope = gelu_parts(inner)
    keep["s"][...] = slope
    keep["g"][...] = active.astype(BRAIN)
    return middle + (dot(keep["g"][...], weights(prefix + "fc2")) + weights(prefix + "fc2b"))


def block_home(grad, keep, weights, prefix, heads, sums):
    width = grad.shape[1]
    d_branch = grad.astype(BRAIN)
    keep["dz"][...] = d_branch
    d_inner = (dot(d_branch, weights(prefix + "fc2"), PAIR) * keep["s"][...]).astype(BRAIN)
    keep["du"][...] = d_inner
    d_second = dot(d_inner, weights(prefix + "fc1"), PAIR)
    d_middle, d_gain, d_shift = norm_back(d_second, keep["m"][...], weights(prefix + "ln2g"))
    sums(prefix + "ln2g", d_gain)
    sums(prefix + "ln2b", d_shift)
    d_middle = d_middle + grad
    d_output = d_middle.astype(BRAIN)
    keep["dy"][...] = d_output
    d_mixed = dot(d_output, weights(prefix + "proj"), PAIR).astype(BRAIN)
    attend_back(d_mixed, keep["t"], keep["dt"], keep["p"], width, heads)
    d_normed = dot(keep["dt"][...], weights(prefix + "qkv"), PAIR)
    d_hidden, d_gain, d_shift = norm_back(d_normed, keep["x"][...], weights(prefix + "ln1g"))
    sums(prefix + "ln1g", d_gain)
    sums(prefix + "ln1b", d_shift)
    return d_middle + d_hidden


def kept_shapes(count, rows, width, hidden, heads):
    return {
        "x": (False, (rows, width), FLOAT),
        "a": (True, (rows, width), BRAIN),
        "t": (False, (rows, 3 * width), BRAIN),
        "p": (False, (heads, rows, rows), FLOAT),
        "o": (True, (rows, width), BRAIN),
        "m": (False, (rows, width), FLOAT),
        "b": (True, (rows, width), BRAIN),
        "s": (False, (rows, hidden), FLOAT),
        "g": (True, (rows, hidden), BRAIN),
        "dz": (True, (rows, width), BRAIN),
        "du": (True, (rows, hidden), BRAIN),
        "dy": (True, (rows, width), BRAIN),
        "dt": (True, (rows, 3 * width), BRAIN),
    }


def kept_scratch(count, rows, width, hidden, heads):
    shapes = []
    for every, shape, kind in kept_shapes(count, rows, width, hidden, heads).values():
        shapes.append(pltpu.VMEM(((count,) + shape) if every and count > 1 else shape, kind))
    return shapes


def kept_view(refs, count, rows, width, hidden, heads, image=None):
    view = {}
    table = kept_shapes(count, rows, width, hidden, heads)
    for ref, (name, (every, shape, kind)) in zip(refs, table.items()):
        view[name] = ref.at[image] if every and count > 1 and image is not None else ref
    return view


def block_grads(keep, prefix, emit):
    def rows_of(name):
        value = keep[name][...]
        return value.reshape(-1, value.shape[-1])

    for left, right, name, bias in (
        ("g", "dz", "fc2", "fc2b"),
        ("b", "du", "fc1", "fc1b"),
        ("o", "dy", "proj", "projb"),
        ("a", "dt", "qkv", "qvb"),
    ):
        emit(prefix + name, prefix + bias, rows_of(left), rows_of(right))


NORMS = ("ln1g", "ln1b", "ln2g", "ln2b", "encg", "encb", "decg", "decb", "mask")


class Images:
    def __init__(self, place, counts_ref, meta_ref):
        spot = place["B"] * 2 + place["C"]
        self.meta_ref = meta_ref
        self.own = counts_ref[0, 0]
        lane = lane_iota(8)
        row = lax.broadcasted_iota(jnp.int32, (8, LANES), 0)

        def count_of(hub):
            corner = jnp.where((lane == LANES - 1) & (row == 0), meta_ref[hub], 0.0)
            return jnp.sum(corner).astype(jnp.int32)

        one, two = count_of(1), count_of(2)
        from_one = jnp.where(spot == 0, 3, jnp.where(spot == 2, 4, 5))
        from_two = jnp.where(spot == 0, 3, jnp.where(spot == 1, 4, 5))
        use_one = (spot == 2) | ((spot != 1) & (one > 2))
        mine = self.own > 2

        def choose(own, first, second):
            return jnp.where(mine, own, jnp.where(use_one, first, second))

        self.third = choose(2, 3, 4)
        self.third_row = choose(2, from_one, from_two)
        self.third_count = choose(self.own, one, two)
        self.third_meta = choose(0, 1, 2)

    def __call__(self, image):
        last = image == 2
        source = jnp.where(last, self.third, image)
        line = jnp.where(last, self.third_row, image)
        live = jnp.where(last, self.third_count, self.own) > line
        kept = self.meta_ref[jnp.where(last, self.third_meta, 0), pl.ds(line, 1), :][:, :HOME]
        return source, kept, live.astype(FLOAT)


def placement(kept, rows):
    number = lax.broadcasted_iota(jnp.int32, (rows, HOME), 0).astype(FLOAT)
    return (number == kept).astype(FLOAT)


def whole_body(
    plan, counts_ref, keep_ref, x_ref, patches_ref, targets_ref, enc_table, dec_table,
    total_out, scalars_out, *scratch
):
    scratch = list(scratch)

    def take(count):
        taken = scratch[:count]
        del scratch[:count]
        return taken

    names = list(layout())
    slots, seen_ref, tgt_own, tgt_ref, wanted, meta_ref, grad_ref, loss_ref = take(8)
    spot_enc, spot_dec, local = take(3)
    line, rolled, pixels, spare, send, recv, hand, taken = take(8)
    even, odd, sums_ref, y_hi, y_lo, dy_home, final_all, dpred_all = take(8)
    weights = Weights(take(len(names)))
    enc_refs, dec_refs = take(13), take(13)
    core_in, tree_in, column_in, own_ref, turned, near, far, mine, column_send, column_recv = take(10)

    place = position()
    device = index_of(place)
    copies = [
        pltpu.make_async_copy(patches_ref, pixels, local.at[0]),
        pltpu.make_async_copy(enc_table, spot_enc, local.at[1]),
        pltpu.make_async_copy(dec_table, spot_dec, local.at[2]),
        pltpu.make_async_copy(
            targets_ref.at[pl.ds(0, LIVE_CAP - 1)], tgt_own, local.at[3]
        ),
        pltpu.make_async_copy(targets_ref.at[LIVE_CAP - 1], tgt_ref.at[0], local.at[4]),
    ]
    for copy in copies:
        copy.start()
    slots[(place["H"], place["L"], place["B"], place["C"], place["r"])] = own_block(
        plan, device, x_ref, line, rolled
    )
    group, column = partners(place, plan.outer)
    meet(group + column)
    sender = Sender(send, recv)
    handing = Handing(place, spare, seen_ref, meta_ref, targets_ref, tgt_ref, hand, taken)

    def between(stage):
        if stage:
            return
        lane = lane_iota(8)
        row = lax.broadcasted_iota(jnp.int32, (8, LANES), 0)
        held = counts_ref[0, 0].astype(FLOAT)
        meta_ref[0] = jnp.where((lane == LANES - 1) & (row == 0), held, -1.0)
        meta_ref[0, pl.ds(0, keep_ref.shape[0]), pl.ds(0, VIS)] = keep_ref[...].astype(FLOAT)
        copies[0].wait()

        def visible(image):
            where = placement(meta_ref[0, pl.ds(image, 1), :][:, :HOME], NP).astype(BRAIN)
            return dot(where, pixels[image], DEEP).astype(BRAIN)

        def prepare(hub):
            for number in range(3):
                spare[number] = visible(3 + number)

        handing.on_hub(prepare)
        handing.start((0, 1))
        for image in range(LIVE_CAP):
            seen_ref[image] = visible(image)

    pending = gather_body(plan, place, slots, sender, between)
    handing.start((2,))
    handing.receive((0, 1))
    for copy in copies[1:]:
        copy.wait()

    assemble(plan, slots, even, odd)
    for name in names:
        read_param(even, odd, name, weights.refs[name])
    clear_frames(plan, even, odd)
    view = odd.at[pl.ds(8, plan.frame_rows)]
    sums_ref[...] = jnp.zeros_like(sums_ref)
    order = {name: number for number, name in enumerate(names)}

    def add_sum(name, value):
        sums_ref[pl.ds(order[name], 1), pl.ds(0, value.shape[1])] += value

    pick = Images(place, counts_ref, meta_ref)

    visible, begin = [], []
    for image in range(LIVE_CAP):
        source, kept, live = pick(image)
        where = placement(kept, ROWS).astype(BRAIN)
        visible.append(seen_ref[source])
        begin.append(dot(where, spot_enc[0], DEEP) + dot(where, spot_enc[1], DEEP))
    visible = jnp.concatenate(visible, axis=0)
    begin = jnp.concatenate(begin, axis=0)
    enc_rows = LIVE_CAP * HOME
    enc_shape = (1, enc_rows, D, FF, HEADS)
    enc = kept_view(enc_refs, *enc_shape)
    down = lax.broadcasted_iota(jnp.int32, (enc_rows, enc_rows), 0)
    over = lax.broadcasted_iota(jnp.int32, (enc_rows, enc_rows), 1)
    usable = (down // HOME == over // HOME) & (down % HOME < VIS)
    first_in = dot(visible, weights("patch")) + weights("patchb") + begin
    encoded = block_ahead(first_in, enc, weights, "enc_", HEADS, usable)
    unit, unused = norm_parts(encoded)
    encoder_out = (unit * weights("encg") + weights("encb")).astype(BRAIN)
    embedded = dot(encoder_out, weights("embed")) + weights("embedb")
    upper, lower = split_two(embedded)
    for image in range(LIVE_CAP):
        y_hi[image] = upper[image * HOME : (image + 1) * HOME]
        y_lo[image] = lower[image * HOME : (image + 1) * HOME]
    dec_shape = (LIVE_CAP, ROWS, E, DFF, DHEADS)
    real = lax.broadcasted_iota(jnp.int32, (ROWS, 1), 0) < NP
    usable_dec = lax.broadcasted_iota(jnp.int32, (ROWS, ROWS), 0) < NP

    def one_image(image, total):
        source, kept, live = pick(image)
        where = placement(kept, ROWS)
        seen = jnp.sum(where, axis=1, keepdims=True)
        where = where.astype(BRAIN)
        grid_in = dot(where, y_hi[image]) + dot(where, y_lo[image])
        grid_in = grid_in + (1.0 - seen) * weights("mask") + spot_dec[...]
        keep = kept_view(dec_refs, *dec_shape, image)
        decoded = block_ahead(grid_in, keep, weights, "dec_", DHEADS, usable_dec)
        unit, unused = norm_parts(decoded)
        final = (unit * weights("decg") + weights("decb")).astype(BRAIN)
        final_all[image] = final
        predicted = dot(final, weights("head")) + weights("headb")
        weight = jnp.where(real, (1.0 - 0.9 * seen) * live, 0.0)

        @pl.when(image == LIVE_CAP - 1)
        def _():
            handing.receive((2,))
            wanted[...] = tgt_ref[pick.third - 2]

        @pl.when(image < LIVE_CAP - 1)
        def _():
            wanted[...] = tgt_own[image]

        error = predicted[:NP] - wanted[...].astype(FLOAT)
        weighted = error * weight[:NP]
        total = total + jnp.sum(weighted * error, axis=0, keepdims=True)
        dpred_all[image, pl.ds(0, NP)] = (weighted * (2.0 / PIX)).astype(BRAIN)
        dpred_all[image, pl.ds(NP, ROWS - NP)] = jnp.zeros((ROWS - NP, PIX), BRAIN)
        d_final = dot(dpred_all[image], weights("head"), PAIR)
        d_decoded, d_gain, d_shift = norm_back(d_final, decoded, weights("decg"))
        add_sum("decg", d_gain)
        add_sum("decb", d_shift)
        d_grid = block_home(d_decoded, keep, weights, "dec_", DHEADS, add_sum)
        add_sum("mask", jnp.sum((1.0 - seen) * d_grid, axis=0, keepdims=True))
        dy_home[image] = dot(where, d_grid.astype(BRAIN), DEEP).astype(BRAIN)
        return total

    total = lax.fori_loop(0, LIVE_CAP, one_image, jnp.zeros((1, PIX), FLOAT))
    loss_ref[0] = jnp.sum(total) * (1.0 / PIX)

    def emit(name, bias, left, right):
        ones = jnp.ones((16, right.shape[0]), BRAIN)
        summed = dot(ones, right)[0:1]
        if bias.endswith("qvb"):
            width = summed.shape[1] // 3
            summed = jnp.concatenate([summed[:, :width], summed[:, 2 * width :]], axis=1)
        write_grad(even, view, bias, lambda start, size: summed[:, start : start + size])
        turned = left.T
        write_grad(even, view, name, lambda start, size: dot(turned, right[:, start : start + size]))

    def emit_norms(prefixes):
        for name in names:
            if name.endswith(NORMS) and name.startswith(prefixes):
                row = pl.ds(order[name], 1)
                write_grad(even, view, name, lambda start, size, row=row: sums_ref[row, pl.ds(start, size)])

    d_embedded = dy_home[...].reshape(enc_rows, E)
    emit("embed", "embedb", encoder_out, d_embedded)
    block_grads(kept_view(dec_refs, *dec_shape), "dec_", emit)
    emit("head", "headb", final_all[...].reshape(-1, E), dpred_all[...].reshape(-1, PIX))
    emit_norms(("dec", "mask"))
    late_values = list(range(plan.edge, plan.outer))
    early_values = list(range(plan.edge))
    emit_slots(plan, even, odd, grad_ref, late_values)
    reducer = Reducer(
        plan, place, grad_ref, core_in, tree_in, column_in, own_ref, sender, (column_send, column_recv)
    )

    def stage(values, reach):
        for value in values:
            reducer.stage(value, reach)

    for value in late_values:
        reducer.share(value)
    d_seen = dot(d_embedded, weights("embed"), PAIR).astype(BRAIN).astype(FLOAT)
    d_encoded, d_gain, d_shift = norm_back(d_seen, encoded, weights("encg"))
    add_sum("encg", d_gain)
    add_sum("encb", d_shift)
    stage(late_values, 2)
    d_first = block_home(d_encoded, enc, weights, "enc_", HEADS, add_sum).astype(BRAIN)
    stage(late_values, 1)
    emit("patch", "patchb", visible, d_first)
    stage(late_values, 0)
    block_grads(enc, "enc_", emit)
    emit_norms(("enc",))
    stage(late_values, -1)
    emit_slots(plan, even, odd, grad_ref, early_values)
    for value in early_values:
        reducer.share(value)
    for reach in (2, 1, 0, -1):
        stage(early_values, reach)
    reducer.finish()
    pending += finish_body(
        plan, place, counts_ref, loss_ref, own_ref, total_out, scalars_out, turned, near, far, mine, sender
    )
    reducer.close()
    handing.finish((0, 1, 2))
    for copy in pending:
        copy.wait_send()


def weight_scratch():
    shapes = []
    for name, (offset, shape) in layout().items():
        if len(shape) == 1:
            shapes.append(pltpu.VMEM((1, *shape), FLOAT))
        else:
            shapes.append(pltpu.VMEM(shape, BRAIN))
    return shapes


def copies_used(plan):
    parts = len(plan.parts)
    spread = parts * (plan.outer - 1) + parts * plan.outer * (7 + 4)
    home = parts * plan.outer * (1 + 7)
    return spread + home + 15 + plan.outer - 1


def whole_step(counts, keep, master, patches, targets, plan):
    outer, rows, lines = plan.outer, plan.rows, plan.lines
    vmem = pl.BlockSpec(memory_space=pltpu.VMEM)
    smem = pl.BlockSpec(memory_space=pltpu.SMEM)
    far = pl.BlockSpec(memory_space=pl.ANY)
    table = place_table(NP, ROWS, D)
    upper = table.astype(BRAIN)
    spot_enc = jnp.asarray(np.stack([upper, (table - upper.astype(np.float32)).astype(BRAIN)]))
    spot_dec = jnp.asarray(place_table(NP, ROWS, E))
    block = pltpu.VMEM((outer, 2, 2, 2, 2, rows, LANES), BRAIN)
    dma = pltpu.SemaphoreType.DMA
    copies = copies_used(plan)
    return pl.pallas_call(
        functools.partial(whole_body, plan),
        out_shape=(
            jax.ShapeDtypeStruct((lines, LANES), FLOAT),
            jax.ShapeDtypeStruct((1, LANES), FLOAT),
        ),
        in_specs=[smem, vmem, vmem, far, far, far, far],
        out_specs=(vmem, vmem),
        scratch_shapes=[
            block,
            pltpu.VMEM((5, HOME, PIX), BRAIN),
            pltpu.VMEM((LIVE_CAP - 1, NP, PIX), BRAIN),
            pltpu.VMEM((3, NP, PIX), BRAIN),
            pltpu.VMEM((NP, PIX), BRAIN),
            pltpu.VMEM((3, 8, LANES), FLOAT),
            block,
            pltpu.SMEM((1,), FLOAT),
            pltpu.VMEM(spot_enc.shape, BRAIN),
            pltpu.VMEM(spot_dec.shape, FLOAT),
            dma((5,)),
            pltpu.VMEM((lines * LANES,), FLOAT),
            pltpu.VMEM((rows + 8, LANES), FLOAT),
            pltpu.VMEM(patches.shape, BRAIN),
            pltpu.VMEM((3, HOME, PIX), BRAIN),
            dma((copies,)),
            dma((copies,)),
            dma((2, 3, 3)),
            dma((2, 3)),
            pltpu.VMEM((plan.border + rows, LANES), FLOAT),
            pltpu.VMEM((plan.frame_rows + 8, LANES), FLOAT),
            pltpu.VMEM((48, E), FLOAT),
            pltpu.VMEM((LIVE_CAP, HOME, E), BRAIN),
            pltpu.VMEM((LIVE_CAP, HOME, E), BRAIN),
            pltpu.VMEM((LIVE_CAP, HOME, E), BRAIN),
            pltpu.VMEM((LIVE_CAP, ROWS, E), BRAIN),
            pltpu.VMEM((LIVE_CAP, ROWS, PIX), BRAIN),
            *weight_scratch(),
            *kept_scratch(1, LIVE_CAP * HOME, D, FF, HEADS),
            *kept_scratch(LIVE_CAP, ROWS, E, DFF, DHEADS),
            pltpu.VMEM((outer, 2, 2, 2, rows, LANES), BRAIN),
            pltpu.VMEM((outer, 8, rows, LANES), BRAIN),
            pltpu.VMEM((outer, rows, LANES), BRAIN),
            pltpu.VMEM((rows, LANES), FLOAT),
            pltpu.VMEM((rows, LANES), FLOAT),
            pltpu.VMEM((16, 8, LANES), FLOAT),
            pltpu.VMEM((outer, 8, LANES), FLOAT),
            pltpu.VMEM((2, 8, LANES), FLOAT),
            dma((outer, len(plan.parts))),
            dma((outer, len(plan.parts))),
        ],
        compiler_params=pltpu.CompilerParams(
            collective_id=0, has_side_effects=True, vmem_limit_bytes=60 << 20
        ),
    )(counts, keep, master, patches, targets, spot_enc, spot_dec)


def on_device(patches, targets, keep, counts, step, master, first, second):
    plan = Plan(master.shape[0], lax.axis_size(("dp", "rep")))
    total, scalars = whole_step(counts, keep, master, patches, targets, plan)
    outs = update(step, total, scalars, master, first, second, plan)
    return (*outs[:4], outs[4].reshape(()), outs[5].reshape(()))


def solution(mesh):
    return jax.shard_map(
        on_device,
        mesh=mesh,
        in_specs=(
            P(("dp", "rep"), None, None),
            P(("dp", "rep"), None, None),
            P(("dp", "rep"), None),
            P("dp", "rep"),
            P(),
            P(("dp", "rep")),
            P(("dp", "rep")),
            P(("dp", "rep")),
        ),
        out_specs=(
            P(("dp", "rep")),
            P(("dp", "rep")),
            P(("dp", "rep")),
            P(("dp", "rep")),
            P(),
            P(),
        ),
        check_vma=False,
    )
```

```python
import functools
import itertools
import math

import jax
import jax.numpy as jnp
import numpy as np
from jax import lax
from jax.experimental import pallas as pl
from jax.experimental.pallas import tpu as pltpu
from jax.sharding import PartitionSpec as P

D = 192
HEADS = 3
FF = 768
E = 256
DHEADS = 8
DFF = 1024
PIX = 768
GRID = 14
VIS = 49
NP = 196

FLOAT = jnp.float32
BRAIN = jnp.bfloat16
CLIP = 0.05
BETA_ONE = 0.5
BETA_TWO = 0.5
LEARN = 0.01
DECAY = 0.05
EPSILON = 1e-08
LN_EPS = 1e-06

ROWS = 208
HOME = 64
LIVE_CAP = 3
PAIR = ((1,), (1,)), ((), ())
DEEP = ((0,), (0,)), ((), ())
LOG_TWO_E = 1.4426950408889634


def block_table(prefix, width, hidden, proj_fan, rate):
    return [
        (prefix + "ln1g", (width,), "gain", 1, rate),
        (prefix + "ln1b", (width,), "bias", 1, rate),
        (prefix + "qkv", (width, 3 * width), "matrix", width, rate),
        (prefix + "qvb", (2 * width,), "bias", 1, rate),
        (prefix + "proj", (width, width), "matrix", proj_fan, rate),
        (prefix + "projb", (width,), "bias", 1, rate),
        (prefix + "ln2g", (width,), "gain", 1, rate),
        (prefix + "ln2b", (width,), "bias", 1, rate),
        (prefix + "fc1", (width, hidden), "matrix", width, rate),
        (prefix + "fc1b", (hidden,), "bias", 1, rate),
        (prefix + "fc2", (hidden, width), "matrix", hidden, rate),
        (prefix + "fc2b", (width,), "bias", 1, rate),
    ]


def param_table():
    table = [("patch", (PIX, D), "matrix", PIX, 0.75), ("patchb", (D,), "bias", 1, 0.75)]
    table = table + block_table("enc_", D, FF, D // 4, 0.9)
    table = table + [
        ("encg", (D,), "gain", 1, 1.0),
        ("encb", (D,), "bias", 1, 1.0),
        ("embed", (D, E), "matrix", D, 1.0),
        ("embedb", (E,), "bias", 1, 1.0),
        ("mask", (E,), "token", 1, 1.0),
    ]
    table = table + block_table("dec_", E, DFF, E // 8, 1.0)
    table = table + [
        ("decg", (E,), "gain", 1, 1.0),
        ("decb", (E,), "bias", 1, 1.0),
        ("head", (E, PIX), "matrix", E, 1.0),
        ("headb", (PIX,), "bias", 1, 1.0),
    ]
    return table


MESH = pl.DeviceIdType.MESH
LANES = 128


def layout():
    table = {}
    offset = 0
    for name, shape, kind, fan, rate in param_table():
        table[name] = (offset, shape)
        offset += math.prod(shape)
    return table


class Plan:
    def __init__(self, length, count):
        self.length = length
        self.count = count
        self.outer = count // 16
        self.lines = -(-length // LANES // 8 * 8)
        self.rows = -(-(7 + (2 * LANES - 2 + length) // LANES) // 16) * 16
        self.split = layout()["embed"][0]
        if self.outer > 2:
            self.parts, self.orders = ((0, self.rows),), ("LCB",)
        else:
            units = self.rows // 16
            first, second = round(0.385 * units), round(0.346 * units)
            sizes = (first * 16, second * 16, (units - first - second) * 16)
            self.parts = ((0, sizes[0]), (sizes[0], sizes[1]), (sizes[0] + sizes[1], sizes[2]))
            self.orders = ("LCB", "BLC", "CBL")
        self.first_late = -(-self.split // length)
        self.depths = count // 8
        pieces = 4 if self.outer == 2 else 1
        cuts = [self.rows // 16 * number // pieces * 16 for number in range(pieces + 1)]
        self.halves = tuple((low, high - low) for low, high in zip(cuts, cuts[1:]))
        self.ways = ("CB", "BC", "CB", "BC")[:pieces]
        last = self.first_late - 1
        self.border = (self.base(last) + self.used(last) + 1 + 7) // 8 * 8 + 8
        self.frame_rows = (length * count // LANES + 7) // 8 * 8 + self.rows + 16

    def depths_from(self, name):
        return min(-(-layout()[name][0] // (8 * self.length)), self.depths)

    def late(self, index):
        return index >= self.first_late

    def start(self, index):
        return index * self.length - (64 if self.late(index) else 0)

    def base(self, index):
        return self.start(index) // LANES

    def lead(self, index):
        return self.start(index) % LANES

    def used(self, index):
        return (self.lead(index) + self.length + LANES - 1) // LANES

    def own(self, index):
        start = index * self.length - jnp.where(index >= self.first_late, 64, 0)
        return lax.rem(lax.div(start, LANES), 8), lax.rem(start, LANES)


def spot_of(index):
    return (index // 16, index // 8 % 2, index // 4 % 2, index // 2 % 2, index % 2)


def position():
    chip = lax.axis_index("dp")
    core = lax.axis_index("rep")
    return {"H": chip // 8, "L": chip // 4 % 2, "B": chip // 2 % 2, "C": chip % 2, "r": core}


def index_of(place):
    return (((place["H"] * 2 + place["L"]) * 2 + place["B"]) * 2 + place["C"]) * 2 + place["r"]


def device_of(place):
    return (((place["H"] * 2 + place["L"]) * 2 + place["B"]) * 2 + place["C"], place["r"])


def moved(place, dim, value):
    changed = dict(place)
    changed[dim] = value
    return changed


def flipped(place, dims):
    changed = dict(place)
    for dim in dims:
        changed[dim] = 1 - place[dim]
    return changed


def meet(places):
    barrier = pltpu.get_barrier_semaphore()
    for place in places:
        pl.semaphore_signal(barrier, inc=1, device_id=device_of(place), device_id_type=MESH)
    pl.semaphore_wait(barrier, len(places))


def partners(place, outer):
    digits = "rCBLH" if outer == 2 else "rCBL"
    group = []
    for number in range(1, 1 << len(digits)):
        group.append(flipped(place, [dim for bit, dim in enumerate(digits) if number >> bit & 1]))
    column = []
    if outer > 2:
        column = [moved(place, "H", lax.rem(place["H"] + step, outer)) for step in range(1, outer)]
    return group, column


def at_depth(place, depth):
    return {**place, "H": depth // 2, "L": depth % 2}


def depth_of(place):
    return place["H"] * 2 + place["L"]


def gates(place, plan):
    group, column = partners(place, plan.outer)
    if plan.outer > 2:
        depth = depth_of(place)
        column = column + [
            at_depth(place, lax.rem(depth + step, plan.depths)) for step in range(1, plan.depths)
        ]
    return group + column


def branches(order):
    nodes = []
    for count in range(len(order) + 1):
        for dims in itertools.combinations(order, count):
            reach = max([order.index(dim) for dim in dims], default=-1)
            nodes.append((reach, count, "".join(dims), order[reach + 1 :]))
    nodes.sort(key=lambda node: node[:2])
    return [(dims, onward) for reach, count, dims, onward in nodes]


class Copy:
    def __init__(self, recipe, send, recv, number):
        self.recipe, self.send, self.recv, self.number = recipe, send, recv, number

    def make(self):
        source, target, place = self.recipe()
        return pltpu.make_async_remote_copy(
            src_ref=source,
            dst_ref=target,
            send_sem=self.send.at[self.number],
            recv_sem=self.recv.at[self.number],
            device_id=device_of(place),
            device_id_type=MESH,
        )

    def start(self):
        self.make().start()

    def wait_recv(self):
        self.make().wait_recv()

    def wait_send(self):
        self.make().wait_send()


class Sender:
    def __init__(self, send, recv):
        self.send, self.recv, self.used = send, recv, 0

    def plan(self, recipe):
        copy = Copy(recipe, self.send, self.recv, self.used)
        self.used += 1
        return copy

    def start(self, recipe):
        copy = self.plan(recipe)
        copy.start()
        return copy


def lane_iota(rows):
    return lax.broadcasted_iota(jnp.int32, (rows, LANES), 1)


HUBS = (1, 2)


def others_of(hub):
    return [spot for spot in range(4) if spot != hub]


def hand_over(place, hub, number, pairs, hand, taken):
    other = others_of(hub)[number]
    target = {**place, "B": other // 2, "C": other % 2}
    return [
        pltpu.make_async_remote_copy(
            src_ref=source,
            dst_ref=to,
            send_sem=hand.at[hub - 1, number, kind],
            recv_sem=taken.at[hub - 1, kind],
            device_id=device_of(target),
            device_id_type=MESH,
        )
        for kind, (source, to) in pairs.items()
    ]


class Handing:
    def __init__(self, place, spare, seen_ref, meta_ref, targets_ref, tgt_ref, hand, taken):
        self.place, self.hand, self.taken = place, hand, taken
        self.spot = place["B"] * 2 + place["C"]
        self.refs = (spare, seen_ref, meta_ref, targets_ref, tgt_ref)

    def copies(self, hub, number, kinds):
        spare, seen_ref, meta_ref, targets_ref, tgt_ref = self.refs
        pairs = {
            0: (spare.at[number], seen_ref.at[2 + hub]),
            1: (meta_ref.at[0], meta_ref.at[hub]),
            2: (targets_ref.at[3 + number], tgt_ref.at[hub]),
        }
        pairs = {kind: pairs[kind] for kind in kinds}
        return hand_over(self.place, hub, number, pairs, self.hand, self.taken)

    def on_hub(self, act):
        for hub in HUBS:

            @pl.when(self.spot == hub)
            def _(hub=hub):
                act(hub)

    def start(self, kinds):
        def act(hub):
            for number in range(3):
                for copy in self.copies(hub, number, kinds):
                    copy.start()

        self.on_hub(act)

    def receive(self, kinds):
        for hub in HUBS:

            @pl.when(self.spot != hub)
            def _(hub=hub):
                for copy in self.copies(hub, 0, kinds):
                    copy.wait_recv()

    def finish(self, kinds):
        def act(hub):
            for number in range(3):
                for copy in self.copies(hub, number, kinds):
                    copy.wait_send()

        self.on_hub(act)


def own_block(plan, device, x_ref, line, rolled):
    rows, lines = plan.rows, plan.lines
    skip, lead = plan.own(device)
    line[...] = jnp.zeros_like(line)
    line[pl.ds(0, plan.length)] = x_ref[...]
    turned = pltpu.roll(line[...].reshape(lines, LANES), lead, 1)
    rolled[...] = jnp.zeros_like(rolled)
    rolled[pl.ds(8 + skip, lines), :] = turned
    upper, lower = rolled[pl.ds(8, rows), :], rolled[pl.ds(7, rows), :]
    return jnp.where(lane_iota(rows) >= lead, upper, lower).astype(BRAIN)


class Gather:
    def __init__(self, plan, place, out_ref, sender, columns):
        self.plan, self.place, self.out_ref, self.sender, self.columns = plan, place, out_ref, sender, columns
        self.flights, self.onwards, self.siblings = {}, [], {}

    def region(self, value, part, fixed, free=""):
        start, size = self.plan.parts[part]
        index = [value]
        for dim in "LBC":
            if dim in free:
                index.append(pl.ds(0, 2))
            else:
                index.append(1 - self.place[dim] if dim in fixed else self.place[dim])
        return self.out_ref.at[(*index, self.place["r"], pl.ds(start, size))]

    def column(self, source, part, target):
        send, recv = self.columns
        ref = self.region(source, part, "")
        return pltpu.make_async_remote_copy(
            src_ref=ref,
            dst_ref=ref,
            send_sem=send.at[target, part],
            recv_sem=recv.at[source, part],
            device_id=device_of(moved(self.place, "H", target)),
            device_id_type=MESH,
        )

    def over_column(self, act):
        high = self.place["H"]
        for target in range(self.plan.outer):

            @pl.when(high != target)
            def _(target=target):
                for part in range(len(self.plan.parts)):
                    act(self.column(high, part, target))

    def begin(self):
        self.over_column(lambda copy: copy.start())

    def roots(self, meanwhile):
        plan, place = self.plan, self.place
        copies = {}
        for value in range(plan.outer):
            copies[value] = []
            for part, order in enumerate(plan.orders):
                copies[value].append(self.spread(value, part, "", order) + [self.give(value, part, -1)])

        for value, groups in copies.items():

            @pl.when(place["H"] == value)
            def _(groups=groups):
                for group in groups:
                    for copy in group:
                        copy.start()

        meanwhile()
        for value, groups in copies.items():

            @pl.when(place["H"] != value)
            def _(value=value, groups=groups):
                for part, group in enumerate(groups):
                    self.column(value, part, place["H"]).wait_recv()
                    for copy in group:
                        copy.start()

    def spread(self, value, part, dims, onward):
        def recipe(dim):
            source = self.region(value, part, dims)
            return source, source, flipped(self.place, dim)

        copies = []
        for dim in onward:
            copy = self.sender.plan(functools.partial(recipe, dim))
            self.flights[value, part, frozenset(dims + dim)] = copy
            copies.append(copy)
        self.onwards += copies
        return copies

    def give(self, value, part, reach):
        order = self.plan.orders[part]

        def recipe():
            source = self.region(value, part, order[reach] if reach >= 0 else "", order[: max(reach, 0)])
            return source, source, flipped(self.place, "r")

        copy = self.sender.plan(recipe)
        self.siblings.setdefault(value, []).append(copy)
        return copy

    def stage(self, value, reach):
        plan = self.plan
        trees = []
        for order in plan.orders:
            trees.append([node for node in branches(order) if node[0] and reach == order.index(node[0][-1])])
        for nodes in zip(*trees):
            for part, (dims, onward) in enumerate(nodes):
                self.flights.pop((value, part, frozenset(dims))).wait_recv()
                for copy in self.spread(value, part, dims, onward):
                    copy.start()
        for part in range(len(plan.orders)):
            self.give(value, part, reach).start()

    def ready(self, value):
        for copy in self.siblings[value]:
            copy.wait_recv()

    def close(self):
        self.over_column(lambda copy: copy.wait_send())
        for copies in [self.onwards] + list(self.siblings.values()):
            for copy in copies:
                copy.wait_send()


class Reducer:
    def __init__(self, plan, place, grad_ref, core_in, tree_in, column_in, own_ref, sender, columns):
        self.plan, self.place, self.sender = plan, place, sender
        self.grad_ref, self.core_in, self.tree_in = grad_ref, core_in, tree_in
        self.column_in, self.own_ref, self.columns = column_in, own_ref, columns
        self.cores = {}
        self.pending = []
        self.trees = [branches(order) for order in plan.ways]
        self.flights = {}

    def share(self, value):
        place = self.place

        def recipe(start, size):
            whole = (value, pl.ds(0, 2), pl.ds(0, 2))
            span = pl.ds(start, size)
            return (
                self.grad_ref.at[(*whole, 1 - place["r"], span)],
                self.core_in.at[(*whole, span)],
                flipped(place, "r"),
            )

        for part, (start, size) in enumerate(self.plan.halves):
            copy = self.sender.start(functools.partial(recipe, start, size))
            self.cores[value, part] = copy
            self.pending.append(copy)

    def stage(self, value, reach):
        plan, place = self.plan, self.place
        steps = []
        for part in range(len(plan.halves)):
            order = plan.ways[part]
            nodes = [
                (dims, onward)
                for dims, onward in reversed(self.trees[part])
                if (order.index(dims[-1]) if dims else -1) == reach
            ]
            steps.append([(part, *node) for node in nodes])
        for group in zip(*steps):
            for part, dims, onward in group:
                self.node(value, part, dims, onward)

    def node(self, value, part, dims, onward):
        plan, place = self.plan, self.place
        start, size = plan.halves[part]
        span = pl.ds(start, size)
        if (value, part) in self.cores:
            self.cores.pop((value, part)).wait_recv()
        for dim in onward:
            self.flights.pop((value, part, frozenset(dims + dim))).wait_recv()
        index = [value] + [1 - place[dim] if dim in dims else place[dim] for dim in "BC"]
        total = self.grad_ref[(*index, place["r"], span)].astype(FLOAT)
        total = total + self.core_in[(*index, span)].astype(FLOAT)

        def number(dims):
            return sum(1 << "BC".index(dim) for dim in dims)

        for dim in onward:
            total = total + self.tree_in[value, number(dims + dim), span].astype(FLOAT)

        def spot():
            index = [value] + [1 - place[dim] if dim in dims else place[dim] for dim in "BC"]
            return self.grad_ref.at[(*index, place["r"], span)]

        def recipe():
            return spot(), self.tree_in.at[value, number(dims), span], flipped(place, dims[-1])

        if dims:
            spot()[...] = total.astype(BRAIN)
            copy = self.sender.start(recipe)
            self.flights[value, part, frozenset(dims)] = copy
            self.pending.append(copy)
            return
        depth = depth_of(place)

        @pl.when(depth == value)
        def _():
            self.own_ref[span, :] = total

        @pl.when(depth != value)
        def _():
            spot()[...] = total.astype(BRAIN)
            self.column(value, part).start()

    def column(self, value, part):
        plan, place = self.plan, self.place
        start, size = plan.halves[part]
        send, recv = self.columns
        index = (value, place["B"], place["C"], place["r"], pl.ds(start, size))
        return pltpu.make_async_remote_copy(
            src_ref=self.grad_ref.at[index],
            dst_ref=self.column_in.at[depth_of(place), pl.ds(start, size)],
            send_sem=send.at[value, part],
            recv_sem=recv.at[depth_of(place), part],
            device_id=device_of(at_depth(place, value)),
            device_id_type=MESH,
        )

    def arrival(self, source, part):
        plan, place = self.plan, self.place
        start, size = plan.halves[part]
        send, recv = self.columns
        return pltpu.make_async_remote_copy(
            src_ref=self.own_in(part),
            dst_ref=self.column_in.at[source, pl.ds(start, size)],
            send_sem=send.at[source, part],
            recv_sem=recv.at[source, part],
            device_id=device_of(at_depth(place, source)),
            device_id_type=MESH,
        )

    def own_in(self, part):
        place = self.place
        start, size = self.plan.halves[part]
        index = (0, place["B"], place["C"], place["r"], pl.ds(start, size))
        return self.grad_ref.at[index]

    def finish(self):
        plan, place = self.plan, self.place
        for part, (start, size) in enumerate(plan.halves):
            for source in range(plan.depths):

                @pl.when(depth_of(place) != source)
                def _(part=part, source=source, start=start, size=size):
                    self.arrival(source, part).wait_recv()
                    span = pl.ds(start, size)
                    self.own_ref[span, :] += self.column_in[source, span].astype(FLOAT)

    def close(self):
        plan, place = self.plan, self.place
        for copy in self.pending:
            copy.wait_send()
        for part in range(len(plan.halves)):
            for value in range(plan.depths):

                @pl.when(depth_of(place) != value)
                def _(part=part, value=value):
                    self.column(value, part).wait_send()


def finish_body(plan, place, held_ref, loss_ref, own_ref, total_out, scalars_out, turned, near, far, mine, sender):
    outer, rows, lines = plan.outer, plan.rows, plan.lines
    group, column = partners(place, outer)
    skip, lead = plan.own(index_of(place))
    position_in = lax.broadcasted_iota(jnp.int32, (lines, LANES), 0) * LANES + lane_iota(lines)
    shift = lax.rem(LANES - lead, LANES)
    turned[pl.ds(0, rows), :] = pltpu.roll(own_ref[...], shift, 1)
    here, below = turned[pl.ds(skip, lines), :], turned[pl.ds(skip + 1, lines), :]
    total = jnp.where(lane_iota(lines) < LANES - lead, here, below)
    total = jnp.where(position_in < plan.length, total, 0.0)
    squares = jnp.sum(total * total)
    lane = lane_iota(8)
    stats = jnp.where(lane == 0, squares, 0.0)
    stats = jnp.where(lane == 1, held_ref[0, 0].astype(FLOAT), stats)
    mine[0] = jnp.where(lane == 2, loss_ref[0], stats)
    count = len(group) + 1
    spot = lax.rem(index_of(place), count)
    near[spot] = mine[0]
    nears = [
        sender.start(functools.partial(lambda other: (mine.at[0], near.at[spot], other), other))
        for other in group
    ]
    total_out[...] = total
    for copy in nears:
        copy.wait_recv()
    together = near[0]
    for other in range(1, count):
        together = together + near[other]
    fars = []
    whole = together
    if column:
        far[place["H"]] = together
        mine[1] = together
        fars = [
            sender.start(functools.partial(lambda other: (mine.at[1], far.at[place["H"]], other), other))
            for other in column
        ]
        for copy in fars:
            copy.wait_recv()
        whole = far[0]
        for other in range(1, outer):
            whole = whole + far[other]
    row = whole[0:1, :]
    lane = lane[0:1]
    held = jnp.sum(jnp.where(lane == 1, row, 0.0))
    weights = jnp.full((1, LANES), held * (0.1 * VIS + (NP - VIS)))
    norms = jnp.sqrt(jnp.full((1, LANES), jnp.sum(jnp.where(lane == 0, row, 0.0)))) / weights
    losses = jnp.full((1, LANES), jnp.sum(jnp.where(lane == 2, row, 0.0))) / weights
    scalars_out[...] = jnp.where(lane == 0, losses, jnp.where(lane == 1, norms, weights))
    return nears + fars


def in_segments(index, segments):
    inside = None
    for start, stop in segments:
        here = (index >= start) & (index < stop)
        inside = here if inside is None else inside | here
    return inside


def matrix_segments():
    found = []
    for name, shape, kind, fan, rate in param_table():
        if kind == "matrix":
            start = layout()[name][0]
            found.append((start, start + math.prod(shape)))
    return found


def update_body(
    plan, step_ref, total_ref, scalars_ref, master_ref, first_ref, second_ref,
    master_out, first_out, second_out, copy_out, loss_out, norm_out, line
):
    rows, length = plan.lines, plan.length
    device = lax.axis_index("dp") * 2 + lax.axis_index("rep")
    position_in = lax.broadcasted_iota(jnp.int32, (rows, LANES), 0) * LANES + lane_iota(rows)
    flat = position_in + device * length
    table = layout()
    early, late = table["enc_ln1g"][0], table["encg"][0]
    rate_part = jnp.where(flat < early, 0.75, jnp.where(flat < late, 0.9, 1.0))
    decay_part = jnp.where(in_segments(flat, matrix_segments()), DECAY, 0.0)
    line[...] = jnp.zeros_like(line)
    line[pl.ds(0, length)] = master_ref[...]
    master = line[...].reshape(rows, LANES)
    line[pl.ds(0, length)] = first_ref[...]
    first = line[...].reshape(rows, LANES)
    line[pl.ds(0, length)] = second_ref[...]
    second = line[...].reshape(rows, LANES)
    loss_out[0, 0] = scalars_ref[0, 0]
    norm_out[0, 0] = scalars_ref[0, 1]
    norms = jnp.full((1, LANES), scalars_ref[0, 1])
    weights = jnp.full((1, LANES), scalars_ref[0, 2])
    gradient = total_ref[...] / weights
    clipped = gradient * jnp.minimum(1.0, CLIP / norms)
    fade = 1.0 / jnp.full((1, LANES), lax.shift_left(1, step_ref[0]).astype(FLOAT))
    new_first = BETA_ONE * first + (1.0 - BETA_ONE) * clipped
    new_second = BETA_TWO * second + (1.0 - BETA_TWO) * clipped * clipped
    first_hat = new_first / (1.0 - fade)
    second_hat = new_second / (1.0 - fade)
    new_master = master - LEARN * rate_part * (
        first_hat / (jnp.sqrt(second_hat) + EPSILON) + decay_part * master
    )
    master_out[...] = new_master.reshape(rows * LANES)[:length]
    first_out[...] = new_first.reshape(rows * LANES)[:length]
    second_out[...] = new_second.reshape(rows * LANES)[:length]
    copy_out[...] = new_master.reshape(rows * LANES)[:length].astype(BRAIN)


def update(step, total, scalars, master, first, second, plan):
    vmem = pl.BlockSpec(memory_space=pltpu.VMEM)
    smem = pl.BlockSpec(memory_space=pltpu.SMEM)
    flat = jax.ShapeDtypeStruct((plan.length,), FLOAT)
    single = jax.ShapeDtypeStruct((1, 1), FLOAT)
    return pl.pallas_call(
        functools.partial(update_body, plan),
        out_shape=(flat, flat, flat, jax.ShapeDtypeStruct((plan.length,), BRAIN), single, single),
        in_specs=[smem, vmem, smem, vmem, vmem, vmem],
        out_specs=(vmem, vmem, vmem, vmem, smem, smem),
        scratch_shapes=[pltpu.VMEM((plan.lines * LANES,), FLOAT)],
        compiler_params=pltpu.CompilerParams(vmem_limit_bytes=16 << 20),
    )(step, total, scalars, master, first, second)


class Frames:
    def __init__(self, plan, slots, even, odd):
        self.plan, self.slots, self.even, self.odd = plan, slots, even, odd
        self.filled = 0

    def add(self, index):
        plan, even = self.plan, self.even
        if index == plan.first_late:
            rest = plan.border - self.filled
            even[pl.ds(self.filled, rest), :] = jnp.zeros((rest, LANES), FLOAT)
            half_turn(plan, even, self.odd)
            self.filled = plan.border
        frame = self.odd if plan.late(index) else even
        start = plan.base(index) // 8 * 8
        rows = -(-(plan.base(index) - start + plan.used(index)) // 8) * 8
        block = self.slots[(*spot_of(index), pl.ds(0, plan.rows))].astype(FLOAT)
        if start < self.filled:
            frame[pl.ds(start, 8), :] += block[:8]
            frame[pl.ds(start + 8, rows - 8), :] = block[8:rows]
        else:
            frame[pl.ds(start, rows), :] = block[:rows]
        self.filled = start + rows


def half_turn(plan, even, odd):
    total = plan.border - 8
    span = 256

    def turn(start, rows):
        here = pltpu.roll(even[pl.ds(start, rows), :], 64, 1)
        below = pltpu.roll(even[pl.ds(start + 1, rows), :], 64, 1)
        odd[pl.ds(start, rows), :] = jnp.where(lane_iota(rows) < 64, here, below)

    @pl.loop(0, total // span)
    def _(step):
        turn(pl.multiple_of(step * span, span), span)

    if total % span:
        turn(total // span * span, total % span)


def read_param(even, odd, name, target):
    offset, shape = layout()[name]
    rows, width = (1, shape[0]) if len(shape) == 1 else shape
    base, late = divmod(offset, LANES)
    frames = (even, odd) if late == 0 else (odd, even)
    whole, half = divmod(width, LANES)
    kind = target.dtype
    if rows == 1:
        for col in range(whole):
            target[:, pl.ds(col * LANES, LANES)] = frames[0][pl.ds(base + col, 1), :].astype(kind)
        if half:
            tail = frames[0][pl.ds(base + whole, 1), :]
            target[:, pl.ds(whole * LANES, half)] = tail[:, :half].astype(kind)
        return
    if not half:
        for col in range(whole):
            piece = frames[0][pl.ds(base + col, rows, stride=whole), :]
            target[:, pl.ds(col * LANES, LANES)] = piece.astype(kind)
        return
    stride = 2 * width // LANES
    shift = whole + (1 if late else 0)

    def interleave(scratch):
        for col in range(whole + 1):
            size = LANES if col < whole else half
            upper = frames[0][pl.ds(base + col, rows // 2, stride=stride), :]
            lower = frames[1][pl.ds(base + shift + col, rows // 2, stride=stride), :]
            scratch[pl.ds(0, rows // 2, stride=2), :] = upper
            scratch[pl.ds(1, rows // 2, stride=2), :] = lower
            target[:, pl.ds(col * LANES, size)] = scratch[...][:, :size].astype(kind)

    pl.run_scoped(interleave, pltpu.VMEM((rows, LANES), FLOAT))


def write_grad(even, odd, name, value):
    offset, shape = layout()[name]
    rows, width = (1, shape[0]) if len(shape) == 1 else shape
    base, late = divmod(offset, LANES)
    frames = (even, odd) if late == 0 else (odd, even)
    whole, half = divmod(width, LANES)

    def columns():
        for col in range(0, whole, 2):
            size = min(2, whole - col) * LANES
            both = value(col * LANES, size)
            for part in range(size // LANES):
                yield col + part, both[:, part * LANES : (part + 1) * LANES]
        if half:
            tail = value(whole * LANES, half)
            yield whole, jnp.concatenate([tail, jnp.zeros((rows, LANES - half), FLOAT)], axis=1)

    if rows == 1:
        for col, piece in columns():
            frames[0][pl.ds(base + col, 1), :] = piece
        return
    if not half:
        for col, piece in columns():
            frames[0][pl.ds(base + col, rows, stride=whole), :] = piece
        return
    stride = 2 * width // LANES
    shift = whole + (1 if late else 0)

    def interleave(scratch):
        for col, piece in columns():
            scratch[...] = piece
            upper = scratch[pl.ds(0, rows // 2, stride=2), :]
            lower = scratch[pl.ds(1, rows // 2, stride=2), :]
            frames[0][pl.ds(base + col, rows // 2, stride=stride), :] = upper
            frames[1][pl.ds(base + shift + col, rows // 2, stride=stride), :] = lower

    pl.run_scoped(interleave, pltpu.VMEM((rows, LANES), FLOAT))


def clear_frames(plan, even, odd):
    even[...] = jnp.zeros_like(even)
    odd[pl.ds(0, plan.border + 16), :] = jnp.zeros((plan.border + 16, LANES), FLOAT)
    table = layout()
    final = (table["headb"][0] // LANES) // 8 * 8
    odd[pl.ds(final, odd.shape[0] - final), :] = jnp.zeros((odd.shape[0] - final, LANES), FLOAT)


def emit_slots(plan, even, odd, slots, depths):
    rows = plan.rows
    for index in [depth * 8 + number for depth in depths for number in range(8)]:
        start = plan.base(index) // 8 * 8
        if plan.late(index):
            block = odd[pl.ds(start + 8, rows), :]
        else:
            here = pltpu.roll(odd[pl.ds(start + 8, rows), :], 64, 1)
            above = pltpu.roll(odd[pl.ds(start + 7, rows), :], 64, 1)
            block = even[pl.ds(start, rows), :] + jnp.where(lane_iota(rows) < 64, above, here)
        slots[(index // 8, index // 4 % 2, index // 2 % 2, index % 2)] = block.astype(BRAIN)


def dot(left, right, dims=(((1,), (0,)), ((), ()))):
    return lax.dot_general(left, right, dims, preferred_element_type=FLOAT)


def place_table(count, rows, width):
    quarter = width // 4
    omega = 1.0 / 10000.0 ** (np.arange(quarter) / quarter)
    index = np.arange(count)
    across = (index // GRID)[:, None] * omega
    along = (index % GRID)[:, None] * omega
    table = np.zeros((rows, width), np.float32)
    table[:count] = np.concatenate(
        [np.sin(across), np.cos(across), np.sin(along), np.cos(along)], axis=-1
    )
    return table


def split_two(value):
    upper = value.astype(BRAIN)
    return upper, (value - upper.astype(FLOAT)).astype(BRAIN)


def norm_parts(value):
    center = value - jnp.mean(value, axis=-1, keepdims=True)
    spread = lax.rsqrt(jnp.mean(center * center, axis=-1, keepdims=True) + LN_EPS)
    return center * spread, spread


def norm_back(grad, value, gain):
    unit, spread = norm_parts(value)
    d_gain = jnp.sum(grad * unit, axis=0, keepdims=True)
    d_shift = jnp.sum(grad, axis=0, keepdims=True)
    scaled = grad * gain
    middle = jnp.mean(scaled, axis=-1, keepdims=True)
    along = jnp.mean(scaled * unit, axis=-1, keepdims=True)
    return spread * (scaled - middle - unit * along), d_gain, d_shift


def gelu_parts(value):
    half = 0.5 + 0.5 * lax.erf(value * 0.7071067811865476)
    bell = jnp.exp2(value * value * (-0.5 * LOG_TWO_E)) * 0.3989422804014327
    return value * half, half + value * bell


def head_only(value, head, size):
    lane = lax.broadcasted_iota(jnp.int32, value.shape, 1)
    inside = (lane >= head * size) & (lane < (head + 1) * size)
    return jnp.where(inside, value, jnp.zeros_like(value))


def attend(t_ref, chance_ref, usable, width, heads):
    size = width // heads
    query, keys = t_ref[:, pl.ds(0, width)], t_ref[:, pl.ds(width, width)]
    values = t_ref[:, pl.ds(2 * width, width)].T
    factor = size ** (-0.5) * LOG_TWO_E
    mixed = []
    for head in range(heads):
        raw = dot(head_only(keys, head, size), query, PAIR)
        raw = jnp.where(usable, raw, -1e30)
        top = jnp.max(raw, axis=0, keepdims=True)
        power = jnp.exp2((raw - top) * factor)
        chance = power * (1.0 / jnp.sum(power, axis=0, keepdims=True))
        chance_ref[head] = chance
        mixed.append(dot(values[head * size : (head + 1) * size], chance.astype(BRAIN)))
    return jnp.concatenate(mixed, axis=0).astype(BRAIN).T


def attend_back(d_mixed, t_ref, dt_ref, chance_ref, width, heads):
    size = width // heads
    scale = size ** (-0.5)
    query, keys = t_ref[:, pl.ds(0, width)], t_ref[:, pl.ds(width, width)]
    values = t_ref[:, pl.ds(2 * width, width)]
    across = keys.T
    d_query = []
    d_keys = d_values = None
    for head in range(heads):
        chance = chance_ref[head]
        d_here = head_only(d_mixed, head, size)
        d_chance = dot(head_only(values, head, size), d_mixed, PAIR)
        along = jnp.sum(chance * d_chance, axis=0, keepdims=True)
        d_scores = (chance * (d_chance - along)).astype(BRAIN)
        part = dot(chance.astype(BRAIN), d_here)
        d_values = part if d_values is None else d_values + part
        part = dot(d_scores, head_only(query, head, size))
        d_keys = part if d_keys is None else d_keys + part
        d_query.append(dot(across[head * size : (head + 1) * size], d_scores))
    d_query = (jnp.concatenate(d_query, axis=0) * scale).astype(BRAIN).T
    dt_ref[:, pl.ds(0, width)] = d_query
    dt_ref[:, pl.ds(width, width)] = (d_keys * scale).astype(BRAIN)
    dt_ref[:, pl.ds(2 * width, width)] = d_values.astype(BRAIN)


class Weights:
    def __init__(self, refs):
        self.refs = dict(zip(layout(), refs))

    def __call__(self, name):
        return self.refs[name][...]


def block_open(hidden, keep, weights, prefix):
    width = hidden.shape[1]
    keep["x"][...] = hidden
    unit, unused = norm_parts(hidden)
    normed = (unit * weights(prefix + "ln1g") + weights(prefix + "ln1b")).astype(BRAIN)
    keep["a"][...] = normed
    bias = weights(prefix + "qvb")
    for part in range(3):
        cols = pl.ds(part * width, width)
        value = dot(normed, weights.refs[prefix + "qkv"][:, cols])
        if part != 1:
            value = value + bias[:, (part // 2) * width : (part // 2 + 1) * width]
        keep["t"][:, cols] = value.astype(BRAIN)


def block_middle(hidden, keep, weights, prefix, heads, usable):
    width = hidden.shape[1]
    mixed = attend(keep["t"], keep["p"], usable, width, heads)
    keep["o"][...] = mixed
    middle = hidden + (dot(mixed, weights(prefix + "proj")) + weights(prefix + "projb"))
    keep["m"][...] = middle
    unit, unused = norm_parts(middle)
    second = (unit * weights(prefix + "ln2g") + weights(prefix + "ln2b")).astype(BRAIN)
    keep["b"][...] = second
    inner = dot(second, weights(prefix + "fc1")) + weights(prefix + "fc1b")
    active, slope = gelu_parts(inner)
    keep["s"][...] = slope
    keep["g"][...] = active.astype(BRAIN)


def block_shut(keep, weights, prefix):
    return keep["m"][...] + (dot(keep["g"][...], weights(prefix + "fc2")) + weights(prefix + "fc2b"))


def home_open(grad, keep, weights, prefix):
    d_branch = grad.astype(BRAIN)
    keep["dz"][...] = d_branch
    keep["du"][...] = (dot(d_branch, weights(prefix + "fc2"), PAIR) * keep["s"][...]).astype(BRAIN)


def home_middle(grad, keep, weights, prefix, heads, sums):
    width = grad.shape[1]
    d_second = dot(keep["du"][...], weights(prefix + "fc1"), PAIR)
    d_middle, d_gain, d_shift = norm_back(d_second, keep["m"][...], weights(prefix + "ln2g"))
    sums(prefix + "ln2g", d_gain)
    sums(prefix + "ln2b", d_shift)
    d_middle = d_middle + grad
    d_output = d_middle.astype(BRAIN)
    keep["dy"][...] = d_output
    d_mixed = dot(d_output, weights(prefix + "proj"), PAIR).astype(BRAIN)
    attend_back(d_mixed, keep["t"], keep["dt"], keep["p"], width, heads)
    d_normed = dot(keep["dt"][...], weights(prefix + "qkv"), PAIR)
    d_hidden, d_gain, d_shift = norm_back(d_normed, keep["x"][...], weights(prefix + "ln1g"))
    sums(prefix + "ln1g", d_gain)
    sums(prefix + "ln1b", d_shift)
    return d_middle + d_hidden


def kept_shapes(rows, width, hidden, heads):
    return {
        "x": ((rows, width), FLOAT),
        "a": ((rows, width), BRAIN),
        "t": ((rows, 3 * width), BRAIN),
        "p": ((heads, rows, rows), FLOAT),
        "o": ((rows, width), BRAIN),
        "m": ((rows, width), FLOAT),
        "b": ((rows, width), BRAIN),
        "s": ((rows, hidden), FLOAT),
        "g": ((rows, hidden), BRAIN),
        "dz": ((rows, width), BRAIN),
        "du": ((rows, hidden), BRAIN),
        "dy": ((rows, width), BRAIN),
        "dt": ((rows, 3 * width), BRAIN),
    }


def kept_scratch(count, *sizes):
    lead = (count,) if count else ()
    return [pltpu.VMEM(lead + shape, kind) for shape, kind in kept_shapes(*sizes).values()]


def kept_view(refs, image=None):
    names = kept_shapes(1, 1, 1, 1)
    return {name: ref if image is None else ref.at[image] for name, ref in zip(names, refs)}


LAYERS = {
    "fc2": ("g", "dz", "fc2b"),
    "fc1": ("b", "du", "fc1b"),
    "proj": ("o", "dy", "projb"),
    "qkv": ("a", "dt", "qvb"),
}


def block_grads(keep, prefix, names, emit):
    def rows_of(name):
        value = keep[name][...]
        return value.reshape(-1, value.shape[-1])

    for name in names:
        left, right, bias = LAYERS[name]
        emit(prefix + name, prefix + bias, rows_of(left), rows_of(right))


NORMS = ("ln1g", "ln1b", "ln2g", "ln2b", "encg", "encb", "decg", "decb", "mask")


class Images:
    def __init__(self, place, counts_ref, meta_ref):
        spot = place["B"] * 2 + place["C"]
        self.meta_ref = meta_ref
        self.own = counts_ref[0, 0]
        lane = lane_iota(8)
        row = lax.broadcasted_iota(jnp.int32, (8, LANES), 0)

        def count_of(hub):
            corner = jnp.where((lane == LANES - 1) & (row == 0), meta_ref[hub], 0.0)
            return jnp.sum(corner).astype(jnp.int32)

        one, two = count_of(1), count_of(2)
        from_one = jnp.where(spot == 0, 3, jnp.where(spot == 2, 4, 5))
        from_two = jnp.where(spot == 0, 3, jnp.where(spot == 1, 4, 5))
        use_one = (spot == 2) | ((spot != 1) & (one > 2))
        mine = self.own > 2

        def choose(own, first, second):
            return jnp.where(mine, own, jnp.where(use_one, first, second))

        self.third = choose(2, 3, 4)
        self.third_row = choose(2, from_one, from_two)
        self.third_count = choose(self.own, one, two)
        self.third_meta = choose(0, 1, 2)

    def __call__(self, image):
        last = image == 2
        source = jnp.where(last, self.third, image)
        line = jnp.where(last, self.third_row, image)
        live = jnp.where(last, self.third_count, self.own) > line
        kept = self.meta_ref[jnp.where(last, self.third_meta, 0), pl.ds(line, 1), :][:, :HOME]
        return source, kept, live.astype(FLOAT)


def placement(kept, rows):
    number = lax.broadcasted_iota(jnp.int32, (rows, HOME), 0).astype(FLOAT)
    return (number == kept).astype(FLOAT)


def whole_body(
    plan, counts_ref, keep_ref, x_ref, patches_ref, targets_ref, enc_table, dec_table,
    total_out, scalars_out, *scratch
):
    scratch = list(scratch)

    def take(count):
        taken = scratch[:count]
        del scratch[:count]
        return taken

    names = list(layout())
    slots, seen_ref, tgt_own, tgt_ref, wanted, meta_ref, grad_ref, loss_ref = take(8)
    spot_enc, spot_dec, local = take(3)
    line, rolled, pixels, spare, send, recv, hand, taken = take(8)
    even, odd, sums_ref, y_hi, y_lo, dy_home, final_all, dpred_all, d_out = take(9)
    weights = Weights(take(len(names)))
    enc_refs, dec_refs = take(13), take(13)
    core_in, tree_in, column_in, own_ref, turned, near, far, mine = take(8)
    spread_send, spread_recv, column_send, column_recv = take(4)

    place = position()
    device = index_of(place)
    copies = [
        pltpu.make_async_copy(patches_ref, pixels, local.at[0]),
        pltpu.make_async_copy(enc_table, spot_enc, local.at[1]),
        pltpu.make_async_copy(dec_table, spot_dec, local.at[2]),
        pltpu.make_async_copy(
            targets_ref.at[pl.ds(0, LIVE_CAP - 1)], tgt_own, local.at[3]
        ),
        pltpu.make_async_copy(targets_ref.at[LIVE_CAP - 1], tgt_ref.at[0], local.at[4]),
    ]
    for copy in copies:
        copy.start()
    slots[(place["H"], place["L"], place["B"], place["C"], place["r"])] = own_block(
        plan, device, x_ref, line, rolled
    )
    meet(gates(place, plan))
    sender = Sender(send, recv)
    handing = Handing(place, spare, seen_ref, meta_ref, targets_ref, tgt_ref, hand, taken)

    def choose_images():
        lane = lane_iota(8)
        row = lax.broadcasted_iota(jnp.int32, (8, LANES), 0)
        held = counts_ref[0, 0].astype(FLOAT)
        meta_ref[0] = jnp.where((lane == LANES - 1) & (row == 0), held, -1.0)
        meta_ref[0, pl.ds(0, keep_ref.shape[0]), pl.ds(0, VIS)] = keep_ref[...].astype(FLOAT)
        copies[0].wait()

        def visible(image):
            where = placement(meta_ref[0, pl.ds(image, 1), :][:, :HOME], NP).astype(BRAIN)
            return dot(where, pixels[image], DEEP).astype(BRAIN)

        def prepare(hub):
            for number in range(3):
                spare[number] = visible(3 + number)

        handing.on_hub(prepare)
        handing.start((0, 1))
        for image in range(LIVE_CAP):
            seen_ref[image] = visible(image)

    early = min(-(-layout()["dec_qkv"][0] // (16 * plan.length)), plan.outer)
    first_values, last_values = range(early), range(early, plan.outer)
    gather = Gather(plan, place, slots, sender, (spread_send, spread_recv))
    frames = Frames(plan, slots, even, odd)

    def spread(values, reach):
        for value in values:
            gather.stage(value, reach)

    def fetch(values, wanted_names):
        for value in values:
            gather.ready(value)
            for index in range(value * 16, value * 16 + 16):
                frames.add(index)
        for name in wanted_names:
            read_param(even, odd, name, weights.refs[name])

    gather.begin()
    gather.roots(choose_images)
    for reach in (0, 1):
        spread(first_values, reach)
        spread(last_values, reach)
    spread(first_values, 2)
    divide = names.index("dec_qkv")
    fetch(first_values, names[:divide])
    handing.receive((0, 1))
    for copy in copies[1:]:
        copy.wait()
    sums_ref[...] = jnp.zeros_like(sums_ref)
    order = {name: number for number, name in enumerate(names)}

    def add_sum(name, value):
        sums_ref[pl.ds(order[name], 1), pl.ds(0, value.shape[1])] += value

    pick = Images(place, counts_ref, meta_ref)

    visible, begin = [], []
    for image in range(LIVE_CAP):
        source, kept, live = pick(image)
        where = placement(kept, ROWS).astype(BRAIN)
        visible.append(seen_ref[source])
        begin.append(dot(where, spot_enc[0], DEEP) + dot(where, spot_enc[1], DEEP))
    visible = jnp.concatenate(visible, axis=0)
    begin = jnp.concatenate(begin, axis=0)
    enc_rows = LIVE_CAP * HOME
    enc = kept_view(enc_refs)
    down = lax.broadcasted_iota(jnp.int32, (enc_rows, enc_rows), 0)
    over = lax.broadcasted_iota(jnp.int32, (enc_rows, enc_rows), 1)
    usable = (down // HOME == over // HOME) & (down % HOME < VIS)
    first_in = dot(visible, weights("patch")) + weights("patchb") + begin
    block_open(first_in, enc, weights, "enc_")
    block_middle(first_in, enc, weights, "enc_", HEADS, usable)
    encoded = block_shut(enc, weights, "enc_")
    unit, unused = norm_parts(encoded)
    encoder_out = (unit * weights("encg") + weights("encb")).astype(BRAIN)
    embedded = dot(encoder_out, weights("embed")) + weights("embedb")
    upper, lower = split_two(embedded)
    for image in range(LIVE_CAP):
        y_hi[image] = upper[image * HOME : (image + 1) * HOME]
        y_lo[image] = lower[image * HOME : (image + 1) * HOME]
    spread(last_values, 2)
    handing.start((2,))
    fetch(last_values, names[divide:])
    clear_frames(plan, even, odd)
    view = odd.at[pl.ds(8, plan.frame_rows)]
    real = lax.broadcasted_iota(jnp.int32, (ROWS, 1), 0) < NP
    usable_dec = lax.broadcasted_iota(jnp.int32, (ROWS, ROWS), 0) < NP

    def seen_of(kept):
        where = placement(kept, ROWS)
        return where.astype(BRAIN), jnp.sum(where, axis=1, keepdims=True)

    @pl.loop(0, LIVE_CAP)
    def _(image):
        source, kept, live = pick(image)
        where, seen = seen_of(kept)
        grid_in = dot(where, y_hi[image]) + dot(where, y_lo[image])
        grid_in = grid_in + (1.0 - seen) * weights("mask") + spot_dec[...]
        keep = kept_view(dec_refs, image)
        block_open(grid_in, keep, weights, "dec_")
        block_middle(grid_in, keep, weights, "dec_", DHEADS, usable_dec)


    def one_image(image, total):
        source, kept, live = pick(image)
        where, seen = seen_of(kept)
        keep = kept_view(dec_refs, image)
        decoded = block_shut(keep, weights, "dec_")
        unit, unused = norm_parts(decoded)
        final = (unit * weights("decg") + weights("decb")).astype(BRAIN)
        final_all[image] = final
        predicted = dot(final, weights("head")) + weights("headb")
        weight = jnp.where(real, (1.0 - 0.9 * seen) * live, 0.0)

        @pl.when(image == LIVE_CAP - 1)
        def _():
            handing.receive((2,))
            wanted[...] = tgt_ref[pick.third - 2]

        @pl.when(image < LIVE_CAP - 1)
        def _():
            wanted[...] = tgt_own[image]

        error = predicted[:NP] - wanted[...].astype(FLOAT)
        weighted = error * weight[:NP]
        total = total + jnp.sum(weighted * error, axis=0, keepdims=True)
        dpred_all[image, pl.ds(0, NP)] = (weighted * (2.0 / PIX)).astype(BRAIN)
        dpred_all[image, pl.ds(NP, ROWS - NP)] = jnp.zeros((ROWS - NP, PIX), BRAIN)
        d_final = dot(dpred_all[image], weights("head"), PAIR)
        d_decoded, d_gain, d_shift = norm_back(d_final, decoded, weights("decg"))
        add_sum("decg", d_gain)
        add_sum("decb", d_shift)
        d_out[image] = d_decoded
        home_open(d_decoded, keep, weights, "dec_")
        return total

    total = lax.fori_loop(0, LIVE_CAP, one_image, jnp.zeros((1, PIX), FLOAT))
    loss_ref[0] = jnp.sum(total) * (1.0 / PIX)

    def emit(name, bias, left, right):
        ones = jnp.ones((16, right.shape[0]), BRAIN)
        summed = dot(ones, right)[0:1]
        if bias.endswith("qvb"):
            width = summed.shape[1] // 3
            summed = jnp.concatenate([summed[:, :width], summed[:, 2 * width :]], axis=1)
        write_grad(even, view, bias, lambda start, size: summed[:, start : start + size])
        turned = left.T
        write_grad(even, view, name, lambda start, size: dot(turned, right[:, start : start + size]))

    def emit_norms(wanted_names):
        for name in wanted_names:
            row = pl.ds(order[name], 1)
            write_grad(even, view, name, lambda start, size, row=row: sums_ref[row, pl.ds(start, size)])

    reducer = Reducer(
        plan, place, grad_ref, core_in, tree_in, column_in, own_ref, sender, (column_send, column_recv)
    )
    floors = [plan.depths_from(name) for name in ("dec_fc2", "embed", "enc_fc1")]
    waves = [range(low, high) for low, high in zip(floors + [0], [plan.depths] + floors)]

    def leave(wave):
        emit_slots(plan, even, odd, grad_ref, waves[wave])
        for depth in waves[wave]:
            reducer.share(depth)

    def collect(wave, reach):
        for depth in waves[wave]:
            reducer.stage(depth, reach)

    dec = kept_view(dec_refs)
    emit("head", "headb", final_all[...].reshape(-1, E), dpred_all[...].reshape(-1, PIX))
    block_grads(dec, "dec_", ("fc2",), emit)
    emit_norms(("decg", "decb"))
    leave(0)
    block_grads(dec, "dec_", ("fc1",), emit)

    @pl.loop(0, LIVE_CAP)
    def _(image):
        @pl.when(image == 1)
        def _():
            collect(0, 1)

        @pl.when(image == 2)
        def _():
            collect(0, 0)

        source, kept, live = pick(image)
        where, seen = seen_of(kept)
        d_grid = home_middle(
            d_out[image], kept_view(dec_refs, image), weights, "dec_", DHEADS, add_sum
        )
        add_sum("mask", jnp.sum((1.0 - seen) * d_grid, axis=0, keepdims=True))
        dy_home[image] = dot(where, d_grid.astype(BRAIN), DEEP).astype(BRAIN)

    collect(0, -1)
    block_grads(dec, "dec_", ("proj", "qkv"), emit)
    d_embedded = dy_home[...].reshape(enc_rows, E)
    emit("embed", "embedb", encoder_out, d_embedded)
    emit_norms(("mask", "dec_ln1g", "dec_ln1b", "dec_ln2g", "dec_ln2b"))
    leave(1)

    d_seen = dot(d_embedded, weights("embed"), PAIR).astype(BRAIN).astype(FLOAT)
    d_encoded, d_gain, d_shift = norm_back(d_seen, encoded, weights("encg"))
    add_sum("encg", d_gain)
    add_sum("encb", d_shift)
    home_open(d_encoded, enc, weights, "enc_")
    block_grads(enc, "enc_", ("fc2", "fc1"), emit)
    emit_norms(("encg", "encb"))
    leave(2)
    collect(1, 1)
    d_first = home_middle(d_encoded, enc, weights, "enc_", HEADS, add_sum).astype(BRAIN)
    collect(2, 1)
    collect(1, 0)
    emit("patch", "patchb", visible, d_first)
    block_grads(enc, "enc_", ("proj", "qkv"), emit)
    emit_norms(("enc_ln1g", "enc_ln1b", "enc_ln2g", "enc_ln2b"))
    leave(3)
    collect(2, 0)
    collect(1, -1)
    collect(3, 1)
    collect(2, -1)
    collect(3, 0)
    collect(3, -1)
    reducer.finish()
    pending = finish_body(
        plan, place, counts_ref, loss_ref, own_ref, total_out, scalars_out, turned, near, far, mine, sender
    )
    gather.close()
    reducer.close()
    handing.finish((0, 1, 2))
    for copy in pending:
        copy.wait_send()


def weight_scratch():
    shapes = []
    for name, (offset, shape) in layout().items():
        if len(shape) == 1:
            shapes.append(pltpu.VMEM((1, *shape), FLOAT))
        else:
            shapes.append(pltpu.VMEM(shape, BRAIN))
    return shapes


def copies_used(plan):
    spread = len(plan.parts) * plan.outer * (7 + 4)
    home = len(plan.halves) * plan.depths * (1 + 3)
    return spread + home + 31 + plan.outer


def whole_step(counts, keep, master, patches, targets, plan):
    outer, depths, rows, lines = plan.outer, plan.depths, plan.rows, plan.lines
    vmem = pl.BlockSpec(memory_space=pltpu.VMEM)
    smem = pl.BlockSpec(memory_space=pltpu.SMEM)
    far = pl.BlockSpec(memory_space=pl.ANY)
    table = place_table(NP, ROWS, D)
    upper = table.astype(BRAIN)
    spot_enc = jnp.asarray(np.stack([upper, (table - upper.astype(np.float32)).astype(BRAIN)]))
    spot_dec = jnp.asarray(place_table(NP, ROWS, E))
    block = pltpu.VMEM((outer, 2, 2, 2, 2, rows, LANES), BRAIN)
    dma = pltpu.SemaphoreType.DMA
    copies = copies_used(plan)
    return pl.pallas_call(
        functools.partial(whole_body, plan),
        out_shape=(
            jax.ShapeDtypeStruct((lines, LANES), FLOAT),
            jax.ShapeDtypeStruct((1, LANES), FLOAT),
        ),
        in_specs=[smem, vmem, vmem, far, far, far, far],
        out_specs=(vmem, vmem),
        scratch_shapes=[
            block,
            pltpu.VMEM((5, HOME, PIX), BRAIN),
            pltpu.VMEM((LIVE_CAP - 1, NP, PIX), BRAIN),
            pltpu.VMEM((3, NP, PIX), BRAIN),
            pltpu.VMEM((NP, PIX), BRAIN),
            pltpu.VMEM((3, 8, LANES), FLOAT),
            pltpu.VMEM((depths, 2, 2, 2, rows, LANES), BRAIN),
            pltpu.SMEM((1,), FLOAT),
            pltpu.VMEM(spot_enc.shape, BRAIN),
            pltpu.VMEM(spot_dec.shape, FLOAT),
            dma((5,)),
            pltpu.VMEM((lines * LANES,), FLOAT),
            pltpu.VMEM((rows + 8, LANES), FLOAT),
            pltpu.VMEM(patches.shape, BRAIN),
            pltpu.VMEM((3, HOME, PIX), BRAIN),
            dma((copies,)),
            dma((copies,)),
            dma((2, 3, 3)),
            dma((2, 3)),
            pltpu.VMEM((plan.border + rows, LANES), FLOAT),
            pltpu.VMEM((plan.frame_rows + 8, LANES), FLOAT),
            pltpu.VMEM((48, E), FLOAT),
            pltpu.VMEM((LIVE_CAP, HOME, E), BRAIN),
            pltpu.VMEM((LIVE_CAP, HOME, E), BRAIN),
            pltpu.VMEM((LIVE_CAP, HOME, E), BRAIN),
            pltpu.VMEM((LIVE_CAP, ROWS, E), BRAIN),
            pltpu.VMEM((LIVE_CAP, ROWS, PIX), BRAIN),
            pltpu.VMEM((LIVE_CAP, ROWS, E), FLOAT),
            *weight_scratch(),
            *kept_scratch(0, LIVE_CAP * HOME, D, FF, HEADS),
            *kept_scratch(LIVE_CAP, ROWS, E, DFF, DHEADS),
            pltpu.VMEM((depths, 2, 2, rows, LANES), BRAIN),
            pltpu.VMEM((depths, 4, rows, LANES), BRAIN),
            pltpu.VMEM((depths, rows, LANES), BRAIN),
            pltpu.VMEM((rows, LANES), FLOAT),
            pltpu.VMEM((rows, LANES), FLOAT),
            pltpu.VMEM((32, 8, LANES), FLOAT),
            pltpu.VMEM((outer, 8, LANES), FLOAT),
            pltpu.VMEM((2, 8, LANES), FLOAT),
            dma((outer, len(plan.parts))),
            dma((outer, len(plan.parts))),
            dma((depths, len(plan.halves))),
            dma((depths, len(plan.halves))),
        ],
        compiler_params=pltpu.CompilerParams(
            collective_id=0, has_side_effects=True, vmem_limit_bytes=60 << 20
        ),
    )(counts, keep, master, patches, targets, spot_enc, spot_dec)


def on_device(patches, targets, keep, counts, step, master, first, second):
    plan = Plan(master.shape[0], lax.axis_size(("dp", "rep")))
    total, scalars = whole_step(counts, keep, master, patches, targets, plan)
    outs = update(step, total, scalars, master, first, second, plan)
    return (*outs[:4], outs[4].reshape(()), outs[5].reshape(()))


def solution(mesh):
    return jax.shard_map(
        on_device,
        mesh=mesh,
        in_specs=(
            P(("dp", "rep"), None, None),
            P(("dp", "rep"), None, None),
            P(("dp", "rep"), None),
            P("dp", "rep"),
            P(),
            P(("dp", "rep")),
            P(("dp", "rep")),
            P(("dp", "rep")),
        ),
        out_specs=(
            P(("dp", "rep")),
            P(("dp", "rep")),
            P(("dp", "rep")),
            P(("dp", "rep")),
            P(),
            P(),
        ),
        check_vma=False,
    )
```

```python
import functools
import itertools
import math

import jax
import jax.numpy as jnp
import numpy as np
from jax import lax
from jax.experimental import pallas as pl
from jax.experimental.pallas import tpu as pltpu
from jax.sharding import PartitionSpec as P

D = 192
HEADS = 3
FF = 768
E = 256
DHEADS = 8
DFF = 1024
PIX = 768
GRID = 14
VIS = 49
NP = 196

FLOAT = jnp.float32
BRAIN = jnp.bfloat16
CLIP = 0.05
BETA_ONE = 0.5
BETA_TWO = 0.5
LEARN = 0.01
DECAY = 0.05
EPSILON = 1e-08
LN_EPS = 1e-06

ROWS = 208
HOME = 64
LIVE_CAP = 3
PAIR = ((1,), (1,)), ((), ())
DEEP = ((0,), (0,)), ((), ())
LOG_TWO_E = 1.4426950408889634


def block_table(prefix, width, hidden, proj_fan, rate):
    return [
        (prefix + "ln1g", (width,), "gain", 1, rate),
        (prefix + "ln1b", (width,), "bias", 1, rate),
        (prefix + "qkv", (width, 3 * width), "matrix", width, rate),
        (prefix + "qvb", (2 * width,), "bias", 1, rate),
        (prefix + "proj", (width, width), "matrix", proj_fan, rate),
        (prefix + "projb", (width,), "bias", 1, rate),
        (prefix + "ln2g", (width,), "gain", 1, rate),
        (prefix + "ln2b", (width,), "bias", 1, rate),
        (prefix + "fc1", (width, hidden), "matrix", width, rate),
        (prefix + "fc1b", (hidden,), "bias", 1, rate),
        (prefix + "fc2", (hidden, width), "matrix", hidden, rate),
        (prefix + "fc2b", (width,), "bias", 1, rate),
    ]


def param_table():
    table = [("patch", (PIX, D), "matrix", PIX, 0.75), ("patchb", (D,), "bias", 1, 0.75)]
    table = table + block_table("enc_", D, FF, D // 4, 0.9)
    table = table + [
        ("encg", (D,), "gain", 1, 1.0),
        ("encb", (D,), "bias", 1, 1.0),
        ("embed", (D, E), "matrix", D, 1.0),
        ("embedb", (E,), "bias", 1, 1.0),
        ("mask", (E,), "token", 1, 1.0),
    ]
    table = table + block_table("dec_", E, DFF, E // 8, 1.0)
    table = table + [
        ("decg", (E,), "gain", 1, 1.0),
        ("decb", (E,), "bias", 1, 1.0),
        ("head", (E, PIX), "matrix", E, 1.0),
        ("headb", (PIX,), "bias", 1, 1.0),
    ]
    return table


MESH = pl.DeviceIdType.MESH
LANES = 128


def layout():
    table = {}
    offset = 0
    for name, shape, kind, fan, rate in param_table():
        table[name] = (offset, shape)
        offset += math.prod(shape)
    return table


class Plan:
    def __init__(self, length, count):
        self.length = length
        self.count = count
        self.outer = count // 16
        self.lines = -(-length // LANES // 8 * 8)
        self.rows = -(-(7 + (2 * LANES - 2 + length) // LANES) // 16) * 16
        self.split = layout()["embed"][0]
        if self.outer > 2:
            self.parts, self.orders = ((0, self.rows),), ("LCB",)
        else:
            units = self.rows // 16
            first, second = round(0.385 * units), round(0.346 * units)
            sizes = (first * 16, second * 16, (units - first - second) * 16)
            self.parts = ((0, sizes[0]), (sizes[0], sizes[1]), (sizes[0] + sizes[1], sizes[2]))
            self.orders = ("LCB", "BLC", "CBL")
        self.first_late = -(-self.split // length)
        self.depths = count // 8
        pieces = 4 if self.outer == 2 else 1
        cuts = [self.rows // 16 * number // pieces * 16 for number in range(pieces + 1)]
        self.halves = tuple((low, high - low) for low, high in zip(cuts, cuts[1:]))
        self.ways = ("CB", "BC", "CB", "BC")[:pieces]
        last = self.first_late - 1
        self.border = (self.base(last) + self.used(last) + 1 + 7) // 8 * 8 + 8
        self.frame_rows = (length * count // LANES + 7) // 8 * 8 + self.rows + 16

    def depths_from(self, name):
        return min(-(-layout()[name][0] // (8 * self.length)), self.depths)

    def late(self, index):
        return index >= self.first_late

    def start(self, index):
        return index * self.length - (64 if self.late(index) else 0)

    def base(self, index):
        return self.start(index) // LANES

    def lead(self, index):
        return self.start(index) % LANES

    def used(self, index):
        return (self.lead(index) + self.length + LANES - 1) // LANES

    def own(self, index):
        start = index * self.length - jnp.where(index >= self.first_late, 64, 0)
        return lax.rem(lax.div(start, LANES), 8), lax.rem(start, LANES)


def spot_of(index):
    return (index // 16, index // 8 % 2, index // 4 % 2, index // 2 % 2, index % 2)


def position():
    chip = lax.axis_index("dp")
    core = lax.axis_index("rep")
    return {"H": chip // 8, "L": chip // 4 % 2, "B": chip // 2 % 2, "C": chip % 2, "r": core}


def index_of(place):
    return (((place["H"] * 2 + place["L"]) * 2 + place["B"]) * 2 + place["C"]) * 2 + place["r"]


def device_of(place):
    return (((place["H"] * 2 + place["L"]) * 2 + place["B"]) * 2 + place["C"], place["r"])


def moved(place, dim, value):
    changed = dict(place)
    changed[dim] = value
    return changed


def flipped(place, dims):
    changed = dict(place)
    for dim in dims:
        changed[dim] = 1 - place[dim]
    return changed


def meet(places):
    barrier = pltpu.get_barrier_semaphore()
    for place in places:
        pl.semaphore_signal(barrier, inc=1, device_id=device_of(place), device_id_type=MESH)
    pl.semaphore_wait(barrier, len(places))


def partners(place, outer):
    digits = "rCBLH" if outer == 2 else "rCBL"
    group = []
    for number in range(1, 1 << len(digits)):
        group.append(flipped(place, [dim for bit, dim in enumerate(digits) if number >> bit & 1]))
    column = []
    if outer > 2:
        column = [moved(place, "H", lax.rem(place["H"] + step, outer)) for step in range(1, outer)]
    return group, column


def at_depth(place, depth):
    return {**place, "H": depth // 2, "L": depth % 2}


def depth_of(place):
    return place["H"] * 2 + place["L"]


def gates(place, plan):
    near = [flipped(place, dims) for dims in ("r", "L", "B", "C", "BC")]
    steps = range(1, plan.outer)
    return near + [moved(place, "H", lax.rem(place["H"] + step, plan.outer)) for step in steps]


def branches(order):
    nodes = []
    for count in range(len(order) + 1):
        for dims in itertools.combinations(order, count):
            reach = max([order.index(dim) for dim in dims], default=-1)
            nodes.append((reach, count, "".join(dims), order[reach + 1 :]))
    nodes.sort(key=lambda node: node[:2])
    return [(dims, onward) for reach, count, dims, onward in nodes]


class Copy:
    def __init__(self, recipe, send, recv, number):
        self.recipe, self.send, self.recv, self.number = recipe, send, recv, number

    def make(self):
        source, target, place = self.recipe()
        return pltpu.make_async_remote_copy(
            src_ref=source,
            dst_ref=target,
            send_sem=self.send.at[self.number],
            recv_sem=self.recv.at[self.number],
            device_id=device_of(place),
            device_id_type=MESH,
        )

    def start(self):
        self.make().start()

    def wait_recv(self):
        self.make().wait_recv()

    def wait_send(self):
        self.make().wait_send()


class Sender:
    def __init__(self, send, recv):
        self.send, self.recv, self.used = send, recv, 0

    def plan(self, recipe):
        copy = Copy(recipe, self.send, self.recv, self.used)
        self.used += 1
        return copy

    def start(self, recipe):
        copy = self.plan(recipe)
        copy.start()
        return copy


def lane_iota(rows):
    return lax.broadcasted_iota(jnp.int32, (rows, LANES), 1)


HUBS = (1, 2)


def others_of(hub):
    return [spot for spot in range(4) if spot != hub]


def hand_over(place, hub, number, pairs, hand, taken):
    other = others_of(hub)[number]
    target = {**place, "B": other // 2, "C": other % 2}
    return [
        pltpu.make_async_remote_copy(
            src_ref=source,
            dst_ref=to,
            send_sem=hand.at[hub - 1, number, kind],
            recv_sem=taken.at[hub - 1, kind],
            device_id=device_of(target),
            device_id_type=MESH,
        )
        for kind, (source, to) in pairs.items()
    ]


class Handing:
    def __init__(self, place, spare, seen_ref, meta_ref, targets_ref, tgt_ref, hand, taken):
        self.place, self.hand, self.taken = place, hand, taken
        self.spot = place["B"] * 2 + place["C"]
        self.refs = (spare, seen_ref, meta_ref, targets_ref, tgt_ref)

    def copies(self, hub, number, kinds):
        spare, seen_ref, meta_ref, targets_ref, tgt_ref = self.refs
        pairs = {
            0: (spare.at[number], seen_ref.at[2 + hub]),
            1: (meta_ref.at[0], meta_ref.at[hub]),
            2: (targets_ref.at[3 + number], tgt_ref.at[hub]),
        }
        pairs = {kind: pairs[kind] for kind in kinds}
        return hand_over(self.place, hub, number, pairs, self.hand, self.taken)

    def on_hub(self, act):
        for hub in HUBS:

            @pl.when(self.spot == hub)
            def _(hub=hub):
                act(hub)

    def start(self, kinds):
        def act(hub):
            for number in range(3):
                for copy in self.copies(hub, number, kinds):
                    copy.start()

        self.on_hub(act)

    def receive(self, kinds):
        for hub in HUBS:

            @pl.when(self.spot != hub)
            def _(hub=hub):
                for copy in self.copies(hub, 0, kinds):
                    copy.wait_recv()

    def finish(self, kinds):
        def act(hub):
            for number in range(3):
                for copy in self.copies(hub, number, kinds):
                    copy.wait_send()

        self.on_hub(act)


def own_block(plan, device, x_ref, line, rolled):
    rows, lines = plan.rows, plan.lines
    skip, lead = plan.own(device)
    line[...] = jnp.zeros_like(line)
    line[pl.ds(0, plan.length)] = x_ref[...]
    turned = pltpu.roll(line[...].reshape(lines, LANES), lead, 1)
    rolled[...] = jnp.zeros_like(rolled)
    rolled[pl.ds(8 + skip, lines), :] = turned
    upper, lower = rolled[pl.ds(8, rows), :], rolled[pl.ds(7, rows), :]
    return jnp.where(lane_iota(rows) >= lead, upper, lower).astype(BRAIN)


class Gather:
    def __init__(self, plan, place, out_ref, sender, columns):
        self.plan, self.place, self.out_ref, self.sender, self.columns = plan, place, out_ref, sender, columns
        self.flights, self.onwards, self.siblings = {}, [], {}

    def region(self, value, part, fixed, free=""):
        start, size = self.plan.parts[part]
        index = [value]
        for dim in "LBC":
            if dim in free:
                index.append(pl.ds(0, 2))
            else:
                index.append(1 - self.place[dim] if dim in fixed else self.place[dim])
        return self.out_ref.at[(*index, self.place["r"], pl.ds(start, size))]

    def column(self, source, part, target):
        send, recv = self.columns
        ref = self.region(source, part, "")
        return pltpu.make_async_remote_copy(
            src_ref=ref,
            dst_ref=ref,
            send_sem=send.at[target, part],
            recv_sem=recv.at[source, part],
            device_id=device_of(moved(self.place, "H", target)),
            device_id_type=MESH,
        )

    def over_column(self, act):
        high = self.place["H"]
        for target in range(self.plan.outer):

            @pl.when(high != target)
            def _(target=target):
                for part in range(len(self.plan.parts)):
                    act(self.column(high, part, target))

    def begin(self):
        self.over_column(lambda copy: copy.start())

    def roots(self, meanwhile):
        plan, place = self.plan, self.place
        copies = {}
        for value in range(plan.outer):
            copies[value] = []
            for part, order in enumerate(plan.orders):
                copies[value].append(self.spread(value, part, "", order) + [self.give(value, part, -1)])

        for value, groups in copies.items():

            @pl.when(place["H"] == value)
            def _(groups=groups):
                for group in groups:
                    for copy in group:
                        copy.start()

        meanwhile()
        for value, groups in copies.items():

            @pl.when(place["H"] != value)
            def _(value=value, groups=groups):
                for part, group in enumerate(groups):
                    self.column(value, part, place["H"]).wait_recv()
                    for copy in group:
                        copy.start()

    def spread(self, value, part, dims, onward):
        def recipe(dim):
            source = self.region(value, part, dims)
            return source, source, flipped(self.place, dim)

        copies = []
        for dim in onward:
            copy = self.sender.plan(functools.partial(recipe, dim))
            self.flights[value, part, frozenset(dims + dim)] = copy
            copies.append(copy)
        self.onwards += copies
        return copies

    def give(self, value, part, reach):
        order = self.plan.orders[part]

        def recipe():
            source = self.region(value, part, order[reach] if reach >= 0 else "", order[: max(reach, 0)])
            return source, source, flipped(self.place, "r")

        copy = self.sender.plan(recipe)
        self.siblings.setdefault(value, []).append(copy)
        return copy

    def stage(self, value, reach):
        plan = self.plan
        trees = []
        for order in plan.orders:
            trees.append([node for node in branches(order) if node[0] and reach == order.index(node[0][-1])])
        for nodes in zip(*trees):
            for part, (dims, onward) in enumerate(nodes):
                self.flights.pop((value, part, frozenset(dims))).wait_recv()
                for copy in self.spread(value, part, dims, onward):
                    copy.start()
        for part in range(len(plan.orders)):
            self.give(value, part, reach).start()

    def ready(self, value):
        for copy in self.siblings[value]:
            copy.wait_recv()

    def close(self):
        self.over_column(lambda copy: copy.wait_send())
        for copies in [self.onwards] + list(self.siblings.values()):
            for copy in copies:
                copy.wait_send()


class Reducer:
    def __init__(self, plan, place, grad_ref, core_in, tree_in, column_in, own_ref, sender, columns):
        self.plan, self.place, self.sender = plan, place, sender
        self.grad_ref, self.core_in, self.tree_in = grad_ref, core_in, tree_in
        self.column_in, self.own_ref, self.columns = column_in, own_ref, columns
        self.cores = {}
        self.pending = []
        self.trees = [branches(order) for order in plan.ways]
        self.flights = {}

    def share(self, value):
        place = self.place

        def recipe(start, size):
            whole = (value, pl.ds(0, 2), pl.ds(0, 2))
            span = pl.ds(start, size)
            return (
                self.grad_ref.at[(*whole, 1 - place["r"], span)],
                self.core_in.at[(*whole, span)],
                flipped(place, "r"),
            )

        for part, (start, size) in enumerate(self.plan.halves):
            copy = self.sender.start(functools.partial(recipe, start, size))
            self.cores[value, part] = copy
            self.pending.append(copy)

    def stage(self, value, reach):
        plan, place = self.plan, self.place
        steps = []
        for part in range(len(plan.halves)):
            order = plan.ways[part]
            nodes = [
                (dims, onward)
                for dims, onward in reversed(self.trees[part])
                if (order.index(dims[-1]) if dims else -1) == reach
            ]
            steps.append([(part, *node) for node in nodes])
        for group in zip(*steps):
            for part, dims, onward in group:
                self.node(value, part, dims, onward)

    def node(self, value, part, dims, onward):
        plan, place = self.plan, self.place
        start, size = plan.halves[part]
        span = pl.ds(start, size)
        if (value, part) in self.cores:
            self.cores.pop((value, part)).wait_recv()
        for dim in onward:
            self.flights.pop((value, part, frozenset(dims + dim))).wait_recv()
        index = [value] + [1 - place[dim] if dim in dims else place[dim] for dim in "BC"]
        total = self.grad_ref[(*index, place["r"], span)].astype(FLOAT)
        total = total + self.core_in[(*index, span)].astype(FLOAT)

        def number(dims):
            return sum(1 << "BC".index(dim) for dim in dims)

        for dim in onward:
            total = total + self.tree_in[value, number(dims + dim), span].astype(FLOAT)

        def spot():
            index = [value] + [1 - place[dim] if dim in dims else place[dim] for dim in "BC"]
            return self.grad_ref.at[(*index, place["r"], span)]

        def recipe():
            return spot(), self.tree_in.at[value, number(dims), span], flipped(place, dims[-1])

        if dims:
            spot()[...] = total.astype(BRAIN)
            copy = self.sender.start(recipe)
            self.flights[value, part, frozenset(dims)] = copy
            self.pending.append(copy)
            return
        depth = depth_of(place)

        @pl.when(depth == value)
        def _():
            self.own_ref[span, :] = total

        @pl.when(depth != value)
        def _():
            spot()[...] = total.astype(BRAIN)
            self.column(value, part).start()

    def column(self, value, part):
        plan, place = self.plan, self.place
        start, size = plan.halves[part]
        send, recv = self.columns
        index = (value, place["B"], place["C"], place["r"], pl.ds(start, size))
        return pltpu.make_async_remote_copy(
            src_ref=self.grad_ref.at[index],
            dst_ref=self.column_in.at[depth_of(place), pl.ds(start, size)],
            send_sem=send.at[value, part],
            recv_sem=recv.at[depth_of(place), part],
            device_id=device_of(at_depth(place, value)),
            device_id_type=MESH,
        )

    def arrival(self, source, part):
        plan, place = self.plan, self.place
        start, size = plan.halves[part]
        send, recv = self.columns
        return pltpu.make_async_remote_copy(
            src_ref=self.own_in(part),
            dst_ref=self.column_in.at[source, pl.ds(start, size)],
            send_sem=send.at[source, part],
            recv_sem=recv.at[source, part],
            device_id=device_of(at_depth(place, source)),
            device_id_type=MESH,
        )

    def own_in(self, part):
        place = self.place
        start, size = self.plan.halves[part]
        index = (0, place["B"], place["C"], place["r"], pl.ds(start, size))
        return self.grad_ref.at[index]

    def finish(self):
        plan, place = self.plan, self.place
        for part, (start, size) in enumerate(plan.halves):
            for source in range(plan.depths):

                @pl.when(depth_of(place) != source)
                def _(part=part, source=source, start=start, size=size):
                    self.arrival(source, part).wait_recv()
                    span = pl.ds(start, size)
                    self.own_ref[span, :] += self.column_in[source, span].astype(FLOAT)

    def close(self):
        plan, place = self.plan, self.place
        for copy in self.pending:
            copy.wait_send()
        for part in range(len(plan.halves)):
            for value in range(plan.depths):

                @pl.when(depth_of(place) != value)
                def _(part=part, value=value):
                    self.column(value, part).wait_send()


def finish_body(plan, place, held_ref, loss_ref, own_ref, total_out, turned, near, far, mine, sender):
    outer, rows, lines = plan.outer, plan.rows, plan.lines
    group, column = partners(place, outer)
    skip, lead = plan.own(index_of(place))
    position_in = lax.broadcasted_iota(jnp.int32, (lines, LANES), 0) * LANES + lane_iota(lines)
    shift = lax.rem(LANES - lead, LANES)
    turned[pl.ds(0, rows), :] = pltpu.roll(own_ref[...], shift, 1)
    here, below = turned[pl.ds(skip, lines), :], turned[pl.ds(skip + 1, lines), :]
    total = jnp.where(lane_iota(lines) < LANES - lead, here, below)
    total = jnp.where(position_in < plan.length, total, 0.0)
    squares = jnp.sum(total * total)
    lane = lane_iota(8)
    stats = jnp.where(lane == 0, squares, 0.0)
    stats = jnp.where(lane == 1, held_ref[0, 0].astype(FLOAT), stats)
    mine[0] = jnp.where(lane == 2, loss_ref[0], stats)
    count = len(group) + 1
    spot = lax.rem(index_of(place), count)
    near[spot] = mine[0]
    nears = [
        sender.start(functools.partial(lambda other: (mine.at[0], near.at[spot], other), other))
        for other in group
    ]
    total_out[pl.ds(0, lines), :] = total
    for copy in nears:
        copy.wait_recv()
    together = near[0]
    for other in range(1, count):
        together = together + near[other]
    fars = []
    whole = together
    if column:
        far[place["H"]] = together
        mine[1] = together
        fars = [
            sender.start(functools.partial(lambda other: (mine.at[1], far.at[place["H"]], other), other))
            for other in column
        ]
        for copy in fars:
            copy.wait_recv()
        whole = far[0]
        for other in range(1, outer):
            whole = whole + far[other]
    row = whole[0:1, :]
    lane = lane[0:1]

    def across(number):
        return jnp.full((1, LANES), jnp.sum(jnp.where(lane == number, row, 0.0)))

    weights = across(1) * (0.1 * VIS + (NP - VIS))
    total_out[pl.ds(lines, 1), :] = across(2) / weights
    total_out[pl.ds(lines + 1, 1), :] = jnp.sqrt(across(0)) / weights
    total_out[pl.ds(lines + 2, 1), :] = weights
    return nears + fars


def in_segments(index, segments):
    inside = None
    for start, stop in segments:
        here = (index >= start) & (index < stop)
        inside = here if inside is None else inside | here
    return inside


def matrix_segments():
    found = []
    for name, shape, kind, fan, rate in param_table():
        if kind == "matrix":
            start = layout()[name][0]
            found.append((start, start + math.prod(shape)))
    return found


def update_body(
    plan, step_ref, total_ref, master_ref, first_ref, second_ref,
    master_out, first_out, second_out, copy_out, loss_out, norm_out, line
):
    rows, length = plan.lines, plan.length
    device = lax.axis_index("dp") * 2 + lax.axis_index("rep")
    position_in = lax.broadcasted_iota(jnp.int32, (rows, LANES), 0) * LANES + lane_iota(rows)
    flat = position_in + device * length
    table = layout()
    early, late = table["enc_ln1g"][0], table["encg"][0]
    rate_part = jnp.where(flat < early, 0.75, jnp.where(flat < late, 0.9, 1.0))
    decay_part = jnp.where(in_segments(flat, matrix_segments()), DECAY, 0.0)
    line[...] = jnp.zeros_like(line)
    line[pl.ds(0, length)] = master_ref[...]
    master = line[...].reshape(rows, LANES)
    line[pl.ds(0, length)] = first_ref[...]
    first = line[...].reshape(rows, LANES)
    line[pl.ds(0, length)] = second_ref[...]
    second = line[...].reshape(rows, LANES)
    norms = total_ref[pl.ds(rows + 1, 1), :]
    loss_out[0, 0] = jnp.max(total_ref[pl.ds(rows, 1), :])
    norm_out[0, 0] = jnp.max(norms)
    gradient = total_ref[pl.ds(0, rows), :] / total_ref[pl.ds(rows + 2, 1), :]
    clipped = gradient * jnp.minimum(1.0, CLIP / norms)
    fade = 1.0 / jnp.full((1, LANES), lax.shift_left(1, step_ref[0]).astype(FLOAT))
    new_first = BETA_ONE * first + (1.0 - BETA_ONE) * clipped
    new_second = BETA_TWO * second + (1.0 - BETA_TWO) * clipped * clipped
    first_hat = new_first / (1.0 - fade)
    second_hat = new_second / (1.0 - fade)
    new_master = master - LEARN * rate_part * (
        first_hat / (jnp.sqrt(second_hat) + EPSILON) + decay_part * master
    )
    master_out[...] = new_master.reshape(rows * LANES)[:length]
    first_out[...] = new_first.reshape(rows * LANES)[:length]
    second_out[...] = new_second.reshape(rows * LANES)[:length]
    copy_out[...] = new_master.reshape(rows * LANES)[:length].astype(BRAIN)


def update(step, total, master, first, second, plan):
    vmem = pl.BlockSpec(memory_space=pltpu.VMEM)
    smem = pl.BlockSpec(memory_space=pltpu.SMEM)
    flat = jax.ShapeDtypeStruct((plan.length,), FLOAT)
    single = jax.ShapeDtypeStruct((1, 1), FLOAT)
    return pl.pallas_call(
        functools.partial(update_body, plan),
        out_shape=(flat, flat, flat, jax.ShapeDtypeStruct((plan.length,), BRAIN), single, single),
        in_specs=[smem, vmem, vmem, vmem, vmem],
        out_specs=(vmem, vmem, vmem, vmem, smem, smem),
        scratch_shapes=[pltpu.VMEM((plan.lines * LANES,), FLOAT)],
        compiler_params=pltpu.CompilerParams(vmem_limit_bytes=16 << 20),
    )(step, total, master, first, second)


class Frames:
    def __init__(self, plan, slots, even, odd):
        self.plan, self.slots, self.even, self.odd = plan, slots, even, odd
        self.filled = 0

    def add(self, index):
        plan, even = self.plan, self.even
        if index == plan.first_late:
            rest = plan.border - self.filled
            even[pl.ds(self.filled, rest), :] = jnp.zeros((rest, LANES), FLOAT)
            half_turn(plan, even, self.odd)
            self.filled = plan.border
        frame = self.odd if plan.late(index) else even
        start = plan.base(index) // 8 * 8
        rows = -(-(plan.base(index) - start + plan.used(index)) // 8) * 8
        block = self.slots[(*spot_of(index), pl.ds(0, plan.rows))].astype(FLOAT)
        if start < self.filled:
            frame[pl.ds(start, 8), :] += block[:8]
            frame[pl.ds(start + 8, rows - 8), :] = block[8:rows]
        else:
            frame[pl.ds(start, rows), :] = block[:rows]
        self.filled = start + rows


def half_turn(plan, even, odd):
    total = plan.border - 8
    span = 256

    def turn(start, rows):
        here = pltpu.roll(even[pl.ds(start, rows), :], 64, 1)
        below = pltpu.roll(even[pl.ds(start + 1, rows), :], 64, 1)
        odd[pl.ds(start, rows), :] = jnp.where(lane_iota(rows) < 64, here, below)

    @pl.loop(0, total // span)
    def _(step):
        turn(pl.multiple_of(step * span, span), span)

    if total % span:
        turn(total // span * span, total % span)


def read_param(even, odd, name, target):
    offset, shape = layout()[name]
    rows, width = (1, shape[0]) if len(shape) == 1 else shape
    base, late = divmod(offset, LANES)
    frames = (even, odd) if late == 0 else (odd, even)
    whole, half = divmod(width, LANES)
    kind = target.dtype
    if rows == 1:
        for col in range(whole):
            target[:, pl.ds(col * LANES, LANES)] = frames[0][pl.ds(base + col, 1), :].astype(kind)
        if half:
            tail = frames[0][pl.ds(base + whole, 1), :]
            target[:, pl.ds(whole * LANES, half)] = tail[:, :half].astype(kind)
        return
    if not half:
        for col in range(whole):
            piece = frames[0][pl.ds(base + col, rows, stride=whole), :]
            target[:, pl.ds(col * LANES, LANES)] = piece.astype(kind)
        return
    stride = 2 * width // LANES
    shift = whole + (1 if late else 0)

    def interleave(scratch):
        for col in range(whole + 1):
            size = LANES if col < whole else half
            upper = frames[0][pl.ds(base + col, rows // 2, stride=stride), :]
            lower = frames[1][pl.ds(base + shift + col, rows // 2, stride=stride), :]
            scratch[pl.ds(0, rows // 2, stride=2), :] = upper
            scratch[pl.ds(1, rows // 2, stride=2), :] = lower
            target[:, pl.ds(col * LANES, size)] = scratch[...][:, :size].astype(kind)

    pl.run_scoped(interleave, pltpu.VMEM((rows, LANES), FLOAT))


def write_grad(even, odd, name, value):
    offset, shape = layout()[name]
    rows, width = (1, shape[0]) if len(shape) == 1 else shape
    base, late = divmod(offset, LANES)
    frames = (even, odd) if late == 0 else (odd, even)
    whole, half = divmod(width, LANES)

    def columns():
        for col in range(0, whole, 2):
            size = min(2, whole - col) * LANES
            both = value(col * LANES, size)
            for part in range(size // LANES):
                yield col + part, both[:, part * LANES : (part + 1) * LANES]
        if half:
            tail = value(whole * LANES, half)
            yield whole, jnp.concatenate([tail, jnp.zeros((rows, LANES - half), FLOAT)], axis=1)

    if rows == 1:
        for col, piece in columns():
            frames[0][pl.ds(base + col, 1), :] = piece
        return
    if not half:
        for col, piece in columns():
            frames[0][pl.ds(base + col, rows, stride=whole), :] = piece
        return
    stride = 2 * width // LANES
    shift = whole + (1 if late else 0)

    def interleave(scratch):
        for col, piece in columns():
            scratch[...] = piece
            upper = scratch[pl.ds(0, rows // 2, stride=2), :]
            lower = scratch[pl.ds(1, rows // 2, stride=2), :]
            frames[0][pl.ds(base + col, rows // 2, stride=stride), :] = upper
            frames[1][pl.ds(base + shift + col, rows // 2, stride=stride), :] = lower

    pl.run_scoped(interleave, pltpu.VMEM((rows, LANES), FLOAT))


def clear_frames(plan, even, odd):
    even[...] = jnp.zeros_like(even)
    odd[pl.ds(0, plan.border + 16), :] = jnp.zeros((plan.border + 16, LANES), FLOAT)
    table = layout()
    final = (table["headb"][0] // LANES) // 8 * 8
    odd[pl.ds(final, odd.shape[0] - final), :] = jnp.zeros((odd.shape[0] - final, LANES), FLOAT)


def emit_slots(plan, even, odd, slots, depths):
    rows = plan.rows
    for index in [depth * 8 + number for depth in depths for number in range(8)]:
        start = plan.base(index) // 8 * 8
        if plan.late(index):
            block = odd[pl.ds(start + 8, rows), :]
        else:
            here = pltpu.roll(odd[pl.ds(start + 8, rows), :], 64, 1)
            above = pltpu.roll(odd[pl.ds(start + 7, rows), :], 64, 1)
            block = even[pl.ds(start, rows), :] + jnp.where(lane_iota(rows) < 64, above, here)
        slots[(index // 8, index // 4 % 2, index // 2 % 2, index % 2)] = block.astype(BRAIN)


def dot(left, right, dims=(((1,), (0,)), ((), ()))):
    return lax.dot_general(left, right, dims, preferred_element_type=FLOAT)


def place_table(count, rows, width):
    quarter = width // 4
    omega = 1.0 / 10000.0 ** (np.arange(quarter) / quarter)
    index = np.arange(count)
    across = (index // GRID)[:, None] * omega
    along = (index % GRID)[:, None] * omega
    table = np.zeros((rows, width), np.float32)
    table[:count] = np.concatenate(
        [np.sin(across), np.cos(across), np.sin(along), np.cos(along)], axis=-1
    )
    return table


def split_two(value):
    upper = value.astype(BRAIN)
    return upper, (value - upper.astype(FLOAT)).astype(BRAIN)


def norm_parts(value):
    center = value - jnp.mean(value, axis=-1, keepdims=True)
    spread = lax.rsqrt(jnp.mean(center * center, axis=-1, keepdims=True) + LN_EPS)
    return center * spread, spread


def norm_back(grad, value, gain):
    unit, spread = norm_parts(value)
    d_gain = jnp.sum(grad * unit, axis=0, keepdims=True)
    d_shift = jnp.sum(grad, axis=0, keepdims=True)
    scaled = grad * gain
    middle = jnp.mean(scaled, axis=-1, keepdims=True)
    along = jnp.mean(scaled * unit, axis=-1, keepdims=True)
    return spread * (scaled - middle - unit * along), d_gain, d_shift


def gelu_parts(value):
    half = 0.5 + 0.5 * lax.erf(value * 0.7071067811865476)
    bell = jnp.exp2(value * value * (-0.5 * LOG_TWO_E)) * 0.3989422804014327
    return value * half, half + value * bell


def head_only(value, head, size):
    lane = lax.broadcasted_iota(jnp.int32, value.shape, 1)
    inside = (lane >= head * size) & (lane < (head + 1) * size)
    return jnp.where(inside, value, jnp.zeros_like(value))


def attend(t_ref, chance_ref, stack_ref, usable, width, heads):
    size = width // heads
    rows = t_ref.shape[0]
    query, keys = t_ref[:, pl.ds(0, width)].T, t_ref[:, pl.ds(width, width)]
    values = t_ref[:, pl.ds(2 * width, width)].T
    factor = size ** (-0.5) * LOG_TWO_E
    mixed = []
    for head in range(heads):
        stack_ref[pl.ds(head * rows, rows), :] = head_only(keys, head, size)
    scores = dot(stack_ref[...], query)
    for head in range(heads):
        raw = jnp.where(usable, scores[head * rows : (head + 1) * rows], -1e30)
        top = jnp.max(raw, axis=0, keepdims=True)
        power = jnp.exp2((raw - top) * factor)
        chance = power * (1.0 / jnp.sum(power, axis=0, keepdims=True))
        chance_ref[head] = chance
        mixed.append(dot(values[head * size : (head + 1) * size], chance.astype(BRAIN)))
    return jnp.concatenate(mixed, axis=0).astype(BRAIN).T


def attend_back(d_mixed, t_ref, dt_ref, chance_ref, stack_ref, width, heads):
    size = width // heads
    rows = t_ref.shape[0]
    scale = size ** (-0.5)
    query, keys = t_ref[:, pl.ds(0, width)], t_ref[:, pl.ds(width, width)].T
    values = t_ref[:, pl.ds(2 * width, width)]
    d_query = []
    d_keys = d_values = None
    for head in range(heads):
        stack_ref[pl.ds(head * rows, rows), :] = head_only(values, head, size)
    d_chances = dot(stack_ref[...], d_mixed.T)
    for head in range(heads):
        chance = chance_ref[head]
        d_chance = d_chances[head * rows : (head + 1) * rows]
        along = jnp.sum(chance * d_chance, axis=0, keepdims=True)
        d_scores = (chance * (d_chance - along)).astype(BRAIN)
        part = dot(chance.astype(BRAIN), head_only(d_mixed, head, size))
        d_values = part if d_values is None else d_values + part
        part = dot(d_scores, head_only(query, head, size))
        d_keys = part if d_keys is None else d_keys + part
        d_query.append(dot(keys[head * size : (head + 1) * size], d_scores))
    d_query = (jnp.concatenate(d_query, axis=0) * scale).astype(BRAIN).T
    dt_ref[:, pl.ds(0, width)] = d_query
    dt_ref[:, pl.ds(width, width)] = (d_keys * scale).astype(BRAIN)
    dt_ref[:, pl.ds(2 * width, width)] = d_values.astype(BRAIN)


class Weights:
    def __init__(self, refs):
        self.refs = dict(zip(layout(), refs))

    def __call__(self, name):
        return self.refs[name][...]


def block_open(hidden, keep, weights, prefix):
    width = hidden.shape[1]
    keep["x"][...] = hidden
    unit, unused = norm_parts(hidden)
    normed = (unit * weights(prefix + "ln1g") + weights(prefix + "ln1b")).astype(BRAIN)
    keep["a"][...] = normed
    bias = weights(prefix + "qvb")
    for part in range(3):
        cols = pl.ds(part * width, width)
        value = dot(normed, weights.refs[prefix + "qkv"][:, cols])
        if part != 1:
            value = value + bias[:, (part // 2) * width : (part // 2 + 1) * width]
        keep["t"][:, cols] = value.astype(BRAIN)


def block_middle(hidden, keep, weights, prefix, heads, usable):
    width = hidden.shape[1]
    mixed = attend(keep["t"], keep["p"], keep["k"], usable, width, heads)
    keep["o"][...] = mixed
    middle = hidden + (dot(mixed, weights(prefix + "proj")) + weights(prefix + "projb"))
    keep["m"][...] = middle
    unit, unused = norm_parts(middle)
    second = (unit * weights(prefix + "ln2g") + weights(prefix + "ln2b")).astype(BRAIN)
    keep["b"][...] = second
    inner = dot(second, weights(prefix + "fc1")) + weights(prefix + "fc1b")
    active, slope = gelu_parts(inner)
    keep["s"][...] = slope
    keep["g"][...] = active.astype(BRAIN)


def block_shut(keep, weights, prefix):
    return keep["m"][...] + (dot(keep["g"][...], weights(prefix + "fc2")) + weights(prefix + "fc2b"))


def home_open(grad, keep, weights, prefix):
    d_branch = grad.astype(BRAIN)
    keep["dz"][...] = d_branch
    keep["du"][...] = (dot(d_branch, weights(prefix + "fc2"), PAIR) * keep["s"][...]).astype(BRAIN)


def home_middle(grad, keep, weights, prefix, heads, sums):
    width = grad.shape[1]
    d_second = dot(keep["du"][...], weights(prefix + "fc1"), PAIR)
    d_middle, d_gain, d_shift = norm_back(d_second, keep["m"][...], weights(prefix + "ln2g"))
    sums(prefix + "ln2g", d_gain)
    sums(prefix + "ln2b", d_shift)
    d_middle = d_middle + grad
    d_output = d_middle.astype(BRAIN)
    keep["dy"][...] = d_output
    d_mixed = dot(d_output, weights(prefix + "proj"), PAIR).astype(BRAIN)
    attend_back(d_mixed, keep["t"], keep["dt"], keep["p"], keep["k"], width, heads)
    d_normed = dot(keep["dt"][...], weights(prefix + "qkv"), PAIR)
    d_hidden, d_gain, d_shift = norm_back(d_normed, keep["x"][...], weights(prefix + "ln1g"))
    sums(prefix + "ln1g", d_gain)
    sums(prefix + "ln1b", d_shift)
    return d_middle + d_hidden


def kept_shapes(rows, width, hidden, heads):
    return {
        "x": ((rows, width), FLOAT),
        "a": ((rows, width), BRAIN),
        "t": ((rows, 3 * width), BRAIN),
        "p": ((heads, rows, rows), FLOAT),
        "k": ((heads * rows, width), BRAIN),
        "o": ((rows, width), BRAIN),
        "m": ((rows, width), FLOAT),
        "b": ((rows, width), BRAIN),
        "s": ((rows, hidden), FLOAT),
        "g": ((rows, hidden), BRAIN),
        "dz": ((rows, width), BRAIN),
        "du": ((rows, hidden), BRAIN),
        "dy": ((rows, width), BRAIN),
        "dt": ((rows, 3 * width), BRAIN),
    }


def kept_scratch(count, *sizes):
    lead = (count,) if count else ()
    return [
        pltpu.VMEM(shape if name == "k" else lead + shape, kind)
        for name, (shape, kind) in kept_shapes(*sizes).items()
    ]


def kept_view(refs, image=None):
    names = kept_shapes(1, 1, 1, 1)
    return {
        name: ref if image is None or name == "k" else ref.at[image] for name, ref in zip(names, refs)
    }


LAYERS = {
    "fc2": ("g", "dz", "fc2b"),
    "fc1": ("b", "du", "fc1b"),
    "proj": ("o", "dy", "projb"),
    "qkv": ("a", "dt", "qvb"),
}


def block_grads(keep, prefix, names, emit):
    def rows_of(name):
        value = keep[name][...]
        return value.reshape(-1, value.shape[-1])

    for name in names:
        left, right, bias = LAYERS[name]
        emit(prefix + name, prefix + bias, rows_of(left), rows_of(right))


NORMS = ("ln1g", "ln1b", "ln2g", "ln2b", "encg", "encb", "decg", "decb", "mask")


class Images:
    def __init__(self, place, counts_ref, meta_ref):
        spot = place["B"] * 2 + place["C"]
        self.meta_ref = meta_ref
        self.own = counts_ref[0, 0]
        lane = lane_iota(8)
        row = lax.broadcasted_iota(jnp.int32, (8, LANES), 0)

        def count_of(hub):
            corner = jnp.where((lane == LANES - 1) & (row == 0), meta_ref[hub], 0.0)
            return jnp.sum(corner).astype(jnp.int32)

        one, two = count_of(1), count_of(2)
        from_one = jnp.where(spot == 0, 3, jnp.where(spot == 2, 4, 5))
        from_two = jnp.where(spot == 0, 3, jnp.where(spot == 1, 4, 5))
        use_one = (spot == 2) | ((spot != 1) & (one > 2))
        mine = self.own > 2

        def choose(own, first, second):
            return jnp.where(mine, own, jnp.where(use_one, first, second))

        self.third = choose(2, 3, 4)
        self.third_row = choose(2, from_one, from_two)
        self.third_count = choose(self.own, one, two)
        self.third_meta = choose(0, 1, 2)

    def __call__(self, image):
        last = image == 2
        source = jnp.where(last, self.third, image)
        line = jnp.where(last, self.third_row, image)
        live = jnp.where(last, self.third_count, self.own) > line
        kept = self.meta_ref[jnp.where(last, self.third_meta, 0), pl.ds(line, 1), :][:, :HOME]
        return source, kept, live.astype(FLOAT)


def placement(kept, rows):
    number = lax.broadcasted_iota(jnp.int32, (rows, HOME), 0).astype(FLOAT)
    return (number == kept).astype(FLOAT)


def whole_body(
    plan, counts_ref, keep_ref, x_ref, patches_ref, targets_ref, enc_table, dec_table,
    total_out, *scratch
):
    scratch = list(scratch)

    def take(count):
        taken = scratch[:count]
        del scratch[:count]
        return taken

    names = list(layout())
    slots, seen_ref, tgt_own, tgt_ref, wanted, meta_ref, grad_ref, loss_ref = take(8)
    spot_enc, spot_dec, local = take(3)
    line, rolled, pixels, spare, send, recv, hand, taken = take(8)
    even, odd, sums_ref, y_hi, y_lo, dy_home, final_all, dpred_all, d_out = take(9)
    weights = Weights(take(len(names)))
    enc_refs, dec_refs = take(14), take(14)
    core_in, tree_in, column_in, own_ref, turned, near, far, mine = take(8)
    spread_send, spread_recv, column_send, column_recv = take(4)

    place = position()
    device = index_of(place)
    copies = [
        pltpu.make_async_copy(patches_ref, pixels, local.at[0]),
        pltpu.make_async_copy(enc_table, spot_enc, local.at[1]),
        pltpu.make_async_copy(dec_table, spot_dec, local.at[2]),
        pltpu.make_async_copy(
            targets_ref.at[pl.ds(0, LIVE_CAP - 1)], tgt_own, local.at[3]
        ),
        pltpu.make_async_copy(targets_ref.at[LIVE_CAP - 1], tgt_ref.at[0], local.at[4]),
    ]
    for copy in copies:
        copy.start()
    slots[(place["H"], place["L"], place["B"], place["C"], place["r"])] = own_block(
        plan, device, x_ref, line, rolled
    )
    meet(gates(place, plan))
    sender = Sender(send, recv)
    handing = Handing(place, spare, seen_ref, meta_ref, targets_ref, tgt_ref, hand, taken)

    def choose_images():
        lane = lane_iota(8)
        row = lax.broadcasted_iota(jnp.int32, (8, LANES), 0)
        held = counts_ref[0, 0].astype(FLOAT)
        meta_ref[0] = jnp.where((lane == LANES - 1) & (row == 0), held, -1.0)
        meta_ref[0, pl.ds(0, keep_ref.shape[0]), pl.ds(0, VIS)] = keep_ref[...].astype(FLOAT)
        copies[0].wait()

        def visible(image):
            where = placement(meta_ref[0, pl.ds(image, 1), :][:, :HOME], NP).astype(BRAIN)
            return dot(where, pixels[image], DEEP).astype(BRAIN)

        def prepare(hub):
            for number in range(3):
                spare[number] = visible(3 + number)

        handing.on_hub(prepare)
        handing.start((0, 1))
        for image in range(LIVE_CAP):
            seen_ref[image] = visible(image)

    early = min(-(-layout()["dec_qkv"][0] // (16 * plan.length)), plan.outer)
    first_values, last_values = range(early), range(early, plan.outer)
    gather = Gather(plan, place, slots, sender, (spread_send, spread_recv))
    frames = Frames(plan, slots, even, odd)

    def spread(values, reach):
        for value in values:
            gather.stage(value, reach)

    def fetch(values, wanted_names):
        for value in values:
            gather.ready(value)
            for index in range(value * 16, value * 16 + 16):
                frames.add(index)
        for name in wanted_names:
            read_param(even, odd, name, weights.refs[name])

    gather.begin()
    gather.roots(choose_images)
    for reach in (0, 1):
        spread(first_values, reach)
        spread(last_values, reach)
    spread(first_values, 2)
    divide = names.index("dec_qkv")
    fetch(first_values, names[:divide])
    handing.receive((0, 1))
    for copy in copies[1:]:
        copy.wait()
    sums_ref[...] = jnp.zeros_like(sums_ref)
    order = {name: number for number, name in enumerate(names)}

    def add_sum(name, value):
        sums_ref[pl.ds(order[name], 1), pl.ds(0, value.shape[1])] += value

    pick = Images(place, counts_ref, meta_ref)

    visible, begin = [], []
    for image in range(LIVE_CAP):
        source, kept, live = pick(image)
        where = placement(kept, ROWS).astype(BRAIN)
        visible.append(seen_ref[source])
        begin.append(dot(where, spot_enc[0], DEEP) + dot(where, spot_enc[1], DEEP))
    visible = jnp.concatenate(visible, axis=0)
    begin = jnp.concatenate(begin, axis=0)
    enc_rows = LIVE_CAP * HOME
    enc = kept_view(enc_refs)
    down = lax.broadcasted_iota(jnp.int32, (enc_rows, enc_rows), 0)
    over = lax.broadcasted_iota(jnp.int32, (enc_rows, enc_rows), 1)
    usable = (down // HOME == over // HOME) & (down % HOME < VIS)
    first_in = dot(visible, weights("patch")) + weights("patchb") + begin
    block_open(first_in, enc, weights, "enc_")
    block_middle(first_in, enc, weights, "enc_", HEADS, usable)
    encoded = block_shut(enc, weights, "enc_")
    unit, unused = norm_parts(encoded)
    encoder_out = (unit * weights("encg") + weights("encb")).astype(BRAIN)
    embedded = dot(encoder_out, weights("embed")) + weights("embedb")
    upper, lower = split_two(embedded)
    for image in range(LIVE_CAP):
        y_hi[image] = upper[image * HOME : (image + 1) * HOME]
        y_lo[image] = lower[image * HOME : (image + 1) * HOME]
    spread(last_values, 2)
    handing.start((2,))
    fetch(last_values, names[divide:])
    clear_frames(plan, even, odd)
    view = odd.at[pl.ds(8, plan.frame_rows)]
    real = lax.broadcasted_iota(jnp.int32, (ROWS, 1), 0) < NP
    usable_dec = lax.broadcasted_iota(jnp.int32, (ROWS, ROWS), 0) < NP

    def seen_of(kept):
        where = placement(kept, ROWS)
        return where.astype(BRAIN), jnp.sum(where, axis=1, keepdims=True)

    @pl.loop(0, LIVE_CAP)
    def _(image):
        source, kept, live = pick(image)
        where, seen = seen_of(kept)
        grid_in = dot(where, y_hi[image]) + dot(where, y_lo[image])
        grid_in = grid_in + (1.0 - seen) * weights("mask") + spot_dec[...]
        keep = kept_view(dec_refs, image)
        block_open(grid_in, keep, weights, "dec_")
        block_middle(grid_in, keep, weights, "dec_", DHEADS, usable_dec)


    def one_image(image, total):
        source, kept, live = pick(image)
        where, seen = seen_of(kept)
        keep = kept_view(dec_refs, image)
        decoded = block_shut(keep, weights, "dec_")
        unit, unused = norm_parts(decoded)
        final = (unit * weights("decg") + weights("decb")).astype(BRAIN)
        final_all[image] = final
        predicted = dot(final, weights("head")) + weights("headb")
        weight = jnp.where(real, (1.0 - 0.9 * seen) * live, 0.0)

        @pl.when(image == LIVE_CAP - 1)
        def _():
            handing.receive((2,))
            wanted[...] = tgt_ref[pick.third - 2]

        @pl.when(image < LIVE_CAP - 1)
        def _():
            wanted[...] = tgt_own[image]

        error = predicted[:NP] - wanted[...].astype(FLOAT)
        weighted = error * weight[:NP]
        total = total + jnp.sum(weighted * error, axis=0, keepdims=True)
        dpred_all[image, pl.ds(0, NP)] = (weighted * (2.0 / PIX)).astype(BRAIN)
        dpred_all[image, pl.ds(NP, ROWS - NP)] = jnp.zeros((ROWS - NP, PIX), BRAIN)
        d_final = dot(dpred_all[image], weights("head"), PAIR)
        d_decoded, d_gain, d_shift = norm_back(d_final, decoded, weights("decg"))
        add_sum("decg", d_gain)
        add_sum("decb", d_shift)
        d_out[image] = d_decoded
        home_open(d_decoded, keep, weights, "dec_")
        return total

    total = lax.fori_loop(0, LIVE_CAP, one_image, jnp.zeros((1, PIX), FLOAT))
    loss_ref[0] = jnp.sum(total) * (1.0 / PIX)

    def emit(name, bias, left, right):
        ones = jnp.ones((16, right.shape[0]), BRAIN)
        summed = dot(ones, right)[0:1]
        if bias.endswith("qvb"):
            width = summed.shape[1] // 3
            summed = jnp.concatenate([summed[:, :width], summed[:, 2 * width :]], axis=1)
        write_grad(even, view, bias, lambda start, size: summed[:, start : start + size])
        turned = left.T
        write_grad(even, view, name, lambda start, size: dot(turned, right[:, start : start + size]))

    def emit_norms(wanted_names):
        for name in wanted_names:
            row = pl.ds(order[name], 1)
            write_grad(even, view, name, lambda start, size, row=row: sums_ref[row, pl.ds(start, size)])

    reducer = Reducer(
        plan, place, grad_ref, core_in, tree_in, column_in, own_ref, sender, (column_send, column_recv)
    )
    floors = [plan.depths_from(name) for name in ("dec_fc2", "embed", "enc_fc1")]
    waves = [range(low, high) for low, high in zip(floors + [0], [plan.depths] + floors)]

    def leave(wave):
        emit_slots(plan, even, odd, grad_ref, waves[wave])
        for depth in waves[wave]:
            reducer.share(depth)

    def collect(wave, reach):
        for depth in waves[wave]:
            reducer.stage(depth, reach)

    dec = kept_view(dec_refs)
    emit("head", "headb", final_all[...].reshape(-1, E), dpred_all[...].reshape(-1, PIX))
    block_grads(dec, "dec_", ("fc2",), emit)
    emit_norms(("decg", "decb"))
    leave(0)
    block_grads(dec, "dec_", ("fc1",), emit)

    @pl.loop(0, LIVE_CAP)
    def _(image):
        @pl.when(image == 1)
        def _():
            collect(0, 1)

        @pl.when(image == 2)
        def _():
            collect(0, 0)

        source, kept, live = pick(image)
        where, seen = seen_of(kept)
        d_grid = home_middle(
            d_out[image], kept_view(dec_refs, image), weights, "dec_", DHEADS, add_sum
        )
        add_sum("mask", jnp.sum((1.0 - seen) * d_grid, axis=0, keepdims=True))
        dy_home[image] = dot(where, d_grid.astype(BRAIN), DEEP).astype(BRAIN)

    collect(0, -1)
    block_grads(dec, "dec_", ("proj", "qkv"), emit)
    d_embedded = dy_home[...].reshape(enc_rows, E)
    emit("embed", "embedb", encoder_out, d_embedded)
    emit_norms(("mask", "dec_ln1g", "dec_ln1b", "dec_ln2g", "dec_ln2b"))
    leave(1)

    d_seen = dot(d_embedded, weights("embed"), PAIR).astype(BRAIN).astype(FLOAT)
    d_encoded, d_gain, d_shift = norm_back(d_seen, encoded, weights("encg"))
    add_sum("encg", d_gain)
    add_sum("encb", d_shift)
    home_open(d_encoded, enc, weights, "enc_")
    block_grads(enc, "enc_", ("fc2", "fc1"), emit)
    emit_norms(("encg", "encb"))
    leave(2)
    collect(1, 1)
    d_first = home_middle(d_encoded, enc, weights, "enc_", HEADS, add_sum).astype(BRAIN)
    collect(2, 1)
    collect(1, 0)
    emit("patch", "patchb", visible, d_first)
    block_grads(enc, "enc_", ("proj", "qkv"), emit)
    emit_norms(("enc_ln1g", "enc_ln1b", "enc_ln2g", "enc_ln2b"))
    leave(3)
    collect(2, 0)
    collect(1, -1)
    collect(3, 1)
    collect(2, -1)
    collect(3, 0)
    collect(3, -1)
    reducer.finish()
    pending = finish_body(
        plan, place, counts_ref, loss_ref, own_ref, total_out, turned, near, far, mine, sender
    )
    gather.close()
    reducer.close()
    handing.finish((0, 1, 2))
    for copy in pending:
        copy.wait_send()


def weight_scratch():
    shapes = []
    for name, (offset, shape) in layout().items():
        if len(shape) == 1:
            shapes.append(pltpu.VMEM((1, *shape), FLOAT))
        else:
            shapes.append(pltpu.VMEM(shape, BRAIN))
    return shapes


def copies_used(plan):
    spread = len(plan.parts) * plan.outer * (7 + 4)
    home = len(plan.halves) * plan.depths * (1 + 3)
    return spread + home + 31 + plan.outer


def whole_step(counts, keep, master, patches, targets, plan):
    outer, depths, rows, lines = plan.outer, plan.depths, plan.rows, plan.lines
    vmem = pl.BlockSpec(memory_space=pltpu.VMEM)
    smem = pl.BlockSpec(memory_space=pltpu.SMEM)
    far = pl.BlockSpec(memory_space=pl.ANY)
    table = place_table(NP, ROWS, D)
    upper = table.astype(BRAIN)
    spot_enc = jnp.asarray(np.stack([upper, (table - upper.astype(np.float32)).astype(BRAIN)]))
    spot_dec = jnp.asarray(place_table(NP, ROWS, E))
    block = pltpu.VMEM((outer, 2, 2, 2, 2, rows, LANES), BRAIN)
    dma = pltpu.SemaphoreType.DMA
    copies = copies_used(plan)
    return pl.pallas_call(
        functools.partial(whole_body, plan),
        out_shape=jax.ShapeDtypeStruct((lines + 8, LANES), FLOAT),
        in_specs=[smem, vmem, vmem, far, far, far, far],
        out_specs=vmem,
        scratch_shapes=[
            block,
            pltpu.VMEM((5, HOME, PIX), BRAIN),
            pltpu.VMEM((LIVE_CAP - 1, NP, PIX), BRAIN),
            pltpu.VMEM((3, NP, PIX), BRAIN),
            pltpu.VMEM((NP, PIX), BRAIN),
            pltpu.VMEM((3, 8, LANES), FLOAT),
            pltpu.VMEM((depths, 2, 2, 2, rows, LANES), BRAIN),
            pltpu.SMEM((1,), FLOAT),
            pltpu.VMEM(spot_enc.shape, BRAIN),
            pltpu.VMEM(spot_dec.shape, FLOAT),
            dma((5,)),
            pltpu.VMEM((lines * LANES,), FLOAT),
            pltpu.VMEM((rows + 8, LANES), FLOAT),
            pltpu.VMEM(patches.shape, BRAIN),
            pltpu.VMEM((3, HOME, PIX), BRAIN),
            dma((copies,)),
            dma((copies,)),
            dma((2, 3, 3)),
            dma((2, 3)),
            pltpu.VMEM((plan.border + rows, LANES), FLOAT),
            pltpu.VMEM((plan.frame_rows + 8, LANES), FLOAT),
            pltpu.VMEM((48, E), FLOAT),
            pltpu.VMEM((LIVE_CAP, HOME, E), BRAIN),
            pltpu.VMEM((LIVE_CAP, HOME, E), BRAIN),
            pltpu.VMEM((LIVE_CAP, HOME, E), BRAIN),
            pltpu.VMEM((LIVE_CAP, ROWS, E), BRAIN),
            pltpu.VMEM((LIVE_CAP, ROWS, PIX), BRAIN),
            pltpu.VMEM((LIVE_CAP, ROWS, E), FLOAT),
            *weight_scratch(),
            *kept_scratch(0, LIVE_CAP * HOME, D, FF, HEADS),
            *kept_scratch(LIVE_CAP, ROWS, E, DFF, DHEADS),
            pltpu.VMEM((depths, 2, 2, rows, LANES), BRAIN),
            pltpu.VMEM((depths, 4, rows, LANES), BRAIN),
            pltpu.VMEM((depths, rows, LANES), BRAIN),
            pltpu.VMEM((rows, LANES), FLOAT),
            pltpu.VMEM((rows, LANES), FLOAT),
            pltpu.VMEM((32, 8, LANES), FLOAT),
            pltpu.VMEM((outer, 8, LANES), FLOAT),
            pltpu.VMEM((2, 8, LANES), FLOAT),
            dma((outer, len(plan.parts))),
            dma((outer, len(plan.parts))),
            dma((depths, len(plan.halves))),
            dma((depths, len(plan.halves))),
        ],
        compiler_params=pltpu.CompilerParams(
            collective_id=0, has_side_effects=True, vmem_limit_bytes=60 << 20
        ),
    )(counts, keep, master, patches, targets, spot_enc, spot_dec)


def on_device(patches, targets, keep, counts, step, master, first, second):
    plan = Plan(master.shape[0], lax.axis_size(("dp", "rep")))
    total = whole_step(counts, keep, master, patches, targets, plan)
    outs = update(step, total, master, first, second, plan)
    return (*outs[:4], outs[4].reshape(()), outs[5].reshape(()))


def solution(mesh):
    return jax.shard_map(
        on_device,
        mesh=mesh,
        in_specs=(
            P(("dp", "rep"), None, None),
            P(("dp", "rep"), None, None),
            P(("dp", "rep"), None),
            P("dp", "rep"),
            P(),
            P(("dp", "rep")),
            P(("dp", "rep")),
            P(("dp", "rep")),
        ),
        out_specs=(
            P(("dp", "rep")),
            P(("dp", "rep")),
            P(("dp", "rep")),
            P(("dp", "rep")),
            P(),
            P(),
        ),
        check_vma=False,
    )
```

```python
import functools
import itertools
import math

import jax
import jax.numpy as jnp
import numpy as np
from jax import lax
from jax.experimental import pallas as pl
from jax.experimental.pallas import tpu as pltpu
from jax.sharding import PartitionSpec as P

D = 192
HEADS = 3
FF = 768
E = 256
DHEADS = 8
DFF = 1024
PIX = 768
GRID = 14
VIS = 49
NP = 196

FLOAT = jnp.float32
BRAIN = jnp.bfloat16
CLIP = 0.05
BETA_ONE = 0.5
BETA_TWO = 0.5
LEARN = 0.01
DECAY = 0.05
EPSILON = 1e-08
LN_EPS = 1e-06

ROWS = 208
HOME = 64
LIVE_CAP = 3
PAIR = ((1,), (1,)), ((), ())
DEEP = ((0,), (0,)), ((), ())
LOG_TWO_E = 1.4426950408889634


def block_table(prefix, width, hidden, proj_fan, rate):
    return [
        (prefix + "ln1g", (width,), "gain", 1, rate),
        (prefix + "ln1b", (width,), "bias", 1, rate),
        (prefix + "qkv", (width, 3 * width), "matrix", width, rate),
        (prefix + "qvb", (2 * width,), "bias", 1, rate),
        (prefix + "proj", (width, width), "matrix", proj_fan, rate),
        (prefix + "projb", (width,), "bias", 1, rate),
        (prefix + "ln2g", (width,), "gain", 1, rate),
        (prefix + "ln2b", (width,), "bias", 1, rate),
        (prefix + "fc1", (width, hidden), "matrix", width, rate),
        (prefix + "fc1b", (hidden,), "bias", 1, rate),
        (prefix + "fc2", (hidden, width), "matrix", hidden, rate),
        (prefix + "fc2b", (width,), "bias", 1, rate),
    ]


def param_table():
    table = [("patch", (PIX, D), "matrix", PIX, 0.75), ("patchb", (D,), "bias", 1, 0.75)]
    table = table + block_table("enc_", D, FF, D // 4, 0.9)
    table = table + [
        ("encg", (D,), "gain", 1, 1.0),
        ("encb", (D,), "bias", 1, 1.0),
        ("embed", (D, E), "matrix", D, 1.0),
        ("embedb", (E,), "bias", 1, 1.0),
        ("mask", (E,), "token", 1, 1.0),
    ]
    table = table + block_table("dec_", E, DFF, E // 8, 1.0)
    table = table + [
        ("decg", (E,), "gain", 1, 1.0),
        ("decb", (E,), "bias", 1, 1.0),
        ("head", (E, PIX), "matrix", E, 1.0),
        ("headb", (PIX,), "bias", 1, 1.0),
    ]
    return table


MESH = pl.DeviceIdType.MESH
LANES = 128


def layout():
    table = {}
    offset = 0
    for name, shape, kind, fan, rate in param_table():
        table[name] = (offset, shape)
        offset += math.prod(shape)
    return table


class Plan:
    def __init__(self, length, count):
        self.length = length
        self.count = count
        self.outer = count // 16
        self.lines = -(-length // LANES // 8 * 8)
        self.rows = -(-(7 + (2 * LANES - 2 + length) // LANES) // 16) * 16
        self.split = layout()["embed"][0]
        if self.outer > 2:
            self.parts, self.orders = ((0, self.rows),), ("LCB",)
        else:
            half = self.rows // 32 * 16
            self.parts = ((0, half), (half, self.rows - half))
            self.orders = ("LCB", "BCL")
        self.first_late = -(-self.split // length)
        self.depths = count // 8
        pieces = 4 if self.outer == 2 else 1
        cuts = [self.rows // 16 * number // pieces * 16 for number in range(pieces + 1)]
        self.halves = tuple((low, high - low) for low, high in zip(cuts, cuts[1:]))
        self.ways = ("CB", "BC", "CB", "BC")[:pieces]
        last = self.first_late - 1
        self.border = (self.base(last) + self.used(last) + 1 + 7) // 8 * 8 + 8
        self.frame_rows = (length * count // LANES + 7) // 8 * 8 + self.rows + 16

    def depths_from(self, name):
        return min(-(-layout()[name][0] // (8 * self.length)), self.depths)

    def late(self, index):
        return index >= self.first_late

    def start(self, index):
        return index * self.length - (64 if self.late(index) else 0)

    def base(self, index):
        return self.start(index) // LANES

    def lead(self, index):
        return self.start(index) % LANES

    def used(self, index):
        return (self.lead(index) + self.length + LANES - 1) // LANES

    def own(self, index):
        start = index * self.length - jnp.where(index >= self.first_late, 64, 0)
        return lax.rem(lax.div(start, LANES), 8), lax.rem(start, LANES)


def spot_of(index):
    return (index // 16, index // 8 % 2, index // 4 % 2, index // 2 % 2, index % 2)


def position():
    chip = lax.axis_index("dp")
    core = lax.axis_index("rep")
    return {"H": chip // 8, "L": chip // 4 % 2, "B": chip // 2 % 2, "C": chip % 2, "r": core}


def index_of(place):
    return (((place["H"] * 2 + place["L"]) * 2 + place["B"]) * 2 + place["C"]) * 2 + place["r"]


def device_of(place):
    return (((place["H"] * 2 + place["L"]) * 2 + place["B"]) * 2 + place["C"], place["r"])


def moved(place, dim, value):
    changed = dict(place)
    changed[dim] = value
    return changed


def flipped(place, dims):
    changed = dict(place)
    for dim in dims:
        changed[dim] = 1 - place[dim]
    return changed


def meet(places):
    barrier = pltpu.get_barrier_semaphore()
    for place in places:
        pl.semaphore_signal(barrier, inc=1, device_id=device_of(place), device_id_type=MESH)
    pl.semaphore_wait(barrier, len(places))


def partners(place, plan):
    group = []
    for number in range(1, 8):
        group.append(flipped(place, [dim for bit, dim in enumerate("rCB") if number >> bit & 1]))
    depth = depth_of(place)
    column = [at_depth(place, lax.rem(depth + step, plan.depths)) for step in range(1, plan.depths)]
    return group, column


def at_depth(place, depth):
    return {**place, "H": depth // 2, "L": depth % 2}


def depth_of(place):
    return place["H"] * 2 + place["L"]


def gates(place, plan):
    near = [flipped(place, dims) for dims in ("r", "L", "B", "C", "BC")]
    steps = range(1, plan.outer)
    return near + [moved(place, "H", lax.rem(place["H"] + step, plan.outer)) for step in steps]


def branches(order):
    nodes = []
    for count in range(len(order) + 1):
        for dims in itertools.combinations(order, count):
            reach = max([order.index(dim) for dim in dims], default=-1)
            nodes.append((reach, count, "".join(dims), order[reach + 1 :]))
    nodes.sort(key=lambda node: node[:2])
    return [(dims, onward) for reach, count, dims, onward in nodes]


class Copy:
    def __init__(self, recipe, send, recv, number):
        self.recipe, self.send, self.recv, self.number = recipe, send, recv, number

    def make(self):
        source, target, place = self.recipe()
        return pltpu.make_async_remote_copy(
            src_ref=source,
            dst_ref=target,
            send_sem=self.send.at[self.number],
            recv_sem=self.recv.at[self.number],
            device_id=device_of(place),
            device_id_type=MESH,
        )

    def start(self):
        self.make().start()

    def wait_recv(self):
        self.make().wait_recv()

    def wait_send(self):
        self.make().wait_send()


class Sender:
    def __init__(self, send, recv):
        self.send, self.recv, self.used = send, recv, 0

    def plan(self, recipe):
        copy = Copy(recipe, self.send, self.recv, self.used)
        self.used += 1
        return copy

    def start(self, recipe):
        copy = self.plan(recipe)
        copy.start()
        return copy


def lane_iota(rows):
    return lax.broadcasted_iota(jnp.int32, (rows, LANES), 1)


HUBS = (1, 2)


def others_of(hub):
    return [spot for spot in range(4) if spot != hub]


def hand_over(place, hub, number, pairs, hand, taken):
    other = others_of(hub)[number]
    target = {**place, "B": other // 2, "C": other % 2}
    return [
        pltpu.make_async_remote_copy(
            src_ref=source,
            dst_ref=to,
            send_sem=hand.at[hub - 1, number, kind],
            recv_sem=taken.at[hub - 1, kind],
            device_id=device_of(target),
            device_id_type=MESH,
        )
        for kind, (source, to) in pairs.items()
    ]


class Handing:
    def __init__(self, place, spare, seen_ref, meta_ref, targets_ref, tgt_ref, hand, taken):
        self.place, self.hand, self.taken = place, hand, taken
        self.spot = place["B"] * 2 + place["C"]
        self.refs = (spare, seen_ref, meta_ref, targets_ref, tgt_ref)

    def copies(self, hub, number, kinds):
        spare, seen_ref, meta_ref, targets_ref, tgt_ref = self.refs
        pairs = {
            0: (spare.at[number], seen_ref.at[2 + hub]),
            1: (meta_ref.at[0], meta_ref.at[hub]),
            2: (targets_ref.at[3 + number], tgt_ref.at[hub]),
        }
        pairs = {kind: pairs[kind] for kind in kinds}
        return hand_over(self.place, hub, number, pairs, self.hand, self.taken)

    def on_hub(self, act):
        for hub in HUBS:

            @pl.when(self.spot == hub)
            def _(hub=hub):
                act(hub)

    def start(self, kinds):
        def act(hub):
            for number in range(3):
                for copy in self.copies(hub, number, kinds):
                    copy.start()

        self.on_hub(act)

    def receive(self, kinds):
        for hub in HUBS:

            @pl.when(self.spot != hub)
            def _(hub=hub):
                for copy in self.copies(hub, 0, kinds):
                    copy.wait_recv()

    def finish(self, kinds):
        def act(hub):
            for number in range(3):
                for copy in self.copies(hub, number, kinds):
                    copy.wait_send()

        self.on_hub(act)


def own_block(plan, device, x_ref, line, rolled):
    rows, lines = plan.rows, plan.lines
    skip, lead = plan.own(device)
    line[...] = jnp.zeros_like(line)
    line[pl.ds(0, plan.length)] = x_ref[...]
    turned = pltpu.roll(line[...].reshape(lines, LANES), lead, 1)
    rolled[...] = jnp.zeros_like(rolled)
    rolled[pl.ds(8 + skip, lines), :] = turned
    upper, lower = rolled[pl.ds(8, rows), :], rolled[pl.ds(7, rows), :]
    return jnp.where(lane_iota(rows) >= lead, upper, lower).astype(BRAIN)


class Gather:
    def __init__(self, plan, place, out_ref, sender, columns):
        self.plan, self.place, self.out_ref, self.sender, self.columns = plan, place, out_ref, sender, columns
        self.flights, self.onwards, self.siblings = {}, [], {}

    def region(self, value, part, fixed, free=""):
        start, size = self.plan.parts[part]
        index = [value]
        for dim in "LBC":
            if dim in free:
                index.append(pl.ds(0, 2))
            else:
                index.append(1 - self.place[dim] if dim in fixed else self.place[dim])
        return self.out_ref.at[(*index, self.place["r"], pl.ds(start, size))]

    def column(self, source, part, target):
        send, recv = self.columns
        ref = self.region(source, part, "")
        return pltpu.make_async_remote_copy(
            src_ref=ref,
            dst_ref=ref,
            send_sem=send.at[target, part],
            recv_sem=recv.at[source, part],
            device_id=device_of(moved(self.place, "H", target)),
            device_id_type=MESH,
        )

    def over_column(self, act):
        high = self.place["H"]
        for target in range(self.plan.outer):

            @pl.when(high != target)
            def _(target=target):
                for part in range(len(self.plan.parts)):
                    act(self.column(high, part, target))

    def begin(self):
        self.over_column(lambda copy: copy.start())

    def roots(self, meanwhile):
        plan, place = self.plan, self.place
        copies = {}
        for value in range(plan.outer):
            copies[value] = []
            for part, order in enumerate(plan.orders):
                copies[value].append(self.spread(value, part, "", order) + [self.give(value, part, -1)])

        for value, groups in copies.items():

            @pl.when(place["H"] == value)
            def _(groups=groups):
                for group in groups:
                    for copy in group:
                        copy.start()

        meanwhile()
        for value, groups in copies.items():

            @pl.when(place["H"] != value)
            def _(value=value, groups=groups):
                for part, group in enumerate(groups):
                    self.column(value, part, place["H"]).wait_recv()
                    for copy in group:
                        copy.start()

    def spread(self, value, part, dims, onward):
        def recipe(dim):
            source = self.region(value, part, dims)
            return source, source, flipped(self.place, dim)

        copies = []
        for dim in onward:
            copy = self.sender.plan(functools.partial(recipe, dim))
            self.flights[value, part, frozenset(dims + dim)] = copy
            copies.append(copy)
        self.onwards += copies
        return copies

    def give(self, value, part, reach):
        order = self.plan.orders[part]

        def recipe():
            source = self.region(value, part, order[reach] if reach >= 0 else "", order[: max(reach, 0)])
            return source, source, flipped(self.place, "r")

        copy = self.sender.plan(recipe)
        self.siblings.setdefault(value, []).append(copy)
        return copy

    def stage(self, value, reach):
        plan = self.plan
        trees = []
        for order in plan.orders:
            trees.append([node for node in branches(order) if node[0] and reach == order.index(node[0][-1])])
        for nodes in zip(*trees):
            for part, (dims, onward) in enumerate(nodes):
                self.flights.pop((value, part, frozenset(dims))).wait_recv()
                for copy in self.spread(value, part, dims, onward):
                    copy.start()
        for part in range(len(plan.orders)):
            self.give(value, part, reach).start()

    def ready(self, value):
        for copy in self.siblings[value]:
            copy.wait_recv()

    def close(self):
        self.over_column(lambda copy: copy.wait_send())
        for copies in [self.onwards] + list(self.siblings.values()):
            for copy in copies:
                copy.wait_send()


class Reducer:
    def __init__(self, plan, place, grad_ref, core_in, tree_in, column_in, own_ref, sender, columns):
        self.plan, self.place, self.sender = plan, place, sender
        self.grad_ref, self.core_in, self.tree_in = grad_ref, core_in, tree_in
        self.column_in, self.own_ref, self.columns = column_in, own_ref, columns
        self.cores = {}
        self.pending = []
        self.trees = [branches(order) for order in plan.ways]
        self.flights = {}

    def share(self, value):
        place = self.place

        def recipe(start, size):
            whole = (value, pl.ds(0, 2), pl.ds(0, 2))
            span = pl.ds(start, size)
            return (
                self.grad_ref.at[(*whole, 1 - place["r"], span)],
                self.core_in.at[(*whole, span)],
                flipped(place, "r"),
            )

        for part, (start, size) in enumerate(self.plan.halves):
            copy = self.sender.start(functools.partial(recipe, start, size))
            self.cores[value, part] = copy
            self.pending.append(copy)

    def stage(self, value, reach):
        plan, place = self.plan, self.place
        steps = []
        for part in range(len(plan.halves)):
            order = plan.ways[part]
            nodes = [
                (dims, onward)
                for dims, onward in reversed(self.trees[part])
                if (order.index(dims[-1]) if dims else -1) == reach
            ]
            steps.append([(part, *node) for node in nodes])
        for group in zip(*steps):
            for part, dims, onward in group:
                self.node(value, part, dims, onward)

    def node(self, value, part, dims, onward):
        plan, place = self.plan, self.place
        start, size = plan.halves[part]
        span = pl.ds(start, size)
        if (value, part) in self.cores:
            self.cores.pop((value, part)).wait_recv()
        for dim in onward:
            self.flights.pop((value, part, frozenset(dims + dim))).wait_recv()
        index = [value] + [1 - place[dim] if dim in dims else place[dim] for dim in "BC"]
        total = self.grad_ref[(*index, place["r"], span)].astype(FLOAT)
        total = total + self.core_in[(*index, span)].astype(FLOAT)

        def number(dims):
            return sum(1 << "BC".index(dim) for dim in dims)

        for dim in onward:
            total = total + self.tree_in[value, number(dims + dim), span].astype(FLOAT)

        def spot():
            index = [value] + [1 - place[dim] if dim in dims else place[dim] for dim in "BC"]
            return self.grad_ref.at[(*index, place["r"], span)]

        def recipe():
            return spot(), self.tree_in.at[value, number(dims), span], flipped(place, dims[-1])

        if dims:
            spot()[...] = total.astype(BRAIN)
            copy = self.sender.start(recipe)
            self.flights[value, part, frozenset(dims)] = copy
            self.pending.append(copy)
            return
        depth = depth_of(place)

        @pl.when(depth == value)
        def _():
            self.own_ref[span, :] = total

        @pl.when(depth != value)
        def _():
            spot()[...] = total.astype(BRAIN)
            self.column(value, part).start()

    def column(self, value, part):
        plan, place = self.plan, self.place
        start, size = plan.halves[part]
        send, recv = self.columns
        index = (value, place["B"], place["C"], place["r"], pl.ds(start, size))
        return pltpu.make_async_remote_copy(
            src_ref=self.grad_ref.at[index],
            dst_ref=self.column_in.at[depth_of(place), pl.ds(start, size)],
            send_sem=send.at[value, part],
            recv_sem=recv.at[depth_of(place), part],
            device_id=device_of(at_depth(place, value)),
            device_id_type=MESH,
        )

    def arrival(self, source, part):
        plan, place = self.plan, self.place
        start, size = plan.halves[part]
        send, recv = self.columns
        return pltpu.make_async_remote_copy(
            src_ref=self.own_in(part),
            dst_ref=self.column_in.at[source, pl.ds(start, size)],
            send_sem=send.at[source, part],
            recv_sem=recv.at[source, part],
            device_id=device_of(at_depth(place, source)),
            device_id_type=MESH,
        )

    def own_in(self, part):
        place = self.place
        start, size = self.plan.halves[part]
        index = (0, place["B"], place["C"], place["r"], pl.ds(start, size))
        return self.grad_ref.at[index]

    def finish(self):
        plan, place = self.plan, self.place
        for part, (start, size) in enumerate(plan.halves):
            for source in range(plan.depths):

                @pl.when(depth_of(place) != source)
                def _(part=part, source=source, start=start, size=size):
                    self.arrival(source, part).wait_recv()
                    span = pl.ds(start, size)
                    self.own_ref[span, :] += self.column_in[source, span].astype(FLOAT)

    def close(self):
        plan, place = self.plan, self.place
        for copy in self.pending:
            copy.wait_send()
        for part in range(len(plan.halves)):
            for value in range(plan.depths):

                @pl.when(depth_of(place) != value)
                def _(part=part, value=value):
                    self.column(value, part).wait_send()


def finish_body(plan, place, held_ref, loss_ref, own_ref, total_out, turned, near, far, mine, sender):
    rows, lines = plan.rows, plan.lines
    group, column = partners(place, plan)
    skip, lead = plan.own(index_of(place))
    position_in = lax.broadcasted_iota(jnp.int32, (lines, LANES), 0) * LANES + lane_iota(lines)
    shift = lax.rem(LANES - lead, LANES)
    turned[pl.ds(0, rows), :] = pltpu.roll(own_ref[...], shift, 1)
    here, below = turned[pl.ds(skip, lines), :], turned[pl.ds(skip + 1, lines), :]
    total = jnp.where(lane_iota(lines) < LANES - lead, here, below)
    total = jnp.where(position_in < plan.length, total, 0.0)
    squares = jnp.sum(total * total)
    lane = lane_iota(8)
    stats = jnp.where(lane == 0, squares, 0.0)
    stats = jnp.where(lane == 1, held_ref[0, 0].astype(FLOAT), stats)
    mine[0] = jnp.where(lane == 2, loss_ref[0], stats)
    count = len(group) + 1
    spot = lax.rem(index_of(place), count)
    near[spot] = mine[0]
    nears = [
        sender.start(functools.partial(lambda other: (mine.at[0], near.at[spot], other), other))
        for other in group
    ]
    total_out[pl.ds(0, lines), :] = total
    for copy in nears:
        copy.wait_recv()
    together = near[0]
    for other in range(1, count):
        together = together + near[other]
    depth = depth_of(place)
    far[depth] = together
    mine[1] = together
    fars = [
        sender.start(functools.partial(lambda other: (mine.at[1], far.at[depth], other), other))
        for other in column
    ]
    for copy in fars:
        copy.wait_recv()
    whole = far[0]
    for other in range(1, plan.depths):
        whole = whole + far[other]
    row = whole[0:1, :]
    lane = lane[0:1]

    def across(number):
        return jnp.full((1, LANES), jnp.sum(jnp.where(lane == number, row, 0.0)))

    weights = across(1) * (0.1 * VIS + (NP - VIS))
    total_out[pl.ds(lines, 1), :] = across(2) / weights
    total_out[pl.ds(lines + 1, 1), :] = jnp.sqrt(across(0)) / weights
    total_out[pl.ds(lines + 2, 1), :] = weights
    return nears + fars


def in_segments(index, segments):
    inside = None
    for start, stop in segments:
        here = (index >= start) & (index < stop)
        inside = here if inside is None else inside | here
    return inside


def matrix_segments():
    found = []
    for name, shape, kind, fan, rate in param_table():
        if kind == "matrix":
            start = layout()[name][0]
            found.append((start, start + math.prod(shape)))
    return found


def update_body(
    plan, step_ref, total_ref, master_ref, first_ref, second_ref,
    master_out, first_out, second_out, copy_out, loss_out, norm_out, line
):
    rows, length = plan.lines, plan.length
    device = lax.axis_index("dp") * 2 + lax.axis_index("rep")
    position_in = lax.broadcasted_iota(jnp.int32, (rows, LANES), 0) * LANES + lane_iota(rows)
    flat = position_in + device * length
    table = layout()
    early, late = table["enc_ln1g"][0], table["encg"][0]
    rate_part = jnp.where(flat < early, 0.75, jnp.where(flat < late, 0.9, 1.0))
    decay_part = jnp.where(in_segments(flat, matrix_segments()), DECAY, 0.0)
    line[...] = jnp.zeros_like(line)
    line[pl.ds(0, length)] = master_ref[...]
    master = line[...].reshape(rows, LANES)
    line[pl.ds(0, length)] = first_ref[...]
    first = line[...].reshape(rows, LANES)
    line[pl.ds(0, length)] = second_ref[...]
    second = line[...].reshape(rows, LANES)
    norms = total_ref[pl.ds(rows + 1, 1), :]
    loss_out[0, 0] = jnp.max(total_ref[pl.ds(rows, 1), :])
    norm_out[0, 0] = jnp.max(norms)
    gradient = total_ref[pl.ds(0, rows), :] / total_ref[pl.ds(rows + 2, 1), :]
    clipped = gradient * jnp.minimum(1.0, CLIP / norms)
    fade = 1.0 / jnp.full((1, LANES), lax.shift_left(1, step_ref[0]).astype(FLOAT))
    new_first = BETA_ONE * first + (1.0 - BETA_ONE) * clipped
    new_second = BETA_TWO * second + (1.0 - BETA_TWO) * clipped * clipped
    first_hat = new_first / (1.0 - fade)
    second_hat = new_second / (1.0 - fade)
    new_master = master - LEARN * rate_part * (
        first_hat / (jnp.sqrt(second_hat) + EPSILON) + decay_part * master
    )
    master_out[...] = new_master.reshape(rows * LANES)[:length]
    first_out[...] = new_first.reshape(rows * LANES)[:length]
    second_out[...] = new_second.reshape(rows * LANES)[:length]
    copy_out[...] = new_master.reshape(rows * LANES)[:length].astype(BRAIN)


def update(step, total, master, first, second, plan):
    vmem = pl.BlockSpec(memory_space=pltpu.VMEM)
    smem = pl.BlockSpec(memory_space=pltpu.SMEM)
    flat = jax.ShapeDtypeStruct((plan.length,), FLOAT)
    single = jax.ShapeDtypeStruct((1, 1), FLOAT)
    return pl.pallas_call(
        functools.partial(update_body, plan),
        out_shape=(flat, flat, flat, jax.ShapeDtypeStruct((plan.length,), BRAIN), single, single),
        in_specs=[smem, vmem, vmem, vmem, vmem],
        out_specs=(vmem, vmem, vmem, vmem, smem, smem),
        scratch_shapes=[pltpu.VMEM((plan.lines * LANES,), FLOAT)],
        compiler_params=pltpu.CompilerParams(vmem_limit_bytes=16 << 20),
    )(step, total, master, first, second)


class Frames:
    def __init__(self, plan, slots, even, odd):
        self.plan, self.slots, self.even, self.odd = plan, slots, even, odd
        self.filled = 0

    def add(self, index):
        plan, even = self.plan, self.even
        if index == plan.first_late:
            rest = plan.border - self.filled
            even[pl.ds(self.filled, rest), :] = jnp.zeros((rest, LANES), FLOAT)
            half_turn(plan, even, self.odd)
            self.filled = plan.border
        frame = self.odd if plan.late(index) else even
        start = plan.base(index) // 8 * 8
        rows = -(-(plan.base(index) - start + plan.used(index)) // 8) * 8
        block = self.slots[(*spot_of(index), pl.ds(0, plan.rows))].astype(FLOAT)
        if start < self.filled:
            frame[pl.ds(start, 8), :] += block[:8]
            frame[pl.ds(start + 8, rows - 8), :] = block[8:rows]
        else:
            frame[pl.ds(start, rows), :] = block[:rows]
        self.filled = start + rows


def half_turn(plan, even, odd):
    total = plan.border - 8
    span = 256

    def turn(start, rows):
        here = pltpu.roll(even[pl.ds(start, rows), :], 64, 1)
        below = pltpu.roll(even[pl.ds(start + 1, rows), :], 64, 1)
        odd[pl.ds(start, rows), :] = jnp.where(lane_iota(rows) < 64, here, below)

    @pl.loop(0, total // span)
    def _(step):
        turn(pl.multiple_of(step * span, span), span)

    if total % span:
        turn(total // span * span, total % span)


def read_param(even, odd, name, target):
    offset, shape = layout()[name]
    rows, width = (1, shape[0]) if len(shape) == 1 else shape
    base, late = divmod(offset, LANES)
    frames = (even, odd) if late == 0 else (odd, even)
    whole, half = divmod(width, LANES)
    kind = target.dtype
    if rows == 1:
        for col in range(whole):
            target[:, pl.ds(col * LANES, LANES)] = frames[0][pl.ds(base + col, 1), :].astype(kind)
        if half:
            tail = frames[0][pl.ds(base + whole, 1), :]
            target[:, pl.ds(whole * LANES, half)] = tail[:, :half].astype(kind)
        return
    if not half:
        for col in range(whole):
            piece = frames[0][pl.ds(base + col, rows, stride=whole), :]
            target[:, pl.ds(col * LANES, LANES)] = piece.astype(kind)
        return
    stride = 2 * width // LANES
    shift = whole + (1 if late else 0)

    def interleave(scratch):
        for col in range(whole + 1):
            size = LANES if col < whole else half
            upper = frames[0][pl.ds(base + col, rows // 2, stride=stride), :]
            lower = frames[1][pl.ds(base + shift + col, rows // 2, stride=stride), :]
            scratch[pl.ds(0, rows // 2, stride=2), :] = upper
            scratch[pl.ds(1, rows // 2, stride=2), :] = lower
            target[:, pl.ds(col * LANES, size)] = scratch[...][:, :size].astype(kind)

    pl.run_scoped(interleave, pltpu.VMEM((rows, LANES), FLOAT))


def write_grad(even, odd, name, value):
    offset, shape = layout()[name]
    rows, width = (1, shape[0]) if len(shape) == 1 else shape
    base, late = divmod(offset, LANES)
    frames = (even, odd) if late == 0 else (odd, even)
    whole, half = divmod(width, LANES)

    def columns():
        for col in range(0, whole, 2):
            size = min(2, whole - col) * LANES
            both = value(col * LANES, size)
            for part in range(size // LANES):
                yield col + part, both[:, part * LANES : (part + 1) * LANES]
        if half:
            tail = value(whole * LANES, half)
            yield whole, jnp.concatenate([tail, jnp.zeros((rows, LANES - half), FLOAT)], axis=1)

    if rows == 1:
        for col, piece in columns():
            frames[0][pl.ds(base + col, 1), :] = piece
        return
    if not half:
        for col, piece in columns():
            frames[0][pl.ds(base + col, rows, stride=whole), :] = piece
        return
    stride = 2 * width // LANES
    shift = whole + (1 if late else 0)

    def interleave(scratch):
        for col, piece in columns():
            scratch[...] = piece
            upper = scratch[pl.ds(0, rows // 2, stride=2), :]
            lower = scratch[pl.ds(1, rows // 2, stride=2), :]
            frames[0][pl.ds(base + col, rows // 2, stride=stride), :] = upper
            frames[1][pl.ds(base + shift + col, rows // 2, stride=stride), :] = lower

    pl.run_scoped(interleave, pltpu.VMEM((rows, LANES), FLOAT))


def clear_frames(plan, even, odd):
    even[...] = jnp.zeros_like(even)
    odd[pl.ds(0, plan.border + 16), :] = jnp.zeros((plan.border + 16, LANES), FLOAT)
    table = layout()
    final = (table["headb"][0] // LANES) // 8 * 8
    odd[pl.ds(final, odd.shape[0] - final), :] = jnp.zeros((odd.shape[0] - final, LANES), FLOAT)


def emit_slots(plan, even, odd, slots, depths):
    rows = plan.rows
    for index in [depth * 8 + number for depth in depths for number in range(8)]:
        start = plan.base(index) // 8 * 8
        if plan.late(index):
            block = odd[pl.ds(start + 8, rows), :]
        else:
            here = pltpu.roll(odd[pl.ds(start + 8, rows), :], 64, 1)
            above = pltpu.roll(odd[pl.ds(start + 7, rows), :], 64, 1)
            block = even[pl.ds(start, rows), :] + jnp.where(lane_iota(rows) < 64, above, here)
        slots[(index // 8, index // 4 % 2, index // 2 % 2, index % 2)] = block.astype(BRAIN)


def dot(left, right, dims=(((1,), (0,)), ((), ()))):
    return lax.dot_general(left, right, dims, preferred_element_type=FLOAT)


def place_table(count, rows, width):
    quarter = width // 4
    omega = 1.0 / 10000.0 ** (np.arange(quarter) / quarter)
    index = np.arange(count)
    across = (index // GRID)[:, None] * omega
    along = (index % GRID)[:, None] * omega
    table = np.zeros((rows, width), np.float32)
    table[:count] = np.concatenate(
        [np.sin(across), np.cos(across), np.sin(along), np.cos(along)], axis=-1
    )
    return table


def split_two(value):
    upper = value.astype(BRAIN)
    return upper, (value - upper.astype(FLOAT)).astype(BRAIN)


def norm_parts(value):
    center = value - jnp.mean(value, axis=-1, keepdims=True)
    spread = lax.rsqrt(jnp.mean(center * center, axis=-1, keepdims=True) + LN_EPS)
    return center * spread, spread


def norm_back(grad, value, gain):
    unit, spread = norm_parts(value)
    d_gain = jnp.sum(grad * unit, axis=0, keepdims=True)
    d_shift = jnp.sum(grad, axis=0, keepdims=True)
    scaled = grad * gain
    middle = jnp.mean(scaled, axis=-1, keepdims=True)
    along = jnp.mean(scaled * unit, axis=-1, keepdims=True)
    return spread * (scaled - middle - unit * along), d_gain, d_shift


def gelu_parts(value):
    half = 0.5 + 0.5 * lax.erf(value * 0.7071067811865476)
    bell = jnp.exp2(value * value * (-0.5 * LOG_TWO_E)) * 0.3989422804014327
    return value * half, half + value * bell


def head_only(value, head, size):
    lane = lax.broadcasted_iota(jnp.int32, value.shape, 1)
    inside = (lane >= head * size) & (lane < (head + 1) * size)
    return jnp.where(inside, value, jnp.zeros_like(value))


def attend(t_ref, chance_ref, stack_ref, usable, width, heads):
    size = width // heads
    rows = t_ref.shape[0]
    query, keys = t_ref[:, pl.ds(0, width)].T, t_ref[:, pl.ds(width, width)]
    values = t_ref[:, pl.ds(2 * width, width)].T
    factor = size ** (-0.5) * LOG_TWO_E
    mixed = []
    for head in range(heads):
        stack_ref[pl.ds(head * rows, rows), :] = head_only(keys, head, size)
    scores = dot(stack_ref[...], query)
    for head in range(heads):
        raw = jnp.where(usable, scores[head * rows : (head + 1) * rows], -1e30)
        top = jnp.max(raw, axis=0, keepdims=True)
        power = jnp.exp2((raw - top) * factor)
        chance = power * (1.0 / jnp.sum(power, axis=0, keepdims=True))
        chance_ref[head] = chance
        mixed.append(dot(values[head * size : (head + 1) * size], chance.astype(BRAIN)))
    return jnp.concatenate(mixed, axis=0).astype(BRAIN).T


def attend_back(d_mixed, t_ref, dt_ref, chance_ref, stack_ref, width, heads):
    size = width // heads
    rows = t_ref.shape[0]
    scale = size ** (-0.5)
    query, keys = t_ref[:, pl.ds(0, width)], t_ref[:, pl.ds(width, width)].T
    values = t_ref[:, pl.ds(2 * width, width)]
    d_query = []
    d_keys = d_values = None
    for head in range(heads):
        stack_ref[pl.ds(head * rows, rows), :] = head_only(values, head, size)
    d_chances = dot(stack_ref[...], d_mixed.T)
    for head in range(heads):
        chance = chance_ref[head]
        d_chance = d_chances[head * rows : (head + 1) * rows]
        along = jnp.sum(chance * d_chance, axis=0, keepdims=True)
        d_scores = (chance * (d_chance - along)).astype(BRAIN)
        part = dot(chance.astype(BRAIN), head_only(d_mixed, head, size))
        d_values = part if d_values is None else d_values + part
        part = dot(d_scores, head_only(query, head, size))
        d_keys = part if d_keys is None else d_keys + part
        d_query.append(dot(keys[head * size : (head + 1) * size], d_scores))
    d_query = (jnp.concatenate(d_query, axis=0) * scale).astype(BRAIN).T
    dt_ref[:, pl.ds(0, width)] = d_query
    dt_ref[:, pl.ds(width, width)] = (d_keys * scale).astype(BRAIN)
    dt_ref[:, pl.ds(2 * width, width)] = d_values.astype(BRAIN)


class Weights:
    def __init__(self, refs):
        self.refs = dict(zip(layout(), refs))

    def __call__(self, name):
        return self.refs[name][...]


def block_open(hidden, keep, weights, prefix):
    width = hidden.shape[1]
    keep["x"][...] = hidden
    unit, unused = norm_parts(hidden)
    normed = (unit * weights(prefix + "ln1g") + weights(prefix + "ln1b")).astype(BRAIN)
    keep["a"][...] = normed
    bias = weights(prefix + "qvb")
    for part in range(3):
        cols = pl.ds(part * width, width)
        value = dot(normed, weights.refs[prefix + "qkv"][:, cols])
        if part != 1:
            value = value + bias[:, (part // 2) * width : (part // 2 + 1) * width]
        keep["t"][:, cols] = value.astype(BRAIN)


def each_group(keep, act):
    count, rows = keep["p"].shape[0], keep["p"].shape[2]
    if count == 1:
        act(0, pl.ds(0, rows))
        return

    @pl.loop(0, count)
    def _(group):
        act(group, pl.ds(pl.multiple_of(group * rows, rows), rows))


def block_middle(hidden, keep, weights, prefix, heads, usable):
    width = hidden.shape[1]

    def mix(group, rows):
        keep["o"][rows, :] = attend(keep["t"].at[rows], keep["p"].at[group], keep["k"], usable, width, heads)

    each_group(keep, mix)
    middle = hidden + (dot(keep["o"][...], weights(prefix + "proj")) + weights(prefix + "projb"))
    keep["m"][...] = middle
    unit, unused = norm_parts(middle)
    second = (unit * weights(prefix + "ln2g") + weights(prefix + "ln2b")).astype(BRAIN)
    keep["b"][...] = second
    inner = dot(second, weights(prefix + "fc1")) + weights(prefix + "fc1b")
    active, slope = gelu_parts(inner)
    keep["s"][...] = slope
    keep["g"][...] = active.astype(BRAIN)


def block_shut(keep, weights, prefix):
    return keep["m"][...] + (dot(keep["g"][...], weights(prefix + "fc2")) + weights(prefix + "fc2b"))


def home_open(grad, keep, weights, prefix):
    d_branch = grad.astype(BRAIN)
    keep["dz"][...] = d_branch
    keep["du"][...] = (dot(d_branch, weights(prefix + "fc2"), PAIR) * keep["s"][...]).astype(BRAIN)


def home_middle(grad, keep, weights, prefix, heads, sums, meanwhile=None):
    width = grad.shape[1]
    d_second = dot(keep["du"][...], weights(prefix + "fc1"), PAIR)
    d_middle, d_gain, d_shift = norm_back(d_second, keep["m"][...], weights(prefix + "ln2g"))
    sums(prefix + "ln2g", d_gain)
    sums(prefix + "ln2b", d_shift)
    d_middle = d_middle + grad
    d_output = d_middle.astype(BRAIN)
    keep["dy"][...] = d_output
    keep["do"][...] = dot(d_output, weights(prefix + "proj"), PAIR).astype(BRAIN)

    def unmix(group, rows):
        if meanwhile is not None:
            meanwhile(group)
        d_mixed = keep["do"][rows, :]
        attend_back(
            d_mixed, keep["t"].at[rows], keep["dt"].at[rows], keep["p"].at[group], keep["k"], width, heads
        )

    each_group(keep, unmix)
    d_normed = dot(keep["dt"][...], weights(prefix + "qkv"), PAIR)
    d_hidden, d_gain, d_shift = norm_back(d_normed, keep["x"][...], weights(prefix + "ln1g"))
    sums(prefix + "ln1g", d_gain)
    sums(prefix + "ln1b", d_shift)
    return d_middle + d_hidden


def kept_shapes(groups, rows, width, hidden, heads):
    every = groups * rows
    return {
        "x": ((every, width), FLOAT),
        "a": ((every, width), BRAIN),
        "t": ((every, 3 * width), BRAIN),
        "p": ((groups, heads, rows, rows), FLOAT),
        "k": ((heads * rows, width), BRAIN),
        "o": ((every, width), BRAIN),
        "m": ((every, width), FLOAT),
        "b": ((every, width), BRAIN),
        "s": ((every, hidden), FLOAT),
        "g": ((every, hidden), BRAIN),
        "dz": ((every, width), BRAIN),
        "du": ((every, hidden), BRAIN),
        "dy": ((every, width), BRAIN),
        "do": ((every, width), BRAIN),
        "dt": ((every, 3 * width), BRAIN),
    }


def kept_scratch(*sizes):
    return [pltpu.VMEM(shape, kind) for shape, kind in kept_shapes(*sizes).values()]


def kept_view(refs):
    return dict(zip(kept_shapes(1, 1, 1, 1, 1), refs))


LAYERS = {
    "fc2": ("g", "dz", "fc2b"),
    "fc1": ("b", "du", "fc1b"),
    "proj": ("o", "dy", "projb"),
    "qkv": ("a", "dt", "qvb"),
}


def block_grads(keep, prefix, names, emit):
    for name in names:
        left, right, bias = LAYERS[name]
        emit(prefix + name, prefix + bias, keep[left][...], keep[right][...])


NORMS = ("ln1g", "ln1b", "ln2g", "ln2b", "encg", "encb", "decg", "decb", "mask")


class Images:
    def __init__(self, place, counts_ref, meta_ref):
        spot = place["B"] * 2 + place["C"]
        self.meta_ref = meta_ref
        self.own = counts_ref[0, 0]
        lane = lane_iota(8)
        row = lax.broadcasted_iota(jnp.int32, (8, LANES), 0)

        def count_of(hub):
            corner = jnp.where((lane == LANES - 1) & (row == 0), meta_ref[hub], 0.0)
            return jnp.sum(corner).astype(jnp.int32)

        one, two = count_of(1), count_of(2)
        from_one = jnp.where(spot == 0, 3, jnp.where(spot == 2, 4, 5))
        from_two = jnp.where(spot == 0, 3, jnp.where(spot == 1, 4, 5))
        use_one = (spot == 2) | ((spot != 1) & (one > 2))
        mine = self.own > 2

        def choose(own, first, second):
            return jnp.where(mine, own, jnp.where(use_one, first, second))

        self.third = choose(2, 3, 4)
        self.third_row = choose(2, from_one, from_two)
        self.third_count = choose(self.own, one, two)
        self.third_meta = choose(0, 1, 2)

    def __call__(self, image):
        last = image == 2
        source = jnp.where(last, self.third, image)
        line = jnp.where(last, self.third_row, image)
        live = jnp.where(last, self.third_count, self.own) > line
        kept = self.meta_ref[jnp.where(last, self.third_meta, 0), pl.ds(line, 1), :][:, :HOME]
        return source, kept, live.astype(FLOAT)


def placement(kept, rows):
    number = lax.broadcasted_iota(jnp.int32, (rows, HOME), 0).astype(FLOAT)
    return (number == kept).astype(FLOAT)


def whole_body(
    plan, counts_ref, keep_ref, x_ref, patches_ref, targets_ref, enc_table, dec_table,
    total_out, *scratch
):
    scratch = list(scratch)

    def take(count):
        taken = scratch[:count]
        del scratch[:count]
        return taken

    names = list(layout())
    slots, seen_ref, tgt_own, tgt_ref, meta_ref, grad_ref, loss_ref = take(7)
    spot_enc, spot_dec, local = take(3)
    line, rolled, pixels, spare, send, recv, hand, taken = take(8)
    even, odd, sums_ref, y_hi, y_lo, dy_home, final_all, dpred_all = take(8)
    weights = Weights(take(len(names)))
    enc_refs, dec_refs = take(15), take(15)
    core_in, tree_in, column_in, own_ref, turned, near, far, mine = take(8)
    spread_send, spread_recv, column_send, column_recv = take(4)

    place = position()
    device = index_of(place)
    copies = [
        pltpu.make_async_copy(patches_ref, pixels, local.at[0]),
        pltpu.make_async_copy(enc_table, spot_enc, local.at[1]),
        pltpu.make_async_copy(dec_table, spot_dec, local.at[2]),
        pltpu.make_async_copy(
            targets_ref.at[pl.ds(0, LIVE_CAP - 1)], tgt_own, local.at[3]
        ),
        pltpu.make_async_copy(targets_ref.at[LIVE_CAP - 1], tgt_ref.at[0], local.at[4]),
    ]
    for copy in copies:
        copy.start()
    slots[(place["H"], place["L"], place["B"], place["C"], place["r"])] = own_block(
        plan, device, x_ref, line, rolled
    )
    meet(gates(place, plan))
    sender = Sender(send, recv)
    handing = Handing(place, spare, seen_ref, meta_ref, targets_ref, tgt_ref, hand, taken)

    def choose_images():
        lane = lane_iota(8)
        row = lax.broadcasted_iota(jnp.int32, (8, LANES), 0)
        held = counts_ref[0, 0].astype(FLOAT)
        meta_ref[0] = jnp.where((lane == LANES - 1) & (row == 0), held, -1.0)
        meta_ref[0, pl.ds(0, keep_ref.shape[0]), pl.ds(0, VIS)] = keep_ref[...].astype(FLOAT)
        copies[0].wait()

        def visible(image):
            where = placement(meta_ref[0, pl.ds(image, 1), :][:, :HOME], NP).astype(BRAIN)
            return dot(where, pixels[image], DEEP).astype(BRAIN)

        def prepare(hub):
            for number in range(3):
                spare[number] = visible(3 + number)

        handing.on_hub(prepare)
        handing.start((0, 1))
        for image in range(LIVE_CAP):
            seen_ref[image] = visible(image)

    early = min(-(-layout()["dec_qkv"][0] // (16 * plan.length)), plan.outer)
    first_values, last_values = range(early), range(early, plan.outer)
    gather = Gather(plan, place, slots, sender, (spread_send, spread_recv))
    frames = Frames(plan, slots, even, odd)

    def spread(values, reach):
        for value in values:
            gather.stage(value, reach)

    def fetch(values, wanted_names):
        for value in values:
            gather.ready(value)
            for index in range(value * 16, value * 16 + 16):
                frames.add(index)
        for name in wanted_names:
            read_param(even, odd, name, weights.refs[name])

    gather.begin()
    gather.roots(choose_images)
    for reach in (0, 1):
        spread(first_values, reach)
        spread(last_values, reach)
    spread(first_values, 2)
    spread(last_values, 2)
    handing.start((2,))
    divide = names.index("dec_qkv")
    fetch(first_values, names[:divide])
    handing.receive((0, 1))
    for copy in copies[1:]:
        copy.wait()
    sums_ref[...] = jnp.zeros_like(sums_ref)
    order = {name: number for number, name in enumerate(names)}

    def add_sum(name, value):
        sums_ref[pl.ds(order[name], 1), pl.ds(0, value.shape[1])] += value

    pick = Images(place, counts_ref, meta_ref)

    visible, begin = [], []
    for image in range(LIVE_CAP):
        source, kept, live = pick(image)
        where = placement(kept, ROWS).astype(BRAIN)
        visible.append(seen_ref[source])
        begin.append(dot(where, spot_enc[0], DEEP) + dot(where, spot_enc[1], DEEP))
    visible = jnp.concatenate(visible, axis=0)
    begin = jnp.concatenate(begin, axis=0)
    enc_rows = LIVE_CAP * HOME
    enc = kept_view(enc_refs)
    down = lax.broadcasted_iota(jnp.int32, (enc_rows, enc_rows), 0)
    over = lax.broadcasted_iota(jnp.int32, (enc_rows, enc_rows), 1)
    usable = (down // HOME == over // HOME) & (down % HOME < VIS)
    first_in = dot(visible, weights("patch")) + weights("patchb") + begin
    block_open(first_in, enc, weights, "enc_")
    block_middle(first_in, enc, weights, "enc_", HEADS, usable)
    encoded = block_shut(enc, weights, "enc_")
    unit, unused = norm_parts(encoded)
    encoder_out = (unit * weights("encg") + weights("encb")).astype(BRAIN)
    embedded = dot(encoder_out, weights("embed")) + weights("embedb")
    upper, lower = split_two(embedded)
    for image in range(LIVE_CAP):
        y_hi[image] = upper[image * HOME : (image + 1) * HOME]
        y_lo[image] = lower[image * HOME : (image + 1) * HOME]
    fetch(last_values, names[divide:])
    clear_frames(plan, even, odd)
    view = odd.at[pl.ds(8, plan.frame_rows)]
    real = lax.broadcasted_iota(jnp.int32, (ROWS, 1), 0) < NP
    usable_dec = lax.broadcasted_iota(jnp.int32, (ROWS, ROWS), 0) < NP

    dec = kept_view(dec_refs)
    dec_rows = [pl.ds(image * ROWS, ROWS) for image in range(LIVE_CAP)]
    wheres, seens, lives = [], [], []
    for image in range(LIVE_CAP):
        source, kept, live = pick(image)
        where = placement(kept, ROWS)
        wheres.append(where.astype(BRAIN))
        seens.append(jnp.sum(where, axis=1, keepdims=True))
        lives.append(live)

    def unseen(image):
        return 1.0 - seens[image]

    grid_in = []
    for image in range(LIVE_CAP):
        where = wheres[image]
        value = dot(where, y_hi[image]) + dot(where, y_lo[image])
        grid_in.append(value + unseen(image) * weights("mask") + spot_dec[...])
    grid_in = jnp.concatenate(grid_in, axis=0)
    block_open(grid_in, dec, weights, "dec_")
    block_middle(grid_in, dec, weights, "dec_", DHEADS, usable_dec)
    decoded = block_shut(dec, weights, "dec_")
    unit, unused = norm_parts(decoded)
    final_all[...] = (unit * weights("decg") + weights("decb")).astype(BRAIN)
    handing.receive((2,))
    total = jnp.zeros((1, PIX), FLOAT)
    for image in range(LIVE_CAP):
        predicted = dot(final_all[dec_rows[image], :], weights("head")) + weights("headb")
        weight = jnp.where(real, (1.0 - 0.9 * seens[image]) * lives[image], 0.0)
        wanted = tgt_ref[pick.third - 2] if image == LIVE_CAP - 1 else tgt_own[image]
        error = predicted[:NP] - wanted.astype(FLOAT)
        weighted = error * weight[:NP]
        total = total + jnp.sum(weighted * error, axis=0, keepdims=True)
        dpred_all[pl.ds(image * ROWS, NP), :] = (weighted * (2.0 / PIX)).astype(BRAIN)
        dpred_all[pl.ds(image * ROWS + NP, ROWS - NP), :] = jnp.zeros((ROWS - NP, PIX), BRAIN)
    d_final = dot(dpred_all[...], weights("head"), PAIR)
    d_decoded, d_gain, d_shift = norm_back(d_final, decoded, weights("decg"))
    add_sum("decg", d_gain)
    add_sum("decb", d_shift)
    home_open(d_decoded, dec, weights, "dec_")
    loss_ref[0] = jnp.sum(total) * (1.0 / PIX)

    def emit(name, bias, left, right):
        ones = jnp.ones((16, right.shape[0]), BRAIN)
        summed = dot(ones, right)[0:1]
        if bias.endswith("qvb"):
            width = summed.shape[1] // 3
            summed = jnp.concatenate([summed[:, :width], summed[:, 2 * width :]], axis=1)
        write_grad(even, view, bias, lambda start, size: summed[:, start : start + size])
        turned = left.T
        write_grad(even, view, name, lambda start, size: dot(turned, right[:, start : start + size]))

    def emit_norms(wanted_names):
        for name in wanted_names:
            row = pl.ds(order[name], 1)
            write_grad(even, view, name, lambda start, size, row=row: sums_ref[row, pl.ds(start, size)])

    reducer = Reducer(
        plan, place, grad_ref, core_in, tree_in, column_in, own_ref, sender, (column_send, column_recv)
    )
    floors = [plan.depths_from(name) for name in ("dec_fc2", "embed", "enc_fc1")]
    waves = [range(low, high) for low, high in zip(floors + [0], [plan.depths] + floors)]

    def leave(wave):
        emit_slots(plan, even, odd, grad_ref, waves[wave])
        for depth in waves[wave]:
            reducer.share(depth)

    def collect(wave, reach):
        for depth in waves[wave]:
            reducer.stage(depth, reach)

    emit("head", "headb", final_all[...], dpred_all[...])
    block_grads(dec, "dec_", ("fc2",), emit)
    emit_norms(("decg", "decb"))
    leave(0)
    block_grads(dec, "dec_", ("fc1",), emit)

    def meanwhile(group):
        @pl.when(group == 1)
        def _():
            collect(0, 1)

        @pl.when(group == 2)
        def _():
            collect(0, 0)

    d_grid = home_middle(d_decoded, dec, weights, "dec_", DHEADS, add_sum, meanwhile)
    d_mask = jnp.zeros((1, E), FLOAT)
    for image in range(LIVE_CAP):
        part = d_grid[image * ROWS : (image + 1) * ROWS]
        d_mask = d_mask + jnp.sum(unseen(image) * part, axis=0, keepdims=True)
        dy_home[image] = dot(wheres[image], part.astype(BRAIN), DEEP).astype(BRAIN)
    add_sum("mask", d_mask)
    collect(0, -1)
    block_grads(dec, "dec_", ("proj", "qkv"), emit)
    d_embedded = dy_home[...].reshape(enc_rows, E)
    emit("embed", "embedb", encoder_out, d_embedded)
    emit_norms(("mask", "dec_ln1g", "dec_ln1b", "dec_ln2g", "dec_ln2b"))
    leave(1)

    d_seen = dot(d_embedded, weights("embed"), PAIR).astype(BRAIN).astype(FLOAT)
    d_encoded, d_gain, d_shift = norm_back(d_seen, encoded, weights("encg"))
    add_sum("encg", d_gain)
    add_sum("encb", d_shift)
    home_open(d_encoded, enc, weights, "enc_")
    block_grads(enc, "enc_", ("fc2", "fc1"), emit)
    emit_norms(("encg", "encb"))
    leave(2)
    collect(1, 1)
    d_first = home_middle(d_encoded, enc, weights, "enc_", HEADS, add_sum).astype(BRAIN)
    collect(2, 1)
    collect(1, 0)
    emit("patch", "patchb", visible, d_first)
    block_grads(enc, "enc_", ("proj", "qkv"), emit)
    emit_norms(("enc_ln1g", "enc_ln1b", "enc_ln2g", "enc_ln2b"))
    leave(3)
    collect(2, 0)
    collect(1, -1)
    collect(3, 1)
    collect(2, -1)
    collect(3, 0)
    collect(3, -1)
    reducer.finish()
    pending = finish_body(
        plan, place, counts_ref, loss_ref, own_ref, total_out, turned, near, far, mine, sender
    )
    gather.close()
    reducer.close()
    handing.finish((0, 1, 2))
    for copy in pending:
        copy.wait_send()


def weight_scratch():
    shapes = []
    for name, (offset, shape) in layout().items():
        if len(shape) == 1:
            shapes.append(pltpu.VMEM((1, *shape), FLOAT))
        else:
            shapes.append(pltpu.VMEM(shape, BRAIN))
    return shapes


def copies_used(plan):
    spread = len(plan.parts) * plan.outer * (7 + 4)
    home = len(plan.halves) * plan.depths * (1 + 3)
    return spread + home + 7 + plan.depths


def whole_step(counts, keep, master, patches, targets, plan):
    outer, depths, rows, lines = plan.outer, plan.depths, plan.rows, plan.lines
    vmem = pl.BlockSpec(memory_space=pltpu.VMEM)
    smem = pl.BlockSpec(memory_space=pltpu.SMEM)
    far = pl.BlockSpec(memory_space=pl.ANY)
    table = place_table(NP, ROWS, D)
    upper = table.astype(BRAIN)
    spot_enc = jnp.asarray(np.stack([upper, (table - upper.astype(np.float32)).astype(BRAIN)]))
    spot_dec = jnp.asarray(place_table(NP, ROWS, E))
    block = pltpu.VMEM((outer, 2, 2, 2, 2, rows, LANES), BRAIN)
    dma = pltpu.SemaphoreType.DMA
    copies = copies_used(plan)
    return pl.pallas_call(
        functools.partial(whole_body, plan),
        out_shape=jax.ShapeDtypeStruct((lines + 8, LANES), FLOAT),
        in_specs=[smem, vmem, vmem, far, far, far, far],
        out_specs=vmem,
        scratch_shapes=[
            block,
            pltpu.VMEM((5, HOME, PIX), BRAIN),
            pltpu.VMEM((LIVE_CAP - 1, NP, PIX), BRAIN),
            pltpu.VMEM((3, NP, PIX), BRAIN),
            pltpu.VMEM((3, 8, LANES), FLOAT),
            pltpu.VMEM((depths, 2, 2, 2, rows, LANES), BRAIN),
            pltpu.SMEM((1,), FLOAT),
            pltpu.VMEM(spot_enc.shape, BRAIN),
            pltpu.VMEM(spot_dec.shape, FLOAT),
            dma((5,)),
            pltpu.VMEM((lines * LANES,), FLOAT),
            pltpu.VMEM((rows + 8, LANES), FLOAT),
            pltpu.VMEM(patches.shape, BRAIN),
            pltpu.VMEM((3, HOME, PIX), BRAIN),
            dma((copies,)),
            dma((copies,)),
            dma((2, 3, 3)),
            dma((2, 3)),
            pltpu.VMEM((plan.border + rows, LANES), FLOAT),
            pltpu.VMEM((plan.frame_rows + 8, LANES), FLOAT),
            pltpu.VMEM((48, E), FLOAT),
            pltpu.VMEM((LIVE_CAP, HOME, E), BRAIN),
            pltpu.VMEM((LIVE_CAP, HOME, E), BRAIN),
            pltpu.VMEM((LIVE_CAP, HOME, E), BRAIN),
            pltpu.VMEM((LIVE_CAP * ROWS, E), BRAIN),
            pltpu.VMEM((LIVE_CAP * ROWS, PIX), BRAIN),
            *weight_scratch(),
            *kept_scratch(1, LIVE_CAP * HOME, D, FF, HEADS),
            *kept_scratch(LIVE_CAP, ROWS, E, DFF, DHEADS),
            pltpu.VMEM((depths, 2, 2, rows, LANES), BRAIN),
            pltpu.VMEM((depths, 4, rows, LANES), BRAIN),
            pltpu.VMEM((depths, rows, LANES), BRAIN),
            pltpu.VMEM((rows, LANES), FLOAT),
            pltpu.VMEM((rows, LANES), FLOAT),
            pltpu.VMEM((8, 8, LANES), FLOAT),
            pltpu.VMEM((depths, 8, LANES), FLOAT),
            pltpu.VMEM((2, 8, LANES), FLOAT),
            dma((outer, len(plan.parts))),
            dma((outer, len(plan.parts))),
            dma((depths, len(plan.halves))),
            dma((depths, len(plan.halves))),
        ],
        compiler_params=pltpu.CompilerParams(
            collective_id=0, has_side_effects=True, vmem_limit_bytes=60 << 20
        ),
    )(counts, keep, master, patches, targets, spot_enc, spot_dec)


def on_device(patches, targets, keep, counts, step, master, first, second):
    plan = Plan(master.shape[0], lax.axis_size(("dp", "rep")))
    total = whole_step(counts, keep, master, patches, targets, plan)
    outs = update(step, total, master, first, second, plan)
    return (*outs[:4], outs[4].reshape(()), outs[5].reshape(()))


def solution(mesh):
    return jax.shard_map(
        on_device,
        mesh=mesh,
        in_specs=(
            P(("dp", "rep"), None, None),
            P(("dp", "rep"), None, None),
            P(("dp", "rep"), None),
            P("dp", "rep"),
            P(),
            P(("dp", "rep")),
            P(("dp", "rep")),
            P(("dp", "rep")),
        ),
        out_specs=(
            P(("dp", "rep")),
            P(("dp", "rep")),
            P(("dp", "rep")),
            P(("dp", "rep")),
            P(),
            P(),
        ),
        check_vma=False,
    )
```

```python
import functools
import itertools
import math

import jax
import jax.numpy as jnp
import numpy as np
from jax import lax
from jax.experimental import pallas as pl
from jax.experimental.pallas import tpu as pltpu
from jax.sharding import PartitionSpec as P

D = 192
HEADS = 3
FF = 768
E = 256
DHEADS = 8
DFF = 1024
PIX = 768
GRID = 14
VIS = 49
NP = 196

FLOAT = jnp.float32
BRAIN = jnp.bfloat16
CLIP = 0.05
BETA_ONE = 0.5
BETA_TWO = 0.5
LEARN = 0.01
DECAY = 0.05
EPSILON = 1e-08
LN_EPS = 1e-06

ROWS = 208
HOME = 64
LIVE_CAP = 3
PAIR = ((1,), (1,)), ((), ())
DEEP = ((0,), (0,)), ((), ())
LOG_TWO_E = 1.4426950408889634


def block_table(prefix, width, hidden, proj_fan, rate):
    return [
        (prefix + "ln1g", (width,), "gain", 1, rate),
        (prefix + "ln1b", (width,), "bias", 1, rate),
        (prefix + "qkv", (width, 3 * width), "matrix", width, rate),
        (prefix + "qvb", (2 * width,), "bias", 1, rate),
        (prefix + "proj", (width, width), "matrix", proj_fan, rate),
        (prefix + "projb", (width,), "bias", 1, rate),
        (prefix + "ln2g", (width,), "gain", 1, rate),
        (prefix + "ln2b", (width,), "bias", 1, rate),
        (prefix + "fc1", (width, hidden), "matrix", width, rate),
        (prefix + "fc1b", (hidden,), "bias", 1, rate),
        (prefix + "fc2", (hidden, width), "matrix", hidden, rate),
        (prefix + "fc2b", (width,), "bias", 1, rate),
    ]


def param_table():
    table = [("patch", (PIX, D), "matrix", PIX, 0.75), ("patchb", (D,), "bias", 1, 0.75)]
    table = table + block_table("enc_", D, FF, D // 4, 0.9)
    table = table + [
        ("encg", (D,), "gain", 1, 1.0),
        ("encb", (D,), "bias", 1, 1.0),
        ("embed", (D, E), "matrix", D, 1.0),
        ("embedb", (E,), "bias", 1, 1.0),
        ("mask", (E,), "token", 1, 1.0),
    ]
    table = table + block_table("dec_", E, DFF, E // 8, 1.0)
    table = table + [
        ("decg", (E,), "gain", 1, 1.0),
        ("decb", (E,), "bias", 1, 1.0),
        ("head", (E, PIX), "matrix", E, 1.0),
        ("headb", (PIX,), "bias", 1, 1.0),
    ]
    return table


MESH = pl.DeviceIdType.MESH
LANES = 128


def layout():
    table = {}
    offset = 0
    for name, shape, kind, fan, rate in param_table():
        table[name] = (offset, shape)
        offset += math.prod(shape)
    return table


class Plan:
    def __init__(self, length, count):
        self.length = length
        self.count = count
        self.outer = count // 16
        self.lines = -(-length // LANES // 8 * 8)
        self.rows = -(-(7 + (2 * LANES - 2 + length) // LANES) // 16) * 16
        self.split = layout()["embed"][0]
        if self.outer > 2:
            self.parts, self.orders = ((0, self.rows),), ("LCB",)
        else:
            half = self.rows // 32 * 16
            self.parts = ((0, half), (half, self.rows - half))
            self.orders = ("LCB", "BCL")
        self.first_late = -(-self.split // length)
        self.depths = count // 8
        pieces = 4 if self.outer == 2 else 1
        cuts = [self.rows // 16 * number // pieces * 16 for number in range(pieces + 1)]
        self.halves = tuple((low, high - low) for low, high in zip(cuts, cuts[1:]))
        self.ways = ("CB", "BC", "CB", "BC")[:pieces]
        last = self.first_late - 1
        self.border = (self.base(last) + self.used(last) + 1 + 7) // 8 * 8 + 8
        self.frame_rows = (length * count // LANES + 7) // 8 * 8 + self.rows + 16

    def depths_from(self, name):
        return min(-(-layout()[name][0] // (8 * self.length)), self.depths)

    def late(self, index):
        return index >= self.first_late

    def start(self, index):
        return index * self.length - (64 if self.late(index) else 0)

    def base(self, index):
        return self.start(index) // LANES

    def lead(self, index):
        return self.start(index) % LANES

    def used(self, index):
        return (self.lead(index) + self.length + LANES - 1) // LANES

    def own(self, index):
        start = index * self.length - jnp.where(index >= self.first_late, 64, 0)
        return lax.rem(lax.div(start, LANES), 8), lax.rem(start, LANES)


def spot_of(index):
    return (index // 16, index // 8 % 2, index // 4 % 2, index // 2 % 2, index % 2)


def position():
    chip = lax.axis_index("dp")
    core = lax.axis_index("rep")
    return {"H": chip // 8, "L": chip // 4 % 2, "B": chip // 2 % 2, "C": chip % 2, "r": core}


def index_of(place):
    return (((place["H"] * 2 + place["L"]) * 2 + place["B"]) * 2 + place["C"]) * 2 + place["r"]


def device_of(place):
    return (((place["H"] * 2 + place["L"]) * 2 + place["B"]) * 2 + place["C"], place["r"])


def moved(place, dim, value):
    changed = dict(place)
    changed[dim] = value
    return changed


def flipped(place, dims):
    changed = dict(place)
    for dim in dims:
        changed[dim] = 1 - place[dim]
    return changed


def meet(places):
    barrier = pltpu.get_barrier_semaphore()
    for place in places:
        pl.semaphore_signal(barrier, inc=1, device_id=device_of(place), device_id_type=MESH)
    pl.semaphore_wait(barrier, len(places))


def partners(place, plan):
    group = []
    for number in range(1, 8):
        group.append(flipped(place, [dim for bit, dim in enumerate("rCB") if number >> bit & 1]))
    depth = depth_of(place)
    column = [at_depth(place, lax.rem(depth + step, plan.depths)) for step in range(1, plan.depths)]
    return group, column


def at_depth(place, depth):
    return {**place, "H": depth // 2, "L": depth % 2}


def depth_of(place):
    return place["H"] * 2 + place["L"]


def gates(place, plan):
    near = [flipped(place, dims) for dims in ("r", "L", "B", "C", "BC")]
    steps = range(1, plan.outer)
    return near + [moved(place, "H", lax.rem(place["H"] + step, plan.outer)) for step in steps]


def branches(order):
    nodes = []
    for count in range(len(order) + 1):
        for dims in itertools.combinations(order, count):
            reach = max([order.index(dim) for dim in dims], default=-1)
            nodes.append((reach, count, "".join(dims), order[reach + 1 :]))
    nodes.sort(key=lambda node: node[:2])
    return [(dims, onward) for reach, count, dims, onward in nodes]


class Copy:
    def __init__(self, recipe, send, recv, number):
        self.recipe, self.send, self.recv, self.number = recipe, send, recv, number

    def make(self):
        source, target, place = self.recipe()
        return pltpu.make_async_remote_copy(
            src_ref=source,
            dst_ref=target,
            send_sem=self.send.at[self.number],
            recv_sem=self.recv.at[self.number],
            device_id=device_of(place),
            device_id_type=MESH,
        )

    def start(self):
        self.make().start()

    def wait_recv(self):
        self.make().wait_recv()

    def wait_send(self):
        self.make().wait_send()


class Sender:
    def __init__(self, send, recv):
        self.send, self.recv, self.used = send, recv, 0

    def plan(self, recipe):
        copy = Copy(recipe, self.send, self.recv, self.used)
        self.used += 1
        return copy

    def start(self, recipe):
        copy = self.plan(recipe)
        copy.start()
        return copy


def lane_iota(rows):
    return lax.broadcasted_iota(jnp.int32, (rows, LANES), 1)


HUBS = (1, 2)


def others_of(hub):
    return [spot for spot in range(4) if spot != hub]


def hand_over(place, hub, number, pairs, hand, taken):
    other = others_of(hub)[number]
    target = {**place, "B": other // 2, "C": other % 2}
    return [
        pltpu.make_async_remote_copy(
            src_ref=source,
            dst_ref=to,
            send_sem=hand.at[hub - 1, number, kind],
            recv_sem=taken.at[hub - 1, kind],
            device_id=device_of(target),
            device_id_type=MESH,
        )
        for kind, (source, to) in pairs.items()
    ]


class Handing:
    def __init__(self, place, spare, seen_ref, meta_ref, targets_ref, tgt_ref, hand, taken):
        self.place, self.hand, self.taken = place, hand, taken
        self.spot = place["B"] * 2 + place["C"]
        self.refs = (spare, seen_ref, meta_ref, targets_ref, tgt_ref)

    def copies(self, hub, number, kinds):
        spare, seen_ref, meta_ref, targets_ref, tgt_ref = self.refs
        pairs = {
            0: (spare.at[number], seen_ref.at[2 + hub]),
            1: (meta_ref.at[0], meta_ref.at[hub]),
            2: (targets_ref.at[3 + number], tgt_ref.at[hub]),
        }
        pairs = {kind: pairs[kind] for kind in kinds}
        return hand_over(self.place, hub, number, pairs, self.hand, self.taken)

    def on_hub(self, act):
        for hub in HUBS:

            @pl.when(self.spot == hub)
            def _(hub=hub):
                act(hub)

    def start(self, kinds):
        def act(hub):
            for number in range(3):
                for copy in self.copies(hub, number, kinds):
                    copy.start()

        self.on_hub(act)

    def receive(self, kinds):
        for hub in HUBS:

            @pl.when(self.spot != hub)
            def _(hub=hub):
                for copy in self.copies(hub, 0, kinds):
                    copy.wait_recv()

    def finish(self, kinds):
        def act(hub):
            for number in range(3):
                for copy in self.copies(hub, number, kinds):
                    copy.wait_send()

        self.on_hub(act)


def own_block(plan, device, x_ref, line, rolled):
    rows, lines = plan.rows, plan.lines
    skip, lead = plan.own(device)
    line[...] = jnp.zeros_like(line)
    line[pl.ds(0, plan.length)] = x_ref[...]
    turned = pltpu.roll(line[...].reshape(lines, LANES), lead, 1)
    rolled[...] = jnp.zeros_like(rolled)
    rolled[pl.ds(8 + skip, lines), :] = turned
    upper, lower = rolled[pl.ds(8, rows), :], rolled[pl.ds(7, rows), :]
    return jnp.where(lane_iota(rows) >= lead, upper, lower).astype(BRAIN)


class Gather:
    def __init__(self, plan, place, out_ref, sender, columns):
        self.plan, self.place, self.out_ref, self.sender, self.columns = plan, place, out_ref, sender, columns
        self.flights, self.onwards, self.siblings = {}, [], {}

    def region(self, value, part, fixed, free=""):
        start, size = self.plan.parts[part]
        index = [value]
        for dim in "LBC":
            if dim in free:
                index.append(pl.ds(0, 2))
            else:
                index.append(1 - self.place[dim] if dim in fixed else self.place[dim])
        return self.out_ref.at[(*index, self.place["r"], pl.ds(start, size))]

    def column(self, source, part, target):
        send, recv = self.columns
        ref = self.region(source, part, "")
        return pltpu.make_async_remote_copy(
            src_ref=ref,
            dst_ref=ref,
            send_sem=send.at[target, part],
            recv_sem=recv.at[source, part],
            device_id=device_of(moved(self.place, "H", target)),
            device_id_type=MESH,
        )

    def over_column(self, act):
        high = self.place["H"]
        for target in range(self.plan.outer):

            @pl.when(high != target)
            def _(target=target):
                for part in range(len(self.plan.parts)):
                    act(self.column(high, part, target))

    def begin(self):
        self.over_column(lambda copy: copy.start())

    def roots(self, meanwhile):
        plan, place = self.plan, self.place
        copies = {}
        for value in range(plan.outer):
            copies[value] = []
            for part, order in enumerate(plan.orders):
                copies[value].append(self.spread(value, part, "", order) + [self.give(value, part, -1)])

        for value, groups in copies.items():

            @pl.when(place["H"] == value)
            def _(groups=groups):
                for group in groups:
                    for copy in group:
                        copy.start()

        meanwhile()
        for value, groups in copies.items():

            @pl.when(place["H"] != value)
            def _(value=value, groups=groups):
                for part, group in enumerate(groups):
                    self.column(value, part, place["H"]).wait_recv()
                    for copy in group:
                        copy.start()

    def spread(self, value, part, dims, onward):
        def recipe(dim):
            source = self.region(value, part, dims)
            return source, source, flipped(self.place, dim)

        copies = []
        for dim in onward:
            copy = self.sender.plan(functools.partial(recipe, dim))
            self.flights[value, part, frozenset(dims + dim)] = copy
            copies.append(copy)
        self.onwards += copies
        return copies

    def give(self, value, part, reach):
        order = self.plan.orders[part]

        def recipe():
            source = self.region(value, part, order[reach] if reach >= 0 else "", order[: max(reach, 0)])
            return source, source, flipped(self.place, "r")

        copy = self.sender.plan(recipe)
        self.siblings.setdefault(value, []).append(copy)
        return copy

    def stage(self, value, reach):
        plan = self.plan
        trees = []
        for order in plan.orders:
            trees.append([node for node in branches(order) if node[0] and reach == order.index(node[0][-1])])
        for nodes in zip(*trees):
            for part, (dims, onward) in enumerate(nodes):
                self.flights.pop((value, part, frozenset(dims))).wait_recv()
                for copy in self.spread(value, part, dims, onward):
                    copy.start()
        for part in range(len(plan.orders)):
            self.give(value, part, reach).start()

    def ready(self, value):
        for copy in self.siblings[value]:
            copy.wait_recv()

    def close(self):
        self.over_column(lambda copy: copy.wait_send())
        for copies in [self.onwards] + list(self.siblings.values()):
            for copy in copies:
                copy.wait_send()


class Reducer:
    def __init__(self, plan, place, grad_ref, core_in, tree_in, column_in, own_ref, sender, columns):
        self.plan, self.place, self.sender = plan, place, sender
        self.grad_ref, self.core_in, self.tree_in = grad_ref, core_in, tree_in
        self.column_in, self.own_ref, self.columns = column_in, own_ref, columns
        self.cores = {}
        self.pending = []
        self.trees = [branches(order) for order in plan.ways]
        self.flights = {}

    def share(self, value):
        place = self.place

        def recipe(start, size):
            whole = (value, pl.ds(0, 2), pl.ds(0, 2))
            span = pl.ds(start, size)
            return (
                self.grad_ref.at[(*whole, 1 - place["r"], span)],
                self.core_in.at[(*whole, span)],
                flipped(place, "r"),
            )

        for part, (start, size) in enumerate(self.plan.halves):
            copy = self.sender.start(functools.partial(recipe, start, size))
            self.cores[value, part] = copy
            self.pending.append(copy)

    def stage(self, value, reach):
        plan, place = self.plan, self.place
        steps = []
        for part in range(len(plan.halves)):
            order = plan.ways[part]
            nodes = [
                (dims, onward)
                for dims, onward in reversed(self.trees[part])
                if (order.index(dims[-1]) if dims else -1) == reach
            ]
            steps.append([(part, *node) for node in nodes])
        for group in zip(*steps):
            for part, dims, onward in group:
                self.node(value, part, dims, onward)

    def node(self, value, part, dims, onward):
        plan, place = self.plan, self.place
        start, size = plan.halves[part]
        span = pl.ds(start, size)
        if (value, part) in self.cores:
            self.cores.pop((value, part)).wait_recv()
        for dim in onward:
            self.flights.pop((value, part, frozenset(dims + dim))).wait_recv()
        index = [value] + [1 - place[dim] if dim in dims else place[dim] for dim in "BC"]
        total = self.grad_ref[(*index, place["r"], span)].astype(FLOAT)
        total = total + self.core_in[(*index, span)].astype(FLOAT)

        def number(dims):
            return sum(1 << "BC".index(dim) for dim in dims) - 1

        for dim in onward:
            total = total + self.tree_in[value, number(dims + dim), span].astype(FLOAT)

        def spot():
            index = [value] + [1 - place[dim] if dim in dims else place[dim] for dim in "BC"]
            return self.grad_ref.at[(*index, place["r"], span)]

        def recipe():
            return spot(), self.tree_in.at[value, number(dims), span], flipped(place, dims[-1])

        if dims:
            spot()[...] = total.astype(BRAIN)
            copy = self.sender.start(recipe)
            self.flights[value, part, frozenset(dims)] = copy
            self.pending.append(copy)
            return
        depth = depth_of(place)

        @pl.when(depth == value)
        def _():
            self.own_ref[span, :] = total

        @pl.when(depth != value)
        def _():
            spot()[...] = total.astype(BRAIN)
            self.column(value, part).start()

    def column(self, value, part):
        plan, place = self.plan, self.place
        start, size = plan.halves[part]
        send, recv = self.columns
        index = (value, place["B"], place["C"], place["r"], pl.ds(start, size))
        return pltpu.make_async_remote_copy(
            src_ref=self.grad_ref.at[index],
            dst_ref=self.column_in.at[depth_of(place), pl.ds(start, size)],
            send_sem=send.at[value, part],
            recv_sem=recv.at[depth_of(place), part],
            device_id=device_of(at_depth(place, value)),
            device_id_type=MESH,
        )

    def arrival(self, source, part):
        plan, place = self.plan, self.place
        start, size = plan.halves[part]
        send, recv = self.columns
        return pltpu.make_async_remote_copy(
            src_ref=self.own_in(part),
            dst_ref=self.column_in.at[source, pl.ds(start, size)],
            send_sem=send.at[source, part],
            recv_sem=recv.at[source, part],
            device_id=device_of(at_depth(place, source)),
            device_id_type=MESH,
        )

    def own_in(self, part):
        place = self.place
        start, size = self.plan.halves[part]
        index = (0, place["B"], place["C"], place["r"], pl.ds(start, size))
        return self.grad_ref.at[index]

    def finish(self):
        plan, place = self.plan, self.place
        for part, (start, size) in enumerate(plan.halves):
            for source in range(plan.depths):

                @pl.when(depth_of(place) != source)
                def _(part=part, source=source, start=start, size=size):
                    self.arrival(source, part).wait_recv()
                    span = pl.ds(start, size)
                    self.own_ref[span, :] += self.column_in[source, span].astype(FLOAT)

    def close(self):
        plan, place = self.plan, self.place
        for copy in self.pending:
            copy.wait_send()
        for part in range(len(plan.halves)):
            for value in range(plan.depths):

                @pl.when(depth_of(place) != value)
                def _(part=part, value=value):
                    self.column(value, part).wait_send()


def finish_body(plan, place, held_ref, loss_ref, own_ref, total_out, turned, near, far, mine, sender):
    rows, lines = plan.rows, plan.lines
    group, column = partners(place, plan)
    skip, lead = plan.own(index_of(place))
    position_in = lax.broadcasted_iota(jnp.int32, (lines, LANES), 0) * LANES + lane_iota(lines)
    shift = lax.rem(LANES - lead, LANES)
    turned[pl.ds(0, rows), :] = pltpu.roll(own_ref[...], shift, 1)
    here, below = turned[pl.ds(skip, lines), :], turned[pl.ds(skip + 1, lines), :]
    total = jnp.where(lane_iota(lines) < LANES - lead, here, below)
    total = jnp.where(position_in < plan.length, total, 0.0)
    squares = jnp.sum(total * total)
    lane = lane_iota(8)
    stats = jnp.where(lane == 0, squares, 0.0)
    stats = jnp.where(lane == 1, held_ref[0, 0].astype(FLOAT), stats)
    mine[0] = jnp.where(lane == 2, loss_ref[0], stats)
    count = len(group) + 1
    spot = lax.rem(index_of(place), count)
    near[spot] = mine[0]
    nears = [
        sender.start(functools.partial(lambda other: (mine.at[0], near.at[spot], other), other))
        for other in group
    ]
    total_out[pl.ds(0, lines), :] = total
    for copy in nears:
        copy.wait_recv()
    together = near[0]
    for other in range(1, count):
        together = together + near[other]
    depth = depth_of(place)
    far[depth] = together
    mine[1] = together
    fars = [
        sender.start(functools.partial(lambda other: (mine.at[1], far.at[depth], other), other))
        for other in column
    ]
    for copy in fars:
        copy.wait_recv()
    whole = far[0]
    for other in range(1, plan.depths):
        whole = whole + far[other]
    row = whole[0:1, :]
    lane = lane[0:1]

    def across(number):
        return jnp.full((1, LANES), jnp.sum(jnp.where(lane == number, row, 0.0)))

    weights = across(1) * (0.1 * VIS + (NP - VIS))
    total_out[pl.ds(lines, 1), :] = across(2) / weights
    total_out[pl.ds(lines + 1, 1), :] = jnp.sqrt(across(0)) / weights
    total_out[pl.ds(lines + 2, 1), :] = weights
    return nears + fars


def in_segments(index, segments):
    inside = None
    for start, stop in segments:
        here = (index >= start) & (index < stop)
        inside = here if inside is None else inside | here
    return inside


def matrix_segments():
    found = []
    for name, shape, kind, fan, rate in param_table():
        if kind == "matrix":
            start = layout()[name][0]
            found.append((start, start + math.prod(shape)))
    return found


def update_body(
    plan, step_ref, total_ref, master_ref, first_ref, second_ref,
    master_out, first_out, second_out, copy_out, loss_out, norm_out, line
):
    rows, length = plan.lines, plan.length
    device = lax.axis_index("dp") * 2 + lax.axis_index("rep")
    position_in = lax.broadcasted_iota(jnp.int32, (rows, LANES), 0) * LANES + lane_iota(rows)
    flat = position_in + device * length
    table = layout()
    early, late = table["enc_ln1g"][0], table["encg"][0]
    rate_part = jnp.where(flat < early, 0.75, jnp.where(flat < late, 0.9, 1.0))
    decay_part = jnp.where(in_segments(flat, matrix_segments()), DECAY, 0.0)
    line[...] = jnp.zeros_like(line)
    line[pl.ds(0, length)] = master_ref[...]
    master = line[...].reshape(rows, LANES)
    line[pl.ds(0, length)] = first_ref[...]
    first = line[...].reshape(rows, LANES)
    line[pl.ds(0, length)] = second_ref[...]
    second = line[...].reshape(rows, LANES)
    norms = total_ref[pl.ds(rows + 1, 1), :]
    loss_out[0, 0] = jnp.max(total_ref[pl.ds(rows, 1), :])
    norm_out[0, 0] = jnp.max(norms)
    gradient = total_ref[pl.ds(0, rows), :] / total_ref[pl.ds(rows + 2, 1), :]
    clipped = gradient * jnp.minimum(1.0, CLIP / norms)
    fade = 1.0 / jnp.full((1, LANES), lax.shift_left(1, step_ref[0]).astype(FLOAT))
    new_first = BETA_ONE * first + (1.0 - BETA_ONE) * clipped
    new_second = BETA_TWO * second + (1.0 - BETA_TWO) * clipped * clipped
    first_hat = new_first / (1.0 - fade)
    second_hat = new_second / (1.0 - fade)
    new_master = master - LEARN * rate_part * (
        first_hat / (jnp.sqrt(second_hat) + EPSILON) + decay_part * master
    )
    master_out[...] = new_master.reshape(rows * LANES)[:length]
    first_out[...] = new_first.reshape(rows * LANES)[:length]
    second_out[...] = new_second.reshape(rows * LANES)[:length]
    copy_out[...] = new_master.reshape(rows * LANES)[:length].astype(BRAIN)


def update(step, total, master, first, second, plan):
    vmem = pl.BlockSpec(memory_space=pltpu.VMEM)
    smem = pl.BlockSpec(memory_space=pltpu.SMEM)
    flat = jax.ShapeDtypeStruct((plan.length,), FLOAT)
    single = jax.ShapeDtypeStruct((1, 1), FLOAT)
    return pl.pallas_call(
        functools.partial(update_body, plan),
        out_shape=(flat, flat, flat, jax.ShapeDtypeStruct((plan.length,), BRAIN), single, single),
        in_specs=[smem, vmem, vmem, vmem, vmem],
        out_specs=(vmem, vmem, vmem, vmem, smem, smem),
        scratch_shapes=[pltpu.VMEM((plan.lines * LANES,), FLOAT)],
        compiler_params=pltpu.CompilerParams(vmem_limit_bytes=16 << 20),
    )(step, total, master, first, second)


class Frames:
    def __init__(self, plan, slots, even, odd):
        self.plan, self.slots, self.even, self.odd = plan, slots, even, odd
        self.filled = 0

    def add(self, index):
        plan, even = self.plan, self.even
        if index == plan.first_late:
            rest = plan.border - self.filled
            even[pl.ds(self.filled, rest), :] = jnp.zeros((rest, LANES), FLOAT)
            half_turn(plan, even, self.odd)
            self.filled = plan.border
        frame = self.odd if plan.late(index) else even
        start = plan.base(index) // 8 * 8
        rows = -(-(plan.base(index) - start + plan.used(index)) // 8) * 8
        block = self.slots[(*spot_of(index), pl.ds(0, plan.rows))].astype(FLOAT)
        if start < self.filled:
            frame[pl.ds(start, 8), :] += block[:8]
            frame[pl.ds(start + 8, rows - 8), :] = block[8:rows]
        else:
            frame[pl.ds(start, rows), :] = block[:rows]
        self.filled = start + rows


def half_turn(plan, even, odd):
    total = plan.border - 8
    span = 256

    def turn(start, rows):
        here = pltpu.roll(even[pl.ds(start, rows), :], 64, 1)
        below = pltpu.roll(even[pl.ds(start + 1, rows), :], 64, 1)
        odd[pl.ds(start, rows), :] = jnp.where(lane_iota(rows) < 64, here, below)

    @pl.loop(0, total // span)
    def _(step):
        turn(pl.multiple_of(step * span, span), span)

    if total % span:
        turn(total // span * span, total % span)


def read_param(even, odd, name, target):
    offset, shape = layout()[name]
    rows, width = (1, shape[0]) if len(shape) == 1 else shape
    base, late = divmod(offset, LANES)
    frames = (even, odd) if late == 0 else (odd, even)
    whole, half = divmod(width, LANES)
    kind = target.dtype
    if rows == 1:
        for col in range(whole):
            target[:, pl.ds(col * LANES, LANES)] = frames[0][pl.ds(base + col, 1), :].astype(kind)
        if half:
            tail = frames[0][pl.ds(base + whole, 1), :]
            target[:, pl.ds(whole * LANES, half)] = tail[:, :half].astype(kind)
        return
    if not half:
        for col in range(whole):
            piece = frames[0][pl.ds(base + col, rows, stride=whole), :]
            target[:, pl.ds(col * LANES, LANES)] = piece.astype(kind)
        return
    stride = 2 * width // LANES
    shift = whole + (1 if late else 0)

    def interleave(scratch):
        for col in range(whole + 1):
            size = LANES if col < whole else half
            upper = frames[0][pl.ds(base + col, rows // 2, stride=stride), :]
            lower = frames[1][pl.ds(base + shift + col, rows // 2, stride=stride), :]
            scratch[pl.ds(0, rows // 2, stride=2), :] = upper
            scratch[pl.ds(1, rows // 2, stride=2), :] = lower
            target[:, pl.ds(col * LANES, size)] = scratch[...][:, :size].astype(kind)

    pl.run_scoped(interleave, pltpu.VMEM((rows, LANES), FLOAT))


def write_grad(even, odd, name, value):
    offset, shape = layout()[name]
    rows, width = (1, shape[0]) if len(shape) == 1 else shape
    base, late = divmod(offset, LANES)
    frames = (even, odd) if late == 0 else (odd, even)
    whole, half = divmod(width, LANES)

    def columns():
        for col in range(0, whole, 2):
            size = min(2, whole - col) * LANES
            both = value(col * LANES, size)
            for part in range(size // LANES):
                yield col + part, both[:, part * LANES : (part + 1) * LANES]
        if half:
            tail = value(whole * LANES, half)
            yield whole, jnp.concatenate([tail, jnp.zeros((rows, LANES - half), FLOAT)], axis=1)

    if rows == 1:
        for col, piece in columns():
            frames[0][pl.ds(base + col, 1), :] = piece
        return
    if not half:
        for col, piece in columns():
            frames[0][pl.ds(base + col, rows, stride=whole), :] = piece
        return
    stride = 2 * width // LANES
    shift = whole + (1 if late else 0)

    def interleave(scratch):
        for col, piece in columns():
            scratch[...] = piece
            upper = scratch[pl.ds(0, rows // 2, stride=2), :]
            lower = scratch[pl.ds(1, rows // 2, stride=2), :]
            frames[0][pl.ds(base + col, rows // 2, stride=stride), :] = upper
            frames[1][pl.ds(base + shift + col, rows // 2, stride=stride), :] = lower

    pl.run_scoped(interleave, pltpu.VMEM((rows, LANES), FLOAT))


def clear_frames(plan, even, odd):
    even[...] = jnp.zeros_like(even)
    odd[pl.ds(0, plan.border + 16), :] = jnp.zeros((plan.border + 16, LANES), FLOAT)
    table = layout()
    final = (table["headb"][0] // LANES) // 8 * 8
    odd[pl.ds(final, odd.shape[0] - final), :] = jnp.zeros((odd.shape[0] - final, LANES), FLOAT)


def emit_slots(plan, even, odd, slots, depths):
    rows = plan.rows
    for index in [depth * 8 + number for depth in depths for number in range(8)]:
        start = plan.base(index) // 8 * 8
        if plan.late(index):
            block = odd[pl.ds(start + 8, rows), :]
        else:
            here = pltpu.roll(odd[pl.ds(start + 8, rows), :], 64, 1)
            above = pltpu.roll(odd[pl.ds(start + 7, rows), :], 64, 1)
            block = even[pl.ds(start, rows), :] + jnp.where(lane_iota(rows) < 64, above, here)
        slots[(index // 8, index // 4 % 2, index // 2 % 2, index % 2)] = block.astype(BRAIN)


def dot(left, right, dims=(((1,), (0,)), ((), ()))):
    return lax.dot_general(left, right, dims, preferred_element_type=FLOAT)


def place_table(count, rows, width):
    quarter = width // 4
    omega = 1.0 / 10000.0 ** (np.arange(quarter) / quarter)
    index = np.arange(count)
    across = (index // GRID)[:, None] * omega
    along = (index % GRID)[:, None] * omega
    table = np.zeros((rows, width), np.float32)
    table[:count] = np.concatenate(
        [np.sin(across), np.cos(across), np.sin(along), np.cos(along)], axis=-1
    )
    return table


def split_two(value):
    upper = value.astype(BRAIN)
    return upper, (value - upper.astype(FLOAT)).astype(BRAIN)


def norm_parts(value):
    center = value - jnp.mean(value, axis=-1, keepdims=True)
    spread = lax.rsqrt(jnp.mean(center * center, axis=-1, keepdims=True) + LN_EPS)
    return center * spread, spread


def norm_back(grad, value, gain):
    unit, spread = norm_parts(value)
    d_gain = jnp.sum(grad * unit, axis=0, keepdims=True)
    d_shift = jnp.sum(grad, axis=0, keepdims=True)
    scaled = grad * gain
    middle = jnp.mean(scaled, axis=-1, keepdims=True)
    along = jnp.mean(scaled * unit, axis=-1, keepdims=True)
    return spread * (scaled - middle - unit * along), d_gain, d_shift


def gelu_parts(value):
    half = 0.5 + 0.5 * lax.erf(value * 0.7071067811865476)
    bell = jnp.exp2(value * value * (-0.5 * LOG_TWO_E)) * 0.3989422804014327
    return value * half, half + value * bell


def head_only(value, head, size):
    lane = lax.broadcasted_iota(jnp.int32, value.shape, 1)
    inside = (lane >= head * size) & (lane < (head + 1) * size)
    return jnp.where(inside, value, jnp.zeros_like(value))


def attend(t_ref, chance_ref, stack_ref, usable, width, heads):
    size = width // heads
    rows = t_ref.shape[0]
    query, keys = t_ref[:, pl.ds(0, width)].T, t_ref[:, pl.ds(width, width)]
    values = t_ref[:, pl.ds(2 * width, width)].T
    factor = size ** (-0.5) * LOG_TWO_E
    mixed = []
    for head in range(heads):
        stack_ref[pl.ds(head * rows, rows), :] = head_only(keys, head, size)
    scores = dot(stack_ref[...], query)
    for head in range(heads):
        raw = jnp.where(usable, scores[head * rows : (head + 1) * rows], -1e30)
        top = jnp.max(raw, axis=0, keepdims=True)
        power = jnp.exp2((raw - top) * factor)
        chance = power * (1.0 / jnp.sum(power, axis=0, keepdims=True))
        chance_ref[head] = chance
        mixed.append(dot(values[head * size : (head + 1) * size], chance.astype(BRAIN)))
    return jnp.concatenate(mixed, axis=0).astype(BRAIN).T


def attend_back(d_mixed, t_ref, dt_ref, chance_ref, stack_ref, width, heads):
    size = width // heads
    rows = t_ref.shape[0]
    scale = size ** (-0.5)
    query, keys = t_ref[:, pl.ds(0, width)], t_ref[:, pl.ds(width, width)].T
    values = t_ref[:, pl.ds(2 * width, width)]
    d_query = []
    d_keys = d_values = None
    for head in range(heads):
        stack_ref[pl.ds(head * rows, rows), :] = head_only(values, head, size)
    d_chances = dot(stack_ref[...], d_mixed.T)
    for head in range(heads):
        chance = chance_ref[head]
        d_chance = d_chances[head * rows : (head + 1) * rows]
        along = jnp.sum(chance * d_chance, axis=0, keepdims=True)
        d_scores = (chance * (d_chance - along)).astype(BRAIN)
        part = dot(chance.astype(BRAIN), head_only(d_mixed, head, size))
        d_values = part if d_values is None else d_values + part
        part = dot(d_scores, head_only(query, head, size))
        d_keys = part if d_keys is None else d_keys + part
        d_query.append(dot(keys[head * size : (head + 1) * size], d_scores))
    d_query = (jnp.concatenate(d_query, axis=0) * scale).astype(BRAIN).T
    dt_ref[:, pl.ds(0, width)] = d_query
    dt_ref[:, pl.ds(width, width)] = (d_keys * scale).astype(BRAIN)
    dt_ref[:, pl.ds(2 * width, width)] = d_values.astype(BRAIN)


class Weights:
    def __init__(self, refs):
        self.refs = dict(zip(layout(), refs))

    def __call__(self, name):
        return self.refs[name][...]


def block_open(hidden, keep, weights, prefix):
    width = hidden.shape[1]
    keep["x"][...] = hidden
    unit, unused = norm_parts(hidden)
    normed = (unit * weights(prefix + "ln1g") + weights(prefix + "ln1b")).astype(BRAIN)
    keep["a"][...] = normed
    bias = weights(prefix + "qvb")
    for part in range(3):
        cols = pl.ds(part * width, width)
        value = dot(normed, weights.refs[prefix + "qkv"][:, cols])
        if part != 1:
            value = value + bias[:, (part // 2) * width : (part // 2 + 1) * width]
        keep["t"][:, cols] = value.astype(BRAIN)


def each_group(keep, act):
    count, rows = keep["p"].shape[0], keep["p"].shape[2]
    if count == 1:
        act(0, pl.ds(0, rows))
        return

    @pl.loop(0, count)
    def _(group):
        act(group, pl.ds(pl.multiple_of(group * rows, rows), rows))


def block_middle(hidden, keep, weights, prefix, heads, usable):
    width = hidden.shape[1]

    def mix(group, rows):
        keep["o"][rows, :] = attend(keep["t"].at[rows], keep["p"].at[group], keep["k"], usable, width, heads)

    each_group(keep, mix)
    middle = hidden + (dot(keep["o"][...], weights(prefix + "proj")) + weights(prefix + "projb"))
    keep["m"][...] = middle
    unit, unused = norm_parts(middle)
    second = (unit * weights(prefix + "ln2g") + weights(prefix + "ln2b")).astype(BRAIN)
    keep["b"][...] = second
    inner = dot(second, weights(prefix + "fc1")) + weights(prefix + "fc1b")
    active, slope = gelu_parts(inner)
    keep["s"][...] = slope
    keep["g"][...] = active.astype(BRAIN)


def block_shut(keep, weights, prefix):
    return keep["m"][...] + (dot(keep["g"][...], weights(prefix + "fc2")) + weights(prefix + "fc2b"))


def home_open(grad, keep, weights, prefix):
    d_branch = grad.astype(BRAIN)
    keep["dz"][...] = d_branch
    keep["du"][...] = (dot(d_branch, weights(prefix + "fc2"), PAIR) * keep["s"][...]).astype(BRAIN)


def home_middle(grad, keep, weights, prefix, heads, sums, meanwhile=None):
    width = grad.shape[1]
    d_second = dot(keep["du"][...], weights(prefix + "fc1"), PAIR)
    d_middle, d_gain, d_shift = norm_back(d_second, keep["m"][...], weights(prefix + "ln2g"))
    sums(prefix + "ln2g", d_gain)
    sums(prefix + "ln2b", d_shift)
    d_middle = d_middle + grad
    d_output = d_middle.astype(BRAIN)
    keep["dy"][...] = d_output
    keep["do"][...] = dot(d_output, weights(prefix + "proj"), PAIR).astype(BRAIN)

    def unmix(group, rows):
        if meanwhile is not None:
            meanwhile(group)
        d_mixed = keep["do"][rows, :]
        attend_back(
            d_mixed, keep["t"].at[rows], keep["dt"].at[rows], keep["p"].at[group], keep["k"], width, heads
        )

    each_group(keep, unmix)
    d_normed = dot(keep["dt"][...], weights(prefix + "qkv"), PAIR)
    d_hidden, d_gain, d_shift = norm_back(d_normed, keep["x"][...], weights(prefix + "ln1g"))
    sums(prefix + "ln1g", d_gain)
    sums(prefix + "ln1b", d_shift)
    return d_middle + d_hidden


def kept_shapes(groups, rows, width, hidden, heads):
    every = groups * rows
    return {
        "x": ((every, width), FLOAT),
        "a": ((every, width), BRAIN),
        "t": ((every, 3 * width), BRAIN),
        "p": ((groups, heads, rows, rows), FLOAT),
        "k": ((heads * rows, width), BRAIN),
        "o": ((every, width), BRAIN),
        "m": ((every, width), FLOAT),
        "b": ((every, width), BRAIN),
        "s": ((every, hidden), FLOAT),
        "g": ((every, hidden), BRAIN),
        "dz": ((every, width), BRAIN),
        "du": ((every, hidden), BRAIN),
        "dy": ((every, width), BRAIN),
        "do": ((every, width), BRAIN),
        "dt": ((every, 3 * width), BRAIN),
    }


def kept_scratch(*sizes):
    return [pltpu.VMEM(shape, kind) for shape, kind in kept_shapes(*sizes).values()]


def kept_view(refs):
    return dict(zip(kept_shapes(1, 1, 1, 1, 1), refs))


LAYERS = {
    "fc2": ("g", "dz", "fc2b"),
    "fc1": ("b", "du", "fc1b"),
    "proj": ("o", "dy", "projb"),
    "qkv": ("a", "dt", "qvb"),
}


def block_grads(keep, prefix, names, emit):
    for name in names:
        left, right, bias = LAYERS[name]
        emit(prefix + name, prefix + bias, keep[left][...], keep[right][...])


NORMS = ("ln1g", "ln1b", "ln2g", "ln2b", "encg", "encb", "decg", "decb", "mask")


class Images:
    def __init__(self, place, counts_ref, meta_ref):
        spot = place["B"] * 2 + place["C"]
        self.meta_ref = meta_ref
        self.own = counts_ref[0, 0]
        lane = lane_iota(8)
        row = lax.broadcasted_iota(jnp.int32, (8, LANES), 0)

        def count_of(hub):
            corner = jnp.where((lane == LANES - 1) & (row == 0), meta_ref[hub], 0.0)
            return jnp.sum(corner).astype(jnp.int32)

        one, two = count_of(1), count_of(2)
        from_one = jnp.where(spot == 0, 3, jnp.where(spot == 2, 4, 5))
        from_two = jnp.where(spot == 0, 3, jnp.where(spot == 1, 4, 5))
        use_one = (spot == 2) | ((spot != 1) & (one > 2))
        mine = self.own > 2

        def choose(own, first, second):
            return jnp.where(mine, own, jnp.where(use_one, first, second))

        self.third = choose(2, 3, 4)
        self.third_row = choose(2, from_one, from_two)
        self.third_count = choose(self.own, one, two)
        self.third_meta = choose(0, 1, 2)

    def __call__(self, image):
        last = image == 2
        source = jnp.where(last, self.third, image)
        line = jnp.where(last, self.third_row, image)
        live = jnp.where(last, self.third_count, self.own) > line
        kept = self.meta_ref[jnp.where(last, self.third_meta, 0), pl.ds(line, 1), :][:, :HOME]
        return source, kept, live.astype(FLOAT)


def placement(kept, rows):
    number = lax.broadcasted_iota(jnp.int32, (rows, HOME), 0).astype(FLOAT)
    return (number == kept).astype(FLOAT)


def whole_body(
    plan, counts_ref, keep_ref, x_ref, patches_ref, targets_ref, enc_table, dec_table,
    total_out, *scratch
):
    scratch = list(scratch)

    def take(count):
        taken = scratch[:count]
        del scratch[:count]
        return taken

    names = list(layout())
    slots, seen_ref, tgt_own, tgt_ref, meta_ref, grad_ref, loss_ref = take(7)
    spot_enc, spot_dec, local = take(3)
    line, rolled, pixels, spare, send, recv, hand, taken = take(8)
    even, odd, grad_even, grad_odd, sums_ref, y_hi, y_lo, dy_home, final_all, dpred_all = take(10)
    weights = Weights(take(len(names)))
    enc_refs, dec_refs = take(15), take(15)
    core_in, tree_in, column_in, own_ref, near, far, mine = take(7)
    spread_send, spread_recv, column_send, column_recv = take(4)

    place = position()
    device = index_of(place)
    copies = [
        pltpu.make_async_copy(patches_ref, pixels, local.at[0]),
        pltpu.make_async_copy(enc_table, spot_enc, local.at[1]),
        pltpu.make_async_copy(dec_table, spot_dec, local.at[2]),
        pltpu.make_async_copy(
            targets_ref.at[pl.ds(0, LIVE_CAP - 1)], tgt_own, local.at[3]
        ),
        pltpu.make_async_copy(targets_ref.at[LIVE_CAP - 1], tgt_ref.at[0], local.at[4]),
    ]
    for copy in copies:
        copy.start()
    slots[(place["H"], place["L"], place["B"], place["C"], place["r"])] = own_block(
        plan, device, x_ref, line, rolled
    )
    meet(gates(place, plan))
    sender = Sender(send, recv)
    handing = Handing(place, spare, seen_ref, meta_ref, targets_ref, tgt_ref, hand, taken)

    def choose_images():
        lane = lane_iota(8)
        row = lax.broadcasted_iota(jnp.int32, (8, LANES), 0)
        held = counts_ref[0, 0].astype(FLOAT)
        meta_ref[0] = jnp.where((lane == LANES - 1) & (row == 0), held, -1.0)
        meta_ref[0, pl.ds(0, keep_ref.shape[0]), pl.ds(0, VIS)] = keep_ref[...].astype(FLOAT)
        copies[0].wait()

        def visible(image):
            where = placement(meta_ref[0, pl.ds(image, 1), :][:, :HOME], NP).astype(BRAIN)
            return dot(where, pixels[image], DEEP).astype(BRAIN)

        def prepare(hub):
            for number in range(3):
                spare[number] = visible(3 + number)

        handing.on_hub(prepare)
        handing.start((0, 1))
        for image in range(LIVE_CAP):
            seen_ref[image] = visible(image)
        clear_frames(plan, grad_even, grad_odd)
        sums_ref[...] = jnp.zeros_like(sums_ref)

    early = min(-(-layout()["dec_qkv"][0] // (16 * plan.length)), plan.outer)
    first_values, last_values = range(early), range(early, plan.outer)
    gather = Gather(plan, place, slots, sender, (spread_send, spread_recv))
    frames = Frames(plan, slots, even, odd)

    def spread(values, reach):
        for value in values:
            gather.stage(value, reach)

    def fetch(values, wanted_names):
        for value in values:
            gather.ready(value)
            for index in range(value * 16, value * 16 + 16):
                frames.add(index)
        for name in wanted_names:
            read_param(even, odd, name, weights.refs[name])

    gather.begin()
    gather.roots(choose_images)
    for reach in (0, 1):
        spread(first_values, reach)
        spread(last_values, reach)
    handing.receive((0, 1))
    for copy in copies[1:]:
        copy.wait()
    pick = Images(place, counts_ref, meta_ref)
    visible, begin, wheres, seens, lives = [], [], [], [], []
    for image in range(LIVE_CAP):
        source, kept, live = pick(image)
        where = placement(kept, ROWS)
        wheres.append(where.astype(BRAIN))
        seens.append(jnp.sum(where, axis=1, keepdims=True))
        lives.append(live)
        visible.append(seen_ref[source])
        begin.append(dot(wheres[image], spot_enc[0], DEEP) + dot(wheres[image], spot_enc[1], DEEP))
    visible = jnp.concatenate(visible, axis=0)
    begin = jnp.concatenate(begin, axis=0)
    spread(first_values, 2)
    spread(last_values, 2)
    handing.start((2,))
    divide = names.index("dec_qkv")
    fetch(first_values, names[:divide])
    order = {name: number for number, name in enumerate(names)}

    def add_sum(name, value):
        sums_ref[pl.ds(order[name], 1), pl.ds(0, value.shape[1])] += value

    enc_rows = LIVE_CAP * HOME
    enc = kept_view(enc_refs)
    down = lax.broadcasted_iota(jnp.int32, (enc_rows, enc_rows), 0)
    over = lax.broadcasted_iota(jnp.int32, (enc_rows, enc_rows), 1)
    usable = (down // HOME == over // HOME) & (down % HOME < VIS)
    first_in = dot(visible, weights("patch")) + weights("patchb") + begin
    block_open(first_in, enc, weights, "enc_")
    block_middle(first_in, enc, weights, "enc_", HEADS, usable)
    encoded = block_shut(enc, weights, "enc_")
    unit, unused = norm_parts(encoded)
    encoder_out = (unit * weights("encg") + weights("encb")).astype(BRAIN)
    embedded = dot(encoder_out, weights("embed")) + weights("embedb")
    upper, lower = split_two(embedded)
    for image in range(LIVE_CAP):
        y_hi[image] = upper[image * HOME : (image + 1) * HOME]
        y_lo[image] = lower[image * HOME : (image + 1) * HOME]
    fetch(last_values, names[divide:])
    view = grad_odd.at[pl.ds(8, plan.frame_rows)]
    real = lax.broadcasted_iota(jnp.int32, (ROWS, 1), 0) < NP
    usable_dec = lax.broadcasted_iota(jnp.int32, (ROWS, ROWS), 0) < NP

    dec = kept_view(dec_refs)
    dec_rows = [pl.ds(image * ROWS, ROWS) for image in range(LIVE_CAP)]
    def unseen(image):
        return 1.0 - seens[image]

    grid_in = []
    for image in range(LIVE_CAP):
        where = wheres[image]
        value = dot(where, y_hi[image]) + dot(where, y_lo[image])
        grid_in.append(value + unseen(image) * weights("mask") + spot_dec[...])
    grid_in = jnp.concatenate(grid_in, axis=0)
    block_open(grid_in, dec, weights, "dec_")
    block_middle(grid_in, dec, weights, "dec_", DHEADS, usable_dec)
    decoded = block_shut(dec, weights, "dec_")
    unit, unused = norm_parts(decoded)
    final_all[...] = (unit * weights("decg") + weights("decb")).astype(BRAIN)
    handing.receive((2,))
    total = jnp.zeros((1, PIX), FLOAT)
    for image in range(LIVE_CAP):
        predicted = dot(final_all[dec_rows[image], :], weights("head")) + weights("headb")
        weight = jnp.where(real, (1.0 - 0.9 * seens[image]) * lives[image], 0.0)
        wanted = tgt_ref[pick.third - 2] if image == LIVE_CAP - 1 else tgt_own[image]
        error = predicted[:NP] - wanted.astype(FLOAT)
        weighted = error * weight[:NP]
        total = total + jnp.sum(weighted * error, axis=0, keepdims=True)
        dpred_all[pl.ds(image * ROWS, NP), :] = (weighted * (2.0 / PIX)).astype(BRAIN)
        dpred_all[pl.ds(image * ROWS + NP, ROWS - NP), :] = jnp.zeros((ROWS - NP, PIX), BRAIN)
    d_final = dot(dpred_all[...], weights("head"), PAIR)
    d_decoded, d_gain, d_shift = norm_back(d_final, decoded, weights("decg"))
    add_sum("decg", d_gain)
    add_sum("decb", d_shift)
    home_open(d_decoded, dec, weights, "dec_")
    loss_ref[0] = jnp.sum(total) * (1.0 / PIX)

    def emit(name, bias, left, right):
        ones = jnp.ones((16, right.shape[0]), BRAIN)
        summed = dot(ones, right)[0:1]
        if bias.endswith("qvb"):
            width = summed.shape[1] // 3
            summed = jnp.concatenate([summed[:, :width], summed[:, 2 * width :]], axis=1)
        write_grad(grad_even, view, bias, lambda start, size: summed[:, start : start + size])
        turned = left.T
        write_grad(grad_even, view, name, lambda start, size: dot(turned, right[:, start : start + size]))

    def emit_norms(wanted_names):
        for name in wanted_names:
            row = pl.ds(order[name], 1)
            write_grad(grad_even, view, name, lambda start, size, row=row: sums_ref[row, pl.ds(start, size)])

    reducer = Reducer(
        plan, place, grad_ref, core_in, tree_in, column_in, own_ref, sender, (column_send, column_recv)
    )
    floors = [plan.depths_from(name) for name in ("dec_fc2", "embed", "enc_fc1")]
    waves = [range(low, high) for low, high in zip(floors + [0], [plan.depths] + floors)]

    def leave(wave):
        emit_slots(plan, grad_even, grad_odd, grad_ref, waves[wave])
        for depth in waves[wave]:
            reducer.share(depth)

    def collect(wave, reach):
        for depth in waves[wave]:
            reducer.stage(depth, reach)

    emit("head", "headb", final_all[...], dpred_all[...])
    block_grads(dec, "dec_", ("fc2",), emit)
    emit_norms(("decg", "decb"))
    leave(0)
    block_grads(dec, "dec_", ("fc1",), emit)

    def meanwhile(group):
        @pl.when(group == 1)
        def _():
            collect(0, 1)

        @pl.when(group == 2)
        def _():
            collect(0, 0)

    d_grid = home_middle(d_decoded, dec, weights, "dec_", DHEADS, add_sum, meanwhile)
    d_mask = jnp.zeros((1, E), FLOAT)
    for image in range(LIVE_CAP):
        part = d_grid[image * ROWS : (image + 1) * ROWS]
        d_mask = d_mask + jnp.sum(unseen(image) * part, axis=0, keepdims=True)
        dy_home[image] = dot(wheres[image], part.astype(BRAIN), DEEP).astype(BRAIN)
    add_sum("mask", d_mask)
    collect(0, -1)
    block_grads(dec, "dec_", ("proj", "qkv"), emit)
    d_embedded = dy_home[...].reshape(enc_rows, E)
    emit("embed", "embedb", encoder_out, d_embedded)
    emit_norms(("mask", "dec_ln1g", "dec_ln1b", "dec_ln2g", "dec_ln2b"))
    leave(1)

    d_seen = dot(d_embedded, weights("embed"), PAIR).astype(BRAIN).astype(FLOAT)
    d_encoded, d_gain, d_shift = norm_back(d_seen, encoded, weights("encg"))
    add_sum("encg", d_gain)
    add_sum("encb", d_shift)
    home_open(d_encoded, enc, weights, "enc_")
    block_grads(enc, "enc_", ("fc2", "fc1"), emit)
    emit_norms(("encg", "encb"))
    leave(2)
    collect(1, 1)
    d_first = home_middle(d_encoded, enc, weights, "enc_", HEADS, add_sum).astype(BRAIN)
    collect(2, 1)
    collect(1, 0)
    emit("patch", "patchb", visible, d_first)
    block_grads(enc, "enc_", ("proj", "qkv"), emit)
    emit_norms(("enc_ln1g", "enc_ln1b", "enc_ln2g", "enc_ln2b"))
    leave(3)
    collect(2, 0)
    collect(1, -1)
    collect(3, 1)
    collect(2, -1)
    collect(3, 0)
    collect(3, -1)
    reducer.finish()
    pending = finish_body(
        plan, place, counts_ref, loss_ref, own_ref, total_out, rolled, near, far, mine, sender
    )
    gather.close()
    reducer.close()
    handing.finish((0, 1, 2))
    for copy in pending:
        copy.wait_send()


def weight_scratch():
    shapes = []
    for name, (offset, shape) in layout().items():
        if len(shape) == 1:
            shapes.append(pltpu.VMEM((1, *shape), FLOAT))
        else:
            shapes.append(pltpu.VMEM(shape, BRAIN))
    return shapes


def copies_used(plan):
    spread = len(plan.parts) * plan.outer * (7 + 4)
    home = len(plan.halves) * plan.depths * (1 + 3)
    return spread + home + 7 + plan.depths


def whole_step(counts, keep, master, patches, targets, plan):
    outer, depths, rows, lines = plan.outer, plan.depths, plan.rows, plan.lines
    vmem = pl.BlockSpec(memory_space=pltpu.VMEM)
    smem = pl.BlockSpec(memory_space=pltpu.SMEM)
    far = pl.BlockSpec(memory_space=pl.ANY)
    table = place_table(NP, ROWS, D)
    upper = table.astype(BRAIN)
    spot_enc = jnp.asarray(np.stack([upper, (table - upper.astype(np.float32)).astype(BRAIN)]))
    spot_dec = jnp.asarray(place_table(NP, ROWS, E))
    block = pltpu.VMEM((outer, 2, 2, 2, 2, rows, LANES), BRAIN)
    dma = pltpu.SemaphoreType.DMA
    copies = copies_used(plan)
    return pl.pallas_call(
        functools.partial(whole_body, plan),
        out_shape=jax.ShapeDtypeStruct((lines + 8, LANES), FLOAT),
        in_specs=[smem, vmem, vmem, far, far, far, far],
        out_specs=vmem,
        scratch_shapes=[
            block,
            pltpu.VMEM((5, HOME, PIX), BRAIN),
            pltpu.VMEM((LIVE_CAP - 1, NP, PIX), BRAIN),
            pltpu.VMEM((3, NP, PIX), BRAIN),
            pltpu.VMEM((3, 8, LANES), FLOAT),
            pltpu.VMEM((depths, 2, 2, 2, rows, LANES), BRAIN),
            pltpu.SMEM((1,), FLOAT),
            pltpu.VMEM(spot_enc.shape, BRAIN),
            pltpu.VMEM(spot_dec.shape, FLOAT),
            dma((5,)),
            pltpu.VMEM((lines * LANES,), FLOAT),
            pltpu.VMEM((rows + 8, LANES), FLOAT),
            pltpu.VMEM(patches.shape, BRAIN),
            pltpu.VMEM((3, HOME, PIX), BRAIN),
            dma((copies,)),
            dma((copies,)),
            dma((2, 3, 3)),
            dma((2, 3)),
            pltpu.VMEM((plan.border + 8, LANES), FLOAT),
            pltpu.VMEM((plan.frame_rows, LANES), FLOAT),
            pltpu.VMEM((plan.border + rows, LANES), FLOAT),
            pltpu.VMEM((plan.frame_rows + 8, LANES), FLOAT),
            pltpu.VMEM((48, E), FLOAT),
            pltpu.VMEM((LIVE_CAP, HOME, E), BRAIN),
            pltpu.VMEM((LIVE_CAP, HOME, E), BRAIN),
            pltpu.VMEM((LIVE_CAP, HOME, E), BRAIN),
            pltpu.VMEM((LIVE_CAP * ROWS, E), BRAIN),
            pltpu.VMEM((LIVE_CAP * ROWS, PIX), BRAIN),
            *weight_scratch(),
            *kept_scratch(1, LIVE_CAP * HOME, D, FF, HEADS),
            *kept_scratch(LIVE_CAP, ROWS, E, DFF, DHEADS),
            pltpu.VMEM((depths, 2, 2, rows, LANES), BRAIN),
            pltpu.VMEM((depths, 3, rows, LANES), BRAIN),
            pltpu.VMEM((depths, rows, LANES), BRAIN),
            pltpu.VMEM((rows, LANES), FLOAT),
            pltpu.VMEM((8, 8, LANES), FLOAT),
            pltpu.VMEM((depths, 8, LANES), FLOAT),
            pltpu.VMEM((2, 8, LANES), FLOAT),
            dma((outer, len(plan.parts))),
            dma((outer, len(plan.parts))),
            dma((depths, len(plan.halves))),
            dma((depths, len(plan.halves))),
        ],
        compiler_params=pltpu.CompilerParams(
            collective_id=0, has_side_effects=True, vmem_limit_bytes=62 << 20
        ),
    )(counts, keep, master, patches, targets, spot_enc, spot_dec)


def on_device(patches, targets, keep, counts, step, master, first, second):
    plan = Plan(master.shape[0], lax.axis_size(("dp", "rep")))
    total = whole_step(counts, keep, master, patches, targets, plan)
    outs = update(step, total, master, first, second, plan)
    return (*outs[:4], outs[4].reshape(()), outs[5].reshape(()))


def solution(mesh):
    return jax.shard_map(
        on_device,
        mesh=mesh,
        in_specs=(
            P(("dp", "rep"), None, None),
            P(("dp", "rep"), None, None),
            P(("dp", "rep"), None),
            P("dp", "rep"),
            P(),
            P(("dp", "rep")),
            P(("dp", "rep")),
            P(("dp", "rep")),
        ),
        out_specs=(
            P(("dp", "rep")),
            P(("dp", "rep")),
            P(("dp", "rep")),
            P(("dp", "rep")),
            P(),
            P(),
        ),
        check_vma=False,
    )
```

```python
import functools
import itertools
import math

import jax
import jax.numpy as jnp
import numpy as np
from jax import lax
from jax.experimental import pallas as pl
from jax.experimental.pallas import tpu as pltpu
from jax.sharding import PartitionSpec as P

D = 192
HEADS = 3
FF = 768
E = 256
DHEADS = 8
DFF = 1024
PIX = 768
GRID = 14
VIS = 49
NP = 196

FLOAT = jnp.float32
BRAIN = jnp.bfloat16
CLIP = 0.05
BETA_ONE = 0.5
BETA_TWO = 0.5
LEARN = 0.01
DECAY = 0.05
EPSILON = 1e-08
LN_EPS = 1e-06

ROWS = 208
HOME = 64
LIVE_CAP = 3
PAIR = ((1,), (1,)), ((), ())
DEEP = ((0,), (0,)), ((), ())
LOG_TWO_E = 1.4426950408889634


def block_table(prefix, width, hidden, proj_fan, rate):
    return [
        (prefix + "ln1g", (width,), "gain", 1, rate),
        (prefix + "ln1b", (width,), "bias", 1, rate),
        (prefix + "qkv", (width, 3 * width), "matrix", width, rate),
        (prefix + "qvb", (2 * width,), "bias", 1, rate),
        (prefix + "proj", (width, width), "matrix", proj_fan, rate),
        (prefix + "projb", (width,), "bias", 1, rate),
        (prefix + "ln2g", (width,), "gain", 1, rate),
        (prefix + "ln2b", (width,), "bias", 1, rate),
        (prefix + "fc1", (width, hidden), "matrix", width, rate),
        (prefix + "fc1b", (hidden,), "bias", 1, rate),
        (prefix + "fc2", (hidden, width), "matrix", hidden, rate),
        (prefix + "fc2b", (width,), "bias", 1, rate),
    ]


def param_table():
    table = [("patch", (PIX, D), "matrix", PIX, 0.75), ("patchb", (D,), "bias", 1, 0.75)]
    table = table + block_table("enc_", D, FF, D // 4, 0.9)
    table = table + [
        ("encg", (D,), "gain", 1, 1.0),
        ("encb", (D,), "bias", 1, 1.0),
        ("embed", (D, E), "matrix", D, 1.0),
        ("embedb", (E,), "bias", 1, 1.0),
        ("mask", (E,), "token", 1, 1.0),
    ]
    table = table + block_table("dec_", E, DFF, E // 8, 1.0)
    table = table + [
        ("decg", (E,), "gain", 1, 1.0),
        ("decb", (E,), "bias", 1, 1.0),
        ("head", (E, PIX), "matrix", E, 1.0),
        ("headb", (PIX,), "bias", 1, 1.0),
    ]
    return table


MESH = pl.DeviceIdType.MESH
LANES = 128


def layout():
    table = {}
    offset = 0
    for name, shape, kind, fan, rate in param_table():
        table[name] = (offset, shape)
        offset += math.prod(shape)
    return table


class Plan:
    def __init__(self, length, count):
        self.length = length
        self.count = count
        self.outer = count // 16
        self.lines = -(-length // LANES // 8 * 8)
        self.rows = -(-(7 + (2 * LANES - 2 + length) // LANES) // 16) * 16
        self.split = layout()["embed"][0]
        if self.outer > 2:
            self.parts, self.orders = ((0, self.rows),), ("LCB",)
        else:
            half = self.rows // 32 * 16
            self.parts = ((0, half), (half, self.rows - half))
            self.orders = ("LCB", "BCL")
        self.first_late = -(-self.split // length)
        self.depths = count // 8
        pieces = 4 if self.outer == 2 else 1
        cuts = [self.rows // 16 * number // pieces * 16 for number in range(pieces + 1)]
        self.halves = tuple((low, high - low) for low, high in zip(cuts, cuts[1:]))
        self.ways = ("CB", "BC", "CB", "BC")[:pieces]
        last = self.first_late - 1
        self.border = (self.base(last) + self.used(last) + 1 + 7) // 8 * 8 + 8
        self.frame_rows = (length * count // LANES + 7) // 8 * 8 + self.rows + 16

    def depths_from(self, name):
        return min(-(-layout()[name][0] // (8 * self.length)), self.depths)

    def late(self, index):
        return index >= self.first_late

    def start(self, index):
        return index * self.length - (64 if self.late(index) else 0)

    def base(self, index):
        return self.start(index) // LANES

    def lead(self, index):
        return self.start(index) % LANES

    def used(self, index):
        return (self.lead(index) + self.length + LANES - 1) // LANES

    def own(self, index):
        start = index * self.length - jnp.where(index >= self.first_late, 64, 0)
        return lax.rem(lax.div(start, LANES), 8), lax.rem(start, LANES)


def spot_of(index):
    return (index // 16, index // 8 % 2, index // 4 % 2, index // 2 % 2, index % 2)


def position():
    chip = lax.axis_index("dp")
    core = lax.axis_index("rep")
    return {"H": chip // 8, "L": chip // 4 % 2, "B": chip // 2 % 2, "C": chip % 2, "r": core}


def index_of(place):
    return (((place["H"] * 2 + place["L"]) * 2 + place["B"]) * 2 + place["C"]) * 2 + place["r"]


def device_of(place):
    return (((place["H"] * 2 + place["L"]) * 2 + place["B"]) * 2 + place["C"], place["r"])


def moved(place, dim, value):
    changed = dict(place)
    changed[dim] = value
    return changed


def flipped(place, dims):
    changed = dict(place)
    for dim in dims:
        changed[dim] = 1 - place[dim]
    return changed


def meet(places):
    barrier = pltpu.get_barrier_semaphore()
    for place in places:
        pl.semaphore_signal(barrier, inc=1, device_id=device_of(place), device_id_type=MESH)
    pl.semaphore_wait(barrier, len(places))


def partners(place, plan):
    group = []
    for number in range(1, 8):
        group.append(flipped(place, [dim for bit, dim in enumerate("rCB") if number >> bit & 1]))
    depth = depth_of(place)
    column = [at_depth(place, lax.rem(depth + step, plan.depths)) for step in range(1, plan.depths)]
    return group, column


def at_depth(place, depth):
    return {**place, "H": depth // 2, "L": depth % 2}


def depth_of(place):
    return place["H"] * 2 + place["L"]


def gates(place, plan):
    near = [flipped(place, dims) for dims in ("r", "L", "B", "C", "BC")]
    steps = range(1, plan.outer)
    return near + [moved(place, "H", lax.rem(place["H"] + step, plan.outer)) for step in steps]


def branches(order):
    nodes = []
    for count in range(len(order) + 1):
        for dims in itertools.combinations(order, count):
            reach = max([order.index(dim) for dim in dims], default=-1)
            nodes.append((reach, count, "".join(dims), order[reach + 1 :]))
    nodes.sort(key=lambda node: node[:2])
    return [(dims, onward) for reach, count, dims, onward in nodes]


class Copy:
    def __init__(self, recipe, send, recv, number):
        self.recipe, self.send, self.recv, self.number = recipe, send, recv, number

    def make(self):
        source, target, place = self.recipe()
        return pltpu.make_async_remote_copy(
            src_ref=source,
            dst_ref=target,
            send_sem=self.send.at[self.number],
            recv_sem=self.recv.at[self.number],
            device_id=device_of(place),
            device_id_type=MESH,
        )

    def start(self):
        self.make().start()

    def wait_recv(self):
        self.make().wait_recv()

    def wait_send(self):
        self.make().wait_send()


class Sender:
    def __init__(self, send, recv):
        self.send, self.recv, self.used = send, recv, 0

    def plan(self, recipe):
        copy = Copy(recipe, self.send, self.recv, self.used)
        self.used += 1
        return copy

    def start(self, recipe):
        copy = self.plan(recipe)
        copy.start()
        return copy


def lane_iota(rows):
    return lax.broadcasted_iota(jnp.int32, (rows, LANES), 1)


HUBS = (1, 2)


def others_of(hub):
    return [spot for spot in range(4) if spot != hub]


def hand_over(place, hub, number, pairs, hand, taken):
    other = others_of(hub)[number]
    target = {**place, "B": other // 2, "C": other % 2}
    return [
        pltpu.make_async_remote_copy(
            src_ref=source,
            dst_ref=to,
            send_sem=hand.at[hub - 1, number, kind],
            recv_sem=taken.at[hub - 1, kind],
            device_id=device_of(target),
            device_id_type=MESH,
        )
        for kind, (source, to) in pairs.items()
    ]


class Handing:
    def __init__(self, place, spare, seen_ref, meta_ref, targets_ref, tgt_ref, hand, taken):
        self.place, self.hand, self.taken = place, hand, taken
        self.spot = place["B"] * 2 + place["C"]
        self.refs = (spare, seen_ref, meta_ref, targets_ref, tgt_ref)

    def copies(self, hub, number, kinds):
        spare, seen_ref, meta_ref, targets_ref, tgt_ref = self.refs
        pairs = {
            0: (spare.at[number], seen_ref.at[2 + hub]),
            1: (meta_ref.at[0], meta_ref.at[hub]),
            2: (targets_ref.at[3 + number], tgt_ref.at[hub]),
        }
        pairs = {kind: pairs[kind] for kind in kinds}
        return hand_over(self.place, hub, number, pairs, self.hand, self.taken)

    def on_hub(self, act):
        for hub in HUBS:

            @pl.when(self.spot == hub)
            def _(hub=hub):
                act(hub)

    def start(self, kinds):
        def act(hub):
            for number in range(3):
                for copy in self.copies(hub, number, kinds):
                    copy.start()

        self.on_hub(act)

    def receive(self, kinds):
        for hub in HUBS:

            @pl.when(self.spot != hub)
            def _(hub=hub):
                for copy in self.copies(hub, 0, kinds):
                    copy.wait_recv()

    def finish(self, kinds):
        def act(hub):
            for number in range(3):
                for copy in self.copies(hub, number, kinds):
                    copy.wait_send()

        self.on_hub(act)


def own_block(plan, device, x_ref, line, rolled):
    rows, lines = plan.rows, plan.lines
    skip, lead = plan.own(device)
    line[...] = jnp.zeros_like(line)
    line[pl.ds(0, plan.length)] = x_ref[...]
    turned = pltpu.roll(line[...].reshape(lines, LANES), lead, 1)
    rolled[...] = jnp.zeros_like(rolled)
    rolled[pl.ds(8 + skip, lines), :] = turned
    upper, lower = rolled[pl.ds(8, rows), :], rolled[pl.ds(7, rows), :]
    return jnp.where(lane_iota(rows) >= lead, upper, lower).astype(BRAIN)


class Gather:
    def __init__(self, plan, place, out_ref, sender, columns):
        self.plan, self.place, self.out_ref, self.sender, self.columns = plan, place, out_ref, sender, columns
        self.flights, self.onwards, self.siblings = {}, [], {}

    def region(self, value, part, fixed, free=""):
        start, size = self.plan.parts[part]
        index = [value]
        for dim in "LBC":
            if dim in free:
                index.append(pl.ds(0, 2))
            else:
                index.append(1 - self.place[dim] if dim in fixed else self.place[dim])
        return self.out_ref.at[(*index, self.place["r"], pl.ds(start, size))]

    def column(self, source, part, target):
        send, recv = self.columns
        ref = self.region(source, part, "")
        return pltpu.make_async_remote_copy(
            src_ref=ref,
            dst_ref=ref,
            send_sem=send.at[target, part],
            recv_sem=recv.at[source, part],
            device_id=device_of(moved(self.place, "H", target)),
            device_id_type=MESH,
        )

    def over_column(self, act):
        high = self.place["H"]
        for target in range(self.plan.outer):

            @pl.when(high != target)
            def _(target=target):
                for part in range(len(self.plan.parts)):
                    act(self.column(high, part, target))

    def begin(self):
        self.over_column(lambda copy: copy.start())

    def roots(self, meanwhile):
        plan, place = self.plan, self.place
        copies = {}
        for value in range(plan.outer):
            copies[value] = []
            for part, order in enumerate(plan.orders):
                copies[value].append(self.spread(value, part, "", order) + [self.give(value, part, -1)])

        for value, groups in copies.items():

            @pl.when(place["H"] == value)
            def _(groups=groups):
                for group in groups:
                    for copy in group:
                        copy.start()

        meanwhile()
        for value, groups in copies.items():

            @pl.when(place["H"] != value)
            def _(value=value, groups=groups):
                for part, group in enumerate(groups):
                    self.column(value, part, place["H"]).wait_recv()
                    for copy in group:
                        copy.start()

    def spread(self, value, part, dims, onward):
        def recipe(dim):
            source = self.region(value, part, dims)
            return source, source, flipped(self.place, dim)

        copies = []
        for dim in onward:
            copy = self.sender.plan(functools.partial(recipe, dim))
            self.flights[value, part, frozenset(dims + dim)] = copy
            copies.append(copy)
        self.onwards += copies
        return copies

    def give(self, value, part, reach):
        order = self.plan.orders[part]

        def recipe():
            source = self.region(value, part, order[reach] if reach >= 0 else "", order[: max(reach, 0)])
            return source, source, flipped(self.place, "r")

        copy = self.sender.plan(recipe)
        self.siblings.setdefault(value, []).append(copy)
        return copy

    def stage(self, value, reach):
        plan = self.plan
        trees = []
        for order in plan.orders:
            trees.append([node for node in branches(order) if node[0] and reach == order.index(node[0][-1])])
        for nodes in zip(*trees):
            for part, (dims, onward) in enumerate(nodes):
                self.flights.pop((value, part, frozenset(dims))).wait_recv()
                for copy in self.spread(value, part, dims, onward):
                    copy.start()
        for part in range(len(plan.orders)):
            self.give(value, part, reach).start()

    def ready(self, value):
        for copy in self.siblings[value]:
            copy.wait_recv()

    def close(self):
        self.over_column(lambda copy: copy.wait_send())
        for copies in [self.onwards] + list(self.siblings.values()):
            for copy in copies:
                copy.wait_send()


class Reducer:
    def __init__(self, plan, place, grad_ref, core_in, tree_in, column_in, own_ref, sender, columns):
        self.plan, self.place, self.sender = plan, place, sender
        self.grad_ref, self.core_in, self.tree_in = grad_ref, core_in, tree_in
        self.column_in, self.own_ref, self.columns = column_in, own_ref, columns
        self.cores = {}
        self.pending = []
        self.trees = [branches(order) for order in plan.ways]
        self.flights = {}

    def share(self, value):
        place = self.place

        def recipe(start, size):
            whole = (value, pl.ds(0, 2), pl.ds(0, 2))
            span = pl.ds(start, size)
            return (
                self.grad_ref.at[(*whole, 1 - place["r"], span)],
                self.core_in.at[(*whole, span)],
                flipped(place, "r"),
            )

        for part, (start, size) in enumerate(self.plan.halves):
            copy = self.sender.start(functools.partial(recipe, start, size))
            self.cores[value, part] = copy
            self.pending.append(copy)

    def stage(self, value, reach):
        plan, place = self.plan, self.place
        steps = []
        for part in range(len(plan.halves)):
            order = plan.ways[part]
            nodes = [
                (dims, onward)
                for dims, onward in reversed(self.trees[part])
                if (order.index(dims[-1]) if dims else -1) == reach
            ]
            steps.append([(part, *node) for node in nodes])
        for group in zip(*steps):
            for part, dims, onward in group:
                self.node(value, part, dims, onward)

    def node(self, value, part, dims, onward):
        plan, place = self.plan, self.place
        start, size = plan.halves[part]
        span = pl.ds(start, size)
        if (value, part) in self.cores:
            self.cores.pop((value, part)).wait_recv()
        for dim in onward:
            self.flights.pop((value, part, frozenset(dims + dim))).wait_recv()
        index = [value] + [1 - place[dim] if dim in dims else place[dim] for dim in "BC"]
        total = self.grad_ref[(*index, place["r"], span)].astype(FLOAT)
        total = total + self.core_in[(*index, span)].astype(FLOAT)

        def number(dims):
            return sum(1 << "BC".index(dim) for dim in dims) - 1

        for dim in onward:
            total = total + self.tree_in[value, number(dims + dim), span].astype(FLOAT)

        def spot():
            index = [value] + [1 - place[dim] if dim in dims else place[dim] for dim in "BC"]
            return self.grad_ref.at[(*index, place["r"], span)]

        def recipe():
            return spot(), self.tree_in.at[value, number(dims), span], flipped(place, dims[-1])

        if dims:
            spot()[...] = total.astype(BRAIN)
            copy = self.sender.start(recipe)
            self.flights[value, part, frozenset(dims)] = copy
            self.pending.append(copy)
            return
        depth = depth_of(place)

        @pl.when(depth == value)
        def _():
            self.own_ref[span, :] = total

        @pl.when(depth != value)
        def _():
            spot()[...] = total.astype(BRAIN)
            self.column(value, part).start()

    def column(self, value, part):
        plan, place = self.plan, self.place
        start, size = plan.halves[part]
        send, recv = self.columns
        index = (value, place["B"], place["C"], place["r"], pl.ds(start, size))
        return pltpu.make_async_remote_copy(
            src_ref=self.grad_ref.at[index],
            dst_ref=self.column_in.at[depth_of(place), pl.ds(start, size)],
            send_sem=send.at[value, part],
            recv_sem=recv.at[depth_of(place), part],
            device_id=device_of(at_depth(place, value)),
            device_id_type=MESH,
        )

    def arrival(self, source, part):
        plan, place = self.plan, self.place
        start, size = plan.halves[part]
        send, recv = self.columns
        return pltpu.make_async_remote_copy(
            src_ref=self.own_in(part),
            dst_ref=self.column_in.at[source, pl.ds(start, size)],
            send_sem=send.at[source, part],
            recv_sem=recv.at[source, part],
            device_id=device_of(at_depth(place, source)),
            device_id_type=MESH,
        )

    def own_in(self, part):
        place = self.place
        start, size = self.plan.halves[part]
        index = (0, place["B"], place["C"], place["r"], pl.ds(start, size))
        return self.grad_ref.at[index]

    def finish(self):
        plan, place = self.plan, self.place
        for part, (start, size) in enumerate(plan.halves):
            for source in range(plan.depths):

                @pl.when(depth_of(place) != source)
                def _(part=part, source=source, start=start, size=size):
                    self.arrival(source, part).wait_recv()
                    span = pl.ds(start, size)
                    self.own_ref[span, :] += self.column_in[source, span].astype(FLOAT)

    def close(self):
        plan, place = self.plan, self.place
        for copy in self.pending:
            copy.wait_send()
        for part in range(len(plan.halves)):
            for value in range(plan.depths):

                @pl.when(depth_of(place) != value)
                def _(part=part, value=value):
                    self.column(value, part).wait_send()


def finish_body(plan, place, held_ref, loss_ref, own_ref, total_out, turned, near, far, mine, sender):
    rows, lines = plan.rows, plan.lines
    group, column = partners(place, plan)
    skip, lead = plan.own(index_of(place))
    position_in = lax.broadcasted_iota(jnp.int32, (lines, LANES), 0) * LANES + lane_iota(lines)
    shift = lax.rem(LANES - lead, LANES)
    turned[pl.ds(0, rows), :] = pltpu.roll(own_ref[...], shift, 1)
    here, below = turned[pl.ds(skip, lines), :], turned[pl.ds(skip + 1, lines), :]
    total = jnp.where(lane_iota(lines) < LANES - lead, here, below)
    total = jnp.where(position_in < plan.length, total, 0.0)
    squares = jnp.sum(total * total)
    lane = lane_iota(8)
    stats = jnp.where(lane == 0, squares, 0.0)
    stats = jnp.where(lane == 1, held_ref[0, 0].astype(FLOAT), stats)
    mine[0] = jnp.where(lane == 2, loss_ref[0], stats)
    count = len(group) + 1
    spot = lax.rem(index_of(place), count)
    near[spot] = mine[0]
    nears = [
        sender.start(functools.partial(lambda other: (mine.at[0], near.at[spot], other), other))
        for other in group
    ]
    total_out[pl.ds(0, lines), :] = total
    for copy in nears:
        copy.wait_recv()
    together = near[0]
    for other in range(1, count):
        together = together + near[other]
    depth = depth_of(place)
    far[depth] = together
    mine[1] = together
    fars = [
        sender.start(functools.partial(lambda other: (mine.at[1], far.at[depth], other), other))
        for other in column
    ]
    for copy in fars:
        copy.wait_recv()
    whole = far[0]
    for other in range(1, plan.depths):
        whole = whole + far[other]
    row = whole[0:1, :]
    lane = lane[0:1]

    def across(number):
        return jnp.full((1, LANES), jnp.sum(jnp.where(lane == number, row, 0.0)))

    weights = across(1) * (0.1 * VIS + (NP - VIS))
    total_out[pl.ds(lines, 1), :] = across(2) / weights
    total_out[pl.ds(lines + 1, 1), :] = jnp.sqrt(across(0)) / weights
    total_out[pl.ds(lines + 2, 1), :] = weights
    return nears + fars


def in_segments(index, segments):
    inside = None
    for start, stop in segments:
        here = (index >= start) & (index < stop)
        inside = here if inside is None else inside | here
    return inside


def matrix_segments():
    found = []
    for name, shape, kind, fan, rate in param_table():
        if kind == "matrix":
            start = layout()[name][0]
            found.append((start, start + math.prod(shape)))
    return found


def update_body(
    plan, step_ref, total_ref, master_ref, first_ref, second_ref,
    master_out, first_out, second_out, copy_out, loss_out, norm_out, line
):
    rows, length = plan.lines, plan.length
    device = lax.axis_index("dp") * 2 + lax.axis_index("rep")
    position_in = lax.broadcasted_iota(jnp.int32, (rows, LANES), 0) * LANES + lane_iota(rows)
    flat = position_in + device * length
    table = layout()
    early, late = table["enc_ln1g"][0], table["encg"][0]
    rate_part = jnp.where(flat < early, 0.75, jnp.where(flat < late, 0.9, 1.0))
    decay_part = jnp.where(in_segments(flat, matrix_segments()), DECAY, 0.0)
    line[...] = jnp.zeros_like(line)
    line[pl.ds(0, length)] = master_ref[...]
    master = line[...].reshape(rows, LANES)
    line[pl.ds(0, length)] = first_ref[...]
    first = line[...].reshape(rows, LANES)
    line[pl.ds(0, length)] = second_ref[...]
    second = line[...].reshape(rows, LANES)
    norms = total_ref[pl.ds(rows + 1, 1), :]
    loss_out[0, 0] = jnp.max(total_ref[pl.ds(rows, 1), :])
    norm_out[0, 0] = jnp.max(norms)
    gradient = total_ref[pl.ds(0, rows), :] / total_ref[pl.ds(rows + 2, 1), :]
    clipped = gradient * jnp.minimum(1.0, CLIP / norms)
    fade = 1.0 / jnp.full((1, LANES), lax.shift_left(1, step_ref[0]).astype(FLOAT))
    new_first = BETA_ONE * first + (1.0 - BETA_ONE) * clipped
    new_second = BETA_TWO * second + (1.0 - BETA_TWO) * clipped * clipped
    first_hat = new_first / (1.0 - fade)
    second_hat = new_second / (1.0 - fade)
    new_master = master - LEARN * rate_part * (
        first_hat / (jnp.sqrt(second_hat) + EPSILON) + decay_part * master
    )
    master_out[...] = new_master.reshape(rows * LANES)[:length]
    first_out[...] = new_first.reshape(rows * LANES)[:length]
    second_out[...] = new_second.reshape(rows * LANES)[:length]
    copy_out[...] = new_master.reshape(rows * LANES)[:length].astype(BRAIN)


def update(step, total, master, first, second, plan):
    vmem = pl.BlockSpec(memory_space=pltpu.VMEM)
    smem = pl.BlockSpec(memory_space=pltpu.SMEM)
    flat = jax.ShapeDtypeStruct((plan.length,), FLOAT)
    single = jax.ShapeDtypeStruct((1, 1), FLOAT)
    return pl.pallas_call(
        functools.partial(update_body, plan),
        out_shape=(flat, flat, flat, jax.ShapeDtypeStruct((plan.length,), BRAIN), single, single),
        in_specs=[smem, vmem, vmem, vmem, vmem],
        out_specs=(vmem, vmem, vmem, vmem, smem, smem),
        scratch_shapes=[pltpu.VMEM((plan.lines * LANES,), FLOAT)],
        compiler_params=pltpu.CompilerParams(vmem_limit_bytes=16 << 20),
    )(step, total, master, first, second)


class Frames:
    def __init__(self, plan, slots, even, odd):
        self.plan, self.slots, self.even, self.odd = plan, slots, even, odd
        self.filled = 0

    def add(self, index):
        plan, even = self.plan, self.even
        if index == plan.first_late:
            rest = plan.border - self.filled
            even[pl.ds(self.filled, rest), :] = jnp.zeros((rest, LANES), FLOAT)
            half_turn(plan, even, self.odd)
            self.filled = plan.border
        frame = self.odd if plan.late(index) else even
        start = plan.base(index) // 8 * 8
        rows = -(-(plan.base(index) - start + plan.used(index)) // 8) * 8
        block = self.slots[(*spot_of(index), pl.ds(0, plan.rows))].astype(FLOAT)
        if start < self.filled:
            frame[pl.ds(start, 8), :] += block[:8]
            frame[pl.ds(start + 8, rows - 8), :] = block[8:rows]
        else:
            frame[pl.ds(start, rows), :] = block[:rows]
        self.filled = start + rows


def half_turn(plan, even, odd):
    total = plan.border - 8
    span = 256

    def turn(start, rows):
        here = pltpu.roll(even[pl.ds(start, rows), :], 64, 1)
        below = pltpu.roll(even[pl.ds(start + 1, rows), :], 64, 1)
        odd[pl.ds(start, rows), :] = jnp.where(lane_iota(rows) < 64, here, below)

    @pl.loop(0, total // span)
    def _(step):
        turn(pl.multiple_of(step * span, span), span)

    if total % span:
        turn(total // span * span, total % span)


def read_param(even, odd, name, target):
    offset, shape = layout()[name]
    rows, width = (1, shape[0]) if len(shape) == 1 else shape
    base, late = divmod(offset, LANES)
    frames = (even, odd) if late == 0 else (odd, even)
    whole, half = divmod(width, LANES)
    kind = target.dtype
    if rows == 1:
        for col in range(whole):
            target[:, pl.ds(col * LANES, LANES)] = frames[0][pl.ds(base + col, 1), :].astype(kind)
        if half:
            tail = frames[0][pl.ds(base + whole, 1), :]
            target[:, pl.ds(whole * LANES, half)] = tail[:, :half].astype(kind)
        return
    if not half:
        for col in range(whole):
            piece = frames[0][pl.ds(base + col, rows, stride=whole), :]
            target[:, pl.ds(col * LANES, LANES)] = piece.astype(kind)
        return
    stride = 2 * width // LANES
    shift = whole + (1 if late else 0)

    def interleave(scratch):
        for col in range(whole + 1):
            size = LANES if col < whole else half
            upper = frames[0][pl.ds(base + col, rows // 2, stride=stride), :]
            lower = frames[1][pl.ds(base + shift + col, rows // 2, stride=stride), :]
            scratch[pl.ds(0, rows // 2, stride=2), :] = upper
            scratch[pl.ds(1, rows // 2, stride=2), :] = lower
            target[:, pl.ds(col * LANES, size)] = scratch[...][:, :size].astype(kind)

    pl.run_scoped(interleave, pltpu.VMEM((rows, LANES), FLOAT))


def write_grad(even, odd, name, value):
    offset, shape = layout()[name]
    rows, width = (1, shape[0]) if len(shape) == 1 else shape
    base, late = divmod(offset, LANES)
    frames = (even, odd) if late == 0 else (odd, even)
    whole, half = divmod(width, LANES)

    def columns():
        for col in range(0, whole, 2):
            size = min(2, whole - col) * LANES
            both = value(col * LANES, size)
            for part in range(size // LANES):
                yield col + part, both[:, part * LANES : (part + 1) * LANES]
        if half:
            tail = value(whole * LANES, half)
            yield whole, jnp.concatenate([tail, jnp.zeros((rows, LANES - half), FLOAT)], axis=1)

    if rows == 1:
        for col, piece in columns():
            frames[0][pl.ds(base + col, 1), :] = piece
        return
    if not half:
        for col, piece in columns():
            frames[0][pl.ds(base + col, rows, stride=whole), :] = piece
        return
    stride = 2 * width // LANES
    shift = whole + (1 if late else 0)

    def interleave(scratch):
        for col, piece in columns():
            scratch[...] = piece
            upper = scratch[pl.ds(0, rows // 2, stride=2), :]
            lower = scratch[pl.ds(1, rows // 2, stride=2), :]
            frames[0][pl.ds(base + col, rows // 2, stride=stride), :] = upper
            frames[1][pl.ds(base + shift + col, rows // 2, stride=stride), :] = lower

    pl.run_scoped(interleave, pltpu.VMEM((rows, LANES), FLOAT))


def clear_frames(plan, even, odd):
    even[...] = jnp.zeros_like(even)
    odd[pl.ds(0, plan.border + 16), :] = jnp.zeros((plan.border + 16, LANES), FLOAT)
    table = layout()
    final = (table["headb"][0] // LANES) // 8 * 8
    odd[pl.ds(final, odd.shape[0] - final), :] = jnp.zeros((odd.shape[0] - final, LANES), FLOAT)


def emit_slots(plan, even, odd, slots, depths):
    rows = plan.rows
    for index in [depth * 8 + number for depth in depths for number in range(8)]:
        start = plan.base(index) // 8 * 8
        if plan.late(index):
            block = odd[pl.ds(start + 8, rows), :]
        else:
            here = pltpu.roll(odd[pl.ds(start + 8, rows), :], 64, 1)
            above = pltpu.roll(odd[pl.ds(start + 7, rows), :], 64, 1)
            block = even[pl.ds(start, rows), :] + jnp.where(lane_iota(rows) < 64, above, here)
        slots[(index // 8, index // 4 % 2, index // 2 % 2, index % 2)] = block.astype(BRAIN)


def dot(left, right, dims=(((1,), (0,)), ((), ()))):
    return lax.dot_general(left, right, dims, preferred_element_type=FLOAT)


def place_table(count, rows, width):
    quarter = width // 4
    omega = 1.0 / 10000.0 ** (np.arange(quarter) / quarter)
    index = np.arange(count)
    across = (index // GRID)[:, None] * omega
    along = (index % GRID)[:, None] * omega
    table = np.zeros((rows, width), np.float32)
    table[:count] = np.concatenate(
        [np.sin(across), np.cos(across), np.sin(along), np.cos(along)], axis=-1
    )
    return table


def split_two(value):
    upper = value.astype(BRAIN)
    return upper, (value - upper.astype(FLOAT)).astype(BRAIN)


def norm_parts(value):
    center = value - jnp.mean(value, axis=-1, keepdims=True)
    spread = lax.rsqrt(jnp.mean(center * center, axis=-1, keepdims=True) + LN_EPS)
    return center * spread, spread


def norm_back(grad, value, gain):
    unit, spread = norm_parts(value)
    d_gain = jnp.sum(grad * unit, axis=0, keepdims=True)
    d_shift = jnp.sum(grad, axis=0, keepdims=True)
    scaled = grad * gain
    middle = jnp.mean(scaled, axis=-1, keepdims=True)
    along = jnp.mean(scaled * unit, axis=-1, keepdims=True)
    return spread * (scaled - middle - unit * along), d_gain, d_shift


def gelu_parts(value):
    half = 0.5 + 0.5 * lax.erf(value * 0.7071067811865476)
    bell = jnp.exp2(value * value * (-0.5 * LOG_TWO_E)) * 0.3989422804014327
    return value * half, half + value * bell


def head_only(value, head, size):
    lane = lax.broadcasted_iota(jnp.int32, value.shape, 1)
    inside = (lane >= head * size) & (lane < (head + 1) * size)
    return jnp.where(inside, value, jnp.zeros_like(value))


def attend(t_ref, chance_ref, stack_ref, usable, width, heads):
    size = width // heads
    rows = t_ref.shape[0]
    query, keys = t_ref[:, pl.ds(0, width)].T, t_ref[:, pl.ds(width, width)]
    values = t_ref[:, pl.ds(2 * width, width)].T
    factor = size ** (-0.5) * LOG_TWO_E
    mixed = []
    for head in range(heads):
        stack_ref[pl.ds(head * rows, rows), :] = head_only(keys, head, size)
    scores = dot(stack_ref[...], query)
    for head in range(heads):
        raw = jnp.where(usable, scores[head * rows : (head + 1) * rows], -1e30)
        top = jnp.max(raw, axis=0, keepdims=True)
        power = jnp.exp2((raw - top) * factor)
        chance = power * (1.0 / jnp.sum(power, axis=0, keepdims=True))
        chance_ref[head] = chance
        mixed.append(dot(values[head * size : (head + 1) * size], chance.astype(BRAIN)))
    return jnp.concatenate(mixed, axis=0).astype(BRAIN).T


def attend_back(d_mixed, t_ref, dt_ref, chance_ref, stack_ref, width, heads):
    size = width // heads
    rows = t_ref.shape[0]
    scale = size ** (-0.5)
    query, keys = t_ref[:, pl.ds(0, width)], t_ref[:, pl.ds(width, width)].T
    values = t_ref[:, pl.ds(2 * width, width)]
    d_query = []
    d_keys = d_values = None
    for head in range(heads):
        stack_ref[pl.ds(head * rows, rows), :] = head_only(values, head, size)
    d_chances = dot(stack_ref[...], d_mixed.T)
    for head in range(heads):
        chance = chance_ref[head]
        d_chance = d_chances[head * rows : (head + 1) * rows]
        along = jnp.sum(chance * d_chance, axis=0, keepdims=True)
        d_scores = (chance * (d_chance - along)).astype(BRAIN)
        part = dot(chance.astype(BRAIN), head_only(d_mixed, head, size))
        d_values = part if d_values is None else d_values + part
        part = dot(d_scores, head_only(query, head, size))
        d_keys = part if d_keys is None else d_keys + part
        d_query.append(dot(keys[head * size : (head + 1) * size], d_scores))
    d_query = (jnp.concatenate(d_query, axis=0) * scale).astype(BRAIN).T
    dt_ref[:, pl.ds(0, width)] = d_query
    dt_ref[:, pl.ds(width, width)] = (d_keys * scale).astype(BRAIN)
    dt_ref[:, pl.ds(2 * width, width)] = d_values.astype(BRAIN)


class Weights:
    def __init__(self, refs):
        self.refs = dict(zip(layout(), refs))

    def __call__(self, name):
        return self.refs[name][...]


def block_open(hidden, keep, weights, prefix):
    width = hidden.shape[1]
    keep["x"][...] = hidden
    unit, unused = norm_parts(hidden)
    normed = (unit * weights(prefix + "ln1g") + weights(prefix + "ln1b")).astype(BRAIN)
    keep["a"][...] = normed
    bias = weights(prefix + "qvb")
    for part in range(3):
        cols = pl.ds(part * width, width)
        value = dot(normed, weights.refs[prefix + "qkv"][:, cols])
        if part != 1:
            value = value + bias[:, (part // 2) * width : (part // 2 + 1) * width]
        keep["t"][:, cols] = value.astype(BRAIN)


def each_group(keep, act):
    count, rows = keep["p"].shape[0], keep["p"].shape[2]
    if count == 1:
        act(0, pl.ds(0, rows))
        return

    @pl.loop(0, count)
    def _(group):
        act(group, pl.ds(pl.multiple_of(group * rows, rows), rows))


def block_middle(hidden, keep, weights, prefix, heads, usable):
    width = hidden.shape[1]

    def mix(group, rows):
        keep["o"][rows, :] = attend(keep["t"].at[rows], keep["p"].at[group], keep["k"], usable, width, heads)

    each_group(keep, mix)
    middle = hidden + (dot(keep["o"][...], weights(prefix + "proj")) + weights(prefix + "projb"))
    keep["m"][...] = middle
    unit, unused = norm_parts(middle)
    second = (unit * weights(prefix + "ln2g") + weights(prefix + "ln2b")).astype(BRAIN)
    keep["b"][...] = second
    inner = dot(second, weights(prefix + "fc1")) + weights(prefix + "fc1b")
    active, slope = gelu_parts(inner)
    keep["s"][...] = slope
    keep["g"][...] = active.astype(BRAIN)


def block_shut(keep, weights, prefix):
    return keep["m"][...] + (dot(keep["g"][...], weights(prefix + "fc2")) + weights(prefix + "fc2b"))


def home_open(grad, keep, weights, prefix):
    d_branch = grad.astype(BRAIN)
    keep["dz"][...] = d_branch
    keep["du"][...] = (dot(d_branch, weights(prefix + "fc2"), PAIR) * keep["s"][...]).astype(BRAIN)


def home_middle(grad, keep, weights, prefix, heads, sums, meanwhile=None):
    width = grad.shape[1]
    d_second = dot(keep["du"][...], weights(prefix + "fc1"), PAIR)
    d_middle, d_gain, d_shift = norm_back(d_second, keep["m"][...], weights(prefix + "ln2g"))
    sums(prefix + "ln2g", d_gain)
    sums(prefix + "ln2b", d_shift)
    d_middle = d_middle + grad
    d_output = d_middle.astype(BRAIN)
    keep["dy"][...] = d_output
    keep["do"][...] = dot(d_output, weights(prefix + "proj"), PAIR).astype(BRAIN)

    def unmix(group, rows):
        if meanwhile is not None:
            meanwhile(group)
        d_mixed = keep["do"][rows, :]
        attend_back(
            d_mixed, keep["t"].at[rows], keep["dt"].at[rows], keep["p"].at[group], keep["k"], width, heads
        )

    each_group(keep, unmix)
    d_normed = dot(keep["dt"][...], weights(prefix + "qkv"), PAIR)
    d_hidden, d_gain, d_shift = norm_back(d_normed, keep["x"][...], weights(prefix + "ln1g"))
    sums(prefix + "ln1g", d_gain)
    sums(prefix + "ln1b", d_shift)
    return d_middle + d_hidden


def kept_shapes(groups, rows, width, hidden, heads):
    every = groups * rows
    return {
        "x": ((every, width), FLOAT),
        "a": ((every, width), BRAIN),
        "t": ((every, 3 * width), BRAIN),
        "p": ((groups, heads, rows, rows), FLOAT),
        "k": ((heads * rows, width), BRAIN),
        "o": ((every, width), BRAIN),
        "m": ((every, width), FLOAT),
        "b": ((every, width), BRAIN),
        "s": ((every, hidden), FLOAT),
        "g": ((every, hidden), BRAIN),
        "dz": ((every, width), BRAIN),
        "du": ((every, hidden), BRAIN),
        "dy": ((every, width), BRAIN),
        "do": ((every, width), BRAIN),
        "dt": ((every, 3 * width), BRAIN),
    }


def kept_scratch(*sizes):
    return [pltpu.VMEM(shape, kind) for shape, kind in kept_shapes(*sizes).values()]


def kept_view(refs):
    return dict(zip(kept_shapes(1, 1, 1, 1, 1), refs))


LAYERS = {
    "fc2": ("g", "dz", "fc2b"),
    "fc1": ("b", "du", "fc1b"),
    "proj": ("o", "dy", "projb"),
    "qkv": ("a", "dt", "qvb"),
}


def block_grads(keep, prefix, names, emit):
    for name in names:
        left, right, bias = LAYERS[name]
        emit(prefix + name, prefix + bias, keep[left][...], keep[right][...])


NORMS = ("ln1g", "ln1b", "ln2g", "ln2b", "encg", "encb", "decg", "decb", "mask")


class Images:
    def __init__(self, place, counts_ref, meta_ref):
        spot = place["B"] * 2 + place["C"]
        self.meta_ref = meta_ref
        self.own = counts_ref[0, 0]
        lane = lane_iota(8)
        row = lax.broadcasted_iota(jnp.int32, (8, LANES), 0)

        def count_of(hub):
            corner = jnp.where((lane == LANES - 1) & (row == 0), meta_ref[hub], 0.0)
            return jnp.sum(corner).astype(jnp.int32)

        one, two = count_of(1), count_of(2)
        from_one = jnp.where(spot == 0, 3, jnp.where(spot == 2, 4, 5))
        from_two = jnp.where(spot == 0, 3, jnp.where(spot == 1, 4, 5))
        use_one = (spot == 2) | ((spot != 1) & (one > 2))
        mine = self.own > 2

        def choose(own, first, second):
            return jnp.where(mine, own, jnp.where(use_one, first, second))

        self.third = choose(2, 3, 4)
        self.third_row = choose(2, from_one, from_two)
        self.third_count = choose(self.own, one, two)
        self.third_meta = choose(0, 1, 2)

    def __call__(self, image):
        last = image == 2
        source = jnp.where(last, self.third, image)
        line = jnp.where(last, self.third_row, image)
        live = jnp.where(last, self.third_count, self.own) > line
        kept = self.meta_ref[jnp.where(last, self.third_meta, 0), pl.ds(line, 1), :][:, :HOME]
        return source, kept, live.astype(FLOAT)


def placement(kept, rows):
    number = lax.broadcasted_iota(jnp.int32, (rows, HOME), 0).astype(FLOAT)
    return (number == kept).astype(FLOAT)


def whole_body(
    plan, counts_ref, keep_ref, x_ref, patches_ref, targets_ref, enc_table, dec_table,
    total_out, *scratch
):
    scratch = list(scratch)

    def take(count):
        taken = scratch[:count]
        del scratch[:count]
        return taken

    names = list(layout())
    slots, seen_ref, tgt_own, tgt_ref, meta_ref, grad_ref, loss_ref = take(7)
    spot_enc, spot_dec, local = take(3)
    line, rolled, pixels, spare, send, recv, hand, taken = take(8)
    even, odd, grad_even, grad_odd, sums_ref, y_hi, y_lo, dy_home, final_all, dpred_all = take(10)
    weights = Weights(take(len(names)))
    enc_refs, dec_refs = take(15), take(15)
    core_in, tree_in, column_in, own_ref, near, far, mine = take(7)
    spread_send, spread_recv, column_send, column_recv = take(4)

    place = position()
    device = index_of(place)
    copies = [
        pltpu.make_async_copy(patches_ref, pixels, local.at[0]),
        pltpu.make_async_copy(enc_table, spot_enc, local.at[1]),
        pltpu.make_async_copy(dec_table, spot_dec, local.at[2]),
        pltpu.make_async_copy(
            targets_ref.at[pl.ds(0, LIVE_CAP - 1)], tgt_own, local.at[3]
        ),
        pltpu.make_async_copy(targets_ref.at[LIVE_CAP - 1], tgt_ref.at[0], local.at[4]),
    ]
    for copy in copies:
        copy.start()
    slots[(place["H"], place["L"], place["B"], place["C"], place["r"])] = own_block(
        plan, device, x_ref, line, rolled
    )
    meet(gates(place, plan))
    sender = Sender(send, recv)
    handing = Handing(place, spare, seen_ref, meta_ref, targets_ref, tgt_ref, hand, taken)

    def choose_images():
        lane = lane_iota(8)
        row = lax.broadcasted_iota(jnp.int32, (8, LANES), 0)
        held = counts_ref[0, 0].astype(FLOAT)
        meta_ref[0] = jnp.where((lane == LANES - 1) & (row == 0), held, -1.0)
        meta_ref[0, pl.ds(0, keep_ref.shape[0]), pl.ds(0, VIS)] = keep_ref[...].astype(FLOAT)
        copies[0].wait()

        def visible(image):
            where = placement(meta_ref[0, pl.ds(image, 1), :][:, :HOME], NP).astype(BRAIN)
            return dot(where, pixels[image], DEEP).astype(BRAIN)

        def prepare(hub):
            for number in range(3):
                spare[number] = visible(3 + number)

        handing.on_hub(prepare)
        handing.start((0, 1))
        for image in range(LIVE_CAP):
            seen_ref[image] = visible(image)
        clear_frames(plan, grad_even, grad_odd)
        sums_ref[...] = jnp.zeros_like(sums_ref)

    early = min(-(-layout()["dec_qkv"][0] // (16 * plan.length)), plan.outer)
    first_values, last_values = range(early), range(early, plan.outer)
    gather = Gather(plan, place, slots, sender, (spread_send, spread_recv))
    frames = Frames(plan, slots, even, odd)

    def spread(values, reach):
        for value in values:
            gather.stage(value, reach)

    def fetch(values, wanted_names):
        for value in values:
            gather.ready(value)
            for index in range(value * 16, value * 16 + 16):
                frames.add(index)
        for name in wanted_names:
            read_param(even, odd, name, weights.refs[name])

    gather.begin()
    gather.roots(choose_images)
    for reach in (0, 1):
        spread(first_values, reach)
        spread(last_values, reach)
    handing.receive((0, 1))
    for copy in copies[1:]:
        copy.wait()
    pick = Images(place, counts_ref, meta_ref)
    visible, begin, wheres, seens, lives = [], [], [], [], []
    for image in range(LIVE_CAP):
        source, kept, live = pick(image)
        where = placement(kept, ROWS)
        wheres.append(where.astype(BRAIN))
        seens.append(jnp.sum(where, axis=1, keepdims=True))
        lives.append(live)
        visible.append(seen_ref[source])
        begin.append(dot(wheres[image], spot_enc[0], DEEP) + dot(wheres[image], spot_enc[1], DEEP))
    visible = jnp.concatenate(visible, axis=0)
    begin = jnp.concatenate(begin, axis=0)
    spread(first_values, 2)
    spread(last_values, 2)
    handing.start((2,))
    divide = names.index("dec_qkv")
    fetch(first_values, names[:divide])
    order = {name: number for number, name in enumerate(names)}

    def add_sum(name, value):
        sums_ref[pl.ds(order[name], 1), pl.ds(0, value.shape[1])] += value

    enc_rows = LIVE_CAP * HOME
    enc = kept_view(enc_refs)
    down = lax.broadcasted_iota(jnp.int32, (enc_rows, enc_rows), 0)
    over = lax.broadcasted_iota(jnp.int32, (enc_rows, enc_rows), 1)
    usable = (down // HOME == over // HOME) & (down % HOME < VIS)
    first_in = dot(visible, weights("patch")) + weights("patchb") + begin
    block_open(first_in, enc, weights, "enc_")
    block_middle(first_in, enc, weights, "enc_", HEADS, usable)
    encoded = block_shut(enc, weights, "enc_")
    unit, unused = norm_parts(encoded)
    encoder_out = (unit * weights("encg") + weights("encb")).astype(BRAIN)
    embedded = dot(encoder_out, weights("embed")) + weights("embedb")
    upper, lower = split_two(embedded)
    for image in range(LIVE_CAP):
        y_hi[image] = upper[image * HOME : (image + 1) * HOME]
        y_lo[image] = lower[image * HOME : (image + 1) * HOME]
    fetch(last_values, names[divide:])
    view = grad_odd.at[pl.ds(8, plan.frame_rows)]
    real = lax.broadcasted_iota(jnp.int32, (ROWS, 1), 0) < NP
    usable_dec = lax.broadcasted_iota(jnp.int32, (ROWS, ROWS), 0) < NP

    dec = kept_view(dec_refs)
    dec_rows = [pl.ds(image * ROWS, ROWS) for image in range(LIVE_CAP)]
    def unseen(image):
        return 1.0 - seens[image]

    grid_in = []
    for image in range(LIVE_CAP):
        where = wheres[image]
        value = dot(where, y_hi[image]) + dot(where, y_lo[image])
        grid_in.append(value + unseen(image) * weights("mask") + spot_dec[...])
    grid_in = jnp.concatenate(grid_in, axis=0)
    block_open(grid_in, dec, weights, "dec_")
    block_middle(grid_in, dec, weights, "dec_", DHEADS, usable_dec)
    decoded = block_shut(dec, weights, "dec_")
    unit, unused = norm_parts(decoded)
    final_all[...] = (unit * weights("decg") + weights("decb")).astype(BRAIN)
    handing.receive((2,))
    total = jnp.zeros((1, PIX), FLOAT)
    for image in range(LIVE_CAP):
        predicted = dot(final_all[dec_rows[image], :], weights("head")) + weights("headb")
        weight = jnp.where(real, (1.0 - 0.9 * seens[image]) * lives[image], 0.0)
        wanted = tgt_ref[pick.third - 2] if image == LIVE_CAP - 1 else tgt_own[image]
        error = predicted[:NP] - wanted.astype(FLOAT)
        weighted = error * weight[:NP]
        total = total + jnp.sum(weighted * error, axis=0, keepdims=True)
        dpred_all[pl.ds(image * ROWS, NP), :] = (weighted * (2.0 / PIX)).astype(BRAIN)
        dpred_all[pl.ds(image * ROWS + NP, ROWS - NP), :] = jnp.zeros((ROWS - NP, PIX), BRAIN)
    d_final = dot(dpred_all[...], weights("head"), PAIR)
    d_decoded, d_gain, d_shift = norm_back(d_final, decoded, weights("decg"))
    add_sum("decg", d_gain)
    add_sum("decb", d_shift)
    home_open(d_decoded, dec, weights, "dec_")
    loss_ref[0] = jnp.sum(total) * (1.0 / PIX)

    def emit(name, bias, left, right):
        ones = jnp.ones((16, right.shape[0]), BRAIN)
        summed = dot(ones, right)[0:1]
        if bias.endswith("qvb"):
            width = summed.shape[1] // 3
            summed = jnp.concatenate([summed[:, :width], summed[:, 2 * width :]], axis=1)
        write_grad(grad_even, view, bias, lambda start, size: summed[:, start : start + size])
        turned = left.T
        write_grad(grad_even, view, name, lambda start, size: dot(turned, right[:, start : start + size]))

    def emit_norms(wanted_names):
        for name in wanted_names:
            row = pl.ds(order[name], 1)
            write_grad(grad_even, view, name, lambda start, size, row=row: sums_ref[row, pl.ds(start, size)])

    reducer = Reducer(
        plan, place, grad_ref, core_in, tree_in, column_in, own_ref, sender, (column_send, column_recv)
    )
    floors = [plan.depths_from(name) for name in ("dec_fc2", "embed", "enc_fc1")]
    waves = [range(low, high) for low, high in zip(floors + [0], [plan.depths] + floors)]

    def leave(wave):
        emit_slots(plan, grad_even, grad_odd, grad_ref, waves[wave])
        for depth in waves[wave]:
            reducer.share(depth)

    def collect(wave, reach):
        for depth in waves[wave]:
            reducer.stage(depth, reach)

    emit("head", "headb", final_all[...], dpred_all[...])
    block_grads(dec, "dec_", ("fc2",), emit)
    emit_norms(("decg", "decb"))
    leave(0)
    block_grads(dec, "dec_", ("fc1",), emit)

    def meanwhile(group):
        @pl.when(group == 1)
        def _():
            collect(0, 1)

        @pl.when(group == 2)
        def _():
            collect(0, 0)

    d_grid = home_middle(d_decoded, dec, weights, "dec_", DHEADS, add_sum, meanwhile)
    d_mask = jnp.zeros((1, E), FLOAT)
    for image in range(LIVE_CAP):
        part = d_grid[image * ROWS : (image + 1) * ROWS]
        d_mask = d_mask + jnp.sum(unseen(image) * part, axis=0, keepdims=True)
        dy_home[image] = dot(wheres[image], part.astype(BRAIN), DEEP).astype(BRAIN)
    add_sum("mask", d_mask)
    collect(0, -1)
    block_grads(dec, "dec_", ("proj", "qkv"), emit)
    d_embedded = dy_home[...].reshape(enc_rows, E)
    emit("embed", "embedb", encoder_out, d_embedded)
    emit_norms(("mask", "dec_ln1g", "dec_ln1b", "dec_ln2g", "dec_ln2b"))
    leave(1)

    d_seen = dot(d_embedded, weights("embed"), PAIR).astype(BRAIN).astype(FLOAT)
    d_encoded, d_gain, d_shift = norm_back(d_seen, encoded, weights("encg"))
    add_sum("encg", d_gain)
    add_sum("encb", d_shift)
    home_open(d_encoded, enc, weights, "enc_")
    block_grads(enc, "enc_", ("fc2", "fc1"), emit)
    emit_norms(("encg", "encb"))
    collect(1, 1)
    leave(2)
    d_first = home_middle(d_encoded, enc, weights, "enc_", HEADS, add_sum).astype(BRAIN)
    collect(2, 1)
    collect(1, 0)
    emit("patch", "patchb", visible, d_first)
    block_grads(enc, "enc_", ("proj", "qkv"), emit)
    emit_norms(("enc_ln1g", "enc_ln1b", "enc_ln2g", "enc_ln2b"))
    leave(3)
    collect(2, 0)
    collect(1, -1)
    collect(3, 1)
    collect(2, -1)
    collect(3, 0)
    collect(3, -1)
    reducer.finish()
    pending = finish_body(
        plan, place, counts_ref, loss_ref, own_ref, total_out, rolled, near, far, mine, sender
    )
    gather.close()
    reducer.close()
    handing.finish((0, 1, 2))
    for copy in pending:
        copy.wait_send()


def weight_scratch():
    shapes = []
    for name, (offset, shape) in layout().items():
        if len(shape) == 1:
            shapes.append(pltpu.VMEM((1, *shape), FLOAT))
        else:
            shapes.append(pltpu.VMEM(shape, BRAIN))
    return shapes


def copies_used(plan):
    spread = len(plan.parts) * plan.outer * (7 + 4)
    home = len(plan.halves) * plan.depths * (1 + 3)
    return spread + home + 7 + plan.depths


def whole_step(counts, keep, master, patches, targets, plan):
    outer, depths, rows, lines = plan.outer, plan.depths, plan.rows, plan.lines
    vmem = pl.BlockSpec(memory_space=pltpu.VMEM)
    smem = pl.BlockSpec(memory_space=pltpu.SMEM)
    far = pl.BlockSpec(memory_space=pl.ANY)
    table = place_table(NP, ROWS, D)
    upper = table.astype(BRAIN)
    spot_enc = jnp.asarray(np.stack([upper, (table - upper.astype(np.float32)).astype(BRAIN)]))
    spot_dec = jnp.asarray(place_table(NP, ROWS, E))
    block = pltpu.VMEM((outer, 2, 2, 2, 2, rows, LANES), BRAIN)
    dma = pltpu.SemaphoreType.DMA
    copies = copies_used(plan)
    return pl.pallas_call(
        functools.partial(whole_body, plan),
        out_shape=jax.ShapeDtypeStruct((lines + 8, LANES), FLOAT),
        in_specs=[smem, vmem, vmem, far, far, far, far],
        out_specs=vmem,
        scratch_shapes=[
            block,
            pltpu.VMEM((5, HOME, PIX), BRAIN),
            pltpu.VMEM((LIVE_CAP - 1, NP, PIX), BRAIN),
            pltpu.VMEM((3, NP, PIX), BRAIN),
            pltpu.VMEM((3, 8, LANES), FLOAT),
            pltpu.VMEM((depths, 2, 2, 2, rows, LANES), BRAIN),
            pltpu.SMEM((1,), FLOAT),
            pltpu.VMEM(spot_enc.shape, BRAIN),
            pltpu.VMEM(spot_dec.shape, FLOAT),
            dma((5,)),
            pltpu.VMEM((lines * LANES,), FLOAT),
            pltpu.VMEM((rows + 8, LANES), FLOAT),
            pltpu.VMEM(patches.shape, BRAIN),
            pltpu.VMEM((3, HOME, PIX), BRAIN),
            dma((copies,)),
            dma((copies,)),
            dma((2, 3, 3)),
            dma((2, 3)),
            pltpu.VMEM((plan.border + 8, LANES), FLOAT),
            pltpu.VMEM((plan.frame_rows, LANES), FLOAT),
            pltpu.VMEM((plan.border + rows, LANES), FLOAT),
            pltpu.VMEM((plan.frame_rows + 8, LANES), FLOAT),
            pltpu.VMEM((48, E), FLOAT),
            pltpu.VMEM((LIVE_CAP, HOME, E), BRAIN),
            pltpu.VMEM((LIVE_CAP, HOME, E), BRAIN),
            pltpu.VMEM((LIVE_CAP, HOME, E), BRAIN),
            pltpu.VMEM((LIVE_CAP * ROWS, E), BRAIN),
            pltpu.VMEM((LIVE_CAP * ROWS, PIX), BRAIN),
            *weight_scratch(),
            *kept_scratch(1, LIVE_CAP * HOME, D, FF, HEADS),
            *kept_scratch(LIVE_CAP, ROWS, E, DFF, DHEADS),
            pltpu.VMEM((depths, 2, 2, rows, LANES), BRAIN),
            pltpu.VMEM((depths, 3, rows, LANES), BRAIN),
            pltpu.VMEM((depths, rows, LANES), BRAIN),
            pltpu.VMEM((rows, LANES), FLOAT),
            pltpu.VMEM((8, 8, LANES), FLOAT),
            pltpu.VMEM((depths, 8, LANES), FLOAT),
            pltpu.VMEM((2, 8, LANES), FLOAT),
            dma((outer, len(plan.parts))),
            dma((outer, len(plan.parts))),
            dma((depths, len(plan.halves))),
            dma((depths, len(plan.halves))),
        ],
        compiler_params=pltpu.CompilerParams(
            collective_id=0, has_side_effects=True, vmem_limit_bytes=62 << 20
        ),
    )(counts, keep, master, patches, targets, spot_enc, spot_dec)


def on_device(patches, targets, keep, counts, step, master, first, second):
    plan = Plan(master.shape[0], lax.axis_size(("dp", "rep")))
    total = whole_step(counts, keep, master, patches, targets, plan)
    outs = update(step, total, master, first, second, plan)
    return (*outs[:4], outs[4].reshape(()), outs[5].reshape(()))


def solution(mesh):
    return jax.shard_map(
        on_device,
        mesh=mesh,
        in_specs=(
            P(("dp", "rep"), None, None),
            P(("dp", "rep"), None, None),
            P(("dp", "rep"), None),
            P("dp", "rep"),
            P(),
            P(("dp", "rep")),
            P(("dp", "rep")),
            P(("dp", "rep")),
        ),
        out_specs=(
            P(("dp", "rep")),
            P(("dp", "rep")),
            P(("dp", "rep")),
            P(("dp", "rep")),
            P(),
            P(),
        ),
        check_vma=False,
    )
```
